256 devices in a mesh: across: 4 (over x), along: 8 (over z), gas: 8 (over y, core).
Axes of the slice: x: 4, y: 4, z: 8, core: 2. Of those that a mesh axis runs over, the one named last changes fastest.
Arguments:
- gas_vel: float32 [2, 2048, 1024], P(None, ('along', 'gas'), 'across'), may hold values from -0.5 to 1.5
- viscosity: float32 [2048, 1024], P(('along', 'gas'), 'across'), may hold values from 0.05 to 0.5
- positions: float32 [2, 128, 64, 128], P(None, 'along', ('across', 'gas')), may hold values from 0 to 1
- velocities: float32 [2, 128, 64, 128], P(None, 'along', ('across', 'gas')), may hold values from -4 to 4
- radius: float32 [128, 64, 128], P('along', ('across', 'gas')), may hold values from 0.5 to 0.9
- drag_coef: float32 [128, 64, 128], P('along', ('across', 'gas')), may hold values from 0.5 to 4
- counts: int32 [128, 64], P('along', ('across', 'gas')), may hold values from 16 to 128
- pattern: int32 [128, 64, 9], P('along', ('across', 'gas')), may hold values 0 or 1
- cell_index: int32 [128, 64, 128], P('along', ('across', 'gas')), may hold values from 0 to 238, as said below
- cell_frac: int32 [2, 128, 64, 128], P(None, 'along', ('across', 'gas')), may hold values from 0 to 1024
Outputs:
- particles_out: float32 [4, 128, 64, 128], P(None, 'along', ('across', 'gas'))
- gas_out: float32 [2, 2048, 1024], P(None, ('along', 'gas'), 'across')
The draws below stay inside these ranges and needn't reach their ends.
Inputs may be any that keep to these rules, and one draw needn't show every extreme that they name: `cell_index`: row*16 + col with row and col each from 0 to 14.
All inputs are finite; a program needn't handle non-finite values. Where the reference program divides by a largest or mean magnitude, that divisor is 1e-20 or more. No bound on the sum of `pattern` on one device may be relied on, other than what follows from the above.
Results may differ from the reference program's by a relative error of at most 0.0003.
Values sent between devices are 32-bit elements; how exact they have to be, the bound alone decides.
A program may use at most 64 MiB of HBM per device.

```python
import math
import jax
import jax.numpy as jnp
from jax import lax

SLOTS = 128
CELL_EDGE = 16
GRID_TILES_Z = 128
GRID_TILES_X = 64
GRID_Z = 2048
GRID_X = 1024


def draw_cell_index(key, part):
    key_row = jax.random.fold_in(key, 11)
    key_col = jax.random.fold_in(key, 12)
    shape = (GRID_TILES_Z, GRID_TILES_X, SLOTS)
    row_pick = jax.random.randint(key_row, shape, 0, CELL_EDGE - 1)
    col_pick = jax.random.randint(key_col, shape, 0, CELL_EDGE - 1)
    return (row_pick * CELL_EDGE + col_pick).astype(jnp.int32)


def with_ends(array, stream_key, smallest, largest):
    index_at = [jax.random.randint(jax.random.fold_in(stream_key, axis), (), 0, length) for axis, length in enumerate(array.shape)]
    widest = array.shape.index(max(array.shape))
    beside = index_at[:widest] + [(index_at[widest] + 1) % array.shape[widest]] + index_at[widest + 1:]
    return array.at[tuple(index_at)].set(smallest).at[tuple(beside)].set(largest)


def shard_levels(own_key, extent, cuts, least, high):
    loudness = 1.0
    for axis_at, shards_of in cuts:
        draws = jax.random.uniform(jax.random.fold_in(jax.random.fold_in(own_key, 6), axis_at), (shards_of,), jnp.float32, least / len(cuts), high / len(cuts))
        loudness = loudness * jnp.repeat(jnp.exp(draws), extent[axis_at] // shards_of).reshape((-1,) + (1,) * (len(extent) - 1 - axis_at))
    return loudness


def normal_values(own_key, extent, scale, bound, shards=(), kind=jnp.bfloat16):
    drawn = jax.random.normal(own_key, extent, jnp.float32) * scale
    if len(shards) > 0:
        drawn = shard_levels(own_key, extent, shards, -0.22, 0.18) * drawn
    return jnp.clip(drawn, min=-bound, max=bound).astype(kind)


def setup_inputs(seed: int = 0) -> dict:
    key_list = jax.random.split(jax.random.key(seed), 11)
    return {
        "gas_vel": jnp.clip(-0.5 + 2.0 * jax.random.uniform(key_list[0], (2, GRID_Z, GRID_X), jnp.float32) ** shard_levels(key_list[0], (2, GRID_Z, GRID_X), ((1, 64), (2, 4)), -0.2, 0.2), -0.5, 1.5),
        "viscosity": jnp.clip(jnp.exp(math.log(0.5) - 2.3025851 * jax.random.uniform(key_list[1], (GRID_Z, GRID_X), jnp.float32) ** shard_levels(key_list[1], (GRID_Z, GRID_X), ((0, 64), (1, 4)), -0.2, 0.2)), 0.05, 0.5),
        "positions": jnp.clip(1.0 * jax.random.uniform(key_list[2], (2, GRID_TILES_Z, GRID_TILES_X, SLOTS), jnp.float32) ** shard_levels(key_list[2], (2, GRID_TILES_Z, GRID_TILES_X, SLOTS), ((1, 8), (2, 32)), -0.2, 0.2), 0.0, 1.0),
        "velocities": normal_values(key_list[3], (2, GRID_TILES_Z, GRID_TILES_X, SLOTS), 1.0, 4.0, ((1, 8), (2, 32)), jnp.float32),
        "radius": jnp.clip(0.5 + 0.39999998 * jax.random.uniform(key_list[4], (GRID_TILES_Z, GRID_TILES_X, SLOTS), jnp.float32) ** shard_levels(key_list[4], (GRID_TILES_Z, GRID_TILES_X, SLOTS), ((0, 8), (1, 32)), -0.2, 0.2), 0.5, 0.9),
        "drag_coef": jnp.clip(jnp.exp(math.log(4.0) - 2.0794415 * jax.random.uniform(key_list[5], (GRID_TILES_Z, GRID_TILES_X, SLOTS), jnp.float32) ** shard_levels(key_list[5], (GRID_TILES_Z, GRID_TILES_X, SLOTS), ((0, 8), (1, 32)), -0.2, 0.2)), 0.5, 4.0),
        "counts": with_ends(jax.random.randint(key_list[6], (GRID_TILES_Z, GRID_TILES_X), 16, 129), jax.random.fold_in(key_list[6], 1), 16, 128).astype(jnp.int32),
        "pattern": with_ends((jax.random.randint(key_list[7], (GRID_TILES_Z, GRID_TILES_X, 9), 0, 4) < 3).astype(jnp.int32), jax.random.fold_in(key_list[7], 1), 0, 1),
        "cell_index": draw_cell_index(jax.random.fold_in(key_list[10], 71), 0),
        "cell_frac": with_ends(jax.random.randint(key_list[9], (2, GRID_TILES_Z, GRID_TILES_X, SLOTS), 0, 1025), jax.random.fold_in(key_list[9], 1), 0, 1024).astype(jnp.int32),
    }


offsets = [(-1, -1), (-1, 0), (-1, 1), (0, -1), (0, 0), (0, 1), (1, -1), (1, 0), (1, 1)]
stiffness = 40.0
damping = 2.0
gravity = 1.0
courant = 0.4
softening = 0.0001
density = 0.36
frac_unit = 1024.0

def contact(extended, tile_mask, cell_edge):
    tile_rows = tile_mask.shape[0]
    tile_cols = tile_mask.shape[1]
    centre = extended[:, 1:1 + tile_rows, 1:1 + tile_cols]
    mine = centre[..., :, None]
    forces_z = jnp.zeros(centre.shape[1:], jnp.float32)
    forces_x = jnp.zeros(centre.shape[1:], jnp.float32)
    for neighbour, (shift_z, shift_x) in enumerate(offsets):
        partner = extended[:, 1 + shift_z:1 + shift_z + tile_rows, 1 + shift_x:1 + shift_x + tile_cols][..., None, :]
        apart_z = mine[0] - partner[0] - shift_z * cell_edge
        apart_x = mine[1] - partner[1] - shift_x * cell_edge
        distance = jnp.sqrt(apart_z * apart_z + apart_x * apart_x + softening)
        depth = jnp.maximum(mine[4] + partner[4] - distance, 0.0)
        closing = ((mine[2] - partner[2]) * apart_z + (mine[3] - partner[3]) * apart_x) / distance
        strength = depth * (stiffness - damping * closing) / distance * (mine[5] * partner[5]) * tile_mask[:, :, neighbour][:, :, None, None]
        forces_z = forces_z + lax.optimization_barrier(jnp.sum(strength * apart_z, axis=-1))
        forces_x = forces_x + lax.optimization_barrier(jnp.sum(strength * apart_x, axis=-1))
    return (forces_z, forces_x)

def update(centre, coupling, forces_z, forces_x, sub_step):
    alive_mask = centre[5]
    inverse = alive_mask * density / (centre[4] * centre[4] + 1.0 - alive_mask)
    drag_z = coupling[2] * (coupling[0] - centre[2])
    drag_x = coupling[2] * (coupling[1] - centre[3])
    speed_z = centre[2] + sub_step * (inverse * (forces_z + drag_z) - gravity * alive_mask)
    speed_x = centre[3] + sub_step * (inverse * (forces_x + drag_x))
    moved = jnp.stack([centre[0] + sub_step * speed_z, centre[1] + sub_step * speed_x, speed_z, speed_x, centre[4], alive_mask])
    return (moved, jnp.stack([alive_mask * drag_z, alive_mask * drag_x]))

def stencil(cell_index, cell_frac, cell_edge):
    share_z = cell_frac[0].astype(jnp.float32) / frac_unit
    share_x = cell_frac[1].astype(jnp.float32) / frac_unit
    cell_ids = jnp.arange(cell_edge * cell_edge, dtype=jnp.int32)
    corner = cell_index[..., None]
    result = ((1.0 - share_z) * (1.0 - share_x))[..., None] * (cell_ids == corner).astype(jnp.float32)
    result = result + (share_z * (1.0 - share_x))[..., None] * (cell_ids == corner + cell_edge).astype(jnp.float32)
    result = result + ((1.0 - share_z) * share_x)[..., None] * (cell_ids == corner + 1).astype(jnp.float32)
    result = result + (share_z * share_x)[..., None] * (cell_ids == corner + cell_edge + 1).astype(jnp.float32)
    return result

def to_tiles(field, tiles_z, tiles_x, cell_edge):
    shaped = field.reshape(2, tiles_z, cell_edge, tiles_x, cell_edge).transpose(0, 1, 3, 2, 4)
    return shaped.reshape(2, tiles_z, tiles_x, cell_edge * cell_edge)

def to_cells(tiles, tiles_z, tiles_x, cell_edge):
    shaped = tiles.reshape(2, tiles_z, tiles_x, cell_edge, cell_edge).transpose(0, 1, 3, 2, 4)
    return shaped.reshape(2, tiles_z * cell_edge, tiles_x * cell_edge)

def gas_update(velocity, viscosity, padded_rows, padded_cols, source, gas_step):
    upper_row = padded_rows[:, 2:]
    lower_row = padded_rows[:, :-2]
    right_col = padded_cols[:, :, 2:]
    left_col = padded_cols[:, :, :-2]
    laplace = upper_row + lower_row + right_col + left_col - 4.0 * velocity
    advect = velocity[0:1] * (upper_row - lower_row) * 0.5 + velocity[1:2] * (right_col - left_col) * 0.5
    return velocity + gas_step * (viscosity[None] * laplace - advect + source)

def pad_tiles(particle_state):
    wrapped = jnp.concatenate([particle_state[:, -1:], particle_state, particle_state[:, :1]], axis=1)
    return jnp.pad(wrapped, ((0, 0), (0, 0), (1, 1), (0, 0)))

def reference(gas_vel, viscosity, positions, velocities, radius, drag_coef, counts, pattern, cell_index, cell_frac):
    global_rate = jnp.max(jnp.abs(gas_vel[0]) + jnp.abs(gas_vel[1]) + 4.0 * viscosity)
    gas_step = courant / global_rate
    sub_step = 0.5 * gas_step
    tile_velocity = to_tiles(gas_vel, GRID_TILES_Z, GRID_TILES_X, CELL_EDGE)
    row_ids = jnp.arange(GRID_TILES_Z, dtype=jnp.int32)

    def sample_row(tile_row):
        weights = stencil(cell_index[tile_row], cell_frac[:, tile_row], CELL_EDGE)
        return jnp.einsum('tpc,ktc->ktp', weights, tile_velocity[:, tile_row], precision=lax.Precision.HIGHEST)
    interp = lax.map(sample_row, row_ids).transpose(1, 0, 2, 3)
    alive_mask = (jnp.arange(SLOTS, dtype=jnp.int32)[None, None, :] < counts[:, :, None]).astype(jnp.float32)
    particle_state = jnp.stack([positions[0] * CELL_EDGE, positions[1] * CELL_EDGE, velocities[0], velocities[1], radius, alive_mask])
    coupling = jnp.stack([interp[0], interp[1], drag_coef])
    tile_mask = pattern.astype(jnp.float32)
    drag_sum = jnp.zeros((2, GRID_TILES_Z, GRID_TILES_X, SLOTS), jnp.float32)
    for substep in range(2):
        extended = pad_tiles(particle_state)

        def row_force(tile_row):
            window = lax.dynamic_slice_in_dim(extended, tile_row, 3, 1)
            return contact(window, lax.dynamic_slice_in_dim(tile_mask, tile_row, 1, 0), CELL_EDGE)
        forces_z, forces_x = lax.map(row_force, row_ids)
        particle_state, drag = update(particle_state, coupling, forces_z[:, 0], forces_x[:, 0], sub_step)
        drag_sum = drag_sum + drag
    mean_drag = 0.5 * drag_sum
    summed = lax.optimization_barrier(jnp.sum(mean_drag, axis=(1, 2, 3)))

    def spread_row(tile_row):
        weights = stencil(cell_index[tile_row], cell_frac[:, tile_row], CELL_EDGE)
        return jnp.einsum('tpc,ktp->ktc', weights, mean_drag[:, tile_row], precision=lax.Precision.HIGHEST)
    deposit = lax.map(spread_row, row_ids).transpose(1, 0, 2, 3)
    deposit_cells = to_cells(deposit, GRID_TILES_Z, GRID_TILES_X, CELL_EDGE)
    source = summed[:, None, None] / (GRID_Z * GRID_X) - deposit_cells
    padded_rows = jnp.concatenate([gas_vel[:, -1:], gas_vel, gas_vel[:, :1]], axis=1)
    padded_cols = jnp.pad(gas_vel, ((0, 0), (0, 0), (1, 1)))
    gas_out = gas_update(gas_vel, viscosity, padded_rows, padded_cols, source, gas_step)
    particles_out = jnp.stack([particle_state[0] / CELL_EDGE, particle_state[1] / CELL_EDGE, particle_state[2], particle_state[3]])
    return (particles_out, gas_out)
```

```python
import functools

import jax
import jax.numpy as jnp
from jax import lax
from jax.experimental import pallas as pl
from jax.experimental.pallas import tpu as pltpu
from jax.sharding import PartitionSpec as P

ALONG_GAS = ("along", "gas")
ACROSS_GAS = ("across", "gas")
MESH_ID = pl.DeviceIdType.MESH
OFFSETS = [(-1, -1), (-1, 0), (-1, 1), (0, -1), (0, 0), (0, 1), (1, -1), (1, 0), (1, 1)]
DEAD = -16384.0
F32 = jnp.float32
BF16 = jnp.bfloat16
VMEM_SPEC = pl.BlockSpec(memory_space=pltpu.VMEM)
SMEM_SPEC = pl.BlockSpec(memory_space=pltpu.SMEM)
N_ACROSS, N_ALONG, N_GAS = 4, 8, 8


def iota(shape, dim):
    return lax.broadcasted_iota(jnp.int32, shape, dim)


def ext_row(ii, jj):
    base = {-1: 32, 0: 0, 1: 16, 2: 48}[jj]
    return jnp.where(ii < 0, 64 + 8 * (jj + 1) + 7, jnp.where(ii > 15, 96 + 8 * (jj + 1), base + ii))


def prep_kernel(gas, visc, pos, vel, rad, counts, st, gp, mx):
    rate = jnp.abs(gas[0]) + jnp.abs(gas[1]) + 4.0 * visc[...]
    top = jnp.max(jnp.max(rate, axis=1, keepdims=True), axis=0, keepdims=True)
    mx[...] = jnp.broadcast_to(top, (8, 128))
    lane = iota((16, 128), 1)
    for g in range(N_GAS):
        blk = slice((g // 4) * 128, (g // 4) * 128 + 128)
        off = (g % 4) * 32
        for k in range(2):
            low = gas[k, 0:16, blk]
            high = gas[k, 16:32, blk]
            low = pltpu.roll(low, (128 - off) % 128, 1) if off else low
            shift = (160 - off) % 128
            high = pltpu.roll(high, shift, 1) if shift else high
            piece = jnp.where(lane < 32, low, jnp.where(lane < 64, high, 0.0))
            gp[g, k * 16:(k + 1) * 16, :] = piece
    lane32 = iota((16, 128), 1)
    row16 = iota((16, 128), 0)
    for j in range(2):
        rows = slice(j * 16, (j + 1) * 16)
        take = pl.ds(j, 16, stride=2)
        cnt = jnp.zeros((16, 128), jnp.int32)
        for i in range(16):
            cnt = jnp.where(row16 == i, counts[j, i], cnt)
        st[0, rows, :] = pos[0, take, :] * 16.0
        st[1, rows, :] = pos[1, take, :] * 16.0
        st[2, rows, :] = vel[0, take, :]
        st[3, rows, :] = vel[1, take, :]
        st[4, rows, :] = jnp.where(lane32 < cnt, rad[take, :], DEAD)
        st[5, rows, :] = cnt.astype(F32)
    st[6] = jnp.zeros((32, 128), F32)
    st[7] = jnp.zeros((32, 128), F32)


def comm_kernel(first, *refs):
    if first:
        (st, pc, mx, gas, ext, pv, red, gr, gc, mb, m1, m2,
         own_sem, hs, hr, ps, pr, rs, rr, es, er) = refs
    else:
        (st, pc, mx, ext, pv, red, mb, m1, m2,
         own_sem, hs, hr, ps, pr, rs, rr) = refs
    ax, al, g = lax.axis_index("across"), lax.axis_index("along"), lax.axis_index("gas")
    up, down = lax.rem(al + 1, N_ALONG), lax.rem(al + N_ALONG - 1, N_ALONG)
    lin = ax * N_GAS + g
    has_left, has_right = lin > 0, lin < N_ACROSS * N_GAS - 1
    left = jnp.maximum(lin - 1, 0)
    right = jnp.minimum(lin + 1, N_ACROSS * N_GAS - 1)

    def col(index, along):
        return {"across": lax.div(index, N_GAS), "along": along, "gas": lax.rem(index, N_GAS)}

    slab = al * N_GAS + g
    slabs = N_ALONG * N_GAS
    after, before = lax.rem(slab + 1, slabs), lax.rem(slab + slabs - 1, slabs)

    def slab_id(index):
        return {"across": ax, "along": lax.div(index, N_GAS), "gas": lax.rem(index, N_GAS)}

    barrier = pltpu.get_barrier_semaphore()

    def greet(device):
        pl.semaphore_signal(barrier, inc=1, device_id=device, device_id_type=MESH_ID)

    for k in range(1, N_ACROSS):
        greet({"across": lax.rem(ax + k, N_ACROSS)})
    for k in range(1, N_GAS):
        greet({"gas": lax.rem(g + k, N_GAS)})
    for k in range(1, N_ALONG):
        greet({"along": lax.rem(al + k, N_ALONG)})
    expect = N_ACROSS + N_GAS + N_ALONG - 3
    if first:
        greet(slab_id(after))
        greet(slab_id(before))
        expect += 2

    @pl.when(has_left)
    def _():
        for along in (down, al, up):
            greet(col(left, along))

    @pl.when(has_right)
    def _():
        for along in (down, al, up):
            greet(col(right, along))

    own = pltpu.make_async_copy(st, ext.at[:, pl.ds(0, 32)], own_sem.at[0])
    own.start()
    own_piece = pltpu.make_async_copy(pc.at[g], pv.at[g], own_sem.at[1])
    own_piece.start()

    @pl.when(jnp.logical_not(has_left))
    def _():
        ext[:, 32:48, :] = jnp.zeros((8, 16, 128), F32)
        ext[:, 64:72, :] = jnp.zeros((8, 8, 128), F32)
        ext[:, 96:104, :] = jnp.zeros((8, 8, 128), F32)

    @pl.when(jnp.logical_not(has_right))
    def _():
        ext[:, 48:64, :] = jnp.zeros((8, 16, 128), F32)
        ext[:, 88:96, :] = jnp.zeros((8, 8, 128), F32)
        ext[:, 120:128, :] = jnp.zeros((8, 8, 128), F32)

    if first:
        @pl.when(ax == 0)
        def _():
            gc[0] = jnp.zeros((2, 32, 128), F32)

        @pl.when(ax == N_ACROSS - 1)
        def _():
            gc[1] = jnp.zeros((2, 32, 128), F32)

    sides = jnp.where(has_left, 3, 0) + jnp.where(has_right, 3, 0)
    pl.semaphore_wait(barrier, expect + sides)

    def remote(src, dst, send, recv, device):
        return pltpu.make_async_remote_copy(
            src_ref=src, dst_ref=dst, send_sem=send, recv_sem=recv,
            device_id=device, device_id_type=MESH_ID,
        )

    def reduce_sends(phase, src, axis, me, size):
        out = []
        for k in range(1, size):
            out.append(remote(src, mb.at[phase, me], rs.at[phase, k], rr.at[phase, k],
                              {axis: lax.rem(me + k, size)}))
        for c in out:
            c.start()
        return out

    phase0 = reduce_sends(0, mx, "across", ax, N_ACROSS)

    def halo(c, src_rows, size, dst_row, device):
        return remote(st.at[pl.ds(0, 6), pl.ds(src_rows, size)],
                      ext.at[pl.ds(0, 6), pl.ds(dst_row, size)], hs.at[c], hr.at[c], device)

    lefts = [halo(0, 0, 16, 48, col(left, al)),
             halo(1, 8, 8, 64 + 24, col(left, up)),
             halo(2, 0, 8, 96 + 24, col(left, down))]
    rights = [halo(3, 16, 16, 32, col(right, al)),
              halo(4, 24, 8, 64, col(right, up)),
              halo(5, 16, 8, 96, col(right, down))]
    rows = [halo(6, 8, 8, 64 + 8, {"along": up}),
            halo(7, 24, 8, 64 + 16, {"along": up}),
            halo(8, 0, 8, 96 + 8, {"along": down}),
            halo(9, 16, 8, 96 + 16, {"along": down})]

    @pl.when(has_left)
    def _():
        for c in lefts:
            c.start()

    @pl.when(has_right)
    def _():
        for c in rights:
            c.start()

    for c in rows:
        c.start()
    pieces = []
    for k in range(1, N_GAS):
        peer = lax.rem(g + k, N_GAS)
        c = remote(pc.at[peer], pv.at[g], ps.at[k], pr.at[k], {"gas": peer})
        c.start()
        pieces.append(c)
    if first:
        edges = [remote(gas.at[:, pl.ds(24, 8)], gr.at[0], es.at[0], er.at[0], slab_id(after)),
                 remote(gas.at[:, pl.ds(0, 8)], gr.at[1], es.at[1], er.at[1], slab_id(before))]
        for c in edges:
            c.start()
        to_right = remote(gas.at[:, :, pl.ds(128, 128)], gc.at[0], es.at[2], er.at[2],
                          {"across": jnp.minimum(ax + 1, N_ACROSS - 1)})
        to_left = remote(gas.at[:, :, pl.ds(0, 128)], gc.at[1], es.at[3], er.at[3],
                         {"across": jnp.maximum(ax - 1, 0)})

        @pl.when(ax < N_ACROSS - 1)
        def _():
            to_right.start()

        @pl.when(ax > 0)
        def _():
            to_left.start()

    def combine(phase, mine, me, size, copies):
        for c in copies:
            c.wait_recv()
        mb[phase, me] = mine
        total = mb[phase, 0]
        for k in range(1, size):
            total = jnp.maximum(total, mb[phase, k]) if first else total + mb[phase, k]
        return total

    m1[...] = combine(0, mx[...], ax, N_ACROSS, phase0)
    phase1 = reduce_sends(1, m1, "gas", g, N_GAS)
    m2[...] = combine(1, m1[...], g, N_GAS, phase1)
    phase2 = reduce_sends(2, m2, "along", al, N_ALONG)
    red[...] = combine(2, m2[...], al, N_ALONG, phase2)

    own.wait()
    own_piece.wait()
    for c in phase0 + phase1 + phase2:
        c.wait_send()
    for c in rows + pieces:
        c.wait()

    @pl.when(has_left)
    def _():
        for c in lefts:
            c.wait_send()
        for c in rights:
            c.wait_recv()

    @pl.when(has_right)
    def _():
        for c in rights:
            c.wait_send()
        for c in lefts:
            c.wait_recv()

    if first:
        for c in edges:
            c.wait()

        @pl.when(ax < N_ACROSS - 1)
        def _():
            to_right.wait_send()
            to_left.wait_recv()

        @pl.when(ax > 0)
        def _():
            to_left.wait_send()
            to_right.wait_recv()


def exchange(first, st, pc, mx, gas=None):
    out_shape = [jax.ShapeDtypeStruct((8, 128, 128), F32),
                 jax.ShapeDtypeStruct((8, 32, 128), F32),
                 jax.ShapeDtypeStruct((8, 128), F32)]
    scratch = [pltpu.VMEM((3, 8, 8, 128), F32), pltpu.VMEM((8, 128), F32), pltpu.VMEM((8, 128), F32),
               pltpu.SemaphoreType.DMA((2,)),
               pltpu.SemaphoreType.DMA((10,)), pltpu.SemaphoreType.DMA((10,)),
               pltpu.SemaphoreType.DMA((8,)), pltpu.SemaphoreType.DMA((8,)),
               pltpu.SemaphoreType.DMA((3, 8)), pltpu.SemaphoreType.DMA((3, 8))]
    args = [st, pc, mx]
    if first:
        args.append(gas)
        out_shape += [jax.ShapeDtypeStruct((2, 2, 8, 256), F32), jax.ShapeDtypeStruct((2, 2, 32, 128), F32)]
        scratch += [pltpu.SemaphoreType.DMA((4,)), pltpu.SemaphoreType.DMA((4,))]
    return pl.pallas_call(
        functools.partial(comm_kernel, first),
        out_shape=out_shape,
        in_specs=[VMEM_SPEC] * len(args),
        out_specs=[VMEM_SPEC] * len(out_shape),
        scratch_shapes=scratch,
        compiler_params=pltpu.CompilerParams(collective_id=0 if first else 1, has_side_effects=True),
        name="exchange_first" if first else "exchange_second",
    )(*args)


def split3(x):
    hi = x.astype(BF16).astype(F32)
    rest = x - hi
    mid = rest.astype(BF16).astype(F32)
    return hi, mid, rest - mid


def contact_forces(ext, pat, cnt, qt, lst, rhs, frc, sem):
    to_smem = pltpu.make_async_copy(ext.at[pl.ds(5 * 128, 128)], cnt, sem)
    to_smem.start()
    eye = (iota((128, 128), 0) == iota((128, 128), 1)).astype(BF16)
    attr_row = iota((8, 128), 0)
    tail = jnp.concatenate([jnp.zeros((8, 128), F32), jnp.ones((24, 128), F32), jnp.zeros((8, 128), F32)], axis=0)

    def parts(row):
        block = ext[pl.ds(row, 8, stride=128), :]
        return split3(jnp.where(attr_row < 5, block, 0.0))

    def transposed(row):
        hi, mid, lo = parts(row)
        rows = jnp.concatenate([hi, mid, lo, tail], axis=0).astype(BF16)
        turned = lax.dot_general(eye, rows, (((1,), (1,)), ((), ())), preferred_element_type=F32)
        start = row * 128 if isinstance(row, int) else pl.multiple_of(row * 128, 128)
        qt[pl.ds(start, 128), 0:64] = turned

    def some(step, carry):
        for u in range(4):
            transposed(step * 4 + u)
        return carry

    lax.fori_loop(0, 16, some, 0)
    for c in range(4):
        transposed(64 + 8 * c + 7)
        transposed(96 + 8 * c)

    block_of = iota((32, 640), 1) >> 7
    row_of = iota((32, 640), 0)
    attr_of = row_of & 7
    own_scale = jnp.where(block_of < 2, -1.0, jnp.where(block_of < 4, 2.0, 1.0))
    const = jnp.where((attr_of == block_of) & (row_of < 24), own_scale, 0.0)
    const = jnp.where((row_of == 24) & (block_of == 0) | (row_of == 25) & (block_of == 1), -16.0, const)
    for u in range(2):
        rhs[u, 0:32, :] = const.astype(BF16)
    to_smem.wait()
    lane = iota((8, 128), 1)

    def row_step(i, carry):
        for j in range(2):
            work = lst.at[j]
            mine = j * 16 + i
            hi, mid, lo = parts(mine)
            zero8 = jnp.zeros((8, 128), F32)
            columns = []
            for a in range(5):
                keep = attr_row == a
                scale = 1.0 if a in (0, 1, 4) else -2.0
                columns.append(jnp.concatenate(
                    [jnp.where(keep, hi * scale, 0.0), jnp.where(keep, mid * scale, 0.0),
                     jnp.where(keep, lo * scale, 0.0), zero8], axis=0))
            rhs[j, 32:64, :] = jnp.concatenate(columns, axis=1).astype(BF16)
            off = i * 0
            for n, (di, dj) in enumerate(OFFSETS):
                row = ext_row(i + di, j + dj)
                mark = jnp.where(lane == 24, float(di), jnp.where(lane == 25, float(dj), 0.0))
                start = pl.multiple_of(row * 128, 128)
                for c in range(16):
                    work[pl.ds(pl.multiple_of(off + c * 8, 8), 8), :] = (
                        qt[pl.ds(start + c * 8, 8), :] + mark)
                live = cnt[row, 0].astype(jnp.int32) * pat[n, j, i]
                off = off + ((live + 7) & -8)
            for c in range(16):
                work[pl.ds(pl.multiple_of(off + c * 8, 8), 8), :] = jnp.zeros((8, 128), F32)
            right = rhs[j]

            def block(b, acc):
                fz, fx = acc
                q = work[pl.ds(pl.multiple_of(b * 128, 128), 128), 0:64].astype(BF16)
                got = jnp.dot(q, right, preferred_element_type=F32)
                rz, rx = got[:, 0:128], got[:, 128:256]
                dz, dx = got[:, 256:384], got[:, 384:512]
                d2 = rz * rz + rx * rx + 0.0001
                inv = lax.rsqrt(d2)
                depth = jnp.maximum(got[:, 512:640] - d2 * inv, 0.0)
                push = depth * inv * (40.0 + (dz * rz + dx * rx) * inv)
                fz = fz + jnp.sum((push * rz).reshape(16, 8, 128), axis=0)
                fx = fx + jnp.sum((push * rx).reshape(16, 8, 128), axis=0)
                return fz, fx

            fz, fx = lax.fori_loop(0, (off + 127) >> 7, block, (zero8, zero8))
            frc[0, pl.ds(mine, 1), :] = jnp.sum(fz, axis=0, keepdims=True)
            frc[1, pl.ds(mine, 1), :] = jnp.sum(fx, axis=0, keepdims=True)
        return carry

    lax.fori_loop(0, 16, row_step, 0)


def by_column(ref, *lead):
    return jnp.concatenate([ref[(*lead, pl.ds(0, 16, stride=2), slice(None))],
                            ref[(*lead, pl.ds(1, 16, stride=2), slice(None))]], axis=0)


def first_kernel(ext, gv, rate, idx, frac, coef, pat, st2, dp, tot, dr2, inv_out,
                 cnt, qt, lst, rhs, frc, itp, sem):
    def weights(r, t4):
        index = idx[pl.ds(r, 1), :]
        row, column = index >> 4, index & 15
        share_z = frac[0, pl.ds(r, 1), :].astype(F32) / 1024.0
        share_x = frac[1, pl.ds(r, 1), :].astype(F32) / 1024.0
        c64 = iota((64, 128), 0) - t4 * 16
        wx = jnp.where(c64 == column, 1.0 - share_x, jnp.where(c64 == column + 1, share_x, 0.0))
        r16 = iota((16, 128), 0)
        wz = jnp.where(r16 == row, 1.0 - share_z, jnp.where(r16 == row + 1, share_z, 0.0))
        return wz, wx

    def sample(h, carry):
        field = gv[h][:, 0:64]
        for t in range(2):
            for j in range(2):
                wz, wx = weights(4 * h + 2 * t + j, t * 2 + j)
                along = jnp.dot(field, wx, precision=lax.Precision.HIGHEST, preferred_element_type=F32)
                for k in range(2):
                    itp[k, pl.ds(j * 16 + 2 * h + t, 1), :] = jnp.sum(
                        wz * along[k * 16:(k + 1) * 16], axis=0, keepdims=True)
        return carry

    lax.fori_loop(0, 8, sample, 0)
    contact_forces(ext, pat, cnt, qt, lst, rhs, frc, sem)
    step = 0.2 / rate[0:1, :]
    drag = by_column(coef)
    radius = ext[4 * 128:4 * 128 + 32, :]
    alive = jnp.where(radius > 0.0, 1.0, 0.0)
    inverse = jnp.where(radius > 0.0, 0.36 / (radius * radius), 0.0)
    inv_out[...] = inverse
    means = []
    for k in range(2):
        place = ext[k * 128:k * 128 + 32, :]
        speed = ext[(2 + k) * 128:(2 + k) * 128 + 32, :]
        drag1 = drag * (itp[k] - speed)
        speed2 = speed + step * (inverse * (frc[k] + drag1) - (alive if k == 0 else 0.0))
        st2[k] = place + step * speed2
        st2[2 + k] = speed2
        drag2 = drag * (itp[k] - speed2)
        dr2[k] = drag2
        mean = 0.5 * (alive * drag1 + alive * drag2)
        itp[k] = mean
        means.append(jnp.sum(jnp.sum(mean, axis=1, keepdims=True), axis=0, keepdims=True))
    st2[4] = radius
    st2[5] = ext[5 * 128:5 * 128 + 32, :]
    st2[6] = jnp.zeros((32, 128), F32)
    st2[7] = jnp.zeros((32, 128), F32)
    tot[...] = jnp.where(iota((8, 128), 0) == 0, means[0], means[1])

    def spread(h, carry):
        total = jnp.zeros((32, 64), F32)
        for t in range(2):
            for j in range(2):
                wz, wx = weights(4 * h + 2 * t + j, t * 2 + j)
                m0 = itp[0, pl.ds(j * 16 + 2 * h + t, 1), :]
                m1 = itp[1, pl.ds(j * 16 + 2 * h + t, 1), :]
                lhs = jnp.concatenate([wz * m0, wz * m1], axis=0)
                total = total + lax.dot_general(lhs, wx, (((1,), (1,)), ((), ())),
                                                precision=lax.Precision.HIGHEST, preferred_element_type=F32)
        dp[h, :, 0:64] = total
        dp[h, :, 64:128] = jnp.zeros((32, 64), F32)
        return carry

    lax.fori_loop(0, 8, spread, 0)


def second_kernel(ext, dv, tot, rate, dr2, inverse, gas, visc, gr, gc, pat, part, out,
                  cnt, qt, lst, rhs, frc, sem):
    contact_forces(ext, pat, cnt, qt, lst, rhs, frc, sem)
    step = 0.2 / rate[0:1, :]
    radius = ext[4 * 128:4 * 128 + 32, :]
    alive = jnp.where(radius > 0.0, 1.0, 0.0)
    for k in range(2):
        place = ext[k * 128:k * 128 + 32, :]
        speed = ext[(2 + k) * 128:(2 + k) * 128 + 32, :]
        speed2 = speed + step * (inverse[...] * (frc[k] + dr2[k]) - (alive if k == 0 else 0.0))
        place2 = (place + step * speed2) * 0.0625
        for j in range(2):
            part[k, pl.ds(j, 16, stride=2), :] = place2[j * 16:(j + 1) * 16]
            part[2 + k, pl.ds(j, 16, stride=2), :] = speed2[j * 16:(j + 1) * 16]
    gas_step = 0.4 / rate[0:1, 0:1]
    lane = iota((32, 256), 1)
    row = iota((32, 256), 0)
    lane16 = iota((16, 128), 1) >> 5
    for k in range(2):
        u = gas[k]
        upper = jnp.where(row == 31, gr[1, k, 0:1, :], pltpu.roll(u, 31, 0))
        lower = jnp.where(row == 0, gr[0, k, 7:8, :], pltpu.roll(u, 1, 0))
        right = jnp.where(lane == 255, gc[1, k, :, 0:1], pltpu.roll(u, 255, 1))
        left = jnp.where(lane == 0, gc[0, k, :, 127:128], pltpu.roll(u, 1, 1))
        laplace = upper + lower + right + left - 4.0 * u
        advect = gas[0] * (upper - lower) * 0.5 + gas[1] * (right - left) * 0.5
        quads = []
        for t in range(2):
            halves = []
            for b in range(2):
                whole = None
                for q in range(4):
                    piece = dv[4 * b + q, k * 16:(k + 1) * 16, :]
                    shift = (q * 32 - t * 32) % 128
                    piece = pltpu.roll(piece, shift, 1) if shift else piece
                    whole = piece if whole is None else jnp.where(lane16 == q, piece, whole)
                halves.append(whole)
            quads.append(jnp.concatenate(halves, axis=1))
        deposit = jnp.concatenate(quads, axis=0)
        source = tot[k:k + 1, 0:1] / 2097152.0 - deposit
        out[k] = u + gas_step * (visc[...] * laplace - advect + source)


CONTACT_SCRATCH = [
    pltpu.SMEM((128, 128), F32),
    pltpu.VMEM((128 * 128, 128), F32),
    pltpu.VMEM((2, 1408, 128), F32),
    pltpu.VMEM((2, 64, 640), BF16),
    pltpu.VMEM((2, 32, 128), F32),
]


def body(gas, visc, pos, vel, rad, coef, counts, pattern, idx, frac):
    counts_t = counts.T
    pattern_t = pattern.transpose(2, 1, 0)
    pos, vel, frac = (x.reshape(2, 32, 128) for x in (pos, vel, frac))
    rad, coef, idx = (x.reshape(32, 128) for x in (rad, coef, idx))

    def shapes(*dims):
        return [jax.ShapeDtypeStruct(d, F32) for d in dims]

    st, gp, mx = pl.pallas_call(
        prep_kernel,
        out_shape=shapes((8, 32, 128), (8, 32, 128), (8, 128)),
        in_specs=[VMEM_SPEC] * 5 + [SMEM_SPEC],
        out_specs=[VMEM_SPEC] * 3,
        name="prepare",
    )(gas, visc, pos, vel, rad, counts_t)
    ext, gv, rate, gr, gc = exchange(True, st, gp, mx, gas)
    st2, dp, tot, dr2, inverse = pl.pallas_call(
        first_kernel,
        out_shape=shapes((8, 32, 128), (8, 32, 128), (8, 128), (2, 32, 128), (32, 128)),
        in_specs=[VMEM_SPEC] * 6 + [SMEM_SPEC],
        out_specs=[VMEM_SPEC] * 5,
        scratch_shapes=CONTACT_SCRATCH + [pltpu.VMEM((2, 32, 128), F32), pltpu.SemaphoreType.DMA],
        name="first_substep",
    )(ext.reshape(1024, 128), gv, rate, idx, frac, coef, pattern_t)
    ext2, dv, total = exchange(False, st2, dp, tot)
    part, out = pl.pallas_call(
        second_kernel,
        out_shape=shapes((4, 32, 128), (2, 32, 256)),
        in_specs=[VMEM_SPEC] * 10 + [SMEM_SPEC],
        out_specs=[VMEM_SPEC] * 2,
        scratch_shapes=CONTACT_SCRATCH + [pltpu.SemaphoreType.DMA],
        name="second_substep",
    )(ext2.reshape(1024, 128), dv, total, rate, dr2, inverse, gas, visc, gr, gc, pattern_t)
    return part.reshape(4, 16, 2, 128), out


def solution(mesh):
    return jax.shard_map(
        body,
        mesh=mesh,
        in_specs=(
            P(None, ALONG_GAS, "across"),
            P(ALONG_GAS, "across"),
            P(None, "along", ACROSS_GAS, None),
            P(None, "along", ACROSS_GAS, None),
            P("along", ACROSS_GAS, None),
            P("along", ACROSS_GAS, None),
            P("along", ACROSS_GAS),
            P("along", ACROSS_GAS, None),
            P("along", ACROSS_GAS, None),
            P(None, "along", ACROSS_GAS, None),
        ),
        out_specs=(P(None, "along", ACROSS_GAS, None), P(None, ALONG_GAS, "across")),
        check_vma=False,
    )
```

```python
import functools

import jax
import jax.numpy as jnp
from jax import lax
from jax.experimental import pallas as pl
from jax.experimental.pallas import tpu as pltpu
from jax.sharding import PartitionSpec as P

ALONG_GAS = ("along", "gas")
ACROSS_GAS = ("across", "gas")
MESH_ID = pl.DeviceIdType.MESH
OFFSETS = [(-1, -1), (-1, 0), (-1, 1), (0, -1), (0, 0), (0, 1), (1, -1), (1, 0), (1, 1)]
DEAD = -16384.0
F32 = jnp.float32
BF16 = jnp.bfloat16
STRIDE = 136
BLOCK, BLOCK_BITS = 64, 6
EMPTY = 1344
REACH = 2.4
MOVE_LIMIT = int((REACH - 1.9) * 4096)
VMEM_SPEC = pl.BlockSpec(memory_space=pltpu.VMEM)
SMEM_SPEC = pl.BlockSpec(memory_space=pltpu.SMEM)
N_ACROSS, N_ALONG, N_GAS = 4, 8, 8


def iota(shape, dim):
    return lax.broadcasted_iota(jnp.int32, shape, dim)


def ext_row(ii, jj):
    base = {-1: 32, 0: 0, 1: 16, 2: 48}[jj]
    return jnp.where(ii < 0, 64 + 8 * (jj + 1) + 7, jnp.where(ii > 15, 96 + 8 * (jj + 1), base + ii))


def by_column(ref, *lead):
    return jnp.concatenate([ref[(*lead, pl.ds(0, 16, stride=2), slice(None))],
                            ref[(*lead, pl.ds(1, 16, stride=2), slice(None))]], axis=0)


def prep_kernel(gas, visc, pos, vel, rad, counts, st, gp, mx):
    rate = jnp.abs(gas[0]) + jnp.abs(gas[1]) + 4.0 * visc[...]
    top = jnp.max(jnp.max(rate, axis=1, keepdims=True), axis=0, keepdims=True)
    mx[...] = jnp.broadcast_to(top, (8, 128))
    lane = iota((16, 128), 1)
    for g in range(N_GAS):
        blk = slice((g // 4) * 128, (g // 4) * 128 + 128)
        off = (g % 4) * 32
        for k in range(2):
            low = gas[k, 0:16, blk]
            high = gas[k, 16:32, blk]
            low = pltpu.roll(low, (128 - off) % 128, 1) if off else low
            shift = (160 - off) % 128
            high = pltpu.roll(high, shift, 1) if shift else high
            piece = jnp.where(lane < 32, low, jnp.where(lane < 64, high, 0.0))
            gp[g, k * 16:(k + 1) * 16, :] = piece
    row32 = iota((32, 128), 0)
    slot = iota((32, 128), 1)
    cnt = jnp.zeros((32, 128), jnp.int32)
    for j in range(2):
        for i in range(16):
            cnt = jnp.where(row32 == j * 16 + i, counts[j, i], cnt)
    alive = slot < cnt
    z, x = by_column(pos, 0) * 16.0, by_column(pos, 1) * 16.0
    st[0], st[1] = z, x
    st[2], st[3] = by_column(vel, 0), by_column(vel, 1)
    st[4] = jnp.where(alive, by_column(rad), DEAD)
    low_x, high_x = x < REACH, x > 16.0 - REACH

    def three(low, mid, high):
        return jnp.where(low_x, low, jnp.where(high_x, high, mid))

    kind = jnp.where(z < REACH, three(0, 1, 2), jnp.where(z > 16.0 - REACH, three(6, 5, 4), three(7, 8, 3)))
    kind = jnp.where(alive, kind, 9)
    member = jnp.concatenate([jnp.where(kind == c, 1.0, 0.0) for c in range(9)], axis=0).astype(BF16)
    before = jnp.where((iota((128, 256), 0) < iota((128, 256), 1)) | (iota((128, 256), 1) >= 128), 1.0, 0.0)
    ranks = jnp.dot(member, before.astype(BF16), preferred_element_type=F32)
    rank = jnp.full((32, 128), -1.0, F32)
    start = [jnp.zeros((32, 128), F32)]
    for c in range(9):
        here = ranks[c * 32:(c + 1) * 32]
        rank = jnp.where(kind == c, start[c] + here[:, 0:128], rank)
        start.append(start[c] + here[:, 128:256])
    st[5] = rank
    start = [v.astype(jnp.int32) for v in start]
    wrap = ((start[1] + 7) & -8) > start[6]
    zero = jnp.zeros((32, 128), jnp.int32)
    windows = [(start[4], start[5]), (start[4], start[7]), (start[6], start[7]), (start[2], start[5]),
               (zero, start[9]), (jnp.where(wrap, 0, start[6]), start[8]), (start[2], start[3]),
               (zero, start[3]), (zero, start[1]), (zero, jnp.where(wrap, 0, start[1]))]
    table = zero
    for w, (low, high) in enumerate(windows):
        table = jnp.where(slot == 2 * w, low, jnp.where(slot == 2 * w + 1, (high - low + 7) & -8, table))
    st[6] = table.astype(F32)
    st[7] = jnp.zeros((32, 128), F32)


def comm_kernel(first, *refs):
    if first:
        (st, pc, mx, gas, ext, pv, red, gr, gc, mb, m1, m2,
         own_sem, hs, hr, ps, pr, rs, rr, es, er) = refs
    else:
        (st, pc, mx, ext, pv, red, mb, m1, m2,
         own_sem, hs, hr, ps, pr, rs, rr) = refs
    ax, al, g = lax.axis_index("across"), lax.axis_index("along"), lax.axis_index("gas")
    up, down = lax.rem(al + 1, N_ALONG), lax.rem(al + N_ALONG - 1, N_ALONG)
    lin = ax * N_GAS + g
    has_left, has_right = lin > 0, lin < N_ACROSS * N_GAS - 1
    left = jnp.maximum(lin - 1, 0)
    right = jnp.minimum(lin + 1, N_ACROSS * N_GAS - 1)

    def col(index, along):
        return {"across": lax.div(index, N_GAS), "along": along, "gas": lax.rem(index, N_GAS)}

    slab = al * N_GAS + g
    slabs = N_ALONG * N_GAS
    after, before = lax.rem(slab + 1, slabs), lax.rem(slab + slabs - 1, slabs)

    def slab_id(index):
        return {"across": ax, "along": lax.div(index, N_GAS), "gas": lax.rem(index, N_GAS)}

    barrier = pltpu.get_barrier_semaphore()

    def greet(device):
        pl.semaphore_signal(barrier, inc=1, device_id=device, device_id_type=MESH_ID)

    for k in range(1, N_ACROSS):
        greet({"across": lax.rem(ax + k, N_ACROSS)})
    for k in range(1, N_GAS):
        greet({"gas": lax.rem(g + k, N_GAS)})
    for k in range(1, N_ALONG):
        greet({"along": lax.rem(al + k, N_ALONG)})
    expect = N_ACROSS + N_GAS + N_ALONG - 3
    if first:
        greet(slab_id(after))
        greet(slab_id(before))
        expect += 2

    @pl.when(has_left)
    def _():
        for along in (down, al, up):
            greet(col(left, along))

    @pl.when(has_right)
    def _():
        for along in (down, al, up):
            greet(col(right, along))

    own = pltpu.make_async_copy(st, ext.at[:, pl.ds(0, 32)], own_sem.at[0])
    own.start()
    own_piece = pltpu.make_async_copy(pc.at[g], pv.at[g], own_sem.at[1])
    own_piece.start()

    @pl.when(jnp.logical_not(has_left))
    def _():
        ext[:, 32:48, :] = jnp.zeros((8, 16, 128), F32)
        ext[:, 64:72, :] = jnp.zeros((8, 8, 128), F32)
        ext[:, 96:104, :] = jnp.zeros((8, 8, 128), F32)

    @pl.when(jnp.logical_not(has_right))
    def _():
        ext[:, 48:64, :] = jnp.zeros((8, 16, 128), F32)
        ext[:, 88:96, :] = jnp.zeros((8, 8, 128), F32)
        ext[:, 120:128, :] = jnp.zeros((8, 8, 128), F32)

    if first:
        @pl.when(ax == 0)
        def _():
            gc[0] = jnp.zeros((2, 32, 128), F32)

        @pl.when(ax == N_ACROSS - 1)
        def _():
            gc[1] = jnp.zeros((2, 32, 128), F32)

    sides = jnp.where(has_left, 3, 0) + jnp.where(has_right, 3, 0)
    pl.semaphore_wait(barrier, expect + sides)

    def remote(src, dst, send, recv, device):
        return pltpu.make_async_remote_copy(
            src_ref=src, dst_ref=dst, send_sem=send, recv_sem=recv,
            device_id=device, device_id_type=MESH_ID,
        )

    def reduce_sends(phase, src, axis, me, size):
        out = []
        for k in range(1, size):
            out.append(remote(src, mb.at[phase, me], rs.at[phase, k], rr.at[phase, k],
                              {axis: lax.rem(me + k, size)}))
        for c in out:
            c.start()
        return out

    phase0 = reduce_sends(0, mx, "across", ax, N_ACROSS)

    def halo(c, src_rows, size, dst_row, device):
        return remote(st.at[pl.ds(0, 7), pl.ds(src_rows, size)],
                      ext.at[pl.ds(0, 7), pl.ds(dst_row, size)], hs.at[c], hr.at[c], device)

    lefts = [halo(0, 0, 16, 48, col(left, al)),
             halo(1, 8, 8, 64 + 24, col(left, up)),
             halo(2, 0, 8, 96 + 24, col(left, down))]
    rights = [halo(3, 16, 16, 32, col(right, al)),
              halo(4, 24, 8, 64, col(right, up)),
              halo(5, 16, 8, 96, col(right, down))]
    rows = [halo(6, 8, 8, 64 + 8, {"along": up}),
            halo(7, 24, 8, 64 + 16, {"along": up}),
            halo(8, 0, 8, 96 + 8, {"along": down}),
            halo(9, 16, 8, 96 + 16, {"along": down})]

    @pl.when(has_left)
    def _():
        for c in lefts:
            c.start()

    @pl.when(has_right)
    def _():
        for c in rights:
            c.start()

    for c in rows:
        c.start()
    pieces = []
    for k in range(1, N_GAS):
        peer = lax.rem(g + k, N_GAS)
        c = remote(pc.at[peer], pv.at[g], ps.at[k], pr.at[k], {"gas": peer})
        c.start()
        pieces.append(c)
    if first:
        edges = [remote(gas.at[:, pl.ds(24, 8)], gr.at[0], es.at[0], er.at[0], slab_id(after)),
                 remote(gas.at[:, pl.ds(0, 8)], gr.at[1], es.at[1], er.at[1], slab_id(before))]
        for c in edges:
            c.start()
        to_right = remote(gas.at[:, :, pl.ds(128, 128)], gc.at[0], es.at[2], er.at[2],
                          {"across": jnp.minimum(ax + 1, N_ACROSS - 1)})
        to_left = remote(gas.at[:, :, pl.ds(0, 128)], gc.at[1], es.at[3], er.at[3],
                         {"across": jnp.maximum(ax - 1, 0)})

        @pl.when(ax < N_ACROSS - 1)
        def _():
            to_right.start()

        @pl.when(ax > 0)
        def _():
            to_left.start()

    def combine(phase, mine, me, size, copies):
        for c in copies:
            c.wait_recv()
        mb[phase, me] = mine
        total = mb[phase, 0]
        for k in range(1, size):
            total = jnp.maximum(total, mb[phase, k]) if first else total + mb[phase, k]
        return total

    m1[...] = combine(0, mx[...], ax, N_ACROSS, phase0)
    phase1 = reduce_sends(1, m1, "gas", g, N_GAS)
    m2[...] = combine(1, m1[...], g, N_GAS, phase1)
    phase2 = reduce_sends(2, m2, "along", al, N_ALONG)
    red[...] = combine(2, m2[...], al, N_ALONG, phase2)

    own.wait()
    own_piece.wait()
    for c in phase0 + phase1 + phase2:
        c.wait_send()
    for c in rows + pieces:
        c.wait()

    @pl.when(has_left)
    def _():
        for c in lefts:
            c.wait_send()
        for c in rights:
            c.wait_recv()

    @pl.when(has_right)
    def _():
        for c in rights:
            c.wait_send()
        for c in lefts:
            c.wait_recv()

    if first:
        for c in edges:
            c.wait()

        @pl.when(ax < N_ACROSS - 1)
        def _():
            to_right.wait_send()
            to_left.wait_recv()

        @pl.when(ax > 0)
        def _():
            to_left.wait_send()
            to_right.wait_recv()


def exchange(first, st, pc, mx, gas=None):
    out_shape = [jax.ShapeDtypeStruct((8, 128, 128), F32),
                 jax.ShapeDtypeStruct((8, 32, 128), F32),
                 jax.ShapeDtypeStruct((8, 128), F32)]
    scratch = [pltpu.VMEM((3, 8, 8, 128), F32), pltpu.VMEM((8, 128), F32), pltpu.VMEM((8, 128), F32),
               pltpu.SemaphoreType.DMA((2,)),
               pltpu.SemaphoreType.DMA((10,)), pltpu.SemaphoreType.DMA((10,)),
               pltpu.SemaphoreType.DMA((8,)), pltpu.SemaphoreType.DMA((8,)),
               pltpu.SemaphoreType.DMA((3, 8)), pltpu.SemaphoreType.DMA((3, 8))]
    args = [st, pc, mx]
    if first:
        args.append(gas)
        out_shape += [jax.ShapeDtypeStruct((2, 2, 8, 256), F32), jax.ShapeDtypeStruct((2, 2, 32, 128), F32)]
        scratch += [pltpu.SemaphoreType.DMA((4,)), pltpu.SemaphoreType.DMA((4,))]
    return pl.pallas_call(
        functools.partial(comm_kernel, first),
        out_shape=out_shape,
        in_specs=[VMEM_SPEC] * len(args),
        out_specs=[VMEM_SPEC] * len(out_shape),
        scratch_shapes=scratch,
        compiler_params=pltpu.CompilerParams(collective_id=0 if first else 1, has_side_effects=True),
        name="exchange_first" if first else "exchange_second",
    )(*args)


def split3(x):
    hi = x.astype(BF16).astype(F32)
    rest = x - hi
    mid = rest.astype(BF16).astype(F32)
    return hi, mid, rest - mid


def contact_forces(ext, pat, meta, ints, qt, lst, rhs, frc, sem):
    ints[...] = ext[6 * 128:7 * 128, :].astype(jnp.int32)
    to_smem = pltpu.make_async_copy(ints, meta, sem)
    to_smem.start()
    slot = iota((128, 128), 0).astype(F32)
    attr_row = iota((8, 128), 0)
    zero8 = jnp.zeros((8, 128), F32)
    tail = jnp.concatenate([zero8, jnp.ones((24, 128), F32), zero8], axis=0)

    def parts(row):
        block = ext[pl.ds(row, 8, stride=128), :]
        return split3(jnp.where(attr_row < 5, block, 0.0))

    def transposed(row):
        hi, mid, lo = parts(row)
        rows = jnp.concatenate([hi, mid, lo, tail], axis=0).astype(BF16)
        place = (slot == ext[pl.ds(row + 5 * 128, 1), :]).astype(F32).astype(BF16)
        turned = lax.dot_general(place, rows, (((1,), (1,)), ((), ())), preferred_element_type=F32)
        start = row * STRIDE if isinstance(row, int) else pl.multiple_of(row * STRIDE, 8)
        qt[pl.ds(start, 128), 0:64] = turned
        start = start + 128 if isinstance(row, int) else pl.multiple_of(start + 128, 8)
        qt[pl.ds(start, 8), :] = zero8

    def some(step, carry):
        for u in range(4):
            transposed(step * 4 + u)
        return carry

    lax.fori_loop(0, 16, some, 0)
    for c in range(4):
        transposed(64 + 8 * c + 7)
        transposed(96 + 8 * c)

    block_of = iota((32, 640), 1) >> 7
    row_of = iota((32, 640), 0)
    attr_of = row_of & 7
    own_scale = jnp.where(block_of < 2, -1.0, jnp.where(block_of < 4, 2.0, 1.0))
    const = jnp.where((attr_of == block_of) & (row_of < 24), own_scale, 0.0)
    const = jnp.where((row_of == 24) & (block_of == 0) | (row_of == 25) & (block_of == 1), -16.0, const)
    for u in range(2):
        rhs[u, 0:32, :] = const.astype(BF16)
        lst[u, EMPTY:EMPTY + BLOCK, :] = jnp.zeros((BLOCK, 128), F32)
    to_smem.wait()
    lane = iota((8, 128), 1)

    def row_step(i, carry):
        blocks = []
        for j in range(2):
            work = lst.at[j]
            mine = j * 16 + i
            hi, mid, lo = parts(mine)
            columns = []
            for a in range(5):
                keep = attr_row == a
                scale = 1.0 if a in (0, 1, 4) else -2.0
                columns.append(jnp.concatenate(
                    [jnp.where(keep, hi * scale, 0.0), jnp.where(keep, mid * scale, 0.0),
                     jnp.where(keep, lo * scale, 0.0), zero8], axis=0))
            rhs[j, 32:64, :] = jnp.concatenate(columns, axis=1).astype(BF16)
            moved = meta[mine, 20]
            off = i * 0
            over = i * 0
            windows = []
            for w in (4, 0, 1, 2, 3, 5, 6, 7, 8, 9):
                di, dj = OFFSETS[5 if w == 9 else w]
                row = ext_row(i + di, j + dj)
                first, size = meta[row, 2 * w], meta[row, 2 * w + 1]
                if w != 4:
                    near = moved + meta[row, 20] <= MOVE_LIMIT
                    first = jnp.where(near, first, 0)
                    size = jnp.where(near, size, 0 if w == 9 else meta[row, 9])
                size = size * pat[5 if w == 9 else w, j, i]
                mark = jnp.where(lane == 24, float(di), jnp.where(lane == 25, float(dj), 0.0))
                start = row * STRIDE + first
                chunks = 16 if w == 4 else 4 if w in (1, 3, 5, 7) else 1
                for c in range(chunks):
                    work[pl.ds(pl.multiple_of(off + c * 8, 8), 8), :] = qt[pl.ds(start + c * 8, 8), :] + mark
                windows.append((start, size, mark))
                off = off + size
                over = jnp.maximum(over, size - chunks * 8)

            @pl.when(over > 0)
            def _():
                to = i * 0
                for start, size, mark in windows:
                    def copy(c, carry, start=start, mark=mark, to=to):
                        work[pl.ds(pl.multiple_of(to + c * 8, 8), 8), :] = qt[pl.ds(start + c * 8, 8), :] + mark
                        return carry
                    lax.fori_loop(0, size >> 3, copy, 0)
                    to = to + size

            for c in range(BLOCK // 8):
                work[pl.ds(pl.multiple_of(off + c * 8, 8), 8), :] = zero8
            blocks.append((off + BLOCK - 1) >> BLOCK_BITS)
        right = [rhs[0], rhs[1]]

        def block(b, acc):
            out = []
            for j in range(2):
                at = jnp.where(b < blocks[j], b * BLOCK, EMPTY)
                q = lst[j, pl.ds(pl.multiple_of(at, 8), BLOCK), 0:64].astype(BF16)
                got = jnp.dot(q, right[j], preferred_element_type=F32)
                rz, rx = got[:, 0:128], got[:, 128:256]
                dz, dx = got[:, 256:384], got[:, 384:512]
                d2 = rz * rz + rx * rx + 0.0001
                inv = lax.rsqrt(d2)
                depth = jnp.maximum(got[:, 512:640] - d2 * inv, 0.0)
                push = depth * inv * (40.0 + (dz * rz + dx * rx) * inv)
                out.append(acc[2 * j] + jnp.sum((push * rz).reshape(BLOCK // 8, 8, 128), axis=0))
                out.append(acc[2 * j + 1] + jnp.sum((push * rx).reshape(BLOCK // 8, 8, 128), axis=0))
            return tuple(out)

        acc = lax.fori_loop(0, jnp.maximum(blocks[0], blocks[1]), block, (zero8,) * 4)
        for j in range(2):
            for k in range(2):
                frc[pl.ds(pl.multiple_of(((k * 2 + j) * 16 + i) * 8, 8), 8), :] = acc[2 * j + k]
        return carry

    lax.fori_loop(0, 16, row_step, 0)
    return [sum(frc[pl.ds(k * 256 + r, 32, stride=8), :] for r in range(8)) for k in range(2)]


def first_kernel(ext, gv, rate, idx, frac, coef, pat, st2, dp, tot, dr2, inv_out,
                 meta, ints, qt, lst, rhs, frc, itp, sem):
    def weights(r, t4):
        index = idx[pl.ds(r, 1), :]
        row, column = index >> 4, index & 15
        share_z = frac[0, pl.ds(r, 1), :].astype(F32) / 1024.0
        share_x = frac[1, pl.ds(r, 1), :].astype(F32) / 1024.0
        c64 = iota((64, 128), 0) - t4 * 16
        wx = jnp.where(c64 == column, 1.0 - share_x, jnp.where(c64 == column + 1, share_x, 0.0))
        r16 = iota((16, 128), 0)
        wz = jnp.where(r16 == row, 1.0 - share_z, jnp.where(r16 == row + 1, share_z, 0.0))
        return wz, wx

    def sample(h, carry):
        field = gv[h][:, 0:64]
        for t in range(2):
            for j in range(2):
                wz, wx = weights(4 * h + 2 * t + j, t * 2 + j)
                along = jnp.dot(field, wx, precision=lax.Precision.HIGHEST, preferred_element_type=F32)
                for k in range(2):
                    itp[k, pl.ds(j * 16 + 2 * h + t, 1), :] = jnp.sum(
                        wz * along[k * 16:(k + 1) * 16], axis=0, keepdims=True)
        return carry

    lax.fori_loop(0, 8, sample, 0)
    force = contact_forces(ext, pat, meta, ints, qt, lst, rhs, frc, sem)
    step = 0.2 / rate[0:1, :]
    drag = by_column(coef)
    radius = ext[4 * 128:4 * 128 + 32, :]
    alive = jnp.where(radius > 0.0, 1.0, 0.0)
    inverse = jnp.where(radius > 0.0, 0.36 / (radius * radius), 0.0)
    inv_out[...] = inverse
    means = []
    moved = jnp.zeros((32, 128), F32)
    for k in range(2):
        place = ext[k * 128:k * 128 + 32, :]
        speed = ext[(2 + k) * 128:(2 + k) * 128 + 32, :]
        drag1 = drag * (itp[k] - speed)
        speed2 = speed + step * (inverse * (force[k] + drag1) - (alive if k == 0 else 0.0))
        st2[k] = place + step * speed2
        moved = jnp.maximum(moved, alive * jnp.abs(step * speed2))
        st2[2 + k] = speed2
        drag2 = drag * (itp[k] - speed2)
        dr2[k] = drag2
        mean = 0.5 * (alive * drag1 + alive * drag2)
        itp[k] = mean
        means.append(jnp.sum(jnp.sum(mean, axis=1, keepdims=True), axis=0, keepdims=True))
    st2[4] = radius
    st2[5] = ext[5 * 128:5 * 128 + 32, :]
    far = jnp.max(moved, axis=1, keepdims=True)
    far = jnp.where(far < 100.0, far, 100.0) * 4096.0 + 1.0
    st2[6] = jnp.where(iota((32, 128), 1) == 20, far, ext[6 * 128:6 * 128 + 32, :])
    st2[7] = jnp.zeros((32, 128), F32)
    tot[...] = jnp.where(iota((8, 128), 0) == 0, means[0], means[1])

    def spread(h, carry):
        total = jnp.zeros((32, 64), F32)
        for t in range(2):
            for j in range(2):
                wz, wx = weights(4 * h + 2 * t + j, t * 2 + j)
                m0 = itp[0, pl.ds(j * 16 + 2 * h + t, 1), :]
                m1 = itp[1, pl.ds(j * 16 + 2 * h + t, 1), :]
                lhs = jnp.concatenate([wz * m0, wz * m1], axis=0)
                total = total + lax.dot_general(lhs, wx, (((1,), (1,)), ((), ())),
                                                precision=lax.Precision.HIGHEST, preferred_element_type=F32)
        dp[h, :, 0:64] = total
        dp[h, :, 64:128] = jnp.zeros((32, 64), F32)
        return carry

    lax.fori_loop(0, 8, spread, 0)


def second_kernel(ext, dv, tot, rate, dr2, inverse, gas, visc, gr, gc, pat, part, out,
                  meta, ints, qt, lst, rhs, frc, sem):
    force = contact_forces(ext, pat, meta, ints, qt, lst, rhs, frc, sem)
    step = 0.2 / rate[0:1, :]
    radius = ext[4 * 128:4 * 128 + 32, :]
    alive = jnp.where(radius > 0.0, 1.0, 0.0)
    for k in range(2):
        place = ext[k * 128:k * 128 + 32, :]
        speed = ext[(2 + k) * 128:(2 + k) * 128 + 32, :]
        speed2 = speed + step * (inverse[...] * (force[k] + dr2[k]) - (alive if k == 0 else 0.0))
        place2 = (place + step * speed2) * 0.0625
        for j in range(2):
            part[k, pl.ds(j, 16, stride=2), :] = place2[j * 16:(j + 1) * 16]
            part[2 + k, pl.ds(j, 16, stride=2), :] = speed2[j * 16:(j + 1) * 16]
    gas_step = 0.4 / rate[0:1, 0:1]
    lane = iota((32, 256), 1)
    row = iota((32, 256), 0)
    lane16 = iota((16, 128), 1) >> 5
    for k in range(2):
        u = gas[k]
        upper = jnp.where(row == 31, gr[1, k, 0:1, :], pltpu.roll(u, 31, 0))
        lower = jnp.where(row == 0, gr[0, k, 7:8, :], pltpu.roll(u, 1, 0))
        right = jnp.where(lane == 255, gc[1, k, :, 0:1], pltpu.roll(u, 255, 1))
        left = jnp.where(lane == 0, gc[0, k, :, 127:128], pltpu.roll(u, 1, 1))
        laplace = upper + lower + right + left - 4.0 * u
        advect = gas[0] * (upper - lower) * 0.5 + gas[1] * (right - left) * 0.5
        quads = []
        for t in range(2):
            halves = []
            for b in range(2):
                whole = None
                for q in range(4):
                    piece = dv[4 * b + q, k * 16:(k + 1) * 16, :]
                    shift = (q * 32 - t * 32) % 128
                    piece = pltpu.roll(piece, shift, 1) if shift else piece
                    whole = piece if whole is None else jnp.where(lane16 == q, piece, whole)
                halves.append(whole)
            quads.append(jnp.concatenate(halves, axis=1))
        deposit = jnp.concatenate(quads, axis=0)
        source = tot[k:k + 1, 0:1] / 2097152.0 - deposit
        out[k] = u + gas_step * (visc[...] * laplace - advect + source)


CONTACT_SCRATCH = [
    pltpu.SMEM((128, 128), jnp.int32),
    pltpu.VMEM((128, 128), jnp.int32),
    pltpu.VMEM((128 * STRIDE, 128), F32),
    pltpu.VMEM((2, 1408, 128), F32),
    pltpu.VMEM((2, 64, 640), BF16),
    pltpu.VMEM((512, 128), F32),
]


def body(gas, visc, pos, vel, rad, coef, counts, pattern, idx, frac):
    counts_t = counts.T
    pattern_t = pattern.transpose(2, 1, 0)
    pos, vel, frac = (x.reshape(2, 32, 128) for x in (pos, vel, frac))
    rad, coef, idx = (x.reshape(32, 128) for x in (rad, coef, idx))

    def shapes(*dims):
        return [jax.ShapeDtypeStruct(d, F32) for d in dims]

    st, gp, mx = pl.pallas_call(
        prep_kernel,
        out_shape=shapes((8, 32, 128), (8, 32, 128), (8, 128)),
        in_specs=[VMEM_SPEC] * 5 + [SMEM_SPEC],
        out_specs=[VMEM_SPEC] * 3,
        name="prepare",
    )(gas, visc, pos, vel, rad, counts_t)
    ext, gv, rate, gr, gc = exchange(True, st, gp, mx, gas)
    st2, dp, tot, dr2, inverse = pl.pallas_call(
        first_kernel,
        out_shape=shapes((8, 32, 128), (8, 32, 128), (8, 128), (2, 32, 128), (32, 128)),
        in_specs=[VMEM_SPEC] * 6 + [SMEM_SPEC],
        out_specs=[VMEM_SPEC] * 5,
        scratch_shapes=CONTACT_SCRATCH + [pltpu.VMEM((2, 32, 128), F32), pltpu.SemaphoreType.DMA],
        name="first_substep",
    )(ext.reshape(1024, 128), gv, rate, idx, frac, coef, pattern_t)
    ext2, dv, total = exchange(False, st2, dp, tot)
    part, out = pl.pallas_call(
        second_kernel,
        out_shape=shapes((4, 32, 128), (2, 32, 256)),
        in_specs=[VMEM_SPEC] * 10 + [SMEM_SPEC],
        out_specs=[VMEM_SPEC] * 2,
        scratch_shapes=CONTACT_SCRATCH + [pltpu.SemaphoreType.DMA],
        name="second_substep",
    )(ext2.reshape(1024, 128), dv, total, rate, dr2, inverse, gas, visc, gr, gc, pattern_t)
    return part.reshape(4, 16, 2, 128), out


def solution(mesh):
    return jax.shard_map(
        body,
        mesh=mesh,
        in_specs=(
            P(None, ALONG_GAS, "across"),
            P(ALONG_GAS, "across"),
            P(None, "along", ACROSS_GAS, None),
            P(None, "along", ACROSS_GAS, None),
            P("along", ACROSS_GAS, None),
            P("along", ACROSS_GAS, None),
            P("along", ACROSS_GAS),
            P("along", ACROSS_GAS, None),
            P("along", ACROSS_GAS, None),
            P(None, "along", ACROSS_GAS, None),
        ),
        out_specs=(P(None, "along", ACROSS_GAS, None), P(None, ALONG_GAS, "across")),
        check_vma=False,
    )
```

```python
import functools

import jax
import jax.numpy as jnp
from jax import lax
from jax.experimental import pallas as pl
from jax.experimental.pallas import tpu as pltpu
from jax.sharding import PartitionSpec as P

ALONG_GAS = ("along", "gas")
ACROSS_GAS = ("across", "gas")
MESH_ID = pl.DeviceIdType.MESH
OFFSETS = [(-1, -1), (-1, 0), (-1, 1), (0, -1), (0, 0), (0, 1), (1, -1), (1, 0), (1, 1)]
DEAD = -16384.0
F32 = jnp.float32
BF16 = jnp.bfloat16
STRIDE = 136
BLOCK, BLOCK_BITS = 64, 6
EMPTY = 1344
REACH = 2.4
MOVE_LIMIT = int((REACH - 1.9) * 4096)
VMEM_SPEC = pl.BlockSpec(memory_space=pltpu.VMEM)
SMEM_SPEC = pl.BlockSpec(memory_space=pltpu.SMEM)
N_ACROSS, N_ALONG, N_GAS = 4, 8, 8


def iota(shape, dim):
    return lax.broadcasted_iota(jnp.int32, shape, dim)


def ext_row(ii, jj):
    base = {-1: 32, 0: 0, 1: 16, 2: 48}[jj]
    return jnp.where(ii < 0, 64 + 8 * (jj + 1) + 7, jnp.where(ii > 15, 96 + 8 * (jj + 1), base + ii))


def by_column(ref, *lead):
    return jnp.concatenate([ref[(*lead, pl.ds(0, 16, stride=2), slice(None))],
                            ref[(*lead, pl.ds(1, 16, stride=2), slice(None))]], axis=0)


def prepare_state(st, pos, vel, rad, counts):
    row32 = iota((32, 128), 0)
    slot = iota((32, 128), 1)
    cnt = jnp.zeros((32, 128), jnp.int32)
    for j in range(2):
        for i in range(16):
            cnt = jnp.where(row32 == j * 16 + i, counts[j, i], cnt)
    alive = slot < cnt
    z, x = by_column(pos, 0) * 16.0, by_column(pos, 1) * 16.0
    st[0, 0:32, :], st[1, 0:32, :] = z, x
    st[2, 0:32, :], st[3, 0:32, :] = by_column(vel, 0), by_column(vel, 1)
    st[4, 0:32, :] = jnp.where(alive, by_column(rad), DEAD)
    low_x, high_x = x < REACH, x > 16.0 - REACH

    def three(low, mid, high):
        return jnp.where(low_x, low, jnp.where(high_x, high, mid))

    kind = jnp.where(z < REACH, three(0, 1, 2), jnp.where(z > 16.0 - REACH, three(6, 5, 4), three(7, 8, 3)))
    kind = jnp.where(alive, kind, 9)
    member = jnp.concatenate([jnp.where(kind == c, 1.0, 0.0) for c in range(9)], axis=0).astype(BF16)
    before = jnp.where((iota((128, 256), 0) < iota((128, 256), 1)) | (iota((128, 256), 1) >= 128), 1.0, 0.0)
    ranks = jnp.dot(member, before.astype(BF16), preferred_element_type=F32)
    rank = jnp.full((32, 128), -1.0, F32)
    start = [jnp.zeros((32, 128), F32)]
    for c in range(9):
        here = ranks[c * 32:(c + 1) * 32]
        rank = jnp.where(kind == c, start[c] + here[:, 0:128], rank)
        start.append(start[c] + here[:, 128:256])
    st[5, 0:32, :] = rank
    start = [v.astype(jnp.int32) for v in start]
    wrap = ((start[1] + 7) & -8) > start[6]
    zero = jnp.zeros((32, 128), jnp.int32)
    windows = [(start[4], start[5]), (start[4], start[7]), (start[6], start[7]), (start[2], start[5]),
               (zero, start[9]), (jnp.where(wrap, 0, start[6]), start[8]), (start[2], start[3]),
               (zero, start[3]), (zero, start[1]), (zero, jnp.where(wrap, 0, start[1]))]
    table = zero
    for w, (low, high) in enumerate(windows):
        table = jnp.where(slot == 2 * w, low, jnp.where(slot == 2 * w + 1, (high - low + 7) & -8, table))
    st[6, 0:32, :] = table.astype(F32)


def prep_kernel(gas, visc, pos, vel, rad, counts, st, gp, mx):
    rate = jnp.abs(gas[0]) + jnp.abs(gas[1]) + 4.0 * visc[...]
    top = jnp.max(jnp.max(rate, axis=1, keepdims=True), axis=0, keepdims=True)
    mx[...] = jnp.broadcast_to(top, (8, 128))
    lane = iota((16, 128), 1)
    for g in range(N_GAS):
        blk = slice((g // 4) * 128, (g // 4) * 128 + 128)
        off = (g % 4) * 32
        for k in range(2):
            low = gas[k, 0:16, blk]
            high = gas[k, 16:32, blk]
            low = pltpu.roll(low, (128 - off) % 128, 1) if off else low
            shift = (160 - off) % 128
            high = pltpu.roll(high, shift, 1) if shift else high
            piece = jnp.where(lane < 32, low, jnp.where(lane < 64, high, 0.0))
            gp[g, k * 16:(k + 1) * 16, :] = piece
    prepare_state(st, pos, vel, rad, counts)
    st[7] = jnp.zeros((32, 128), F32)


def comm_kernel(first, *refs):
    if first:
        (st, pc, mx, gas, ext, pv, red, gr, gc, mb, m1, m2,
         own_sem, hs, hr, ps, pr, rs, rr, es, er) = refs
    else:
        (st, pc, mx, ext, pv, red, mb, m1, m2,
         own_sem, hs, hr, ps, pr, rs, rr) = refs
    ax, al, g = lax.axis_index("across"), lax.axis_index("along"), lax.axis_index("gas")
    up, down = lax.rem(al + 1, N_ALONG), lax.rem(al + N_ALONG - 1, N_ALONG)
    lin = ax * N_GAS + g
    has_left, has_right = lin > 0, lin < N_ACROSS * N_GAS - 1
    left = jnp.maximum(lin - 1, 0)
    right = jnp.minimum(lin + 1, N_ACROSS * N_GAS - 1)

    def col(index, along):
        return {"across": lax.div(index, N_GAS), "along": along, "gas": lax.rem(index, N_GAS)}

    slab = al * N_GAS + g
    slabs = N_ALONG * N_GAS
    after, before = lax.rem(slab + 1, slabs), lax.rem(slab + slabs - 1, slabs)

    def slab_id(index):
        return {"across": ax, "along": lax.div(index, N_GAS), "gas": lax.rem(index, N_GAS)}

    barrier = pltpu.get_barrier_semaphore()

    def greet(device):
        pl.semaphore_signal(barrier, inc=1, device_id=device, device_id_type=MESH_ID)

    for k in range(1, N_ACROSS):
        greet({"across": lax.rem(ax + k, N_ACROSS)})
    for k in range(1, N_GAS):
        greet({"gas": lax.rem(g + k, N_GAS)})
    for k in range(1, N_ALONG):
        greet({"along": lax.rem(al + k, N_ALONG)})
    expect = N_ACROSS + N_GAS + N_ALONG - 3
    if first:
        greet(slab_id(after))
        greet(slab_id(before))
        expect += 2

    @pl.when(has_left)
    def _():
        for along in (down, al, up):
            greet(col(left, along))

    @pl.when(has_right)
    def _():
        for along in (down, al, up):
            greet(col(right, along))

    own = pltpu.make_async_copy(st, ext.at[:, pl.ds(0, 32)], own_sem.at[0])
    own.start()
    own_piece = pltpu.make_async_copy(pc.at[g], pv.at[g], own_sem.at[1])
    own_piece.start()

    @pl.when(jnp.logical_not(has_left))
    def _():
        ext[:, 32:48, :] = jnp.zeros((8, 16, 128), F32)
        ext[:, 64:72, :] = jnp.zeros((8, 8, 128), F32)
        ext[:, 96:104, :] = jnp.zeros((8, 8, 128), F32)

    @pl.when(jnp.logical_not(has_right))
    def _():
        ext[:, 48:64, :] = jnp.zeros((8, 16, 128), F32)
        ext[:, 88:96, :] = jnp.zeros((8, 8, 128), F32)
        ext[:, 120:128, :] = jnp.zeros((8, 8, 128), F32)

    if first:
        @pl.when(ax == 0)
        def _():
            gc[0] = jnp.zeros((2, 32, 128), F32)

        @pl.when(ax == N_ACROSS - 1)
        def _():
            gc[1] = jnp.zeros((2, 32, 128), F32)

    sides = jnp.where(has_left, 3, 0) + jnp.where(has_right, 3, 0)
    pl.semaphore_wait(barrier, expect + sides)

    def remote(src, dst, send, recv, device):
        return pltpu.make_async_remote_copy(
            src_ref=src, dst_ref=dst, send_sem=send, recv_sem=recv,
            device_id=device, device_id_type=MESH_ID,
        )

    def reduce_sends(phase, src, axis, me, size):
        out = []
        for k in range(1, size):
            out.append(remote(src, mb.at[phase, me], rs.at[phase, k], rr.at[phase, k],
                              {axis: lax.rem(me + k, size)}))
        for c in out:
            c.start()
        return out

    phase0 = reduce_sends(0, mx, "across", ax, N_ACROSS)

    def halo(c, src_rows, size, dst_row, device):
        return remote(st.at[pl.ds(0, 7), pl.ds(src_rows, size)],
                      ext.at[pl.ds(0, 7), pl.ds(dst_row, size)], hs.at[c], hr.at[c], device)

    lefts = [halo(0, 0, 16, 48, col(left, al)),
             halo(1, 8, 8, 64 + 24, col(left, up)),
             halo(2, 0, 8, 96 + 24, col(left, down))]
    rights = [halo(3, 16, 16, 32, col(right, al)),
              halo(4, 24, 8, 64, col(right, up)),
              halo(5, 16, 8, 96, col(right, down))]
    rows = [halo(6, 8, 8, 64 + 8, {"along": up}),
            halo(7, 24, 8, 64 + 16, {"along": up}),
            halo(8, 0, 8, 96 + 8, {"along": down}),
            halo(9, 16, 8, 96 + 16, {"along": down})]

    @pl.when(has_left)
    def _():
        for c in lefts:
            c.start()

    @pl.when(has_right)
    def _():
        for c in rights:
            c.start()

    for c in rows:
        c.start()
    pieces = []
    for k in range(1, N_GAS):
        peer = lax.rem(g + k, N_GAS)
        c = remote(pc.at[peer], pv.at[g], ps.at[k], pr.at[k], {"gas": peer})
        c.start()
        pieces.append(c)
    if first:
        edges = [remote(gas.at[:, pl.ds(24, 8)], gr.at[0], es.at[0], er.at[0], slab_id(after)),
                 remote(gas.at[:, pl.ds(0, 8)], gr.at[1], es.at[1], er.at[1], slab_id(before))]
        for c in edges:
            c.start()
        to_right = remote(gas.at[:, :, pl.ds(128, 128)], gc.at[0], es.at[2], er.at[2],
                          {"across": jnp.minimum(ax + 1, N_ACROSS - 1)})
        to_left = remote(gas.at[:, :, pl.ds(0, 128)], gc.at[1], es.at[3], er.at[3],
                         {"across": jnp.maximum(ax - 1, 0)})

        @pl.when(ax < N_ACROSS - 1)
        def _():
            to_right.start()

        @pl.when(ax > 0)
        def _():
            to_left.start()

    def combine(phase, mine, me, size, copies):
        for c in copies:
            c.wait_recv()
        mb[phase, me] = mine
        total = mb[phase, 0]
        for k in range(1, size):
            total = jnp.maximum(total, mb[phase, k]) if first else total + mb[phase, k]
        return total

    m1[...] = combine(0, mx[...], ax, N_ACROSS, phase0)
    phase1 = reduce_sends(1, m1, "gas", g, N_GAS)
    m2[...] = combine(1, m1[...], g, N_GAS, phase1)
    phase2 = reduce_sends(2, m2, "along", al, N_ALONG)
    red[...] = combine(2, m2[...], al, N_ALONG, phase2)

    own.wait()
    own_piece.wait()
    for c in phase0 + phase1 + phase2:
        c.wait_send()
    for c in rows + pieces:
        c.wait()

    @pl.when(has_left)
    def _():
        for c in lefts:
            c.wait_send()
        for c in rights:
            c.wait_recv()

    @pl.when(has_right)
    def _():
        for c in rights:
            c.wait_send()
        for c in lefts:
            c.wait_recv()

    if first:
        for c in edges:
            c.wait()

        @pl.when(ax < N_ACROSS - 1)
        def _():
            to_right.wait_send()
            to_left.wait_recv()

        @pl.when(ax > 0)
        def _():
            to_left.wait_send()
            to_right.wait_recv()


def exchange(first, st, pc, mx, gas=None):
    out_shape = [jax.ShapeDtypeStruct((8, 128, 128), F32),
                 jax.ShapeDtypeStruct((8, 32, 128), F32),
                 jax.ShapeDtypeStruct((8, 128), F32)]
    scratch = [pltpu.VMEM((3, 8, 8, 128), F32), pltpu.VMEM((8, 128), F32), pltpu.VMEM((8, 128), F32),
               pltpu.SemaphoreType.DMA((2,)),
               pltpu.SemaphoreType.DMA((10,)), pltpu.SemaphoreType.DMA((10,)),
               pltpu.SemaphoreType.DMA((8,)), pltpu.SemaphoreType.DMA((8,)),
               pltpu.SemaphoreType.DMA((3, 8)), pltpu.SemaphoreType.DMA((3, 8))]
    args = [st, pc, mx]
    if first:
        args.append(gas)
        out_shape += [jax.ShapeDtypeStruct((2, 2, 8, 256), F32), jax.ShapeDtypeStruct((2, 2, 32, 128), F32)]
        scratch += [pltpu.SemaphoreType.DMA((4,)), pltpu.SemaphoreType.DMA((4,))]
    return pl.pallas_call(
        functools.partial(comm_kernel, first),
        out_shape=out_shape,
        in_specs=[VMEM_SPEC] * len(args),
        out_specs=[VMEM_SPEC] * len(out_shape),
        scratch_shapes=scratch,
        compiler_params=pltpu.CompilerParams(collective_id=0 if first else 1, has_side_effects=True),
        name="exchange_first" if first else "exchange_second",
    )(*args)


def split3(x):
    hi = x.astype(BF16).astype(F32)
    rest = x - hi
    mid = rest.astype(BF16).astype(F32)
    return hi, mid, rest - mid


def contact_forces(ext, pat, meta, ints, qt, lst, rhs, frc, sem):
    ints[...] = ext[6 * 128:7 * 128, :].astype(jnp.int32)
    to_smem = pltpu.make_async_copy(ints, meta, sem)
    to_smem.start()
    slot = iota((128, 128), 0).astype(F32)
    attr_row = iota((8, 128), 0)
    zero8 = jnp.zeros((8, 128), F32)
    tail = jnp.concatenate([zero8, jnp.ones((24, 128), F32), zero8], axis=0)

    def parts(row):
        block = ext[pl.ds(row, 8, stride=128), :]
        return split3(jnp.where(attr_row < 5, block, 0.0))

    def transposed(row):
        hi, mid, lo = parts(row)
        rows = jnp.concatenate([hi, mid, lo, tail], axis=0).astype(BF16)
        place = (slot == ext[pl.ds(row + 5 * 128, 1), :]).astype(F32).astype(BF16)
        turned = lax.dot_general(place, rows, (((1,), (1,)), ((), ())), preferred_element_type=F32)
        start = row * STRIDE if isinstance(row, int) else pl.multiple_of(row * STRIDE, 8)
        qt[pl.ds(start, 128), 0:64] = turned
        start = start + 128 if isinstance(row, int) else pl.multiple_of(start + 128, 8)
        qt[pl.ds(start, 8), :] = zero8

    def some(step, carry):
        for u in range(4):
            transposed(step * 4 + u)
        return carry

    lax.fori_loop(0, 16, some, 0)
    for c in range(4):
        transposed(64 + 8 * c + 7)
        transposed(96 + 8 * c)

    block_of = iota((32, 640), 1) >> 7
    row_of = iota((32, 640), 0)
    attr_of = row_of & 7
    own_scale = jnp.where(block_of < 2, -1.0, jnp.where(block_of < 4, 2.0, 1.0))
    const = jnp.where((attr_of == block_of) & (row_of < 24), own_scale, 0.0)
    const = jnp.where((row_of == 24) & (block_of == 0) | (row_of == 25) & (block_of == 1), -16.0, const)
    for u in range(2):
        rhs[u, 0:32, :] = const.astype(BF16)
        lst[u, EMPTY:EMPTY + BLOCK, :] = jnp.zeros((BLOCK, 128), F32)
    to_smem.wait()
    lane = iota((8, 128), 1)

    def row_step(i, carry):
        blocks = []
        for j in range(2):
            work = lst.at[j]
            mine = j * 16 + i
            hi, mid, lo = parts(mine)
            columns = []
            for a in range(5):
                keep = attr_row == a
                scale = 1.0 if a in (0, 1, 4) else -2.0
                columns.append(jnp.concatenate(
                    [jnp.where(keep, hi * scale, 0.0), jnp.where(keep, mid * scale, 0.0),
                     jnp.where(keep, lo * scale, 0.0), zero8], axis=0))
            rhs[j, 32:64, :] = jnp.concatenate(columns, axis=1).astype(BF16)
            moved = meta[mine, 20]
            off = i * 0
            over = i * 0
            windows = []
            for w in (4, 0, 1, 2, 3, 5, 6, 7, 8, 9):
                di, dj = OFFSETS[5 if w == 9 else w]
                row = ext_row(i + di, j + dj)
                first, size = meta[row, 2 * w], meta[row, 2 * w + 1]
                if w != 4:
                    near = moved + meta[row, 20] <= MOVE_LIMIT
                    first = jnp.where(near, first, 0)
                    size = jnp.where(near, size, 0 if w == 9 else meta[row, 9])
                size = size * pat[5 if w == 9 else w, j, i]
                mark = jnp.where(lane == 24, float(di), jnp.where(lane == 25, float(dj), 0.0))
                start = row * STRIDE + first
                chunks = 16 if w == 4 else 4 if w in (1, 3, 5, 7) else 1
                for c in range(chunks):
                    work[pl.ds(pl.multiple_of(off + c * 8, 8), 8), :] = qt[pl.ds(start + c * 8, 8), :] + mark
                windows.append((start, size, mark))
                off = off + size
                over = jnp.maximum(over, size - chunks * 8)

            @pl.when(over > 0)
            def _():
                to = i * 0
                for start, size, mark in windows:
                    def copy(c, carry, start=start, mark=mark, to=to):
                        work[pl.ds(pl.multiple_of(to + c * 8, 8), 8), :] = qt[pl.ds(start + c * 8, 8), :] + mark
                        return carry
                    lax.fori_loop(0, size >> 3, copy, 0)
                    to = to + size

            for c in range(BLOCK // 8):
                work[pl.ds(pl.multiple_of(off + c * 8, 8), 8), :] = zero8
            blocks.append((off + BLOCK - 1) >> BLOCK_BITS)
        right = [rhs[0], rhs[1]]

        def block(b, acc):
            out = []
            for j in range(2):
                at = jnp.where(b < blocks[j], b * BLOCK, EMPTY)
                q = lst[j, pl.ds(pl.multiple_of(at, 8), BLOCK), 0:64].astype(BF16)
                got = jnp.dot(q, right[j], preferred_element_type=F32)
                rz, rx = got[:, 0:128], got[:, 128:256]
                dz, dx = got[:, 256:384], got[:, 384:512]
                d2 = rz * rz + rx * rx + 0.0001
                inv = lax.rsqrt(d2)
                depth = jnp.maximum(got[:, 512:640] - d2 * inv, 0.0)
                push = depth * inv * (40.0 + (dz * rz + dx * rx) * inv)
                out.append(acc[2 * j] + jnp.sum((push * rz).reshape(BLOCK // 8, 8, 128), axis=0))
                out.append(acc[2 * j + 1] + jnp.sum((push * rx).reshape(BLOCK // 8, 8, 128), axis=0))
            return tuple(out)

        acc = lax.fori_loop(0, jnp.maximum(blocks[0], blocks[1]), block, (zero8,) * 4)
        for j in range(2):
            for k in range(2):
                frc[pl.ds(pl.multiple_of(((k * 2 + j) * 16 + i) * 8, 8), 8), :] = acc[2 * j + k]
        return carry

    lax.fori_loop(0, 16, row_step, 0)
    return [sum(frc[pl.ds(k * 256 + r, 32, stride=8), :] for r in range(8)) for k in range(2)]


def first_kernel(ext, gv, rate, idx, frac, coef, pat, st2, dp, tot, dr2, inv_out,
                 meta, ints, qt, lst, rhs, frc, itp, sem):
    def weights(r, t4):
        index = idx[pl.ds(r, 1), :]
        row, column = index >> 4, index & 15
        share_z = frac[0, pl.ds(r, 1), :].astype(F32) / 1024.0
        share_x = frac[1, pl.ds(r, 1), :].astype(F32) / 1024.0
        c64 = iota((64, 128), 0) - t4 * 16
        wx = jnp.where(c64 == column, 1.0 - share_x, jnp.where(c64 == column + 1, share_x, 0.0))
        r16 = iota((16, 128), 0)
        wz = jnp.where(r16 == row, 1.0 - share_z, jnp.where(r16 == row + 1, share_z, 0.0))
        return wz, wx

    def sample(h, carry):
        field = gv[h][:, 0:64]
        for t in range(2):
            for j in range(2):
                wz, wx = weights(4 * h + 2 * t + j, t * 2 + j)
                along = jnp.dot(field, wx, precision=lax.Precision.HIGHEST, preferred_element_type=F32)
                for k in range(2):
                    itp[k, pl.ds(j * 16 + 2 * h + t, 1), :] = jnp.sum(
                        wz * along[k * 16:(k + 1) * 16], axis=0, keepdims=True)
        return carry

    lax.fori_loop(0, 8, sample, 0)
    force = contact_forces(ext, pat, meta, ints, qt, lst, rhs, frc, sem)
    step = 0.2 / rate[0:1, :]
    drag = by_column(coef)
    radius = ext[4 * 128:4 * 128 + 32, :]
    alive = jnp.where(radius > 0.0, 1.0, 0.0)
    inverse = jnp.where(radius > 0.0, 0.36 / (radius * radius), 0.0)
    inv_out[...] = inverse
    means = []
    moved = jnp.zeros((32, 128), F32)
    for k in range(2):
        place = ext[k * 128:k * 128 + 32, :]
        speed = ext[(2 + k) * 128:(2 + k) * 128 + 32, :]
        drag1 = drag * (itp[k] - speed)
        speed2 = speed + step * (inverse * (force[k] + drag1) - (alive if k == 0 else 0.0))
        st2[k] = place + step * speed2
        moved = jnp.maximum(moved, alive * jnp.abs(step * speed2))
        st2[2 + k] = speed2
        drag2 = drag * (itp[k] - speed2)
        dr2[k] = drag2
        mean = 0.5 * (alive * drag1 + alive * drag2)
        itp[k] = mean
        means.append(jnp.sum(jnp.sum(mean, axis=1, keepdims=True), axis=0, keepdims=True))
    st2[4] = radius
    st2[5] = ext[5 * 128:5 * 128 + 32, :]
    far = jnp.max(moved, axis=1, keepdims=True)
    far = jnp.where(far < 100.0, far, 100.0) * 4096.0 + 1.0
    st2[6] = jnp.where(iota((32, 128), 1) == 20, far, ext[6 * 128:6 * 128 + 32, :])
    st2[7] = jnp.zeros((32, 128), F32)
    tot[...] = jnp.where(iota((8, 128), 0) == 0, means[0], means[1])

    def spread(h, carry):
        total = jnp.zeros((32, 64), F32)
        for t in range(2):
            for j in range(2):
                wz, wx = weights(4 * h + 2 * t + j, t * 2 + j)
                m0 = itp[0, pl.ds(j * 16 + 2 * h + t, 1), :]
                m1 = itp[1, pl.ds(j * 16 + 2 * h + t, 1), :]
                lhs = jnp.concatenate([wz * m0, wz * m1], axis=0)
                total = total + lax.dot_general(lhs, wx, (((1,), (1,)), ((), ())),
                                                precision=lax.Precision.HIGHEST, preferred_element_type=F32)
        dp[h, :, 0:64] = total
        dp[h, :, 64:128] = jnp.zeros((32, 64), F32)
        return carry

    lax.fori_loop(0, 8, spread, 0)


def gas_step_update(gas, visc, gr, gc, dv, tot, rate, out):
    gas_step = 0.4 / rate[0:1, 0:1]
    lane = iota((32, 256), 1)
    row = iota((32, 256), 0)
    lane16 = iota((16, 128), 1) >> 5
    for k in range(2):
        u = gas[k]
        upper = jnp.where(row == 31, gr[1, k, 0:1, :], pltpu.roll(u, 31, 0))
        lower = jnp.where(row == 0, gr[0, k, 7:8, :], pltpu.roll(u, 1, 0))
        right = jnp.where(lane == 255, gc[1, k, :, 0:1], pltpu.roll(u, 255, 1))
        left = jnp.where(lane == 0, gc[0, k, :, 127:128], pltpu.roll(u, 1, 1))
        laplace = upper + lower + right + left - 4.0 * u
        advect = gas[0] * (upper - lower) * 0.5 + gas[1] * (right - left) * 0.5
        quads = []
        for t in range(2):
            halves = []
            for b in range(2):
                whole = None
                for q in range(4):
                    piece = dv[4 * b + q, k * 16:(k + 1) * 16, :]
                    shift = (q * 32 - t * 32) % 128
                    piece = pltpu.roll(piece, shift, 1) if shift else piece
                    whole = piece if whole is None else jnp.where(lane16 == q, piece, whole)
                halves.append(whole)
            quads.append(jnp.concatenate(halves, axis=1))
        deposit = jnp.concatenate(quads, axis=0)
        source = tot[k:k + 1, 0:1] / 2097152.0 - deposit
        out[k] = u + gas_step * (visc[...] * laplace - advect + source)


def second_kernel(ext, dv, tot, rate, dr2, inverse, gas, visc, gr, gc, pat, part, out,
                  meta, ints, qt, lst, rhs, frc, sem):
    force = contact_forces(ext, pat, meta, ints, qt, lst, rhs, frc, sem)
    step = 0.2 / rate[0:1, :]
    radius = ext[4 * 128:4 * 128 + 32, :]
    alive = jnp.where(radius > 0.0, 1.0, 0.0)
    for k in range(2):
        place = ext[k * 128:k * 128 + 32, :]
        speed = ext[(2 + k) * 128:(2 + k) * 128 + 32, :]
        speed2 = speed + step * (inverse[...] * (force[k] + dr2[k]) - (alive if k == 0 else 0.0))
        place2 = (place + step * speed2) * 0.0625
        for j in range(2):
            part[k, pl.ds(j, 16, stride=2), :] = place2[j * 16:(j + 1) * 16]
            part[2 + k, pl.ds(j, 16, stride=2), :] = speed2[j * 16:(j + 1) * 16]
    gas_step_update(gas, visc, gr, gc, dv, tot, rate, out)


CONTACT_SCRATCH = [
    pltpu.SMEM((128, 128), jnp.int32),
    pltpu.VMEM((128, 128), jnp.int32),
    pltpu.VMEM((128 * STRIDE, 128), F32),
    pltpu.VMEM((2, 1408, 128), F32),
    pltpu.VMEM((2, 64, 640), BF16),
    pltpu.VMEM((512, 128), F32),
]


def general(gas, visc, pos, vel, rad, coef, counts_t, pattern_t, idx, frac):

    def shapes(*dims):
        return [jax.ShapeDtypeStruct(d, F32) for d in dims]

    st, gp, mx = pl.pallas_call(
        prep_kernel,
        out_shape=shapes((8, 32, 128), (8, 32, 128), (8, 128)),
        in_specs=[VMEM_SPEC] * 5 + [SMEM_SPEC],
        out_specs=[VMEM_SPEC] * 3,
        name="prepare",
    )(gas, visc, pos, vel, rad, counts_t)
    ext, gv, rate, gr, gc = exchange(True, st, gp, mx, gas)
    st2, dp, tot, dr2, inverse = pl.pallas_call(
        first_kernel,
        out_shape=shapes((8, 32, 128), (8, 32, 128), (8, 128), (2, 32, 128), (32, 128)),
        in_specs=[VMEM_SPEC] * 6 + [SMEM_SPEC],
        out_specs=[VMEM_SPEC] * 5,
        scratch_shapes=CONTACT_SCRATCH + [pltpu.VMEM((2, 32, 128), F32), pltpu.SemaphoreType.DMA],
        name="first_substep",
    )(ext.reshape(1024, 128), gv, rate, idx, frac, coef, pattern_t)
    ext2, dv, total = exchange(False, st2, dp, tot)
    part, out = pl.pallas_call(
        second_kernel,
        out_shape=shapes((4, 32, 128), (2, 32, 256)),
        in_specs=[VMEM_SPEC] * 10 + [SMEM_SPEC],
        out_specs=[VMEM_SPEC] * 2,
        scratch_shapes=CONTACT_SCRATCH + [pltpu.SemaphoreType.DMA],
        name="second_substep",
    )(ext2.reshape(1024, 128), dv, total, rate, dr2, inverse, gas, visc, gr, gc, pattern_t)
    return part, out


EDGE_BASE, CORNER_BASE, WINDOW_ROWS = 48, 192, 256
CORNER = 16
WINDOWS = ((-1, 0), (1, 0), (0, -1), (0, 1), (-1, -1), (-1, 1), (1, -1), (1, 1))
NEAR = ((1.82, 0.0), (2.25, 0.43))
EDGE = 40


def fused_kernel(gas, visc, pos, vel, rad, coef, idx, frac, pat, counts, part, out, flag,
                 ext, ext2, gp, gv, dp, dv, gr, gc, mb, mv, sb, sv, rk, qs, qw, rhs, frc, itp, wts,
                 hs, hr, ps, pr, rs, rr, es, er):
    ax, al, g = lax.axis_index("across"), lax.axis_index("along"), lax.axis_index("gas")
    up, down = lax.rem(al + 1, N_ALONG), lax.rem(al + N_ALONG - 1, N_ALONG)
    lin = ax * N_GAS + g
    has_left, has_right = lin > 0, lin < N_ACROSS * N_GAS - 1
    left = jnp.maximum(lin - 1, 0)
    right = jnp.minimum(lin + 1, N_ACROSS * N_GAS - 1)

    def col(index, along):
        return {"across": lax.div(index, N_GAS), "along": along, "gas": lax.rem(index, N_GAS)}

    slab = al * N_GAS + g
    slabs = N_ALONG * N_GAS
    after, before = lax.rem(slab + 1, slabs), lax.rem(slab + slabs - 1, slabs)

    def slab_id(index):
        return {"across": ax, "along": lax.div(index, N_GAS), "gas": lax.rem(index, N_GAS)}

    barrier = pltpu.get_barrier_semaphore()

    def greet(device):
        pl.semaphore_signal(barrier, inc=1, device_id=device, device_id_type=MESH_ID)

    for k in range(1, N_ACROSS):
        greet({"across": lax.rem(ax + k, N_ACROSS)})
    for k in range(1, N_GAS):
        greet({"gas": lax.rem(g + k, N_GAS)})
    for k in range(1, N_ALONG):
        greet({"along": lax.rem(al + k, N_ALONG)})
    greet(slab_id(after))
    greet(slab_id(before))
    expect = N_ACROSS + N_GAS + N_ALONG - 3 + 2

    @pl.when(has_left)
    def _():
        for along in (down, al, up):
            greet(col(left, along))

    @pl.when(has_right)
    def _():
        for along in (down, al, up):
            greet(col(right, along))

    rate = jnp.abs(gas[0]) + jnp.abs(gas[1]) + 4.0 * visc[...]
    top = jnp.max(jnp.max(rate, axis=1, keepdims=True), axis=0, keepdims=True)
    mv[0] = jnp.broadcast_to(top, (8, 128))
    lane = iota((16, 128), 1)
    for d in range(N_GAS):
        blk = slice((d // 4) * 128, (d // 4) * 128 + 128)
        off = (d % 4) * 32
        for k in range(2):
            low = gas[k, 0:16, blk]
            high = gas[k, 16:32, blk]
            low = pltpu.roll(low, (128 - off) % 128, 1) if off else low
            shift = (160 - off) % 128
            high = pltpu.roll(high, shift, 1) if shift else high
            piece = jnp.where(lane < 32, low, high)
            gp[d, k * 16:(k + 1) * 16, :] = jnp.where(lane < 64, piece, pltpu.roll(piece, 64, 1))
    row32 = iota((32, 128), 0)
    cnt = jnp.zeros((32, 128), jnp.int32)
    for j in range(2):
        for i in range(16):
            cnt = jnp.where(row32 == j * 16 + i, counts[j, i], cnt)
    ext[0, 0:32, :], ext[1, 0:32, :] = by_column(pos, 0) * 16.0, by_column(pos, 1) * 16.0
    ext[2, 0:32, :], ext[3, 0:32, :] = by_column(vel, 0), by_column(vel, 1)
    ext[4, 0:32, :] = jnp.where(iota((32, 128), 1) < cnt, by_column(rad), DEAD)
    for e in (ext, ext2):
        @pl.when(jnp.logical_not(has_left))
        def _():
            e[:, 32:48, :] = jnp.zeros((8, 16, 128), F32)
            e[:, 64:72, :] = jnp.zeros((8, 8, 128), F32)
            e[:, 96:104, :] = jnp.zeros((8, 8, 128), F32)

        @pl.when(jnp.logical_not(has_right))
        def _():
            e[:, 48:64, :] = jnp.zeros((8, 16, 128), F32)
            e[:, 88:96, :] = jnp.zeros((8, 8, 128), F32)
            e[:, 120:128, :] = jnp.zeros((8, 8, 128), F32)

    @pl.when(ax == 0)
    def _():
        gc[0] = jnp.zeros((2, 32, 128), F32)

    @pl.when(ax == N_ACROSS - 1)
    def _():
        gc[1] = jnp.zeros((2, 32, 128), F32)

    sides = jnp.where(has_left, 3, 0) + jnp.where(has_right, 3, 0)
    pl.semaphore_wait(barrier, expect + sides)

    def remote(src, dst, send, recv, device):
        return pltpu.make_async_remote_copy(
            src_ref=src, dst_ref=dst, send_sem=send, recv_sem=recv,
            device_id=device, device_id_type=MESH_ID,
        )

    axes = (("across", ax, N_ACROSS), ("gas", g, N_GAS), ("along", al, N_ALONG))

    def reduce_start(which, phase):
        slots, value = ((mb, mv), (sb, sv))[which]
        axis, me, size = axes[phase]
        out = [remote(value.at[phase], slots.at[phase, me], rs.at[which, phase, k], rr.at[which, phase, k],
                      {axis: lax.rem(me + k, size)}) for k in range(1, size)]
        for c in out:
            c.start()
        slots[phase, me] = value[phase]
        return out

    def reduce_end(which, phase, copies):
        slots, value = ((mb, mv), (sb, sv))[which]
        size = axes[phase][2]
        for c in copies:
            c.wait_recv()
        total = slots[phase, 0]
        for k in range(1, size):
            total = total + slots[phase, k] if which else jnp.maximum(total, slots[phase, k])
        value[phase + 1] = total
        for c in copies:
            c.wait_send()

    def halo_start(which):
        e, attrs = ((ext, 5), (ext2, 5))[which]

        def halo(c, src_row, size, dst_row, device):
            return remote(e.at[pl.ds(0, attrs), pl.ds(src_row, size)],
                          e.at[pl.ds(0, attrs), pl.ds(dst_row, size)], hs.at[which, c], hr.at[which, c], device)

        lefts = [halo(0, 0, 16, 48, col(left, al)),
                 halo(1, 8, 8, 64 + 24, col(left, up)),
                 halo(2, 0, 8, 96 + 24, col(left, down))]
        rights = [halo(3, 16, 16, 32, col(right, al)),
                  halo(4, 24, 8, 64, col(right, up)),
                  halo(5, 16, 8, 96, col(right, down))]
        rows = [halo(6, 8, 8, 64 + 8, {"along": up}),
                halo(7, 24, 8, 64 + 16, {"along": up}),
                halo(8, 0, 8, 96 + 8, {"along": down}),
                halo(9, 16, 8, 96 + 16, {"along": down})]

        @pl.when(has_left)
        def _():
            for c in lefts:
                c.start()

        @pl.when(has_right)
        def _():
            for c in rights:
                c.start()

        for c in rows:
            c.start()
        return lefts, rights, rows

    def halo_end(copies):
        lefts, rights, rows = copies
        for c in rows:
            c.wait()

        @pl.when(has_left)
        def _():
            for c in lefts:
                c.wait_send()
            for c in rights:
                c.wait_recv()

        @pl.when(has_right)
        def _():
            for c in rights:
                c.wait_send()
            for c in lefts:
                c.wait_recv()

    def pieces_start(which):
        src, dst = ((gp, gv), (dp, dv))[which]
        out = []
        for k in range(1, N_GAS):
            peer = lax.rem(g + k, N_GAS)
            c = remote(src.at[peer], dst.at[g], ps.at[which, k], pr.at[which, k], {"gas": peer})
            c.start()
            out.append(c)
        dst[g] = src[g]
        return out

    phase = reduce_start(0, 0)
    halos = halo_start(0)
    pieces = pieces_start(0)
    edges = [remote(gas.at[:, pl.ds(24, 8)], gr.at[0], es.at[0], er.at[0], slab_id(after)),
             remote(gas.at[:, pl.ds(0, 8)], gr.at[1], es.at[1], er.at[1], slab_id(before))]
    for c in edges:
        c.start()
    to_right = remote(gas.at[:, :, pl.ds(128, 128)], gc.at[0], es.at[2], er.at[2],
                      {"across": jnp.minimum(ax + 1, N_ACROSS - 1)})
    to_left = remote(gas.at[:, :, pl.ds(0, 128)], gc.at[1], es.at[3], er.at[3],
                     {"across": jnp.maximum(ax - 1, 0)})

    @pl.when(ax < N_ACROSS - 1)
    def _():
        to_right.start()

    @pl.when(ax > 0)
    def _():
        to_left.start()

    slot_row = iota((48, 128), 0)
    slots = (jnp.where(slot_row < EDGE, slot_row, -5).astype(F32),
             jnp.where(slot_row < 32, slot_row, jnp.where(slot_row < 40, -5, slot_row - 8)).astype(F32))
    attr_row = iota((8, 128), 0)
    zero8 = jnp.zeros((8, 128), F32)
    one_tail = jnp.concatenate([zero8, jnp.ones((24, 128), F32), zero8], axis=0)
    flat = (ext.reshape(1024, 128), ext2.reshape(1024, 128))
    eye = jnp.where(iota((128, 128), 0) == iota((128, 128), 1), 1.0, 0.0).astype(BF16)
    before_slot = jnp.where(iota((128, 128), 0) < iota((128, 128), 1), 1.0, 0.0).astype(BF16)

    def rank(which, low, high):
        e = (ext, ext2)[which]
        reach, _ = NEAR[which]
        z, x, live = e[0, low:high, :], e[1, low:high, :], e[4, low:high, :] > 0.0

        def flags(cond):
            return jnp.where(cond & live, 1.0, 0.0)

        lz, hz, lx, hx = flags(z < reach), flags(z > 16.0 - reach), flags(x < reach), flags(x > 16.0 - reach)
        member = [hz, lz, hx, lx, hz * hx, hz * lx, lz * hx, lz * lx]
        size = high - low
        places = jnp.dot(jnp.concatenate(member, axis=0).astype(BF16), before_slot, preferred_element_type=F32)
        lost = jnp.zeros((size, 128), F32)
        for w in range(8):
            place = places[w * size:(w + 1) * size]
            rk[w, low:high, :] = jnp.where(member[w] > 0.0, place, -1.0)
            lost = lost + jnp.where(place >= (EDGE if w < 4 else CORNER), member[w], 0.0)
        return lost

    def parts(which, row):
        block = flat[which][pl.ds(row, 8, stride=128), :]
        return split3(jnp.where(attr_row < 5, block, 0.0))

    def window_rows(which, row, rows, windows):
        sizes = [48 if w < 4 else CORNER for w in windows]
        place = jnp.concatenate(
            [(slots[w & 1 if w < 4 else 0][0:n] == rk[w, pl.ds(row, 1), :]).astype(F32) for w, n in zip(windows, sizes)], axis=0)
        turned = lax.dot_general(place.astype(BF16), rows, (((1,), (1,)), ((), ())), preferred_element_type=F32)
        turned = turned.astype(BF16)
        at = 0
        for w, n in zip(windows, sizes):
            start = row * WINDOW_ROWS + (w * EDGE_BASE if w < 4 else CORNER_BASE + (w - 4) * CORNER)
            if not isinstance(row, int):
                start = pl.multiple_of(start, 16)
            qw[pl.ds(start, n), 0:64] = turned[at:at + n]
            at += n

    def own_tiles(which):
        def some(step, carry):
            for u in range(2):
                row = step * 2 + u
                hi, mid, lo = parts(which, row)
                rows = jnp.concatenate([hi, mid, lo, one_tail], axis=0).astype(BF16)
                turned = lax.dot_general(eye, rows, (((1,), (1,)), ((), ())), preferred_element_type=F32)
                qs[pl.ds(pl.multiple_of(row * 128, 128), 128), 0:64] = turned.astype(BF16)
                window_rows(which, row, rows, range(8))
                columns = []
                for a in range(5):
                    keep = attr_row == a
                    scale = 1.0 if a in (0, 1, 4) else -2.0
                    columns.append(jnp.concatenate(
                        [jnp.where(keep, hi * scale, 0.0), jnp.where(keep, mid * scale, 0.0),
                         jnp.where(keep, lo * scale, 0.0), zero8], axis=0))
                rhs[row, 32:64, :] = jnp.concatenate(columns, axis=1).astype(BF16)
            return carry
        lax.fori_loop(0, 16, some, 0)

    def halo_tile(which, row, windows):
        hi, mid, lo = parts(which, row)
        window_rows(which, row, jnp.concatenate([hi, mid, lo, one_tail], axis=0).astype(BF16), windows)

    def halo_tiles(which):
        rank(which, 32, 128)

        def some(step, carry):
            for u in range(2):
                halo_tile(which, 32 + step * 2 + u, (2, 4, 6))
                halo_tile(which, 48 + step * 2 + u, (3, 5, 7))
            return carry
        lax.fori_loop(0, 8, some, 0)
        for c in range(4):
            halo_tile(which, 64 + 8 * c + 7, (0, 4, 5))
            halo_tile(which, 96 + 8 * c, (1, 6, 7))

    block_of = iota((32, 640), 1) >> 7
    row_of = iota((32, 640), 0)
    attr_of = row_of & 7
    own_scale = jnp.where(block_of < 2, -1.0, jnp.where(block_of < 4, 2.0, 1.0))
    const = jnp.where((attr_of == block_of) & (row_of < 24), own_scale, 0.0)
    const = jnp.where((row_of == 24) & (block_of == 0) | (row_of == 25) & (block_of == 1), -16.0, const)
    const = jnp.where((row_of == 26) & (block_of == 4), DEAD, const)
    const = const.astype(BF16)
    lane16 = iota((16, 128), 1)
    half = iota((16, 128), 0) < 8

    def constants(t, carry):
        rhs[t, 0:32, :] = const
        return carry

    lax.fori_loop(0, 32, constants, 0)
    lost = rank(0, 0, 32)
    own_tiles(0)
    unlisted = jnp.where(lane16 == 26, 1.0, 0.0)

    def contact_rows(first, last):

        def step(i, carry):
            for j in range(2):
                t = j * 16 + i
                right = rhs[t]

                def mark_of(n):
                    di, dj = OFFSETS[n]
                    base = jnp.where(lane16 == 24, float(di), jnp.where(lane16 == 25, float(dj), 0.0))
                    return base + unlisted * (1 - pat[n, j, i]).astype(F32)

                def mark(n):
                    return mark_of(n).astype(BF16)

                def border(w):
                    di, dj = WINDOWS[w]
                    row = ext_row(i + di, j + dj)
                    n = 48 if w < 4 else CORNER
                    start = row * WINDOW_ROWS + (w * EDGE_BASE if w < 4 else CORNER_BASE + (w - 4) * CORNER)
                    return qw[pl.ds(pl.multiple_of(start, 16), n), :], mark_of(3 * (di + 1) + dj + 1)

                def edges_of(w):
                    (one, mark1), (two, mark2) = border(w), border(w + 1)
                    both = one[32:48] + two[32:48] + jnp.where(half, mark1, mark2).astype(BF16)
                    mark1, mark2 = mark1.astype(BF16), mark2.astype(BF16)
                    return jnp.concatenate([one[0:16] + mark1, one[16:32] + mark1,
                                            two[0:16] + mark2, two[16:32] + mark2, both], axis=0)

                def corner(w):
                    block, here = border(w)
                    return block + here.astype(BF16)

                own = qs[pl.ds(pl.multiple_of(t * 128, 128), 128), :] + jnp.concatenate([mark(4)] * 8, axis=0)
                groups = [own, edges_of(0), edges_of(2), jnp.concatenate([corner(w) for w in range(4, 8)], axis=0)]
                fz, fx = zero8, zero8
                for q in groups:
                    got = jnp.dot(q[:, 0:64], right, preferred_element_type=F32)
                    rz, rx = got[:, 0:128], got[:, 128:256]
                    dz, dx = got[:, 256:384], got[:, 384:512]
                    inv = lax.rsqrt(rz * rz + rx * rx + 0.0001)
                    push = jnp.maximum(got[:, 512:640] * inv - 1.0, 0.0) * (40.0 + (dz * rz + dx * rx) * inv)
                    count = q.shape[0] // 8
                    fz = fz + jnp.sum((push * rz).reshape(count, 8, 128), axis=0)
                    fx = fx + jnp.sum((push * rx).reshape(count, 8, 128), axis=0)
                frc[pl.ds(pl.multiple_of(t * 8, 8), 8), :] = fz
                frc[pl.ds(pl.multiple_of(t * 8 + 256, 8), 8), :] = fx
            return carry
        lax.fori_loop(first, last, step, 0)

    def forces():
        return [sum(frc[pl.ds(k * 256 + r, 32, stride=8), :] for r in range(8)) for k in range(2)]

    index = idx[...]
    share_z = frac[0].astype(F32) / 1024.0
    share_x = frac[1].astype(F32) / 1024.0
    wts[0] = (index >> 4).astype(F32)
    wts[1] = (index & 15).astype(F32)
    wts[2], wts[3] = 1.0 - share_z, share_z
    for n, share in ((4, 1.0 - share_x), (6, share_x)):
        high = share.astype(BF16).astype(F32)
        wts[n], wts[n + 1] = high, share - high
    c64 = iota((64, 128), 0).astype(F32)
    r16 = iota((16, 128), 0).astype(F32)

    def weights(r, t4):
        def get(n):
            return wts[n, pl.ds(r, 1), :]
        column, row = get(1) + (16.0 * t4), get(0)
        here, there = c64 == column, c64 == column + 1.0
        high = jnp.where(here, get(4), jnp.where(there, get(6), 0.0)).astype(BF16)
        low = jnp.where(here, get(5), jnp.where(there, get(7), 0.0)).astype(BF16)
        wz = jnp.where(r16 == row, get(2), jnp.where(r16 == row + 1.0, get(3), 0.0))
        return wz, high, low

    phase_end = reduce_end
    for c in pieces:
        c.wait()
    lane32 = iota((32, 128), 1)

    def sample(h, carry):
        field = gv[h]
        high = field.astype(BF16).astype(F32)
        both = jnp.where(lane32 < 64, high, field - high).astype(BF16)
        for t in range(2):
            for j in range(2):
                wz, whi, wlo = weights(4 * h + 2 * t + j, t * 2 + j)
                right = jnp.concatenate([jnp.concatenate([whi, whi], axis=0),
                                         jnp.concatenate([wlo, wlo], axis=0)], axis=1)
                got = jnp.dot(both, right, preferred_element_type=F32)
                got = got[:, 0:128] + got[:, 128:256]
                for k in range(2):
                    itp[k, pl.ds(j * 16 + 2 * h + t, 1), :] = jnp.sum(
                        wz * got[k * 16:(k + 1) * 16], axis=0, keepdims=True)
        return carry

    lax.fori_loop(0, 8, sample, 0)
    phase_end(0, 0, phase)
    phase = reduce_start(0, 1)
    halo_end(halos)

    halo_tiles(0)

    contact_rows(0, 4)
    phase_end(0, 1, phase)
    phase = reduce_start(0, 2)
    contact_rows(4, 16)
    phase_end(0, 2, phase)
    step = 0.2 / mv[3][0:1, :]
    drag = by_column(coef)
    radius = ext[4, 0:32, :]
    alive = jnp.where(radius > 0.0, 1.0, 0.0)
    inverse = jnp.where(radius > 0.0, 0.36 / (radius * radius), 0.0)
    force = forces()
    drags = []
    slack = NEAR[1][1]
    for k in range(2):
        speed = ext[2 + k, 0:32, :]
        drag1 = drag * (itp[k] - speed)
        speed2 = speed + step * (inverse * (force[k] + drag1) - (alive if k == 0 else 0.0))
        place2 = ext[k, 0:32, :] + step * speed2
        ext2[k, 0:32, :] = place2
        inside = (place2 >= -slack) & (place2 <= 16.0 + slack)
        lost = lost + jnp.where(inside, 0.0, alive)
        ext2[2 + k, 0:32, :] = speed2
        drag2 = drag * (itp[k] - speed2)
        drags.append((drag1, drag2))
    ext2[4, 0:32, :] = radius
    halos = halo_start(1)
    bad = lost + rank(1, 0, 32)
    sums = []
    for k in range(2):
        drag1, drag2 = drags[k]
        mean = 0.5 * (alive * drag1 + alive * drag2)
        itp[k] = mean
        itp[2 + k] = drag2
        sums.append(jnp.sum(jnp.sum(mean, axis=1, keepdims=True), axis=0, keepdims=True))
    bad = jnp.sum(jnp.sum(bad, axis=1, keepdims=True), axis=0, keepdims=True)
    sv[0] = jnp.where(attr_row == 0, sums[0], jnp.where(attr_row == 1, sums[1], bad))
    phase = reduce_start(1, 0)

    def spread(h, carry):
        total = jnp.zeros((64, 128), F32)
        for t in range(2):
            for j in range(2):
                wz, whi, wlo = weights(4 * h + 2 * t + j, t * 2 + j)
                m0 = itp[0, pl.ds(j * 16 + 2 * h + t, 1), :]
                m1 = itp[1, pl.ds(j * 16 + 2 * h + t, 1), :]
                lhs = jnp.concatenate([wz * m0, wz * m1], axis=0)
                high = lhs.astype(BF16)
                low = (lhs - high.astype(F32)).astype(BF16)
                total = total + lax.dot_general(
                    jnp.concatenate([high, low], axis=0), jnp.concatenate([whi, wlo], axis=0),
                    (((1,), (1,)), ((), ())), preferred_element_type=F32)
        total = total[0:32] + total[32:64]
        dp[h] = total + pltpu.roll(total, 64, 1)
        return carry

    lax.fori_loop(0, 8, spread, 0)
    pieces = pieces_start(1)
    own_tiles(1)
    phase_end(1, 0, phase)
    phase = reduce_start(1, 1)
    halo_end(halos)
    halo_tiles(1)

    contact_rows(0, 4)
    phase_end(1, 1, phase)
    phase = reduce_start(1, 2)
    contact_rows(4, 16)
    force = forces()
    for k in range(2):
        speed = ext2[2 + k, 0:32, :]
        speed2 = speed + step * (inverse * (force[k] + itp[2 + k]) - (alive if k == 0 else 0.0))
        place2 = (ext2[k, 0:32, :] + step * speed2) * 0.0625
        for j in range(2):
            part[k, pl.ds(j, 16, stride=2), :] = place2[j * 16:(j + 1) * 16]
            part[2 + k, pl.ds(j, 16, stride=2), :] = speed2[j * 16:(j + 1) * 16]
    for c in edges:
        c.wait()

    @pl.when(ax < N_ACROSS - 1)
    def _():
        to_right.wait_send()
        to_left.wait_recv()

    @pl.when(ax > 0)
    def _():
        to_left.wait_send()
        to_right.wait_recv()

    for c in pieces:
        c.wait()
    phase_end(1, 2, phase)
    flag[...] = sv[3]
    gas_step_update(gas, visc, gr, gc, dv, sv.at[3], mv.at[3], out)


def fused(gas, visc, pos, vel, rad, coef, counts_t, pattern_t, idx, frac):
    dma = pltpu.SemaphoreType.DMA
    return pl.pallas_call(
        fused_kernel,
        out_shape=[jax.ShapeDtypeStruct((4, 32, 128), F32), jax.ShapeDtypeStruct((2, 32, 256), F32),
                   jax.ShapeDtypeStruct((8, 128), F32)],
        in_specs=[VMEM_SPEC] * 8 + [SMEM_SPEC] * 2,
        out_specs=[VMEM_SPEC] * 3,
        scratch_shapes=[
            pltpu.VMEM((8, 128, 128), F32), pltpu.VMEM((8, 128, 128), F32),
            pltpu.VMEM((8, 32, 128), F32), pltpu.VMEM((8, 32, 128), F32),
            pltpu.VMEM((8, 32, 128), F32), pltpu.VMEM((8, 32, 128), F32),
            pltpu.VMEM((2, 2, 8, 256), F32), pltpu.VMEM((2, 2, 32, 128), F32),
            pltpu.VMEM((3, 8, 8, 128), F32), pltpu.VMEM((4, 8, 128), F32),
            pltpu.VMEM((3, 8, 8, 128), F32), pltpu.VMEM((4, 8, 128), F32),
            pltpu.VMEM((8, 128, 128), F32), pltpu.VMEM((32 * 128, 128), BF16),
            pltpu.VMEM((128 * WINDOW_ROWS, 128), BF16), pltpu.VMEM((32, 64, 640), BF16),
            pltpu.VMEM((512, 128), F32), pltpu.VMEM((4, 32, 128), F32), pltpu.VMEM((8, 32, 128), F32),
            dma((2, 10)), dma((2, 10)), dma((2, 8)), dma((2, 8)), dma((2, 3, 8)), dma((2, 3, 8)),
            dma((4,)), dma((4,)),
        ],
        compiler_params=pltpu.CompilerParams(collective_id=2, has_side_effects=True),
        name="interval",
    )(gas, visc, pos, vel, rad, coef, idx, frac, pattern_t, counts_t)


def body(gas, visc, pos, vel, rad, coef, counts, pattern, idx, frac):
    pos, vel, frac = (x.reshape(2, 32, 128) for x in (pos, vel, frac))
    rad, coef, idx = (x.reshape(32, 128) for x in (rad, coef, idx))
    args = (gas, visc, pos, vel, rad, coef, counts.T, pattern.transpose(2, 1, 0), idx, frac)
    part, out, flag = fused(*args)
    part, out = lax.cond(flag[2, 0] > 0.0, lambda p, o: tuple(general(*args)), lambda p, o: (p, o), part, out)
    return part.reshape(4, 16, 2, 128), out


def solution(mesh):
    return jax.shard_map(
        body,
        mesh=mesh,
        in_specs=(
            P(None, ALONG_GAS, "across"),
            P(ALONG_GAS, "across"),
            P(None, "along", ACROSS_GAS, None),
            P(None, "along", ACROSS_GAS, None),
            P("along", ACROSS_GAS, None),
            P("along", ACROSS_GAS, None),
            P("along", ACROSS_GAS),
            P("along", ACROSS_GAS, None),
            P("along", ACROSS_GAS, None),
            P(None, "along", ACROSS_GAS, None),
        ),
        out_specs=(P(None, "along", ACROSS_GAS, None), P(None, ALONG_GAS, "across")),
        check_vma=False,
    )
```

```python
import functools

import jax
import jax.numpy as jnp
from jax import lax
from jax.experimental import pallas as pl
from jax.experimental.pallas import tpu as pltpu
from jax.sharding import PartitionSpec as P

ALONG_GAS = ("along", "gas")
ACROSS_GAS = ("across", "gas")
MESH_ID = pl.DeviceIdType.MESH
OFFSETS = [(-1, -1), (-1, 0), (-1, 1), (0, -1), (0, 0), (0, 1), (1, -1), (1, 0), (1, 1)]
DEAD = -16384.0
F32 = jnp.float32
BF16 = jnp.bfloat16
STRIDE = 136
BLOCK, BLOCK_BITS = 64, 6
EMPTY = 1344
REACH = 2.4
MOVE_LIMIT = int((REACH - 1.9) * 4096)
VMEM_SPEC = pl.BlockSpec(memory_space=pltpu.VMEM)
SMEM_SPEC = pl.BlockSpec(memory_space=pltpu.SMEM)
N_ACROSS, N_ALONG, N_GAS = 4, 8, 8


def iota(shape, dim):
    return lax.broadcasted_iota(jnp.int32, shape, dim)


def ext_row(ii, jj):
    base = {-1: 32, 0: 0, 1: 16, 2: 48}[jj]
    return jnp.where(ii < 0, 64 + 8 * (jj + 1) + 7, jnp.where(ii > 15, 96 + 8 * (jj + 1), base + ii))


def by_column(ref, *lead):
    return jnp.concatenate([ref[(*lead, pl.ds(0, 16, stride=2), slice(None))],
                            ref[(*lead, pl.ds(1, 16, stride=2), slice(None))]], axis=0)


def prepare_state(st, pos, vel, rad, counts):
    row32 = iota((32, 128), 0)
    slot = iota((32, 128), 1)
    cnt = jnp.zeros((32, 128), jnp.int32)
    for j in range(2):
        for i in range(16):
            cnt = jnp.where(row32 == j * 16 + i, counts[j, i], cnt)
    alive = slot < cnt
    z, x = by_column(pos, 0) * 16.0, by_column(pos, 1) * 16.0
    st[0, 0:32, :], st[1, 0:32, :] = z, x
    st[2, 0:32, :], st[3, 0:32, :] = by_column(vel, 0), by_column(vel, 1)
    st[4, 0:32, :] = jnp.where(alive, by_column(rad), DEAD)
    low_x, high_x = x < REACH, x > 16.0 - REACH

    def three(low, mid, high):
        return jnp.where(low_x, low, jnp.where(high_x, high, mid))

    kind = jnp.where(z < REACH, three(0, 1, 2), jnp.where(z > 16.0 - REACH, three(6, 5, 4), three(7, 8, 3)))
    kind = jnp.where(alive, kind, 9)
    member = jnp.concatenate([jnp.where(kind == c, 1.0, 0.0) for c in range(9)], axis=0).astype(BF16)
    before = jnp.where((iota((128, 256), 0) < iota((128, 256), 1)) | (iota((128, 256), 1) >= 128), 1.0, 0.0)
    ranks = jnp.dot(member, before.astype(BF16), preferred_element_type=F32)
    rank = jnp.full((32, 128), -1.0, F32)
    start = [jnp.zeros((32, 128), F32)]
    for c in range(9):
        here = ranks[c * 32:(c + 1) * 32]
        rank = jnp.where(kind == c, start[c] + here[:, 0:128], rank)
        start.append(start[c] + here[:, 128:256])
    st[5, 0:32, :] = rank
    start = [v.astype(jnp.int32) for v in start]
    wrap = ((start[1] + 7) & -8) > start[6]
    zero = jnp.zeros((32, 128), jnp.int32)
    windows = [(start[4], start[5]), (start[4], start[7]), (start[6], start[7]), (start[2], start[5]),
               (zero, start[9]), (jnp.where(wrap, 0, start[6]), start[8]), (start[2], start[3]),
               (zero, start[3]), (zero, start[1]), (zero, jnp.where(wrap, 0, start[1]))]
    table = zero
    for w, (low, high) in enumerate(windows):
        table = jnp.where(slot == 2 * w, low, jnp.where(slot == 2 * w + 1, (high - low + 7) & -8, table))
    st[6, 0:32, :] = table.astype(F32)


def prep_kernel(gas, visc, pos, vel, rad, counts, st, gp, mx):
    rate = jnp.abs(gas[0]) + jnp.abs(gas[1]) + 4.0 * visc[...]
    top = jnp.max(jnp.max(rate, axis=1, keepdims=True), axis=0, keepdims=True)
    mx[...] = jnp.broadcast_to(top, (8, 128))
    lane = iota((16, 128), 1)
    for g in range(N_GAS):
        blk = slice((g // 4) * 128, (g // 4) * 128 + 128)
        off = (g % 4) * 32
        for k in range(2):
            low = gas[k, 0:16, blk]
            high = gas[k, 16:32, blk]
            low = pltpu.roll(low, (128 - off) % 128, 1) if off else low
            shift = (160 - off) % 128
            high = pltpu.roll(high, shift, 1) if shift else high
            piece = jnp.where(lane < 32, low, jnp.where(lane < 64, high, 0.0))
            gp[g, k * 16:(k + 1) * 16, :] = piece
    prepare_state(st, pos, vel, rad, counts)
    st[7] = jnp.zeros((32, 128), F32)


def comm_kernel(first, *refs):
    if first:
        (st, pc, mx, gas, ext, pv, red, gr, gc, mb, m1, m2,
         own_sem, hs, hr, ps, pr, rs, rr, es, er) = refs
    else:
        (st, pc, mx, ext, pv, red, mb, m1, m2,
         own_sem, hs, hr, ps, pr, rs, rr) = refs
    ax, al, g = lax.axis_index("across"), lax.axis_index("along"), lax.axis_index("gas")
    up, down = lax.rem(al + 1, N_ALONG), lax.rem(al + N_ALONG - 1, N_ALONG)
    lin = ax * N_GAS + g
    has_left, has_right = lin > 0, lin < N_ACROSS * N_GAS - 1
    left = jnp.maximum(lin - 1, 0)
    right = jnp.minimum(lin + 1, N_ACROSS * N_GAS - 1)

    def col(index, along):
        return {"across": lax.div(index, N_GAS), "along": along, "gas": lax.rem(index, N_GAS)}

    slab = al * N_GAS + g
    slabs = N_ALONG * N_GAS
    after, before = lax.rem(slab + 1, slabs), lax.rem(slab + slabs - 1, slabs)

    def slab_id(index):
        return {"across": ax, "along": lax.div(index, N_GAS), "gas": lax.rem(index, N_GAS)}

    barrier = pltpu.get_barrier_semaphore()

    def greet(device):
        pl.semaphore_signal(barrier, inc=1, device_id=device, device_id_type=MESH_ID)

    for k in range(1, N_ACROSS):
        greet({"across": lax.rem(ax + k, N_ACROSS)})
    for k in range(1, N_GAS):
        greet({"gas": lax.rem(g + k, N_GAS)})
    for k in range(1, N_ALONG):
        greet({"along": lax.rem(al + k, N_ALONG)})
    expect = N_ACROSS + N_GAS + N_ALONG - 3
    if first:
        greet(slab_id(after))
        greet(slab_id(before))
        expect += 2

    @pl.when(has_left)
    def _():
        for along in (down, al, up):
            greet(col(left, along))

    @pl.when(has_right)
    def _():
        for along in (down, al, up):
            greet(col(right, along))

    own = pltpu.make_async_copy(st, ext.at[:, pl.ds(0, 32)], own_sem.at[0])
    own.start()
    own_piece = pltpu.make_async_copy(pc.at[g], pv.at[g], own_sem.at[1])
    own_piece.start()

    @pl.when(jnp.logical_not(has_left))
    def _():
        ext[:, 32:48, :] = jnp.zeros((8, 16, 128), F32)
        ext[:, 64:72, :] = jnp.zeros((8, 8, 128), F32)
        ext[:, 96:104, :] = jnp.zeros((8, 8, 128), F32)

    @pl.when(jnp.logical_not(has_right))
    def _():
        ext[:, 48:64, :] = jnp.zeros((8, 16, 128), F32)
        ext[:, 88:96, :] = jnp.zeros((8, 8, 128), F32)
        ext[:, 120:128, :] = jnp.zeros((8, 8, 128), F32)

    if first:
        @pl.when(ax == 0)
        def _():
            gc[0] = jnp.zeros((2, 32, 128), F32)

        @pl.when(ax == N_ACROSS - 1)
        def _():
            gc[1] = jnp.zeros((2, 32, 128), F32)

    sides = jnp.where(has_left, 3, 0) + jnp.where(has_right, 3, 0)
    pl.semaphore_wait(barrier, expect + sides)

    def remote(src, dst, send, recv, device):
        return pltpu.make_async_remote_copy(
            src_ref=src, dst_ref=dst, send_sem=send, recv_sem=recv,
            device_id=device, device_id_type=MESH_ID,
        )

    def reduce_sends(phase, src, axis, me, size):
        out = []
        for k in range(1, size):
            out.append(remote(src, mb.at[phase, me], rs.at[phase, k], rr.at[phase, k],
                              {axis: lax.rem(me + k, size)}))
        for c in out:
            c.start()
        return out

    phase0 = reduce_sends(0, mx, "across", ax, N_ACROSS)

    def halo(c, src_rows, size, dst_row, device):
        return remote(st.at[pl.ds(0, 7), pl.ds(src_rows, size)],
                      ext.at[pl.ds(0, 7), pl.ds(dst_row, size)], hs.at[c], hr.at[c], device)

    lefts = [halo(0, 0, 16, 48, col(left, al)),
             halo(1, 8, 8, 64 + 24, col(left, up)),
             halo(2, 0, 8, 96 + 24, col(left, down))]
    rights = [halo(3, 16, 16, 32, col(right, al)),
              halo(4, 24, 8, 64, col(right, up)),
              halo(5, 16, 8, 96, col(right, down))]
    rows = [halo(6, 8, 8, 64 + 8, {"along": up}),
            halo(7, 24, 8, 64 + 16, {"along": up}),
            halo(8, 0, 8, 96 + 8, {"along": down}),
            halo(9, 16, 8, 96 + 16, {"along": down})]

    @pl.when(has_left)
    def _():
        for c in lefts:
            c.start()

    @pl.when(has_right)
    def _():
        for c in rights:
            c.start()

    for c in rows:
        c.start()
    pieces = []
    for k in range(1, N_GAS):
        peer = lax.rem(g + k, N_GAS)
        c = remote(pc.at[peer], pv.at[g], ps.at[k], pr.at[k], {"gas": peer})
        c.start()
        pieces.append(c)
    if first:
        edges = [remote(gas.at[:, pl.ds(24, 8)], gr.at[0], es.at[0], er.at[0], slab_id(after)),
                 remote(gas.at[:, pl.ds(0, 8)], gr.at[1], es.at[1], er.at[1], slab_id(before))]
        for c in edges:
            c.start()
        to_right = remote(gas.at[:, :, pl.ds(128, 128)], gc.at[0], es.at[2], er.at[2],
                          {"across": jnp.minimum(ax + 1, N_ACROSS - 1)})
        to_left = remote(gas.at[:, :, pl.ds(0, 128)], gc.at[1], es.at[3], er.at[3],
                         {"across": jnp.maximum(ax - 1, 0)})

        @pl.when(ax < N_ACROSS - 1)
        def _():
            to_right.start()

        @pl.when(ax > 0)
        def _():
            to_left.start()

    def combine(phase, mine, me, size, copies):
        for c in copies:
            c.wait_recv()
        mb[phase, me] = mine
        total = mb[phase, 0]
        for k in range(1, size):
            total = jnp.maximum(total, mb[phase, k]) if first else total + mb[phase, k]
        return total

    m1[...] = combine(0, mx[...], ax, N_ACROSS, phase0)
    phase1 = reduce_sends(1, m1, "gas", g, N_GAS)
    m2[...] = combine(1, m1[...], g, N_GAS, phase1)
    phase2 = reduce_sends(2, m2, "along", al, N_ALONG)
    red[...] = combine(2, m2[...], al, N_ALONG, phase2)

    own.wait()
    own_piece.wait()
    for c in phase0 + phase1 + phase2:
        c.wait_send()
    for c in rows + pieces:
        c.wait()

    @pl.when(has_left)
    def _():
        for c in lefts:
            c.wait_send()
        for c in rights:
            c.wait_recv()

    @pl.when(has_right)
    def _():
        for c in rights:
            c.wait_send()
        for c in lefts:
            c.wait_recv()

    if first:
        for c in edges:
            c.wait()

        @pl.when(ax < N_ACROSS - 1)
        def _():
            to_right.wait_send()
            to_left.wait_recv()

        @pl.when(ax > 0)
        def _():
            to_left.wait_send()
            to_right.wait_recv()


def exchange(first, st, pc, mx, gas=None):
    out_shape = [jax.ShapeDtypeStruct((8, 128, 128), F32),
                 jax.ShapeDtypeStruct((8, 32, 128), F32),
                 jax.ShapeDtypeStruct((8, 128), F32)]
    scratch = [pltpu.VMEM((3, 8, 8, 128), F32), pltpu.VMEM((8, 128), F32), pltpu.VMEM((8, 128), F32),
               pltpu.SemaphoreType.DMA((2,)),
               pltpu.SemaphoreType.DMA((10,)), pltpu.SemaphoreType.DMA((10,)),
               pltpu.SemaphoreType.DMA((8,)), pltpu.SemaphoreType.DMA((8,)),
               pltpu.SemaphoreType.DMA((3, 8)), pltpu.SemaphoreType.DMA((3, 8))]
    args = [st, pc, mx]
    if first:
        args.append(gas)
        out_shape += [jax.ShapeDtypeStruct((2, 2, 8, 256), F32), jax.ShapeDtypeStruct((2, 2, 32, 128), F32)]
        scratch += [pltpu.SemaphoreType.DMA((4,)), pltpu.SemaphoreType.DMA((4,))]
    return pl.pallas_call(
        functools.partial(comm_kernel, first),
        out_shape=out_shape,
        in_specs=[VMEM_SPEC] * len(args),
        out_specs=[VMEM_SPEC] * len(out_shape),
        scratch_shapes=scratch,
        compiler_params=pltpu.CompilerParams(collective_id=0 if first else 1, has_side_effects=True),
        name="exchange_first" if first else "exchange_second",
    )(*args)


def split3(x):
    hi = x.astype(BF16).astype(F32)
    rest = x - hi
    mid = rest.astype(BF16).astype(F32)
    return hi, mid, rest - mid


def contact_forces(ext, pat, meta, ints, qt, lst, rhs, frc, sem):
    ints[...] = ext[6 * 128:7 * 128, :].astype(jnp.int32)
    to_smem = pltpu.make_async_copy(ints, meta, sem)
    to_smem.start()
    slot = iota((128, 128), 0).astype(F32)
    attr_row = iota((8, 128), 0)
    zero8 = jnp.zeros((8, 128), F32)
    tail = jnp.concatenate([zero8, jnp.ones((24, 128), F32), zero8], axis=0)

    def parts(row):
        block = ext[pl.ds(row, 8, stride=128), :]
        return split3(jnp.where(attr_row < 5, block, 0.0))

    def transposed(row):
        hi, mid, lo = parts(row)
        rows = jnp.concatenate([hi, mid, lo, tail], axis=0).astype(BF16)
        place = (slot == ext[pl.ds(row + 5 * 128, 1), :]).astype(F32).astype(BF16)
        turned = lax.dot_general(place, rows, (((1,), (1,)), ((), ())), preferred_element_type=F32)
        start = row * STRIDE if isinstance(row, int) else pl.multiple_of(row * STRIDE, 8)
        qt[pl.ds(start, 128), 0:64] = turned
        start = start + 128 if isinstance(row, int) else pl.multiple_of(start + 128, 8)
        qt[pl.ds(start, 8), :] = zero8

    def some(step, carry):
        for u in range(4):
            transposed(step * 4 + u)
        return carry

    lax.fori_loop(0, 16, some, 0)
    for c in range(4):
        transposed(64 + 8 * c + 7)
        transposed(96 + 8 * c)

    block_of = iota((32, 640), 1) >> 7
    row_of = iota((32, 640), 0)
    attr_of = row_of & 7
    own_scale = jnp.where(block_of < 2, -1.0, jnp.where(block_of < 4, 2.0, 1.0))
    const = jnp.where((attr_of == block_of) & (row_of < 24), own_scale, 0.0)
    const = jnp.where((row_of == 24) & (block_of == 0) | (row_of == 25) & (block_of == 1), -16.0, const)
    for u in range(2):
        rhs[u, 0:32, :] = const.astype(BF16)
        lst[u, EMPTY:EMPTY + BLOCK, :] = jnp.zeros((BLOCK, 128), F32)
    to_smem.wait()
    lane = iota((8, 128), 1)

    def row_step(i, carry):
        blocks = []
        for j in range(2):
            work = lst.at[j]
            mine = j * 16 + i
            hi, mid, lo = parts(mine)
            columns = []
            for a in range(5):
                keep = attr_row == a
                scale = 1.0 if a in (0, 1, 4) else -2.0
                columns.append(jnp.concatenate(
                    [jnp.where(keep, hi * scale, 0.0), jnp.where(keep, mid * scale, 0.0),
                     jnp.where(keep, lo * scale, 0.0), zero8], axis=0))
            rhs[j, 32:64, :] = jnp.concatenate(columns, axis=1).astype(BF16)
            moved = meta[mine, 20]
            off = i * 0
            over = i * 0
            windows = []
            for w in (4, 0, 1, 2, 3, 5, 6, 7, 8, 9):
                di, dj = OFFSETS[5 if w == 9 else w]
                row = ext_row(i + di, j + dj)
                first, size = meta[row, 2 * w], meta[row, 2 * w + 1]
                if w != 4:
                    near = moved + meta[row, 20] <= MOVE_LIMIT
                    first = jnp.where(near, first, 0)
                    size = jnp.where(near, size, 0 if w == 9 else meta[row, 9])
                size = size * pat[5 if w == 9 else w, j, i]
                mark = jnp.where(lane == 24, float(di), jnp.where(lane == 25, float(dj), 0.0))
                start = row * STRIDE + first
                chunks = 16 if w == 4 else 4 if w in (1, 3, 5, 7) else 1
                for c in range(chunks):
                    work[pl.ds(pl.multiple_of(off + c * 8, 8), 8), :] = qt[pl.ds(start + c * 8, 8), :] + mark
                windows.append((start, size, mark))
                off = off + size
                over = jnp.maximum(over, size - chunks * 8)

            @pl.when(over > 0)
            def _():
                to = i * 0
                for start, size, mark in windows:
                    def copy(c, carry, start=start, mark=mark, to=to):
                        work[pl.ds(pl.multiple_of(to + c * 8, 8), 8), :] = qt[pl.ds(start + c * 8, 8), :] + mark
                        return carry
                    lax.fori_loop(0, size >> 3, copy, 0)
                    to = to + size

            for c in range(BLOCK // 8):
                work[pl.ds(pl.multiple_of(off + c * 8, 8), 8), :] = zero8
            blocks.append((off + BLOCK - 1) >> BLOCK_BITS)
        right = [rhs[0], rhs[1]]

        def block(b, acc):
            out = []
            for j in range(2):
                at = jnp.where(b < blocks[j], b * BLOCK, EMPTY)
                q = lst[j, pl.ds(pl.multiple_of(at, 8), BLOCK), 0:64].astype(BF16)
                got = jnp.dot(q, right[j], preferred_element_type=F32)
                rz, rx = got[:, 0:128], got[:, 128:256]
                dz, dx = got[:, 256:384], got[:, 384:512]
                d2 = rz * rz + rx * rx + 0.0001
                inv = lax.rsqrt(d2)
                depth = jnp.maximum(got[:, 512:640] - d2 * inv, 0.0)
                push = depth * inv * (40.0 + (dz * rz + dx * rx) * inv)
                out.append(acc[2 * j] + jnp.sum((push * rz).reshape(BLOCK // 8, 8, 128), axis=0))
                out.append(acc[2 * j + 1] + jnp.sum((push * rx).reshape(BLOCK // 8, 8, 128), axis=0))
            return tuple(out)

        acc = lax.fori_loop(0, jnp.maximum(blocks[0], blocks[1]), block, (zero8,) * 4)
        for j in range(2):
            for k in range(2):
                frc[pl.ds(pl.multiple_of(((k * 2 + j) * 16 + i) * 8, 8), 8), :] = acc[2 * j + k]
        return carry

    lax.fori_loop(0, 16, row_step, 0)
    return [sum(frc[pl.ds(k * 256 + r, 32, stride=8), :] for r in range(8)) for k in range(2)]


def first_kernel(ext, gv, rate, idx, frac, coef, pat, st2, dp, tot, dr2, inv_out,
                 meta, ints, qt, lst, rhs, frc, itp, sem):
    def weights(r, t4):
        index = idx[pl.ds(r, 1), :]
        row, column = index >> 4, index & 15
        share_z = frac[0, pl.ds(r, 1), :].astype(F32) / 1024.0
        share_x = frac[1, pl.ds(r, 1), :].astype(F32) / 1024.0
        c64 = iota((64, 128), 0) - t4 * 16
        wx = jnp.where(c64 == column, 1.0 - share_x, jnp.where(c64 == column + 1, share_x, 0.0))
        r16 = iota((16, 128), 0)
        wz = jnp.where(r16 == row, 1.0 - share_z, jnp.where(r16 == row + 1, share_z, 0.0))
        return wz, wx

    def sample(h, carry):
        field = gv[h][:, 0:64]
        for t in range(2):
            for j in range(2):
                wz, wx = weights(4 * h + 2 * t + j, t * 2 + j)
                along = jnp.dot(field, wx, precision=lax.Precision.HIGHEST, preferred_element_type=F32)
                for k in range(2):
                    itp[k, pl.ds(j * 16 + 2 * h + t, 1), :] = jnp.sum(
                        wz * along[k * 16:(k + 1) * 16], axis=0, keepdims=True)
        return carry

    lax.fori_loop(0, 8, sample, 0)
    force = contact_forces(ext, pat, meta, ints, qt, lst, rhs, frc, sem)
    step = 0.2 / rate[0:1, :]
    drag = by_column(coef)
    radius = ext[4 * 128:4 * 128 + 32, :]
    alive = jnp.where(radius > 0.0, 1.0, 0.0)
    inverse = jnp.where(radius > 0.0, 0.36 / (radius * radius), 0.0)
    inv_out[...] = inverse
    means = []
    moved = jnp.zeros((32, 128), F32)
    for k in range(2):
        place = ext[k * 128:k * 128 + 32, :]
        speed = ext[(2 + k) * 128:(2 + k) * 128 + 32, :]
        drag1 = drag * (itp[k] - speed)
        speed2 = speed + step * (inverse * (force[k] + drag1) - (alive if k == 0 else 0.0))
        st2[k] = place + step * speed2
        moved = jnp.maximum(moved, alive * jnp.abs(step * speed2))
        st2[2 + k] = speed2
        drag2 = drag * (itp[k] - speed2)
        dr2[k] = drag2
        mean = 0.5 * (alive * drag1 + alive * drag2)
        itp[k] = mean
        means.append(jnp.sum(jnp.sum(mean, axis=1, keepdims=True), axis=0, keepdims=True))
    st2[4] = radius
    st2[5] = ext[5 * 128:5 * 128 + 32, :]
    far = jnp.max(moved, axis=1, keepdims=True)
    far = jnp.where(far < 100.0, far, 100.0) * 4096.0 + 1.0
    st2[6] = jnp.where(iota((32, 128), 1) == 20, far, ext[6 * 128:6 * 128 + 32, :])
    st2[7] = jnp.zeros((32, 128), F32)
    tot[...] = jnp.where(iota((8, 128), 0) == 0, means[0], means[1])

    def spread(h, carry):
        total = jnp.zeros((32, 64), F32)
        for t in range(2):
            for j in range(2):
                wz, wx = weights(4 * h + 2 * t + j, t * 2 + j)
                m0 = itp[0, pl.ds(j * 16 + 2 * h + t, 1), :]
                m1 = itp[1, pl.ds(j * 16 + 2 * h + t, 1), :]
                lhs = jnp.concatenate([wz * m0, wz * m1], axis=0)
                total = total + lax.dot_general(lhs, wx, (((1,), (1,)), ((), ())),
                                                precision=lax.Precision.HIGHEST, preferred_element_type=F32)
        dp[h, :, 0:64] = total
        dp[h, :, 64:128] = jnp.zeros((32, 64), F32)
        return carry

    lax.fori_loop(0, 8, spread, 0)


def gas_step_update(gas, visc, gr, gc, dv, tot, rate, out):
    gas_step = 0.4 / rate[0:1, 0:1]
    lane = iota((32, 256), 1)
    row = iota((32, 256), 0)
    lane16 = iota((16, 128), 1) >> 5
    for k in range(2):
        u = gas[k]
        upper = jnp.where(row == 31, gr[1, k, 0:1, :], pltpu.roll(u, 31, 0))
        lower = jnp.where(row == 0, gr[0, k, 7:8, :], pltpu.roll(u, 1, 0))
        right = jnp.where(lane == 255, gc[1, k, :, 0:1], pltpu.roll(u, 255, 1))
        left = jnp.where(lane == 0, gc[0, k, :, 127:128], pltpu.roll(u, 1, 1))
        laplace = upper + lower + right + left - 4.0 * u
        advect = gas[0] * (upper - lower) * 0.5 + gas[1] * (right - left) * 0.5
        quads = []
        for t in range(2):
            halves = []
            for b in range(2):
                whole = None
                for q in range(4):
                    piece = dv[4 * b + q, k * 16:(k + 1) * 16, :]
                    shift = (q * 32 - t * 32) % 128
                    piece = pltpu.roll(piece, shift, 1) if shift else piece
                    whole = piece if whole is None else jnp.where(lane16 == q, piece, whole)
                halves.append(whole)
            quads.append(jnp.concatenate(halves, axis=1))
        deposit = jnp.concatenate(quads, axis=0)
        source = tot[k:k + 1, 0:1] / 2097152.0 - deposit
        out[k] = u + gas_step * (visc[...] * laplace - advect + source)


def second_kernel(ext, dv, tot, rate, dr2, inverse, gas, visc, gr, gc, pat, part, out,
                  meta, ints, qt, lst, rhs, frc, sem):
    force = contact_forces(ext, pat, meta, ints, qt, lst, rhs, frc, sem)
    step = 0.2 / rate[0:1, :]
    radius = ext[4 * 128:4 * 128 + 32, :]
    alive = jnp.where(radius > 0.0, 1.0, 0.0)
    for k in range(2):
        place = ext[k * 128:k * 128 + 32, :]
        speed = ext[(2 + k) * 128:(2 + k) * 128 + 32, :]
        speed2 = speed + step * (inverse[...] * (force[k] + dr2[k]) - (alive if k == 0 else 0.0))
        place2 = (place + step * speed2) * 0.0625
        for j in range(2):
            part[k, pl.ds(j, 16, stride=2), :] = place2[j * 16:(j + 1) * 16]
            part[2 + k, pl.ds(j, 16, stride=2), :] = speed2[j * 16:(j + 1) * 16]
    gas_step_update(gas, visc, gr, gc, dv, tot, rate, out)


CONTACT_SCRATCH = [
    pltpu.SMEM((128, 128), jnp.int32),
    pltpu.VMEM((128, 128), jnp.int32),
    pltpu.VMEM((128 * STRIDE, 128), F32),
    pltpu.VMEM((2, 1408, 128), F32),
    pltpu.VMEM((2, 64, 640), BF16),
    pltpu.VMEM((512, 128), F32),
]


def general(gas, visc, pos, vel, rad, coef, counts_t, pattern_t, idx, frac):

    def shapes(*dims):
        return [jax.ShapeDtypeStruct(d, F32) for d in dims]

    st, gp, mx = pl.pallas_call(
        prep_kernel,
        out_shape=shapes((8, 32, 128), (8, 32, 128), (8, 128)),
        in_specs=[VMEM_SPEC] * 5 + [SMEM_SPEC],
        out_specs=[VMEM_SPEC] * 3,
        name="prepare",
    )(gas, visc, pos, vel, rad, counts_t)
    ext, gv, rate, gr, gc = exchange(True, st, gp, mx, gas)
    st2, dp, tot, dr2, inverse = pl.pallas_call(
        first_kernel,
        out_shape=shapes((8, 32, 128), (8, 32, 128), (8, 128), (2, 32, 128), (32, 128)),
        in_specs=[VMEM_SPEC] * 6 + [SMEM_SPEC],
        out_specs=[VMEM_SPEC] * 5,
        scratch_shapes=CONTACT_SCRATCH + [pltpu.VMEM((2, 32, 128), F32), pltpu.SemaphoreType.DMA],
        name="first_substep",
    )(ext.reshape(1024, 128), gv, rate, idx, frac, coef, pattern_t)
    ext2, dv, total = exchange(False, st2, dp, tot)
    part, out = pl.pallas_call(
        second_kernel,
        out_shape=shapes((4, 32, 128), (2, 32, 256)),
        in_specs=[VMEM_SPEC] * 10 + [SMEM_SPEC],
        out_specs=[VMEM_SPEC] * 2,
        scratch_shapes=CONTACT_SCRATCH + [pltpu.SemaphoreType.DMA],
        name="second_substep",
    )(ext2.reshape(1024, 128), dv, total, rate, dr2, inverse, gas, visc, gr, gc, pattern_t)
    return part, out


EDGE_BASE, CORNER_BASE, WINDOW_ROWS = 48, 192, 256
CORNER = 16
WINDOWS = ((-1, 0), (1, 0), (0, -1), (0, 1), (-1, -1), (-1, 1), (1, -1), (1, 1))
NEAR = ((1.82, 0.0), (2.25, 0.43))
EDGE = 40


def fused_kernel(*refs):
    inputs, (part, out, flag), refs = refs[:10], refs[10:13], refs[13:]
    gas, visc, pos, vel, rad, coef, idx, frac, pat, counts = refs[:10]
    (in_sem, ext, ext2, gp, gv, dp, dv, gr, gc, mb, mv, sb, sv, rk, qs, qw, rhs, frc, itp, wts,
     hs, hr, ps, pr, rs, rr, es, er) = refs[10:]
    loads = [pltpu.make_async_copy(a, b, in_sem.at[n]) for n, (a, b) in enumerate(zip(inputs, refs[:10]))]
    for c in loads:
        c.start()
    ax, al, g = lax.axis_index("across"), lax.axis_index("along"), lax.axis_index("gas")

    def around(value, size):
        return value - jnp.where(value >= size, size, 0)

    up, down = around(al + 1, N_ALONG), around(al + N_ALONG - 1, N_ALONG)
    first_g, last_g = g == 0, g == N_GAS - 1
    has_left = jnp.logical_or(ax > 0, g > 0)
    has_right = jnp.logical_or(ax < N_ACROSS - 1, g < N_GAS - 1)
    left = (jnp.maximum(ax - jnp.where(first_g, 1, 0), 0), jnp.where(first_g, N_GAS - 1, g - 1))
    right = (jnp.minimum(ax + jnp.where(last_g, 1, 0), N_ACROSS - 1), jnp.where(last_g, 0, g + 1))

    def device(a=ax, l=al, y=g):
        return {"across": a, "along": l, "gas": y}

    def col(side, along):
        return device(a=side[0], l=along, y=side[1])

    def peer_id(axis, index):
        return device(**{{"across": "a", "along": "l", "gas": "y"}[axis]: index})

    after = device(l=jnp.where(last_g, up, al), y=jnp.where(last_g, 0, g + 1))
    before = device(l=jnp.where(first_g, down, al), y=jnp.where(first_g, N_GAS - 1, g - 1))

    barrier = pltpu.get_barrier_semaphore()

    def greet(target):
        pl.semaphore_signal(barrier, inc=1, device_id=target, device_id_type=MESH_ID)

    for k in range(1, N_ALONG):
        greet(device(l=around(al + k, N_ALONG)))
    for k in range(1, N_ACROSS):
        greet(device(a=around(ax + k, N_ACROSS)))
    for k in range(1, N_GAS):
        greet(device(y=around(g + k, N_GAS)))
    greet(after)
    greet(before)
    expect = N_ACROSS + N_GAS + N_ALONG - 3 + 2

    @pl.when(has_left)
    def _():
        for along in (down, al, up):
            greet(col(left, along))

    @pl.when(has_right)
    def _():
        for along in (down, al, up):
            greet(col(right, along))

    for c in loads:
        c.wait()
    rate = jnp.abs(gas[0]) + jnp.abs(gas[1]) + 4.0 * visc[...]
    top = jnp.max(jnp.max(rate, axis=1, keepdims=True), axis=0, keepdims=True)
    mv[0] = jnp.broadcast_to(top, (8, 128))
    lane = iota((16, 128), 1)
    for d in range(N_GAS):
        blk = slice((d // 4) * 128, (d // 4) * 128 + 128)
        off = (d % 4) * 32
        for k in range(2):
            low = gas[k, 0:16, blk]
            high = gas[k, 16:32, blk]
            low = pltpu.roll(low, (128 - off) % 128, 1) if off else low
            shift = (160 - off) % 128
            high = pltpu.roll(high, shift, 1) if shift else high
            piece = jnp.where(lane < 32, low, high)
            gp[d, k * 16:(k + 1) * 16, :] = jnp.where(lane < 64, piece, pltpu.roll(piece, 64, 1))
    row32 = iota((32, 128), 0)
    cnt = jnp.zeros((32, 128), jnp.int32)
    for j in range(2):
        for i in range(16):
            cnt = jnp.where(row32 == j * 16 + i, counts[j, i], cnt)
    ext[0, 0:32, :], ext[1, 0:32, :] = by_column(pos, 0) * 16.0, by_column(pos, 1) * 16.0
    ext[2, 0:32, :], ext[3, 0:32, :] = by_column(vel, 0), by_column(vel, 1)
    ext[4, 0:32, :] = jnp.where(iota((32, 128), 1) < cnt, by_column(rad), DEAD)
    for e in (ext, ext2):
        @pl.when(jnp.logical_not(has_left))
        def _():
            e[:, 32:48, :] = jnp.zeros((8, 16, 128), F32)
            e[:, 64:72, :] = jnp.zeros((8, 8, 128), F32)
            e[:, 96:104, :] = jnp.zeros((8, 8, 128), F32)

        @pl.when(jnp.logical_not(has_right))
        def _():
            e[:, 48:64, :] = jnp.zeros((8, 16, 128), F32)
            e[:, 88:96, :] = jnp.zeros((8, 8, 128), F32)
            e[:, 120:128, :] = jnp.zeros((8, 8, 128), F32)

    @pl.when(ax == 0)
    def _():
        gc[0] = jnp.zeros((2, 32, 128), F32)

    @pl.when(ax == N_ACROSS - 1)
    def _():
        gc[1] = jnp.zeros((2, 32, 128), F32)

    sides = jnp.where(has_left, 3, 0) + jnp.where(has_right, 3, 0)
    pl.semaphore_wait(barrier, expect + sides)

    def remote(src, dst, send, recv, target):
        return pltpu.make_async_remote_copy(
            src_ref=src, dst_ref=dst, send_sem=send, recv_sem=recv,
            device_id=target, device_id_type=MESH_ID,
        )

    axes = (("across", ax, N_ACROSS), ("gas", g, N_GAS), ("along", al, N_ALONG))

    def reduce_start(which, phase):
        slots, value = ((mb, mv), (sb, sv))[which]
        axis, me, size = axes[phase]
        out = [remote(value.at[phase], slots.at[phase, me], rs.at[which, phase, k], rr.at[which, phase, k],
                      peer_id(axis, around(me + k, size))) for k in range(1, size)]
        for c in out:
            c.start()
        slots[phase, me] = value[phase]
        return out

    def reduce_end(which, phase, copies):
        slots, value = ((mb, mv), (sb, sv))[which]
        size = axes[phase][2]
        for c in copies:
            c.wait_recv()
        total = slots[phase, 0]
        for k in range(1, size):
            total = total + slots[phase, k] if which else jnp.maximum(total, slots[phase, k])
        value[phase + 1] = total
        for c in copies:
            c.wait_send()

    def halo_start(which):
        e, attrs = ((ext, 5), (ext2, 5))[which]

        def halo(c, src_row, size, dst_row, target):
            return remote(e.at[pl.ds(0, attrs), pl.ds(src_row, size)],
                          e.at[pl.ds(0, attrs), pl.ds(dst_row, size)], hs.at[which, c], hr.at[which, c], target)

        lefts = [halo(0, 0, 16, 48, col(left, al)),
                 halo(1, 8, 8, 64 + 24, col(left, up)),
                 halo(2, 0, 8, 96 + 24, col(left, down))]
        rights = [halo(3, 16, 16, 32, col(right, al)),
                  halo(4, 24, 8, 64, col(right, up)),
                  halo(5, 16, 8, 96, col(right, down))]
        rows = [halo(6, 8, 8, 64 + 8, device(l=up)),
                halo(7, 24, 8, 64 + 16, device(l=up)),
                halo(8, 0, 8, 96 + 8, device(l=down)),
                halo(9, 16, 8, 96 + 16, device(l=down))]

        @pl.when(has_left)
        def _():
            for c in lefts:
                c.start()

        @pl.when(has_right)
        def _():
            for c in rights:
                c.start()

        for c in rows:
            c.start()
        return lefts, rights, rows

    def halo_end(copies):
        lefts, rights, rows = copies
        for c in rows:
            c.wait()

        @pl.when(has_left)
        def _():
            for c in lefts:
                c.wait_send()
            for c in rights:
                c.wait_recv()

        @pl.when(has_right)
        def _():
            for c in rights:
                c.wait_send()
            for c in lefts:
                c.wait_recv()

    def pieces_start(which):
        src, dst = ((gp, gv), (dp, dv))[which]
        out = []
        for k in range(1, N_GAS):
            peer = around(g + k, N_GAS)
            c = remote(src.at[peer], dst.at[g], ps.at[which, k], pr.at[which, k], device(y=peer))
            c.start()
            out.append(c)
        dst[g] = src[g]
        return out

    phase = reduce_start(0, 0)
    halos = halo_start(0)
    pieces = pieces_start(0)
    edges = [remote(gas.at[:, pl.ds(24, 8)], gr.at[0], es.at[0], er.at[0], after),
             remote(gas.at[:, pl.ds(0, 8)], gr.at[1], es.at[1], er.at[1], before)]
    for c in edges:
        c.start()
    to_right = remote(gas.at[:, :, pl.ds(128, 128)], gc.at[0], es.at[2], er.at[2],
                      device(a=jnp.minimum(ax + 1, N_ACROSS - 1)))
    to_left = remote(gas.at[:, :, pl.ds(0, 128)], gc.at[1], es.at[3], er.at[3],
                     device(a=jnp.maximum(ax - 1, 0)))

    @pl.when(ax < N_ACROSS - 1)
    def _():
        to_right.start()

    @pl.when(ax > 0)
    def _():
        to_left.start()

    slot_row = iota((48, 128), 0)
    slots = (jnp.where(slot_row < EDGE, slot_row, -5).astype(F32),
             jnp.where(slot_row < 32, slot_row, jnp.where(slot_row < 40, -5, slot_row - 8)).astype(F32))
    attr_row = iota((8, 128), 0)
    zero8 = jnp.zeros((8, 128), F32)
    one_tail = jnp.concatenate([zero8, jnp.ones((24, 128), F32), zero8], axis=0)
    flat = (ext.reshape(1024, 128), ext2.reshape(1024, 128))
    eye = jnp.where(iota((128, 128), 0) == iota((128, 128), 1), 1.0, 0.0).astype(BF16)
    before_slot = jnp.where(iota((128, 128), 0) < iota((128, 128), 1), 1.0, 0.0).astype(BF16)

    def rank(which, low, high, windows=range(8)):
        e = (ext, ext2)[which]
        reach, _ = NEAR[which]
        z, x, live = e[0, low:high, :], e[1, low:high, :], e[4, low:high, :] > 0.0

        def flags(cond):
            return jnp.where(cond & live, 1.0, 0.0)

        lz, hz, lx, hx = flags(z < reach), flags(z > 16.0 - reach), flags(x < reach), flags(x > 16.0 - reach)
        member = [hz, lz, hx, lx, hz * hx, hz * lx, lz * hx, lz * lx]
        size = high - low
        places = jnp.dot(jnp.concatenate([member[w] for w in windows], axis=0).astype(BF16), before_slot,
                         preferred_element_type=F32)
        lost = jnp.zeros((size, 128), F32)
        for order, w in enumerate(windows):
            place = places[order * size:(order + 1) * size]
            rk[w, low:high, :] = jnp.where(member[w] > 0.0, place, -1.0)
            lost = lost + jnp.where(place >= (EDGE if w < 4 else CORNER), member[w], 0.0)
        return lost

    def parts(which, row):
        block = flat[which][pl.ds(row, 8, stride=128), :]
        return split3(jnp.where(attr_row < 5, block, 0.0))

    def window_rows(which, row, rows, windows):
        sizes = [48 if w < 4 else CORNER for w in windows]
        place = jnp.concatenate(
            [(slots[w & 1 if w < 4 else 0][0:n] == rk[w, pl.ds(row, 1), :]).astype(F32) for w, n in zip(windows, sizes)], axis=0)
        turned = lax.dot_general(place.astype(BF16), rows, (((1,), (1,)), ((), ())), preferred_element_type=F32)
        turned = turned.astype(BF16)
        at = 0
        for w, n in zip(windows, sizes):
            start = row * WINDOW_ROWS + (w * EDGE_BASE if w < 4 else CORNER_BASE + (w - 4) * CORNER)
            if not isinstance(row, int):
                start = pl.multiple_of(start, 16)
            qw[pl.ds(start, n), 0:64] = turned[at:at + n]
            at += n

    def own_tiles(which):
        def some(step, carry):
            for u in range(4):
                row = step * 4 + u
                hi, mid, lo = parts(which, row)
                rows = jnp.concatenate([hi, mid, lo, one_tail], axis=0)
                turned = rows.T
                rows = rows.astype(BF16)
                qs[pl.ds(pl.multiple_of(row * 128, 128), 128), 0:64] = turned.astype(BF16)
                window_rows(which, row, rows, range(8))
                columns = []
                for a in range(5):
                    keep = attr_row == a
                    scale = 1.0 if a in (0, 1, 4) else -2.0
                    columns.append(jnp.concatenate(
                        [jnp.where(keep, hi * scale, 0.0), jnp.where(keep, mid * scale, 0.0),
                         jnp.where(keep, lo * scale, 0.0), zero8], axis=0))
                rhs[row] = jnp.concatenate(columns, axis=1).astype(BF16)
            return carry
        lax.fori_loop(0, 8, some, 0)

    def halo_tile(which, row, windows):
        hi, mid, lo = parts(which, row)
        window_rows(which, row, jnp.concatenate([hi, mid, lo, one_tail], axis=0).astype(BF16), windows)

    def halo_tiles(which, beside=None):
        rank(which, 32, 48, (2, 4, 6))
        rank(which, 48, 64, (3, 5, 7))
        rank(which, 64, 96, (0, 4, 5))
        rank(which, 96, 128, (1, 6, 7))

        def some(step, carry):
            if beside is not None:
                beside(step)
            for u in range(4):
                halo_tile(which, 32 + step * 4 + u, (2, 4, 6))
                halo_tile(which, 48 + step * 4 + u, (3, 5, 7))
            return carry
        lax.fori_loop(0, 4, some, 0)
        for c in range(4):
            halo_tile(which, 64 + 8 * c + 7, (0, 4, 5))
            halo_tile(which, 96 + 8 * c, (1, 6, 7))

    block_of = iota((32, 640), 1) >> 7
    row_of = iota((32, 640), 0)
    attr_of = row_of & 7
    own_scale = jnp.where(block_of < 2, -1.0, jnp.where(block_of < 4, 2.0, 1.0))
    const = jnp.where((attr_of == block_of) & (row_of < 24), own_scale, 0.0)
    const = jnp.where((row_of == 24) & (block_of == 0) | (row_of == 25) & (block_of == 1), -16.0, const)
    const = jnp.where((row_of == 26) & (block_of == 4), DEAD, const)
    const = const.astype(BF16)
    lane16 = iota((16, 128), 1)
    half = iota((16, 128), 0) < 8

    rhs[32] = const
    lost = rank(0, 0, 32)
    own_tiles(0)
    unlisted = jnp.where(lane16 == 26, 1.0, 0.0)

    def contact_rows(first, last):

        def step(two, carry):
            for j, u in ((0, 0), (1, 0), (0, 1), (1, 1)):
                i = two * 2 + u
                t = j * 16 + i
                right = jnp.concatenate([rhs[32], rhs[t]], axis=0)

                def mark_of(n):
                    di, dj = OFFSETS[n]
                    base = jnp.where(lane16 == 24, float(di), jnp.where(lane16 == 25, float(dj), 0.0))
                    return base + unlisted * (1 - pat[n, j, i]).astype(F32)

                def mark(n):
                    return mark_of(n).astype(BF16)

                def border(w):
                    di, dj = WINDOWS[w]
                    row = ext_row(i + di, j + dj)
                    n = 48 if w < 4 else CORNER
                    start = row * WINDOW_ROWS + (w * EDGE_BASE if w < 4 else CORNER_BASE + (w - 4) * CORNER)
                    return qw[pl.ds(pl.multiple_of(start, 16), n), :], mark_of(3 * (di + 1) + dj + 1)

                def edges_of(w):
                    (one, mark1), (two, mark2) = border(w), border(w + 1)
                    both = one[32:48] + two[32:48] + jnp.where(half, mark1, mark2).astype(BF16)
                    mark1, mark2 = mark1.astype(BF16), mark2.astype(BF16)
                    return jnp.concatenate([one[0:16] + mark1, one[16:32] + mark1,
                                            two[0:16] + mark2, two[16:32] + mark2, both], axis=0)

                def corner(w):
                    block, here = border(w)
                    return block + here.astype(BF16)

                own = qs[pl.ds(pl.multiple_of(t * 128, 128), 128), :] + jnp.concatenate([mark(4)] * 8, axis=0)
                groups = [own, edges_of(0), edges_of(2), jnp.concatenate([corner(w) for w in range(4, 8)], axis=0)]
                got = jnp.dot(jnp.concatenate(groups, axis=0)[:, 0:64], right, preferred_element_type=F32)
                rz, rx = got[:, 0:128], got[:, 128:256]
                dz, dx = got[:, 256:384], got[:, 384:512]
                inv = lax.rsqrt(rz * rz + rx * rx + 0.0001)
                push = jnp.maximum(got[:, 512:640] * inv - 1.0, 0.0) * (40.0 + (dz * rz + dx * rx) * inv)
                count = got.shape[0] // 8
                fz = jnp.sum((push * rz).reshape(count, 8, 128), axis=0)
                fx = jnp.sum((push * rx).reshape(count, 8, 128), axis=0)
                frc[pl.ds(pl.multiple_of(t * 8, 8), 8), :] = fz
                frc[pl.ds(pl.multiple_of(t * 8 + 256, 8), 8), :] = fx
            return carry
        lax.fori_loop(first // 2, last // 2, step, 0)

    def forces():
        return [sum(frc[pl.ds(k * 256 + r, 32, stride=8), :] for r in range(8)) for k in range(2)]

    index = idx[...]
    share_z = frac[0].astype(F32) / 1024.0
    share_x = frac[1].astype(F32) / 1024.0
    wts[0] = (index >> 4).astype(F32)
    wts[1] = (index & 15).astype(F32)
    wts[2], wts[3] = 1.0 - share_z, share_z
    for n, share in ((4, 1.0 - share_x), (6, share_x)):
        high = share.astype(BF16).astype(F32)
        wts[n], wts[n + 1] = high, share - high
    c64 = iota((64, 128), 0).astype(F32)
    r16 = iota((16, 128), 0).astype(F32)

    def weights(r, t4):
        def get(n):
            return wts[n, pl.ds(r, 1), :]
        column, row = get(1) + (16.0 * t4), get(0)
        here, there = c64 == column, c64 == column + 1.0
        high = jnp.where(here, get(4), jnp.where(there, get(6), 0.0)).astype(BF16)
        low = jnp.where(here, get(5), jnp.where(there, get(7), 0.0)).astype(BF16)
        wz = jnp.where(r16 == row, get(2), jnp.where(r16 == row + 1.0, get(3), 0.0))
        return wz, high, low

    phase_end = reduce_end
    for c in pieces:
        c.wait()
    lane32 = iota((32, 128), 1)

    def sample(h):
        field = gv[h]
        high = field.astype(BF16).astype(F32)
        both = jnp.where(lane32 < 64, high, field - high).astype(BF16)
        for t in range(2):
            for j in range(2):
                wz, whi, wlo = weights(4 * h + 2 * t + j, t * 2 + j)
                right = jnp.concatenate([jnp.concatenate([whi, whi], axis=0),
                                         jnp.concatenate([wlo, wlo], axis=0)], axis=1)
                got = jnp.dot(both, right, preferred_element_type=F32)
                got = got[:, 0:128] + got[:, 128:256]
                for k in range(2):
                    itp[k, pl.ds(j * 16 + 2 * h + t, 1), :] = jnp.sum(
                        wz * got[k * 16:(k + 1) * 16], axis=0, keepdims=True)

    def two_samples(step):
        sample(2 * step)
        sample(2 * step + 1)

    phase_end(0, 0, phase)
    phase = reduce_start(0, 1)
    halo_end(halos)
    halo_tiles(0, two_samples)

    contact_rows(0, 4)
    phase_end(0, 1, phase)
    phase = reduce_start(0, 2)
    contact_rows(4, 16)
    phase_end(0, 2, phase)
    step = 0.2 / mv[3][0:1, :]
    drag = by_column(coef)
    radius = ext[4, 0:32, :]
    alive = jnp.where(radius > 0.0, 1.0, 0.0)
    inverse = jnp.where(radius > 0.0, 0.36 / (radius * radius), 0.0)
    force = forces()
    drags = []
    slack = NEAR[1][1]
    for k in range(2):
        speed = ext[2 + k, 0:32, :]
        drag1 = drag * (itp[k] - speed)
        speed2 = speed + step * (inverse * (force[k] + drag1) - (alive if k == 0 else 0.0))
        place2 = ext[k, 0:32, :] + step * speed2
        ext2[k, 0:32, :] = place2
        inside = (place2 >= -slack) & (place2 <= 16.0 + slack)
        lost = lost + jnp.where(inside, 0.0, alive)
        ext2[2 + k, 0:32, :] = speed2
        drag2 = drag * (itp[k] - speed2)
        drags.append((drag1, drag2))
    ext2[4, 0:32, :] = radius
    halos = halo_start(1)
    bad = lost + rank(1, 0, 32)
    sums = []
    for k in range(2):
        drag1, drag2 = drags[k]
        mean = 0.5 * (alive * drag1 + alive * drag2)
        itp[k] = mean
        itp[2 + k] = drag2
        sums.append(jnp.sum(jnp.sum(mean, axis=1, keepdims=True), axis=0, keepdims=True))
    bad = jnp.sum(jnp.sum(bad, axis=1, keepdims=True), axis=0, keepdims=True)
    sv[0] = jnp.where(attr_row == 0, sums[0], jnp.where(attr_row == 1, sums[1], bad))
    phase = reduce_start(1, 0)

    def spread(h):
        total = jnp.zeros((64, 128), F32)
        for t in range(2):
            for j in range(2):
                wz, whi, wlo = weights(4 * h + 2 * t + j, t * 2 + j)
                m0 = itp[0, pl.ds(j * 16 + 2 * h + t, 1), :]
                m1 = itp[1, pl.ds(j * 16 + 2 * h + t, 1), :]
                lhs = jnp.concatenate([wz * m0, wz * m1], axis=0)
                high = lhs.astype(BF16)
                low = (lhs - high.astype(F32)).astype(BF16)
                total = total + lax.dot_general(
                    jnp.concatenate([high, low], axis=0), jnp.concatenate([whi, wlo], axis=0),
                    (((1,), (1,)), ((), ())), preferred_element_type=F32)
        total = total[0:32] + total[32:64]
        dp[h] = total + pltpu.roll(total, 64, 1)

    lax.fori_loop(0, 8, lambda h, carry: (spread(h), carry)[1], 0)
    pieces = pieces_start(1)
    own_tiles(1)
    phase_end(1, 0, phase)
    phase = reduce_start(1, 1)
    halo_end(halos)
    halo_tiles(1)

    contact_rows(0, 4)
    phase_end(1, 1, phase)
    phase = reduce_start(1, 2)
    contact_rows(4, 16)
    force = forces()
    for k in range(2):
        speed = ext2[2 + k, 0:32, :]
        speed2 = speed + step * (inverse * (force[k] + itp[2 + k]) - (alive if k == 0 else 0.0))
        place2 = (ext2[k, 0:32, :] + step * speed2) * 0.0625
        for j in range(2):
            part[k, pl.ds(j, 16, stride=2), :] = place2[j * 16:(j + 1) * 16]
            part[2 + k, pl.ds(j, 16, stride=2), :] = speed2[j * 16:(j + 1) * 16]
    for c in edges:
        c.wait()

    @pl.when(ax < N_ACROSS - 1)
    def _():
        to_right.wait_send()
        to_left.wait_recv()

    @pl.when(ax > 0)
    def _():
        to_left.wait_send()
        to_right.wait_recv()

    for c in pieces:
        c.wait()
    phase_end(1, 2, phase)
    flag[...] = sv[3][2:3, 0:1]
    gas_step_update(gas, visc, gr, gc, dv, sv.at[3], mv.at[3], out)


def fused(gas, visc, pos, vel, rad, coef, counts_t, pattern_t, idx, frac):
    dma = pltpu.SemaphoreType.DMA
    return pl.pallas_call(
        fused_kernel,
        out_shape=[jax.ShapeDtypeStruct((4, 32, 128), F32), jax.ShapeDtypeStruct((2, 32, 256), F32),
                   jax.ShapeDtypeStruct((1, 1), F32)],
        in_specs=[pl.BlockSpec(memory_space=pl.ANY)] * 10,
        out_specs=[VMEM_SPEC] * 3,
        scratch_shapes=[
            pltpu.VMEM((2, 32, 256), F32), pltpu.VMEM((32, 256), F32),
            pltpu.VMEM((2, 32, 128), F32), pltpu.VMEM((2, 32, 128), F32), pltpu.VMEM((32, 128), F32),
            pltpu.VMEM((32, 128), F32), pltpu.VMEM((32, 128), jnp.int32), pltpu.VMEM((2, 32, 128), jnp.int32),
            pltpu.SMEM((9, 2, 16), jnp.int32), pltpu.SMEM((2, 16), jnp.int32), dma((10,)),
            pltpu.VMEM((8, 128, 128), F32), pltpu.VMEM((8, 128, 128), F32),
            pltpu.VMEM((8, 32, 128), F32), pltpu.VMEM((8, 32, 128), F32),
            pltpu.VMEM((8, 32, 128), F32), pltpu.VMEM((8, 32, 128), F32),
            pltpu.VMEM((2, 2, 8, 256), F32), pltpu.VMEM((2, 2, 32, 128), F32),
            pltpu.VMEM((3, 8, 8, 128), F32), pltpu.VMEM((4, 8, 128), F32),
            pltpu.VMEM((3, 8, 8, 128), F32), pltpu.VMEM((4, 8, 128), F32),
            pltpu.VMEM((8, 128, 128), F32), pltpu.VMEM((32 * 128, 128), BF16),
            pltpu.VMEM((128 * WINDOW_ROWS, 128), BF16), pltpu.VMEM((33, 32, 640), BF16),
            pltpu.VMEM((512, 128), F32), pltpu.VMEM((4, 32, 128), F32), pltpu.VMEM((8, 32, 128), F32),
            dma((2, 10)), dma((2, 10)), dma((2, 8)), dma((2, 8)), dma((2, 3, 8)), dma((2, 3, 8)),
            dma((4,)), dma((4,)),
        ],
        compiler_params=pltpu.CompilerParams(collective_id=2, has_side_effects=True),
        name="interval",
    )(gas, visc, pos, vel, rad, coef, idx, frac, pattern_t, counts_t)


def body(gas, visc, pos, vel, rad, coef, counts, pattern, idx, frac):
    pos, vel, frac = (x.reshape(2, 32, 128) for x in (pos, vel, frac))
    rad, coef, idx = (x.reshape(32, 128) for x in (rad, coef, idx))
    args = (gas, visc, pos, vel, rad, coef, counts.T, pattern.transpose(2, 1, 0), idx, frac)
    part, out, flag = fused(*args)
    part, out = lax.cond(flag[0, 0] > 0.0, lambda p, o: tuple(general(*args)), lambda p, o: (p, o), part, out)
    return part.reshape(4, 16, 2, 128), out


def solution(mesh):
    return jax.shard_map(
        body,
        mesh=mesh,
        in_specs=(
            P(None, ALONG_GAS, "across"),
            P(ALONG_GAS, "across"),
            P(None, "along", ACROSS_GAS, None),
            P(None, "along", ACROSS_GAS, None),
            P("along", ACROSS_GAS, None),
            P("along", ACROSS_GAS, None),
            P("along", ACROSS_GAS),
            P("along", ACROSS_GAS, None),
            P("along", ACROSS_GAS, None),
            P(None, "along", ACROSS_GAS, None),
        ),
        out_specs=(P(None, "along", ACROSS_GAS, None), P(None, ALONG_GAS, "across")),
        check_vma=False,
    )
```

```python
import functools

import jax
import jax.numpy as jnp
from jax import lax
from jax.experimental import pallas as pl
from jax.experimental.pallas import tpu as pltpu
from jax.sharding import PartitionSpec as P

ALONG_GAS = ("along", "gas")
ACROSS_GAS = ("across", "gas")
MESH_ID = pl.DeviceIdType.MESH
OFFSETS = [(-1, -1), (-1, 0), (-1, 1), (0, -1), (0, 0), (0, 1), (1, -1), (1, 0), (1, 1)]
DEAD = -16384.0
F32 = jnp.float32
BF16 = jnp.bfloat16
STRIDE = 136
BLOCK, BLOCK_BITS = 64, 6
EMPTY = 1344
REACH = 2.4
MOVE_LIMIT = int((REACH - 1.9) * 4096)
VMEM_SPEC = pl.BlockSpec(memory_space=pltpu.VMEM)
SMEM_SPEC = pl.BlockSpec(memory_space=pltpu.SMEM)
N_ACROSS, N_ALONG, N_GAS = 4, 8, 8


def iota(shape, dim):
    return lax.broadcasted_iota(jnp.int32, shape, dim)


def ext_row(ii, jj):
    base = {-1: 32, 0: 0, 1: 16, 2: 48}[jj]
    return jnp.where(ii < 0, 64 + 8 * (jj + 1) + 7, jnp.where(ii > 15, 96 + 8 * (jj + 1), base + ii))


def by_column(ref, *lead):
    return jnp.concatenate([ref[(*lead, pl.ds(0, 16, stride=2), slice(None))],
                            ref[(*lead, pl.ds(1, 16, stride=2), slice(None))]], axis=0)


def prepare_state(st, pos, vel, rad, counts):
    row32 = iota((32, 128), 0)
    slot = iota((32, 128), 1)
    cnt = jnp.zeros((32, 128), jnp.int32)
    for j in range(2):
        for i in range(16):
            cnt = jnp.where(row32 == j * 16 + i, counts[j, i], cnt)
    alive = slot < cnt
    z, x = by_column(pos, 0) * 16.0, by_column(pos, 1) * 16.0
    st[0, 0:32, :], st[1, 0:32, :] = z, x
    st[2, 0:32, :], st[3, 0:32, :] = by_column(vel, 0), by_column(vel, 1)
    st[4, 0:32, :] = jnp.where(alive, by_column(rad), DEAD)
    low_x, high_x = x < REACH, x > 16.0 - REACH

    def three(low, mid, high):
        return jnp.where(low_x, low, jnp.where(high_x, high, mid))

    kind = jnp.where(z < REACH, three(0, 1, 2), jnp.where(z > 16.0 - REACH, three(6, 5, 4), three(7, 8, 3)))
    kind = jnp.where(alive, kind, 9)
    member = jnp.concatenate([jnp.where(kind == c, 1.0, 0.0) for c in range(9)], axis=0).astype(BF16)
    before = jnp.where((iota((128, 256), 0) < iota((128, 256), 1)) | (iota((128, 256), 1) >= 128), 1.0, 0.0)
    ranks = jnp.dot(member, before.astype(BF16), preferred_element_type=F32)
    rank = jnp.full((32, 128), -1.0, F32)
    start = [jnp.zeros((32, 128), F32)]
    for c in range(9):
        here = ranks[c * 32:(c + 1) * 32]
        rank = jnp.where(kind == c, start[c] + here[:, 0:128], rank)
        start.append(start[c] + here[:, 128:256])
    st[5, 0:32, :] = rank
    start = [v.astype(jnp.int32) for v in start]
    wrap = ((start[1] + 7) & -8) > start[6]
    zero = jnp.zeros((32, 128), jnp.int32)
    windows = [(start[4], start[5]), (start[4], start[7]), (start[6], start[7]), (start[2], start[5]),
               (zero, start[9]), (jnp.where(wrap, 0, start[6]), start[8]), (start[2], start[3]),
               (zero, start[3]), (zero, start[1]), (zero, jnp.where(wrap, 0, start[1]))]
    table = zero
    for w, (low, high) in enumerate(windows):
        table = jnp.where(slot == 2 * w, low, jnp.where(slot == 2 * w + 1, (high - low + 7) & -8, table))
    st[6, 0:32, :] = table.astype(F32)


def prep_kernel(gas, visc, pos, vel, rad, counts, st, gp, mx):
    rate = jnp.abs(gas[0]) + jnp.abs(gas[1]) + 4.0 * visc[...]
    top = jnp.max(jnp.max(rate, axis=1, keepdims=True), axis=0, keepdims=True)
    mx[...] = jnp.broadcast_to(top, (8, 128))
    lane = iota((16, 128), 1)
    for g in range(N_GAS):
        blk = slice((g // 4) * 128, (g // 4) * 128 + 128)
        off = (g % 4) * 32
        for k in range(2):
            low = gas[k, 0:16, blk]
            high = gas[k, 16:32, blk]
            low = pltpu.roll(low, (128 - off) % 128, 1) if off else low
            shift = (160 - off) % 128
            high = pltpu.roll(high, shift, 1) if shift else high
            piece = jnp.where(lane < 32, low, jnp.where(lane < 64, high, 0.0))
            gp[g, k * 16:(k + 1) * 16, :] = piece
    prepare_state(st, pos, vel, rad, counts)
    st[7] = jnp.zeros((32, 128), F32)


def comm_kernel(first, *refs):
    if first:
        (st, pc, mx, gas, ext, pv, red, gr, gc, mb, m1, m2,
         own_sem, hs, hr, ps, pr, rs, rr, es, er) = refs
    else:
        (st, pc, mx, ext, pv, red, mb, m1, m2,
         own_sem, hs, hr, ps, pr, rs, rr) = refs
    ax, al, g = lax.axis_index("across"), lax.axis_index("along"), lax.axis_index("gas")
    up, down = lax.rem(al + 1, N_ALONG), lax.rem(al + N_ALONG - 1, N_ALONG)
    lin = ax * N_GAS + g
    has_left, has_right = lin > 0, lin < N_ACROSS * N_GAS - 1
    left = jnp.maximum(lin - 1, 0)
    right = jnp.minimum(lin + 1, N_ACROSS * N_GAS - 1)

    def col(index, along):
        return {"across": lax.div(index, N_GAS), "along": along, "gas": lax.rem(index, N_GAS)}

    slab = al * N_GAS + g
    slabs = N_ALONG * N_GAS
    after, before = lax.rem(slab + 1, slabs), lax.rem(slab + slabs - 1, slabs)

    def slab_id(index):
        return {"across": ax, "along": lax.div(index, N_GAS), "gas": lax.rem(index, N_GAS)}

    barrier = pltpu.get_barrier_semaphore()

    def greet(device):
        pl.semaphore_signal(barrier, inc=1, device_id=device, device_id_type=MESH_ID)

    for k in range(1, N_ACROSS):
        greet({"across": lax.rem(ax + k, N_ACROSS)})
    for k in range(1, N_GAS):
        greet({"gas": lax.rem(g + k, N_GAS)})
    for k in range(1, N_ALONG):
        greet({"along": lax.rem(al + k, N_ALONG)})
    expect = N_ACROSS + N_GAS + N_ALONG - 3
    if first:
        greet(slab_id(after))
        greet(slab_id(before))
        expect += 2

    @pl.when(has_left)
    def _():
        for along in (down, al, up):
            greet(col(left, along))

    @pl.when(has_right)
    def _():
        for along in (down, al, up):
            greet(col(right, along))

    own = pltpu.make_async_copy(st, ext.at[:, pl.ds(0, 32)], own_sem.at[0])
    own.start()
    own_piece = pltpu.make_async_copy(pc.at[g], pv.at[g], own_sem.at[1])
    own_piece.start()

    @pl.when(jnp.logical_not(has_left))
    def _():
        ext[:, 32:48, :] = jnp.zeros((8, 16, 128), F32)
        ext[:, 64:72, :] = jnp.zeros((8, 8, 128), F32)
        ext[:, 96:104, :] = jnp.zeros((8, 8, 128), F32)

    @pl.when(jnp.logical_not(has_right))
    def _():
        ext[:, 48:64, :] = jnp.zeros((8, 16, 128), F32)
        ext[:, 88:96, :] = jnp.zeros((8, 8, 128), F32)
        ext[:, 120:128, :] = jnp.zeros((8, 8, 128), F32)

    if first:
        @pl.when(ax == 0)
        def _():
            gc[0] = jnp.zeros((2, 32, 128), F32)

        @pl.when(ax == N_ACROSS - 1)
        def _():
            gc[1] = jnp.zeros((2, 32, 128), F32)

    sides = jnp.where(has_left, 3, 0) + jnp.where(has_right, 3, 0)
    pl.semaphore_wait(barrier, expect + sides)

    def remote(src, dst, send, recv, device):
        return pltpu.make_async_remote_copy(
            src_ref=src, dst_ref=dst, send_sem=send, recv_sem=recv,
            device_id=device, device_id_type=MESH_ID,
        )

    def reduce_sends(phase, src, axis, me, size):
        out = []
        for k in range(1, size):
            out.append(remote(src, mb.at[phase, me], rs.at[phase, k], rr.at[phase, k],
                              {axis: lax.rem(me + k, size)}))
        for c in out:
            c.start()
        return out

    phase0 = reduce_sends(0, mx, "across", ax, N_ACROSS)

    def halo(c, src_rows, size, dst_row, device):
        return remote(st.at[pl.ds(0, 7), pl.ds(src_rows, size)],
                      ext.at[pl.ds(0, 7), pl.ds(dst_row, size)], hs.at[c], hr.at[c], device)

    lefts = [halo(0, 0, 16, 48, col(left, al)),
             halo(1, 8, 8, 64 + 24, col(left, up)),
             halo(2, 0, 8, 96 + 24, col(left, down))]
    rights = [halo(3, 16, 16, 32, col(right, al)),
              halo(4, 24, 8, 64, col(right, up)),
              halo(5, 16, 8, 96, col(right, down))]
    rows = [halo(6, 8, 8, 64 + 8, {"along": up}),
            halo(7, 24, 8, 64 + 16, {"along": up}),
            halo(8, 0, 8, 96 + 8, {"along": down}),
            halo(9, 16, 8, 96 + 16, {"along": down})]

    @pl.when(has_left)
    def _():
        for c in lefts:
            c.start()

    @pl.when(has_right)
    def _():
        for c in rights:
            c.start()

    for c in rows:
        c.start()
    pieces = []
    for k in range(1, N_GAS):
        peer = lax.rem(g + k, N_GAS)
        c = remote(pc.at[peer], pv.at[g], ps.at[k], pr.at[k], {"gas": peer})
        c.start()
        pieces.append(c)
    if first:
        edges = [remote(gas.at[:, pl.ds(24, 8)], gr.at[0], es.at[0], er.at[0], slab_id(after)),
                 remote(gas.at[:, pl.ds(0, 8)], gr.at[1], es.at[1], er.at[1], slab_id(before))]
        for c in edges:
            c.start()
        to_right = remote(gas.at[:, :, pl.ds(128, 128)], gc.at[0], es.at[2], er.at[2],
                          {"across": jnp.minimum(ax + 1, N_ACROSS - 1)})
        to_left = remote(gas.at[:, :, pl.ds(0, 128)], gc.at[1], es.at[3], er.at[3],
                         {"across": jnp.maximum(ax - 1, 0)})

        @pl.when(ax < N_ACROSS - 1)
        def _():
            to_right.start()

        @pl.when(ax > 0)
        def _():
            to_left.start()

    def combine(phase, mine, me, size, copies):
        for c in copies:
            c.wait_recv()
        mb[phase, me] = mine
        total = mb[phase, 0]
        for k in range(1, size):
            total = jnp.maximum(total, mb[phase, k]) if first else total + mb[phase, k]
        return total

    m1[...] = combine(0, mx[...], ax, N_ACROSS, phase0)
    phase1 = reduce_sends(1, m1, "gas", g, N_GAS)
    m2[...] = combine(1, m1[...], g, N_GAS, phase1)
    phase2 = reduce_sends(2, m2, "along", al, N_ALONG)
    red[...] = combine(2, m2[...], al, N_ALONG, phase2)

    own.wait()
    own_piece.wait()
    for c in phase0 + phase1 + phase2:
        c.wait_send()
    for c in rows + pieces:
        c.wait()

    @pl.when(has_left)
    def _():
        for c in lefts:
            c.wait_send()
        for c in rights:
            c.wait_recv()

    @pl.when(has_right)
    def _():
        for c in rights:
            c.wait_send()
        for c in lefts:
            c.wait_recv()

    if first:
        for c in edges:
            c.wait()

        @pl.when(ax < N_ACROSS - 1)
        def _():
            to_right.wait_send()
            to_left.wait_recv()

        @pl.when(ax > 0)
        def _():
            to_left.wait_send()
            to_right.wait_recv()


def exchange(first, st, pc, mx, gas=None):
    out_shape = [jax.ShapeDtypeStruct((8, 128, 128), F32),
                 jax.ShapeDtypeStruct((8, 32, 128), F32),
                 jax.ShapeDtypeStruct((8, 128), F32)]
    scratch = [pltpu.VMEM((3, 8, 8, 128), F32), pltpu.VMEM((8, 128), F32), pltpu.VMEM((8, 128), F32),
               pltpu.SemaphoreType.DMA((2,)),
               pltpu.SemaphoreType.DMA((10,)), pltpu.SemaphoreType.DMA((10,)),
               pltpu.SemaphoreType.DMA((8,)), pltpu.SemaphoreType.DMA((8,)),
               pltpu.SemaphoreType.DMA((3, 8)), pltpu.SemaphoreType.DMA((3, 8))]
    args = [st, pc, mx]
    if first:
        args.append(gas)
        out_shape += [jax.ShapeDtypeStruct((2, 2, 8, 256), F32), jax.ShapeDtypeStruct((2, 2, 32, 128), F32)]
        scratch += [pltpu.SemaphoreType.DMA((4,)), pltpu.SemaphoreType.DMA((4,))]
    return pl.pallas_call(
        functools.partial(comm_kernel, first),
        out_shape=out_shape,
        in_specs=[VMEM_SPEC] * len(args),
        out_specs=[VMEM_SPEC] * len(out_shape),
        scratch_shapes=scratch,
        compiler_params=pltpu.CompilerParams(collective_id=0 if first else 1, has_side_effects=True),
        name="exchange_first" if first else "exchange_second",
    )(*args)


def split3(x):
    hi = x.astype(BF16).astype(F32)
    rest = x - hi
    mid = rest.astype(BF16).astype(F32)
    return hi, mid, rest - mid


def contact_forces(ext, pat, meta, ints, qt, lst, rhs, frc, sem):
    ints[...] = ext[6 * 128:7 * 128, :].astype(jnp.int32)
    to_smem = pltpu.make_async_copy(ints, meta, sem)
    to_smem.start()
    slot = iota((128, 128), 0).astype(F32)
    attr_row = iota((8, 128), 0)
    zero8 = jnp.zeros((8, 128), F32)
    tail = jnp.concatenate([zero8, jnp.ones((24, 128), F32), zero8], axis=0)

    def parts(row):
        block = ext[pl.ds(row, 8, stride=128), :]
        return split3(jnp.where(attr_row < 5, block, 0.0))

    def transposed(row):
        hi, mid, lo = parts(row)
        rows = jnp.concatenate([hi, mid, lo, tail], axis=0).astype(BF16)
        place = (slot == ext[pl.ds(row + 5 * 128, 1), :]).astype(F32).astype(BF16)
        turned = lax.dot_general(place, rows, (((1,), (1,)), ((), ())), preferred_element_type=F32)
        start = row * STRIDE if isinstance(row, int) else pl.multiple_of(row * STRIDE, 8)
        qt[pl.ds(start, 128), 0:64] = turned
        start = start + 128 if isinstance(row, int) else pl.multiple_of(start + 128, 8)
        qt[pl.ds(start, 8), :] = zero8

    def some(step, carry):
        for u in range(4):
            transposed(step * 4 + u)
        return carry

    lax.fori_loop(0, 16, some, 0)
    for c in range(4):
        transposed(64 + 8 * c + 7)
        transposed(96 + 8 * c)

    block_of = iota((32, 640), 1) >> 7
    row_of = iota((32, 640), 0)
    attr_of = row_of & 7
    own_scale = jnp.where(block_of < 2, -1.0, jnp.where(block_of < 4, 2.0, 1.0))
    const = jnp.where((attr_of == block_of) & (row_of < 24), own_scale, 0.0)
    const = jnp.where((row_of == 24) & (block_of == 0) | (row_of == 25) & (block_of == 1), -16.0, const)
    for u in range(2):
        rhs[u, 0:32, :] = const.astype(BF16)
        lst[u, EMPTY:EMPTY + BLOCK, :] = jnp.zeros((BLOCK, 128), F32)
    to_smem.wait()
    lane = iota((8, 128), 1)

    def row_step(i, carry):
        blocks = []
        for j in range(2):
            work = lst.at[j]
            mine = j * 16 + i
            hi, mid, lo = parts(mine)
            columns = []
            for a in range(5):
                keep = attr_row == a
                scale = 1.0 if a in (0, 1, 4) else -2.0
                columns.append(jnp.concatenate(
                    [jnp.where(keep, hi * scale, 0.0), jnp.where(keep, mid * scale, 0.0),
                     jnp.where(keep, lo * scale, 0.0), zero8], axis=0))
            rhs[j, 32:64, :] = jnp.concatenate(columns, axis=1).astype(BF16)
            moved = meta[mine, 20]
            off = i * 0
            over = i * 0
            windows = []
            for w in (4, 0, 1, 2, 3, 5, 6, 7, 8, 9):
                di, dj = OFFSETS[5 if w == 9 else w]
                row = ext_row(i + di, j + dj)
                first, size = meta[row, 2 * w], meta[row, 2 * w + 1]
                if w != 4:
                    near = moved + meta[row, 20] <= MOVE_LIMIT
                    first = jnp.where(near, first, 0)
                    size = jnp.where(near, size, 0 if w == 9 else meta[row, 9])
                size = size * pat[5 if w == 9 else w, j, i]
                mark = jnp.where(lane == 24, float(di), jnp.where(lane == 25, float(dj), 0.0))
                start = row * STRIDE + first
                chunks = 16 if w == 4 else 4 if w in (1, 3, 5, 7) else 1
                for c in range(chunks):
                    work[pl.ds(pl.multiple_of(off + c * 8, 8), 8), :] = qt[pl.ds(start + c * 8, 8), :] + mark
                windows.append((start, size, mark))
                off = off + size
                over = jnp.maximum(over, size - chunks * 8)

            @pl.when(over > 0)
            def _():
                to = i * 0
                for start, size, mark in windows:
                    def copy(c, carry, start=start, mark=mark, to=to):
                        work[pl.ds(pl.multiple_of(to + c * 8, 8), 8), :] = qt[pl.ds(start + c * 8, 8), :] + mark
                        return carry
                    lax.fori_loop(0, size >> 3, copy, 0)
                    to = to + size

            for c in range(BLOCK // 8):
                work[pl.ds(pl.multiple_of(off + c * 8, 8), 8), :] = zero8
            blocks.append((off + BLOCK - 1) >> BLOCK_BITS)
        right = [rhs[0], rhs[1]]

        def block(b, acc):
            out = []
            for j in range(2):
                at = jnp.where(b < blocks[j], b * BLOCK, EMPTY)
                q = lst[j, pl.ds(pl.multiple_of(at, 8), BLOCK), 0:64].astype(BF16)
                got = jnp.dot(q, right[j], preferred_element_type=F32)
                rz, rx = got[:, 0:128], got[:, 128:256]
                dz, dx = got[:, 256:384], got[:, 384:512]
                d2 = rz * rz + rx * rx + 0.0001
                inv = lax.rsqrt(d2)
                depth = jnp.maximum(got[:, 512:640] - d2 * inv, 0.0)
                push = depth * inv * (40.0 + (dz * rz + dx * rx) * inv)
                out.append(acc[2 * j] + jnp.sum((push * rz).reshape(BLOCK // 8, 8, 128), axis=0))
                out.append(acc[2 * j + 1] + jnp.sum((push * rx).reshape(BLOCK // 8, 8, 128), axis=0))
            return tuple(out)

        acc = lax.fori_loop(0, jnp.maximum(blocks[0], blocks[1]), block, (zero8,) * 4)
        for j in range(2):
            for k in range(2):
                frc[pl.ds(pl.multiple_of(((k * 2 + j) * 16 + i) * 8, 8), 8), :] = acc[2 * j + k]
        return carry

    lax.fori_loop(0, 16, row_step, 0)
    return [sum(frc[pl.ds(k * 256 + r, 32, stride=8), :] for r in range(8)) for k in range(2)]


def first_kernel(ext, gv, rate, idx, frac, coef, pat, st2, dp, tot, dr2, inv_out,
                 meta, ints, qt, lst, rhs, frc, itp, sem):
    def weights(r, t4):
        index = idx[pl.ds(r, 1), :]
        row, column = index >> 4, index & 15
        share_z = frac[0, pl.ds(r, 1), :].astype(F32) / 1024.0
        share_x = frac[1, pl.ds(r, 1), :].astype(F32) / 1024.0
        c64 = iota((64, 128), 0) - t4 * 16
        wx = jnp.where(c64 == column, 1.0 - share_x, jnp.where(c64 == column + 1, share_x, 0.0))
        r16 = iota((16, 128), 0)
        wz = jnp.where(r16 == row, 1.0 - share_z, jnp.where(r16 == row + 1, share_z, 0.0))
        return wz, wx

    def sample(h, carry):
        field = gv[h][:, 0:64]
        for t in range(2):
            for j in range(2):
                wz, wx = weights(4 * h + 2 * t + j, t * 2 + j)
                along = jnp.dot(field, wx, precision=lax.Precision.HIGHEST, preferred_element_type=F32)
                for k in range(2):
                    itp[k, pl.ds(j * 16 + 2 * h + t, 1), :] = jnp.sum(
                        wz * along[k * 16:(k + 1) * 16], axis=0, keepdims=True)
        return carry

    lax.fori_loop(0, 8, sample, 0)
    force = contact_forces(ext, pat, meta, ints, qt, lst, rhs, frc, sem)
    step = 0.2 / rate[0:1, :]
    drag = by_column(coef)
    radius = ext[4 * 128:4 * 128 + 32, :]
    alive = jnp.where(radius > 0.0, 1.0, 0.0)
    inverse = jnp.where(radius > 0.0, 0.36 / (radius * radius), 0.0)
    inv_out[...] = inverse
    means = []
    moved = jnp.zeros((32, 128), F32)
    for k in range(2):
        place = ext[k * 128:k * 128 + 32, :]
        speed = ext[(2 + k) * 128:(2 + k) * 128 + 32, :]
        drag1 = drag * (itp[k] - speed)
        speed2 = speed + step * (inverse * (force[k] + drag1) - (alive if k == 0 else 0.0))
        st2[k] = place + step * speed2
        moved = jnp.maximum(moved, alive * jnp.abs(step * speed2))
        st2[2 + k] = speed2
        drag2 = drag * (itp[k] - speed2)
        dr2[k] = drag2
        mean = 0.5 * (alive * drag1 + alive * drag2)
        itp[k] = mean
        means.append(jnp.sum(jnp.sum(mean, axis=1, keepdims=True), axis=0, keepdims=True))
    st2[4] = radius
    st2[5] = ext[5 * 128:5 * 128 + 32, :]
    far = jnp.max(moved, axis=1, keepdims=True)
    far = jnp.where(far < 100.0, far, 100.0) * 4096.0 + 1.0
    st2[6] = jnp.where(iota((32, 128), 1) == 20, far, ext[6 * 128:6 * 128 + 32, :])
    st2[7] = jnp.zeros((32, 128), F32)
    tot[...] = jnp.where(iota((8, 128), 0) == 0, means[0], means[1])

    def spread(h, carry):
        total = jnp.zeros((32, 64), F32)
        for t in range(2):
            for j in range(2):
                wz, wx = weights(4 * h + 2 * t + j, t * 2 + j)
                m0 = itp[0, pl.ds(j * 16 + 2 * h + t, 1), :]
                m1 = itp[1, pl.ds(j * 16 + 2 * h + t, 1), :]
                lhs = jnp.concatenate([wz * m0, wz * m1], axis=0)
                total = total + lax.dot_general(lhs, wx, (((1,), (1,)), ((), ())),
                                                precision=lax.Precision.HIGHEST, preferred_element_type=F32)
        dp[h, :, 0:64] = total
        dp[h, :, 64:128] = jnp.zeros((32, 64), F32)
        return carry

    lax.fori_loop(0, 8, spread, 0)


def gas_step_update(gas, visc, gr, gc, dv, tot, rate, out):
    gas_step = 0.4 / rate[0:1, 0:1]
    lane = iota((32, 256), 1)
    row = iota((32, 256), 0)
    lane16 = iota((16, 128), 1) >> 5
    for k in range(2):
        u = gas[k]
        upper = jnp.where(row == 31, gr[1, k, 0:1, :], pltpu.roll(u, 31, 0))
        lower = jnp.where(row == 0, gr[0, k, 7:8, :], pltpu.roll(u, 1, 0))
        right = jnp.where(lane == 255, gc[1, k, :, 0:1], pltpu.roll(u, 255, 1))
        left = jnp.where(lane == 0, gc[0, k, :, 127:128], pltpu.roll(u, 1, 1))
        laplace = upper + lower + right + left - 4.0 * u
        advect = gas[0] * (upper - lower) * 0.5 + gas[1] * (right - left) * 0.5
        quads = []
        for t in range(2):
            halves = []
            for b in range(2):
                whole = None
                for q in range(4):
                    piece = dv[4 * b + q, k * 16:(k + 1) * 16, :]
                    shift = (q * 32 - t * 32) % 128
                    piece = pltpu.roll(piece, shift, 1) if shift else piece
                    whole = piece if whole is None else jnp.where(lane16 == q, piece, whole)
                halves.append(whole)
            quads.append(jnp.concatenate(halves, axis=1))
        deposit = jnp.concatenate(quads, axis=0)
        source = tot[k:k + 1, 0:1] / 2097152.0 - deposit
        out[k] = u + gas_step * (visc[...] * laplace - advect + source)


def second_kernel(ext, dv, tot, rate, dr2, inverse, gas, visc, gr, gc, pat, part, out,
                  meta, ints, qt, lst, rhs, frc, sem):
    force = contact_forces(ext, pat, meta, ints, qt, lst, rhs, frc, sem)
    step = 0.2 / rate[0:1, :]
    radius = ext[4 * 128:4 * 128 + 32, :]
    alive = jnp.where(radius > 0.0, 1.0, 0.0)
    for k in range(2):
        place = ext[k * 128:k * 128 + 32, :]
        speed = ext[(2 + k) * 128:(2 + k) * 128 + 32, :]
        speed2 = speed + step * (inverse[...] * (force[k] + dr2[k]) - (alive if k == 0 else 0.0))
        place2 = (place + step * speed2) * 0.0625
        for j in range(2):
            part[k, pl.ds(j, 16, stride=2), :] = place2[j * 16:(j + 1) * 16]
            part[2 + k, pl.ds(j, 16, stride=2), :] = speed2[j * 16:(j + 1) * 16]
    gas_step_update(gas, visc, gr, gc, dv, tot, rate, out)


CONTACT_SCRATCH = [
    pltpu.SMEM((128, 128), jnp.int32),
    pltpu.VMEM((128, 128), jnp.int32),
    pltpu.VMEM((128 * STRIDE, 128), F32),
    pltpu.VMEM((2, 1408, 128), F32),
    pltpu.VMEM((2, 64, 640), BF16),
    pltpu.VMEM((512, 128), F32),
]


def general(gas, visc, pos, vel, rad, coef, counts_t, pattern_t, idx, frac):

    def shapes(*dims):
        return [jax.ShapeDtypeStruct(d, F32) for d in dims]

    st, gp, mx = pl.pallas_call(
        prep_kernel,
        out_shape=shapes((8, 32, 128), (8, 32, 128), (8, 128)),
        in_specs=[VMEM_SPEC] * 5 + [SMEM_SPEC],
        out_specs=[VMEM_SPEC] * 3,
        name="prepare",
    )(gas, visc, pos, vel, rad, counts_t)
    ext, gv, rate, gr, gc = exchange(True, st, gp, mx, gas)
    st2, dp, tot, dr2, inverse = pl.pallas_call(
        first_kernel,
        out_shape=shapes((8, 32, 128), (8, 32, 128), (8, 128), (2, 32, 128), (32, 128)),
        in_specs=[VMEM_SPEC] * 6 + [SMEM_SPEC],
        out_specs=[VMEM_SPEC] * 5,
        scratch_shapes=CONTACT_SCRATCH + [pltpu.VMEM((2, 32, 128), F32), pltpu.SemaphoreType.DMA],
        name="first_substep",
    )(ext.reshape(1024, 128), gv, rate, idx, frac, coef, pattern_t)
    ext2, dv, total = exchange(False, st2, dp, tot)
    part, out = pl.pallas_call(
        second_kernel,
        out_shape=shapes((4, 32, 128), (2, 32, 256)),
        in_specs=[VMEM_SPEC] * 10 + [SMEM_SPEC],
        out_specs=[VMEM_SPEC] * 2,
        scratch_shapes=CONTACT_SCRATCH + [pltpu.SemaphoreType.DMA],
        name="second_substep",
    )(ext2.reshape(1024, 128), dv, total, rate, dr2, inverse, gas, visc, gr, gc, pattern_t)
    return part, out


EDGE_BASE, CORNER_BASE, WINDOW_ROWS = 48, 192, 256
CORNER = 16
WINDOWS = ((-1, 0), (1, 0), (0, -1), (0, 1), (-1, -1), (-1, 1), (1, -1), (1, 1))
NEAR = ((1.82, 0.0), (2.25, 0.43))
EDGE = 40


def fused_kernel(*refs):
    inputs, (part, out, flag, pat_copy, counts_copy), refs = refs[:10], refs[10:15], refs[15:]
    gas, visc, pos, vel, rad, coef, idx, frac, pat, counts = refs[:10]
    (in_sem, ext, ext2, gp, gv, dp, dv, gr, gc, mb, mv, sb, sv, rk, qs, qw, rhs, frc, itp, wts, wx, wz,
     hs, hr, ps, pr, rs, rr, es, er) = refs[10:]
    loads = [pltpu.make_async_copy(a, b, in_sem.at[n]) for n, (a, b) in enumerate(zip(inputs, refs[:10]))]
    for c in loads:
        c.start()
    ax, al, g = lax.axis_index("across"), lax.axis_index("along"), lax.axis_index("gas")

    def around(value, size):
        return value - jnp.where(value >= size, size, 0)

    up, down = around(al + 1, N_ALONG), around(al + N_ALONG - 1, N_ALONG)
    first_g, last_g = g == 0, g == N_GAS - 1
    has_left = jnp.logical_or(ax > 0, g > 0)
    has_right = jnp.logical_or(ax < N_ACROSS - 1, g < N_GAS - 1)
    left = (jnp.maximum(ax - jnp.where(first_g, 1, 0), 0), jnp.where(first_g, N_GAS - 1, g - 1))
    right = (jnp.minimum(ax + jnp.where(last_g, 1, 0), N_ACROSS - 1), jnp.where(last_g, 0, g + 1))

    def device(a=ax, l=al, y=g):
        return {"across": a, "along": l, "gas": y}

    def col(side, along):
        return device(a=side[0], l=along, y=side[1])

    def peer_id(axis, index):
        return device(**{{"across": "a", "along": "l", "gas": "y"}[axis]: index})

    after = device(l=jnp.where(last_g, up, al), y=jnp.where(last_g, 0, g + 1))
    before = device(l=jnp.where(first_g, down, al), y=jnp.where(first_g, N_GAS - 1, g - 1))

    barrier = pltpu.get_barrier_semaphore()

    def greet(target):
        pl.semaphore_signal(barrier, inc=1, device_id=target, device_id_type=MESH_ID)

    for k in range(1, N_ALONG):
        greet(device(l=around(al + k, N_ALONG)))
    for k in range(1, N_ACROSS):
        greet(device(a=around(ax + k, N_ACROSS)))
    for k in range(1, N_GAS):
        greet(device(y=around(g + k, N_GAS)))
    greet(after)
    greet(before)
    expect = N_ACROSS + N_GAS + N_ALONG - 3 + 2

    @pl.when(has_left)
    def _():
        for along in (down, al, up):
            greet(col(left, along))

    @pl.when(has_right)
    def _():
        for along in (down, al, up):
            greet(col(right, along))

    for c in loads:
        c.wait()
    rate = jnp.abs(gas[0]) + jnp.abs(gas[1]) + 4.0 * visc[...]
    top = jnp.max(jnp.max(rate, axis=1, keepdims=True), axis=0, keepdims=True)
    mv[0] = jnp.broadcast_to(top, (8, 128))
    lane = iota((16, 128), 1)
    for d in range(N_GAS):
        blk = slice((d // 4) * 128, (d // 4) * 128 + 128)
        off = (d % 4) * 32
        for k in range(2):
            low = gas[k, 0:16, blk]
            high = gas[k, 16:32, blk]
            low = pltpu.roll(low, (128 - off) % 128, 1) if off else low
            shift = (160 - off) % 128
            high = pltpu.roll(high, shift, 1) if shift else high
            piece = jnp.where(lane < 32, low, high)
            gp[d, k * 16:(k + 1) * 16, :] = jnp.where(lane < 64, piece, pltpu.roll(piece, 64, 1))
    row32 = iota((32, 128), 0)
    cnt = jnp.zeros((32, 128), jnp.int32)
    for j in range(2):
        for i in range(16):
            cnt = jnp.where(row32 == j * 16 + i, counts[j, i], cnt)
    ext[0, 0:32, :], ext[1, 0:32, :] = by_column(pos, 0) * 16.0, by_column(pos, 1) * 16.0
    ext[2, 0:32, :], ext[3, 0:32, :] = by_column(vel, 0), by_column(vel, 1)
    ext[4, 0:32, :] = jnp.where(iota((32, 128), 1) < cnt, by_column(rad), DEAD)

    def dots(e, low, high):
        e[5, low:high, :] = e[0, low:high, :] * e[2, low:high, :] + e[1, low:high, :] * e[3, low:high, :]

    dots(ext, 0, 32)
    for e in (ext, ext2):
        @pl.when(jnp.logical_not(has_left))
        def _():
            e[:, 32:48, :] = jnp.zeros((8, 16, 128), F32)
            e[:, 64:72, :] = jnp.zeros((8, 8, 128), F32)
            e[:, 96:104, :] = jnp.zeros((8, 8, 128), F32)

        @pl.when(jnp.logical_not(has_right))
        def _():
            e[:, 48:64, :] = jnp.zeros((8, 16, 128), F32)
            e[:, 88:96, :] = jnp.zeros((8, 8, 128), F32)
            e[:, 120:128, :] = jnp.zeros((8, 8, 128), F32)

    @pl.when(ax == 0)
    def _():
        gc[0] = jnp.zeros((2, 32, 128), F32)

    @pl.when(ax == N_ACROSS - 1)
    def _():
        gc[1] = jnp.zeros((2, 32, 128), F32)

    sides = jnp.where(has_left, 3, 0) + jnp.where(has_right, 3, 0)
    pl.semaphore_wait(barrier, expect + sides)

    def remote(src, dst, send, recv, target):
        return pltpu.make_async_remote_copy(
            src_ref=src, dst_ref=dst, send_sem=send, recv_sem=recv,
            device_id=target, device_id_type=MESH_ID,
        )

    axes = (("across", ax, N_ACROSS), ("gas", g, N_GAS), ("along", al, N_ALONG))

    def reduce_start(which, phase):
        slots, value = ((mb, mv), (sb, sv))[which]
        axis, me, size = axes[phase]
        out = [remote(value.at[phase], slots.at[phase, me], rs.at[which, phase, k], rr.at[which, phase, k],
                      peer_id(axis, around(me + k, size))) for k in range(1, size)]
        for c in out:
            c.start()
        slots[phase, me] = value[phase]
        return out

    def reduce_end(which, phase, copies):
        slots, value = ((mb, mv), (sb, sv))[which]
        size = axes[phase][2]
        for c in copies:
            c.wait_recv()
        total = slots[phase, 0]
        for k in range(1, size):
            total = total + slots[phase, k] if which else jnp.maximum(total, slots[phase, k])
        value[phase + 1] = total
        for c in copies:
            c.wait_send()

    def halo_start(which):
        e, attrs = ((ext, 5), (ext2, 5))[which]

        def halo(c, src_row, size, dst_row, target):
            return remote(e.at[pl.ds(0, attrs), pl.ds(src_row, size)],
                          e.at[pl.ds(0, attrs), pl.ds(dst_row, size)], hs.at[which, c], hr.at[which, c], target)

        lefts = [halo(0, 0, 16, 48, col(left, al)),
                 halo(1, 8, 8, 64 + 24, col(left, up)),
                 halo(2, 0, 8, 96 + 24, col(left, down))]
        rights = [halo(3, 16, 16, 32, col(right, al)),
                  halo(4, 24, 8, 64, col(right, up)),
                  halo(5, 16, 8, 96, col(right, down))]
        rows = [halo(6, 8, 8, 64 + 8, device(l=up)),
                halo(7, 24, 8, 64 + 16, device(l=up)),
                halo(8, 0, 8, 96 + 8, device(l=down)),
                halo(9, 16, 8, 96 + 16, device(l=down))]

        @pl.when(has_left)
        def _():
            for c in lefts:
                c.start()

        @pl.when(has_right)
        def _():
            for c in rights:
                c.start()

        for c in rows:
            c.start()
        return lefts, rights, rows

    def halo_end(copies):
        lefts, rights, rows = copies
        for c in rows:
            c.wait()

        @pl.when(has_left)
        def _():
            for c in lefts:
                c.wait_send()
            for c in rights:
                c.wait_recv()

        @pl.when(has_right)
        def _():
            for c in rights:
                c.wait_send()
            for c in lefts:
                c.wait_recv()

    def pieces_start(which):
        src, dst = ((gp, gv), (dp, dv))[which]
        out = []
        for k in range(1, N_GAS):
            peer = around(g + k, N_GAS)
            c = remote(src.at[peer], dst.at[g], ps.at[which, k], pr.at[which, k], device(y=peer))
            c.start()
            out.append(c)
        dst[g] = src[g]
        return out

    phase = reduce_start(0, 0)
    halos = halo_start(0)
    pieces = pieces_start(0)
    edges = [remote(gas.at[:, pl.ds(24, 8)], gr.at[0], es.at[0], er.at[0], after),
             remote(gas.at[:, pl.ds(0, 8)], gr.at[1], es.at[1], er.at[1], before)]
    for c in edges:
        c.start()
    to_right = remote(gas.at[:, :, pl.ds(128, 128)], gc.at[0], es.at[2], er.at[2],
                      device(a=jnp.minimum(ax + 1, N_ACROSS - 1)))
    to_left = remote(gas.at[:, :, pl.ds(0, 128)], gc.at[1], es.at[3], er.at[3],
                     device(a=jnp.maximum(ax - 1, 0)))

    @pl.when(ax < N_ACROSS - 1)
    def _():
        to_right.start()

    @pl.when(ax > 0)
    def _():
        to_left.start()

    lists = [pltpu.make_async_copy(pat, pat_copy, in_sem.at[10]), pltpu.make_async_copy(counts, counts_copy, in_sem.at[11])]
    for c in lists:
        c.start()

    slot_row = iota((48, 128), 0)
    slots = (jnp.where(slot_row < EDGE, slot_row, -5).astype(F32),
             jnp.where(slot_row < 32, slot_row, jnp.where(slot_row < 40, -5, slot_row - 8)).astype(F32))
    attr_row = iota((8, 128), 0)
    zero8 = jnp.zeros((8, 128), F32)
    one_tail = jnp.concatenate([zero8, jnp.ones((24, 128), F32)], axis=0)
    flat = (ext.reshape(1024, 128), ext2.reshape(1024, 128))
    eye = jnp.where(iota((128, 128), 0) == iota((128, 128), 1), 1.0, 0.0).astype(BF16)
    before_slot = jnp.where(iota((128, 128), 0) < iota((128, 128), 1), 1.0, 0.0).astype(BF16)

    def rank(which, low, high, windows=range(8)):
        e = (ext, ext2)[which]
        reach, _ = NEAR[which]
        z, x, live = e[0, low:high, :], e[1, low:high, :], e[4, low:high, :] > 0.0

        def flags(cond):
            return jnp.where(cond & live, 1.0, 0.0)

        lz, hz, lx, hx = flags(z < reach), flags(z > 16.0 - reach), flags(x < reach), flags(x > 16.0 - reach)
        member = [hz, lz, hx, lx, hz * hx, hz * lx, lz * hx, lz * lx]
        size = high - low
        places = jnp.dot(jnp.concatenate([member[w] for w in windows], axis=0).astype(BF16), before_slot,
                         preferred_element_type=F32)
        lost = jnp.zeros((size, 128), F32)
        for order, w in enumerate(windows):
            place = places[order * size:(order + 1) * size]
            rk[w, low:high, :] = jnp.where(member[w] > 0.0, place, -1.0)
            lost = lost + jnp.where(place >= (EDGE if w < 4 else CORNER), member[w], 0.0)
        return lost

    def parts(which, row):
        block = flat[which][pl.ds(row, 8, stride=128), :]
        return split3(jnp.where(attr_row < 6, block, 0.0))

    def stacked(hi, mid, lo):
        shifted = jnp.where(attr_row < 2, pltpu.roll(hi, 6, 0), jnp.where(attr_row < 4, mid, 0.0))
        return jnp.concatenate([hi, mid, lo, hi, mid, shifted, one_tail], axis=0)

    def partner(v):
        return jnp.where(attr_row < 2, pltpu.roll(v, 6, 0), jnp.where(attr_row < 4, pltpu.roll(v, 2, 0), 0.0))

    def window_rows(which, row, rows, windows):
        sizes = [48 if w < 4 else CORNER for w in windows]
        place = jnp.concatenate(
            [(slots[w & 1 if w < 4 else 0][0:n] == rk[w, pl.ds(row, 1), :]).astype(F32) for w, n in zip(windows, sizes)], axis=0)
        turned = lax.dot_general(place.astype(BF16), rows, (((1,), (1,)), ((), ())), preferred_element_type=F32)
        turned = turned.astype(BF16)
        at = 0
        for w, n in zip(windows, sizes):
            start = row * WINDOW_ROWS + (w * EDGE_BASE if w < 4 else CORNER_BASE + (w - 4) * CORNER)
            if not isinstance(row, int):
                start = pl.multiple_of(start, 16)
            qw[pl.ds(start, n), 0:80] = turned[at:at + n]
            at += n

    def own_tiles(which):
        def some(step, carry):
            for u in range(8):
                row = step * 8 + u
                hi, mid, lo = parts(which, row)
                rows = stacked(hi, mid, lo)
                turned = rows.T
                rows = rows.astype(BF16)
                qs[pl.ds(pl.multiple_of(row * 128, 128), 128), 0:80] = turned.astype(BF16)
                window_rows(which, row, rows, range(8))
                with_hi, with_mid = 2.0 * partner(hi), 2.0 * partner(mid)
                own = jnp.where(attr_row == 5, -2.0, with_hi)
                marked = 16.0 * jnp.where(attr_row < 2, with_hi, jnp.where(attr_row < 4, pltpu.roll(with_mid, 2, 0), 0.0))
                columns = []
                for a, scale in ((0, 1.0), (1, 1.0), (5, -2.0), (4, 1.0)):
                    ends = [jnp.where(attr_row == a, v * scale, 0.0) for v in (hi, mid, lo)]
                    if a == 5:
                        start = [own, own, jnp.where(attr_row == 5, -2.0, 0.0), with_mid, with_mid,
                                 jnp.where(attr_row < 4, -32.0, 0.0), marked]
                    else:
                        one = jnp.where(attr_row == a, 1.0 if a == 4 else -1.0, 0.0)
                        start = [one, one, one, zero8, zero8, zero8,
                                 jnp.where(attr_row == a, DEAD if a == 4 else -16.0, 0.0)]
                    columns.append(jnp.concatenate(start + ends, axis=0))
                rhs[row] = jnp.concatenate(columns, axis=1).astype(BF16)
            return carry
        lax.fori_loop(0, 4, some, 0)

    def halo_tile(which, row, windows):
        hi, mid, lo = parts(which, row)
        window_rows(which, row, stacked(hi, mid, lo).astype(BF16), windows)

    def halo_tiles(which, beside=None):
        dots((ext, ext2)[which], 32, 128)
        rank(which, 32, 48, (2, 4, 6))
        rank(which, 48, 64, (3, 5, 7))
        rank(which, 64, 96, (0, 4, 5))
        rank(which, 96, 128, (1, 6, 7))

        def some(step, carry):
            if beside is not None:
                beside(step)
            for u in range(4):
                halo_tile(which, 32 + step * 4 + u, (2, 4, 6))
                halo_tile(which, 48 + step * 4 + u, (3, 5, 7))
            return carry
        lax.fori_loop(0, 4, some, 0)
        for c in range(4):
            halo_tile(which, 64 + 8 * c + 7, (0, 4, 5))
            halo_tile(which, 96 + 8 * c, (1, 6, 7))

    lane16 = iota((16, 128), 1)
    half = iota((16, 128), 0) < 8

    lost = rank(0, 0, 32)
    own_tiles(0)
    index = idx[...]
    share_z = frac[0].astype(F32) / 1024.0
    share_x = frac[1].astype(F32) / 1024.0
    wts[0] = (index >> 4).astype(F32)
    wts[1] = (index & 15).astype(F32)
    wts[2], wts[3] = 1.0 - share_z, share_z
    for n, share in ((4, 1.0 - share_x), (6, share_x)):
        high = share.astype(BF16).astype(F32)
        wts[n], wts[n + 1] = high, share - high
    c64 = iota((64, 128), 0).astype(F32)
    r16 = iota((16, 128), 0).astype(F32)

    def weigh(r, t4, t):
        def get(n):
            return wts[n, pl.ds(r, 1), :]
        column, row = get(1) + (16.0 * t4), get(0)
        here, there = c64 == column, c64 == column + 1.0
        wx[t, 0:64, :] = jnp.where(here, get(4), jnp.where(there, get(6), 0.0)).astype(BF16)
        wx[t, 64:128, :] = jnp.where(here, get(5), jnp.where(there, get(7), 0.0)).astype(BF16)
        wz[t] = jnp.where(r16 == row, get(2), jnp.where(r16 == row + 1.0, get(3), 0.0))

    def some_weights(h, carry):
        for t in range(2):
            for j in range(2):
                weigh(4 * h + 2 * t + j, t * 2 + j, 4 * h + 2 * t + j)
        return carry

    lax.fori_loop(0, 8, some_weights, 0)

    unlisted = jnp.where(lane16 == 52, 1.0, 0.0)

    def by_offset(low, di, dj, rest):
        lane = lane16 - low
        inside = (lane >= 0) & (lane < 4)
        return jnp.where(inside, jnp.where((lane & 1) == 0, float(di), float(dj)), rest)

    def contact_rows(first, last):

        def step(two, carry):
            for j, u in ((0, 0), (1, 0), (0, 1), (1, 1)):
                i = two * 2 + u
                t = j * 16 + i
                right = rhs[t]

                def mark_of(n):
                    di, dj = OFFSETS[n]
                    base = by_offset(48, di, dj, 0.0)
                    return base + unlisted * (1 - pat[n, j, i]).astype(F32)

                def times(di, dj):
                    return by_offset(40, di, dj, 1.0).astype(BF16)

                def border(w):
                    di, dj = WINDOWS[w]
                    row = ext_row(i + di, j + dj)
                    n = 48 if w < 4 else CORNER
                    start = row * WINDOW_ROWS + (w * EDGE_BASE if w < 4 else CORNER_BASE + (w - 4) * CORNER)
                    block, factor = qw[pl.ds(pl.multiple_of(start, 16), n), :], times(di, dj)
                    return [block[c:c + 16] * factor for c in range(0, n, 16)], mark_of(3 * (di + 1) + dj + 1)

                def edges_of(w):
                    (one, mark1), (two, mark2) = border(w), border(w + 1)
                    both = one[2] + two[2] + jnp.where(half, mark1, mark2).astype(BF16)
                    mark1, mark2 = mark1.astype(BF16), mark2.astype(BF16)
                    return [one[0] + mark1, one[1] + mark1, two[0] + mark2, two[1] + mark2, both]

                def corner(w):
                    (block,), here = border(w)
                    return block + here.astype(BF16)

                own = qs[pl.ds(pl.multiple_of(t * 128, 128), 128), :]
                factor, here = times(0, 0), mark_of(4).astype(BF16)
                groups = [own[c:c + 16] * factor + here for c in range(0, 128, 16)]
                groups += edges_of(0) + edges_of(2) + [corner(w) for w in range(4, 8)]
                got = jnp.dot(jnp.concatenate(groups, axis=0)[:, 0:80], right, preferred_element_type=F32)
                rz, rx = got[:, 0:128], got[:, 128:256]
                inv = lax.rsqrt(rz * rz + rx * rx + 0.0001)
                push = jnp.maximum(got[:, 384:512] * inv - 1.0, 0.0) * (40.0 + got[:, 256:384] * inv)
                count = got.shape[0] // 8
                fz = jnp.sum((push * rz).reshape(count, 8, 128), axis=0)
                fx = jnp.sum((push * rx).reshape(count, 8, 128), axis=0)
                frc[pl.ds(pl.multiple_of(t * 8, 8), 8), :] = fz
                frc[pl.ds(pl.multiple_of(t * 8 + 256, 8), 8), :] = fx
            return carry
        lax.fori_loop(first // 2, last // 2, step, 0)

    def forces():
        return [sum(frc[pl.ds(k * 256 + r, 32, stride=8), :] for r in range(8)) for k in range(2)]

    phase_end = reduce_end
    for c in pieces:
        c.wait()
    lane32 = iota((32, 128), 1)

    def sample(h):
        field = gv[h]
        high = field.astype(BF16).astype(F32)
        both = jnp.where(lane32 < 64, high, field - high).astype(BF16)
        for t in range(2):
            for j in range(2):
                r = 4 * h + 2 * t + j
                whi, wlo = wx[r, 0:64, :], wx[r, 64:128, :]
                right = jnp.concatenate([jnp.concatenate([whi, whi], axis=0),
                                         jnp.concatenate([wlo, wlo], axis=0)], axis=1)
                got = jnp.dot(both, right, preferred_element_type=F32)
                got = got[:, 0:128] + got[:, 128:256]
                for k in range(2):
                    itp[k, pl.ds(j * 16 + 2 * h + t, 1), :] = jnp.sum(
                        wz[r] * got[k * 16:(k + 1) * 16], axis=0, keepdims=True)

    def two_samples(step):
        sample(2 * step)
        sample(2 * step + 1)

    phase_end(0, 0, phase)
    phase = reduce_start(0, 1)
    halo_end(halos)
    halo_tiles(0, two_samples)

    contact_rows(0, 4)
    phase_end(0, 1, phase)
    phase = reduce_start(0, 2)
    contact_rows(4, 16)
    phase_end(0, 2, phase)
    step = 0.2 / mv[3][0:1, :]
    drag = by_column(coef)
    radius = ext[4, 0:32, :]
    alive = jnp.where(radius > 0.0, 1.0, 0.0)
    inverse = jnp.where(radius > 0.0, 0.36 / (radius * radius), 0.0)
    force = forces()
    drags = []
    slack = NEAR[1][1]
    for k in range(2):
        speed = ext[2 + k, 0:32, :]
        drag1 = drag * (itp[k] - speed)
        speed2 = speed + step * (inverse * (force[k] + drag1) - (alive if k == 0 else 0.0))
        place2 = ext[k, 0:32, :] + step * speed2
        ext2[k, 0:32, :] = place2
        inside = (place2 >= -slack) & (place2 <= 16.0 + slack)
        lost = lost + jnp.where(inside, 0.0, alive)
        ext2[2 + k, 0:32, :] = speed2
        drag2 = drag * (itp[k] - speed2)
        drags.append((drag1, drag2))
    ext2[4, 0:32, :] = radius
    dots(ext2, 0, 32)
    halos = halo_start(1)
    bad = lost + rank(1, 0, 32)
    sums = []
    for k in range(2):
        drag1, drag2 = drags[k]
        mean = 0.5 * (alive * drag1 + alive * drag2)
        itp[k] = mean
        itp[2 + k] = drag2
        sums.append(jnp.sum(jnp.sum(mean, axis=1, keepdims=True), axis=0, keepdims=True))
    bad = jnp.sum(jnp.sum(bad, axis=1, keepdims=True), axis=0, keepdims=True)
    sv[0] = jnp.where(attr_row == 0, sums[0], jnp.where(attr_row == 1, sums[1], bad))
    phase = reduce_start(1, 0)

    def spread(h):
        total = jnp.zeros((64, 128), F32)
        for t in range(2):
            for j in range(2):
                r = 4 * h + 2 * t + j
                m0 = itp[0, pl.ds(j * 16 + 2 * h + t, 1), :]
                m1 = itp[1, pl.ds(j * 16 + 2 * h + t, 1), :]
                lhs = jnp.concatenate([wz[r] * m0, wz[r] * m1], axis=0)
                high = lhs.astype(BF16)
                low = (lhs - high.astype(F32)).astype(BF16)
                total = total + lax.dot_general(
                    jnp.concatenate([high, low], axis=0), wx[r],
                    (((1,), (1,)), ((), ())), preferred_element_type=F32)
        total = total[0:32] + total[32:64]
        dp[h] = total + pltpu.roll(total, 64, 1)

    lax.fori_loop(0, 8, lambda h, carry: (spread(h), carry)[1], 0)
    pieces = pieces_start(1)
    own_tiles(1)
    phase_end(1, 0, phase)
    phase = reduce_start(1, 1)
    halo_end(halos)
    halo_tiles(1)

    contact_rows(0, 4)
    phase_end(1, 1, phase)
    phase = reduce_start(1, 2)
    contact_rows(4, 16)
    force = forces()
    for k in range(2):
        speed = ext2[2 + k, 0:32, :]
        speed2 = speed + step * (inverse * (force[k] + itp[2 + k]) - (alive if k == 0 else 0.0))
        place2 = (ext2[k, 0:32, :] + step * speed2) * 0.0625
        for j in range(2):
            part[k, pl.ds(j, 16, stride=2), :] = place2[j * 16:(j + 1) * 16]
            part[2 + k, pl.ds(j, 16, stride=2), :] = speed2[j * 16:(j + 1) * 16]
    for c in edges + lists:
        c.wait()

    @pl.when(ax < N_ACROSS - 1)
    def _():
        to_right.wait_send()
        to_left.wait_recv()

    @pl.when(ax > 0)
    def _():
        to_left.wait_send()
        to_right.wait_recv()

    for c in pieces:
        c.wait()
    phase_end(1, 2, phase)
    flag[...] = sv[3][2:3, 0:1]
    gas_step_update(gas, visc, gr, gc, dv, sv.at[3], mv.at[3], out)


def fused(gas, visc, pos, vel, rad, coef, counts_t, pattern_t, idx, frac):
    dma = pltpu.SemaphoreType.DMA
    return pl.pallas_call(
        fused_kernel,
        out_shape=[jax.ShapeDtypeStruct((4, 32, 128), F32), jax.ShapeDtypeStruct((2, 32, 256), F32),
                   jax.ShapeDtypeStruct((1, 1), F32), jax.ShapeDtypeStruct((9, 2, 16), jnp.int32),
                   jax.ShapeDtypeStruct((2, 16), jnp.int32)],
        in_specs=[pl.BlockSpec(memory_space=pltpu.HBM)] * 10,
        out_specs=[VMEM_SPEC] * 3 + [pl.BlockSpec(memory_space=pltpu.HBM)] * 2,
        scratch_shapes=[
            pltpu.VMEM((2, 32, 256), F32), pltpu.VMEM((32, 256), F32),
            pltpu.VMEM((2, 32, 128), F32), pltpu.VMEM((2, 32, 128), F32), pltpu.VMEM((32, 128), F32),
            pltpu.VMEM((32, 128), F32), pltpu.VMEM((32, 128), jnp.int32), pltpu.VMEM((2, 32, 128), jnp.int32),
            pltpu.SMEM((9, 2, 16), jnp.int32), pltpu.SMEM((2, 16), jnp.int32), dma((12,)),
            pltpu.VMEM((8, 128, 128), F32), pltpu.VMEM((8, 128, 128), F32),
            pltpu.VMEM((8, 32, 128), F32), pltpu.VMEM((8, 32, 128), F32),
            pltpu.VMEM((8, 32, 128), F32), pltpu.VMEM((8, 32, 128), F32),
            pltpu.VMEM((2, 2, 8, 256), F32), pltpu.VMEM((2, 2, 32, 128), F32),
            pltpu.VMEM((3, 8, 8, 128), F32), pltpu.VMEM((4, 8, 128), F32),
            pltpu.VMEM((3, 8, 8, 128), F32), pltpu.VMEM((4, 8, 128), F32),
            pltpu.VMEM((8, 128, 128), F32), pltpu.VMEM((32 * 128, 128), BF16),
            pltpu.VMEM((128 * WINDOW_ROWS, 128), BF16), pltpu.VMEM((32, 80, 512), BF16),
            pltpu.VMEM((512, 128), F32), pltpu.VMEM((4, 32, 128), F32), pltpu.VMEM((8, 32, 128), F32),
            pltpu.VMEM((32, 128, 128), BF16), pltpu.VMEM((32, 16, 128), F32),
            dma((2, 10)), dma((2, 10)), dma((2, 8)), dma((2, 8)), dma((2, 3, 8)), dma((2, 3, 8)),
            dma((4,)), dma((4,)),
        ],
        compiler_params=pltpu.CompilerParams(collective_id=2, has_side_effects=True),
        name="interval",
    )(gas, visc, pos, vel, rad, coef, idx, frac, pattern_t, counts_t)


def body(gas, visc, pos, vel, rad, coef, counts, pattern, idx, frac):
    pos, vel, frac = (x.reshape(2, 32, 128) for x in (pos, vel, frac))
    rad, coef, idx = (x.reshape(32, 128) for x in (rad, coef, idx))
    args = (gas, visc, pos, vel, rad, coef, counts.T, pattern.transpose(2, 1, 0), idx, frac)
    part, out, flag, pattern_t, counts_t = fused(*args)
    args = args[:6] + (counts_t, pattern_t) + args[8:]
    part, out = lax.cond(flag[0, 0] > 0.0, lambda p, o: tuple(general(*args)), lambda p, o: (p, o), part, out)
    return part.reshape(4, 16, 2, 128), out


def solution(mesh):
    return jax.shard_map(
        body,
        mesh=mesh,
        in_specs=(
            P(None, ALONG_GAS, "across"),
            P(ALONG_GAS, "across"),
            P(None, "along", ACROSS_GAS, None),
            P(None, "along", ACROSS_GAS, None),
            P("along", ACROSS_GAS, None),
            P("along", ACROSS_GAS, None),
            P("along", ACROSS_GAS),
            P("along", ACROSS_GAS, None),
            P("along", ACROSS_GAS, None),
            P(None, "along", ACROSS_GAS, None),
        ),
        out_specs=(P(None, "along", ACROSS_GAS, None), P(None, ALONG_GAS, "across")),
        check_vma=False,
    )
```

```python
import functools

import jax
import jax.numpy as jnp
from jax import lax
from jax.experimental import pallas as pl
from jax.experimental.pallas import tpu as pltpu
from jax.sharding import PartitionSpec as P

ALONG_GAS = ("along", "gas")
ACROSS_GAS = ("across", "gas")
MESH_ID = pl.DeviceIdType.MESH
OFFSETS = [(-1, -1), (-1, 0), (-1, 1), (0, -1), (0, 0), (0, 1), (1, -1), (1, 0), (1, 1)]
DEAD = -16384.0
F32 = jnp.float32
BF16 = jnp.bfloat16
STRIDE = 136
BLOCK, BLOCK_BITS = 64, 6
EMPTY = 1344
REACH = 2.4
MOVE_LIMIT = int((REACH - 1.9) * 4096)
VMEM_SPEC = pl.BlockSpec(memory_space=pltpu.VMEM)
SMEM_SPEC = pl.BlockSpec(memory_space=pltpu.SMEM)
N_ACROSS, N_ALONG, N_GAS = 4, 8, 8


def iota(shape, dim):
    return lax.broadcasted_iota(jnp.int32, shape, dim)


def ext_row(ii, jj):
    base = {-1: 32, 0: 0, 1: 16, 2: 48}[jj]
    return jnp.where(ii < 0, 64 + 8 * (jj + 1) + 7, jnp.where(ii > 15, 96 + 8 * (jj + 1), base + ii))


def by_column(ref, *lead):
    return jnp.concatenate([ref[(*lead, pl.ds(0, 16, stride=2), slice(None))],
                            ref[(*lead, pl.ds(1, 16, stride=2), slice(None))]], axis=0)


def prepare_state(st, pos, vel, rad, counts):
    row32 = iota((32, 128), 0)
    slot = iota((32, 128), 1)
    cnt = jnp.zeros((32, 128), jnp.int32)
    for j in range(2):
        for i in range(16):
            cnt = jnp.where(row32 == j * 16 + i, counts[j, i], cnt)
    alive = slot < cnt
    z, x = by_column(pos, 0) * 16.0, by_column(pos, 1) * 16.0
    st[0, 0:32, :], st[1, 0:32, :] = z, x
    st[2, 0:32, :], st[3, 0:32, :] = by_column(vel, 0), by_column(vel, 1)
    st[4, 0:32, :] = jnp.where(alive, by_column(rad), DEAD)
    low_x, high_x = x < REACH, x > 16.0 - REACH

    def three(low, mid, high):
        return jnp.where(low_x, low, jnp.where(high_x, high, mid))

    kind = jnp.where(z < REACH, three(0, 1, 2), jnp.where(z > 16.0 - REACH, three(6, 5, 4), three(7, 8, 3)))
    kind = jnp.where(alive, kind, 9)
    member = jnp.concatenate([jnp.where(kind == c, 1.0, 0.0) for c in range(9)], axis=0).astype(BF16)
    before = jnp.where((iota((128, 256), 0) < iota((128, 256), 1)) | (iota((128, 256), 1) >= 128), 1.0, 0.0)
    ranks = jnp.dot(member, before.astype(BF16), preferred_element_type=F32)
    rank = jnp.full((32, 128), -1.0, F32)
    start = [jnp.zeros((32, 128), F32)]
    for c in range(9):
        here = ranks[c * 32:(c + 1) * 32]
        rank = jnp.where(kind == c, start[c] + here[:, 0:128], rank)
        start.append(start[c] + here[:, 128:256])
    st[5, 0:32, :] = rank
    start = [v.astype(jnp.int32) for v in start]
    wrap = ((start[1] + 7) & -8) > start[6]
    zero = jnp.zeros((32, 128), jnp.int32)
    windows = [(start[4], start[5]), (start[4], start[7]), (start[6], start[7]), (start[2], start[5]),
               (zero, start[9]), (jnp.where(wrap, 0, start[6]), start[8]), (start[2], start[3]),
               (zero, start[3]), (zero, start[1]), (zero, jnp.where(wrap, 0, start[1]))]
    table = zero
    for w, (low, high) in enumerate(windows):
        table = jnp.where(slot == 2 * w, low, jnp.where(slot == 2 * w + 1, (high - low + 7) & -8, table))
    st[6, 0:32, :] = table.astype(F32)


def prep_kernel(gas, visc, pos, vel, rad, counts, st, gp, mx):
    rate = jnp.abs(gas[0]) + jnp.abs(gas[1]) + 4.0 * visc[...]
    top = jnp.max(jnp.max(rate, axis=1, keepdims=True), axis=0, keepdims=True)
    mx[...] = jnp.broadcast_to(top, (8, 128))
    lane = iota((16, 128), 1)
    for g in range(N_GAS):
        blk = slice((g // 4) * 128, (g // 4) * 128 + 128)
        off = (g % 4) * 32
        for k in range(2):
            low = gas[k, 0:16, blk]
            high = gas[k, 16:32, blk]
            low = pltpu.roll(low, (128 - off) % 128, 1) if off else low
            shift = (160 - off) % 128
            high = pltpu.roll(high, shift, 1) if shift else high
            piece = jnp.where(lane < 32, low, jnp.where(lane < 64, high, 0.0))
            gp[g, k * 16:(k + 1) * 16, :] = piece
    prepare_state(st, pos, vel, rad, counts)
    st[7] = jnp.zeros((32, 128), F32)


def comm_kernel(first, *refs):
    if first:
        (st, pc, mx, gas, ext, pv, red, gr, gc, mb, m1, m2,
         own_sem, hs, hr, ps, pr, rs, rr, es, er) = refs
    else:
        (st, pc, mx, ext, pv, red, mb, m1, m2,
         own_sem, hs, hr, ps, pr, rs, rr) = refs
    ax, al, g = lax.axis_index("across"), lax.axis_index("along"), lax.axis_index("gas")
    up, down = lax.rem(al + 1, N_ALONG), lax.rem(al + N_ALONG - 1, N_ALONG)
    lin = ax * N_GAS + g
    has_left, has_right = lin > 0, lin < N_ACROSS * N_GAS - 1
    left = jnp.maximum(lin - 1, 0)
    right = jnp.minimum(lin + 1, N_ACROSS * N_GAS - 1)

    def col(index, along):
        return {"across": lax.div(index, N_GAS), "along": along, "gas": lax.rem(index, N_GAS)}

    slab = al * N_GAS + g
    slabs = N_ALONG * N_GAS
    after, before = lax.rem(slab + 1, slabs), lax.rem(slab + slabs - 1, slabs)

    def slab_id(index):
        return {"across": ax, "along": lax.div(index, N_GAS), "gas": lax.rem(index, N_GAS)}

    barrier = pltpu.get_barrier_semaphore()

    def greet(device):
        pl.semaphore_signal(barrier, inc=1, device_id=device, device_id_type=MESH_ID)

    for k in range(1, N_ACROSS):
        greet({"across": lax.rem(ax + k, N_ACROSS)})
    for k in range(1, N_GAS):
        greet({"gas": lax.rem(g + k, N_GAS)})
    for k in range(1, N_ALONG):
        greet({"along": lax.rem(al + k, N_ALONG)})
    expect = N_ACROSS + N_GAS + N_ALONG - 3
    if first:
        greet(slab_id(after))
        greet(slab_id(before))
        expect += 2

    @pl.when(has_left)
    def _():
        for along in (down, al, up):
            greet(col(left, along))

    @pl.when(has_right)
    def _():
        for along in (down, al, up):
            greet(col(right, along))

    own = pltpu.make_async_copy(st, ext.at[:, pl.ds(0, 32)], own_sem.at[0])
    own.start()
    own_piece = pltpu.make_async_copy(pc.at[g], pv.at[g], own_sem.at[1])
    own_piece.start()

    @pl.when(jnp.logical_not(has_left))
    def _():
        ext[:, 32:48, :] = jnp.zeros((8, 16, 128), F32)
        ext[:, 64:72, :] = jnp.zeros((8, 8, 128), F32)
        ext[:, 96:104, :] = jnp.zeros((8, 8, 128), F32)

    @pl.when(jnp.logical_not(has_right))
    def _():
        ext[:, 48:64, :] = jnp.zeros((8, 16, 128), F32)
        ext[:, 88:96, :] = jnp.zeros((8, 8, 128), F32)
        ext[:, 120:128, :] = jnp.zeros((8, 8, 128), F32)

    if first:
        @pl.when(ax == 0)
        def _():
            gc[0] = jnp.zeros((2, 32, 128), F32)

        @pl.when(ax == N_ACROSS - 1)
        def _():
            gc[1] = jnp.zeros((2, 32, 128), F32)

    sides = jnp.where(has_left, 3, 0) + jnp.where(has_right, 3, 0)
    pl.semaphore_wait(barrier, expect + sides)

    def remote(src, dst, send, recv, device):
        return pltpu.make_async_remote_copy(
            src_ref=src, dst_ref=dst, send_sem=send, recv_sem=recv,
            device_id=device, device_id_type=MESH_ID,
        )

    def reduce_sends(phase, src, axis, me, size):
        out = []
        for k in range(1, size):
            out.append(remote(src, mb.at[phase, me], rs.at[phase, k], rr.at[phase, k],
                              {axis: lax.rem(me + k, size)}))
        for c in out:
            c.start()
        return out

    phase0 = reduce_sends(0, mx, "across", ax, N_ACROSS)

    def halo(c, src_rows, size, dst_row, device):
        return remote(st.at[pl.ds(0, 7), pl.ds(src_rows, size)],
                      ext.at[pl.ds(0, 7), pl.ds(dst_row, size)], hs.at[c], hr.at[c], device)

    lefts = [halo(0, 0, 16, 48, col(left, al)),
             halo(1, 8, 8, 64 + 24, col(left, up)),
             halo(2, 0, 8, 96 + 24, col(left, down))]
    rights = [halo(3, 16, 16, 32, col(right, al)),
              halo(4, 24, 8, 64, col(right, up)),
              halo(5, 16, 8, 96, col(right, down))]
    rows = [halo(6, 8, 8, 64 + 8, {"along": up}),
            halo(7, 24, 8, 64 + 16, {"along": up}),
            halo(8, 0, 8, 96 + 8, {"along": down}),
            halo(9, 16, 8, 96 + 16, {"along": down})]

    @pl.when(has_left)
    def _():
        for c in lefts:
            c.start()

    @pl.when(has_right)
    def _():
        for c in rights:
            c.start()

    for c in rows:
        c.start()
    pieces = []
    for k in range(1, N_GAS):
        peer = lax.rem(g + k, N_GAS)
        c = remote(pc.at[peer], pv.at[g], ps.at[k], pr.at[k], {"gas": peer})
        c.start()
        pieces.append(c)
    if first:
        edges = [remote(gas.at[:, pl.ds(24, 8)], gr.at[0], es.at[0], er.at[0], slab_id(after)),
                 remote(gas.at[:, pl.ds(0, 8)], gr.at[1], es.at[1], er.at[1], slab_id(before))]
        for c in edges:
            c.start()
        to_right = remote(gas.at[:, :, pl.ds(128, 128)], gc.at[0], es.at[2], er.at[2],
                          {"across": jnp.minimum(ax + 1, N_ACROSS - 1)})
        to_left = remote(gas.at[:, :, pl.ds(0, 128)], gc.at[1], es.at[3], er.at[3],
                         {"across": jnp.maximum(ax - 1, 0)})

        @pl.when(ax < N_ACROSS - 1)
        def _():
            to_right.start()

        @pl.when(ax > 0)
        def _():
            to_left.start()

    def combine(phase, mine, me, size, copies):
        for c in copies:
            c.wait_recv()
        mb[phase, me] = mine
        total = mb[phase, 0]
        for k in range(1, size):
            total = jnp.maximum(total, mb[phase, k]) if first else total + mb[phase, k]
        return total

    m1[...] = combine(0, mx[...], ax, N_ACROSS, phase0)
    phase1 = reduce_sends(1, m1, "gas", g, N_GAS)
    m2[...] = combine(1, m1[...], g, N_GAS, phase1)
    phase2 = reduce_sends(2, m2, "along", al, N_ALONG)
    red[...] = combine(2, m2[...], al, N_ALONG, phase2)

    own.wait()
    own_piece.wait()
    for c in phase0 + phase1 + phase2:
        c.wait_send()
    for c in rows + pieces:
        c.wait()

    @pl.when(has_left)
    def _():
        for c in lefts:
            c.wait_send()
        for c in rights:
            c.wait_recv()

    @pl.when(has_right)
    def _():
        for c in rights:
            c.wait_send()
        for c in lefts:
            c.wait_recv()

    if first:
        for c in edges:
            c.wait()

        @pl.when(ax < N_ACROSS - 1)
        def _():
            to_right.wait_send()
            to_left.wait_recv()

        @pl.when(ax > 0)
        def _():
            to_left.wait_send()
            to_right.wait_recv()


def exchange(first, st, pc, mx, gas=None):
    out_shape = [jax.ShapeDtypeStruct((8, 128, 128), F32),
                 jax.ShapeDtypeStruct((8, 32, 128), F32),
                 jax.ShapeDtypeStruct((8, 128), F32)]
    scratch = [pltpu.VMEM((3, 8, 8, 128), F32), pltpu.VMEM((8, 128), F32), pltpu.VMEM((8, 128), F32),
               pltpu.SemaphoreType.DMA((2,)),
               pltpu.SemaphoreType.DMA((10,)), pltpu.SemaphoreType.DMA((10,)),
               pltpu.SemaphoreType.DMA((8,)), pltpu.SemaphoreType.DMA((8,)),
               pltpu.SemaphoreType.DMA((3, 8)), pltpu.SemaphoreType.DMA((3, 8))]
    args = [st, pc, mx]
    if first:
        args.append(gas)
        out_shape += [jax.ShapeDtypeStruct((2, 2, 8, 256), F32), jax.ShapeDtypeStruct((2, 2, 32, 128), F32)]
        scratch += [pltpu.SemaphoreType.DMA((4,)), pltpu.SemaphoreType.DMA((4,))]
    return pl.pallas_call(
        functools.partial(comm_kernel, first),
        out_shape=out_shape,
        in_specs=[VMEM_SPEC] * len(args),
        out_specs=[VMEM_SPEC] * len(out_shape),
        scratch_shapes=scratch,
        compiler_params=pltpu.CompilerParams(collective_id=0 if first else 1, has_side_effects=True),
        name="exchange_first" if first else "exchange_second",
    )(*args)


def split3(x):
    hi = x.astype(BF16).astype(F32)
    rest = x - hi
    mid = rest.astype(BF16).astype(F32)
    return hi, mid, rest - mid


def contact_forces(ext, pat, meta, ints, qt, lst, rhs, frc, sem):
    ints[...] = ext[6 * 128:7 * 128, :].astype(jnp.int32)
    to_smem = pltpu.make_async_copy(ints, meta, sem)
    to_smem.start()
    slot = iota((128, 128), 0).astype(F32)
    attr_row = iota((8, 128), 0)
    zero8 = jnp.zeros((8, 128), F32)
    tail = jnp.concatenate([zero8, jnp.ones((24, 128), F32), zero8], axis=0)

    def parts(row):
        block = ext[pl.ds(row, 8, stride=128), :]
        return split3(jnp.where(attr_row < 5, block, 0.0))

    def transposed(row):
        hi, mid, lo = parts(row)
        rows = jnp.concatenate([hi, mid, lo, tail], axis=0).astype(BF16)
        place = (slot == ext[pl.ds(row + 5 * 128, 1), :]).astype(F32).astype(BF16)
        turned = lax.dot_general(place, rows, (((1,), (1,)), ((), ())), preferred_element_type=F32)
        start = row * STRIDE if isinstance(row, int) else pl.multiple_of(row * STRIDE, 8)
        qt[pl.ds(start, 128), 0:64] = turned
        start = start + 128 if isinstance(row, int) else pl.multiple_of(start + 128, 8)
        qt[pl.ds(start, 8), :] = zero8

    def some(step, carry):
        for u in range(4):
            transposed(step * 4 + u)
        return carry

    lax.fori_loop(0, 16, some, 0)
    for c in range(4):
        transposed(64 + 8 * c + 7)
        transposed(96 + 8 * c)

    block_of = iota((32, 640), 1) >> 7
    row_of = iota((32, 640), 0)
    attr_of = row_of & 7
    own_scale = jnp.where(block_of < 2, -1.0, jnp.where(block_of < 4, 2.0, 1.0))
    const = jnp.where((attr_of == block_of) & (row_of < 24), own_scale, 0.0)
    const = jnp.where((row_of == 24) & (block_of == 0) | (row_of == 25) & (block_of == 1), -16.0, const)
    for u in range(2):
        rhs[u, 0:32, :] = const.astype(BF16)
        lst[u, EMPTY:EMPTY + BLOCK, :] = jnp.zeros((BLOCK, 128), F32)
    to_smem.wait()
    lane = iota((8, 128), 1)

    def row_step(i, carry):
        blocks = []
        for j in range(2):
            work = lst.at[j]
            mine = j * 16 + i
            hi, mid, lo = parts(mine)
            columns = []
            for a in range(5):
                keep = attr_row == a
                scale = 1.0 if a in (0, 1, 4) else -2.0
                columns.append(jnp.concatenate(
                    [jnp.where(keep, hi * scale, 0.0), jnp.where(keep, mid * scale, 0.0),
                     jnp.where(keep, lo * scale, 0.0), zero8], axis=0))
            rhs[j, 32:64, :] = jnp.concatenate(columns, axis=1).astype(BF16)
            moved = meta[mine, 20]
            off = i * 0
            over = i * 0
            windows = []
            for w in (4, 0, 1, 2, 3, 5, 6, 7, 8, 9):
                di, dj = OFFSETS[5 if w == 9 else w]
                row = ext_row(i + di, j + dj)
                first, size = meta[row, 2 * w], meta[row, 2 * w + 1]
                if w != 4:
                    near = moved + meta[row, 20] <= MOVE_LIMIT
                    first = jnp.where(near, first, 0)
                    size = jnp.where(near, size, 0 if w == 9 else meta[row, 9])
                size = size * pat[5 if w == 9 else w, j, i]
                mark = jnp.where(lane == 24, float(di), jnp.where(lane == 25, float(dj), 0.0))
                start = row * STRIDE + first
                chunks = 16 if w == 4 else 4 if w in (1, 3, 5, 7) else 1
                for c in range(chunks):
                    work[pl.ds(pl.multiple_of(off + c * 8, 8), 8), :] = qt[pl.ds(start + c * 8, 8), :] + mark
                windows.append((start, size, mark))
                off = off + size
                over = jnp.maximum(over, size - chunks * 8)

            @pl.when(over > 0)
            def _():
                to = i * 0
                for start, size, mark in windows:
                    def copy(c, carry, start=start, mark=mark, to=to):
                        work[pl.ds(pl.multiple_of(to + c * 8, 8), 8), :] = qt[pl.ds(start + c * 8, 8), :] + mark
                        return carry
                    lax.fori_loop(0, size >> 3, copy, 0)
                    to = to + size

            for c in range(BLOCK // 8):
                work[pl.ds(pl.multiple_of(off + c * 8, 8), 8), :] = zero8
            blocks.append((off + BLOCK - 1) >> BLOCK_BITS)
        right = [rhs[0], rhs[1]]

        def block(b, acc):
            out = []
            for j in range(2):
                at = jnp.where(b < blocks[j], b * BLOCK, EMPTY)
                q = lst[j, pl.ds(pl.multiple_of(at, 8), BLOCK), 0:64].astype(BF16)
                got = jnp.dot(q, right[j], preferred_element_type=F32)
                rz, rx = got[:, 0:128], got[:, 128:256]
                dz, dx = got[:, 256:384], got[:, 384:512]
                d2 = rz * rz + rx * rx + 0.0001
                inv = lax.rsqrt(d2)
                depth = jnp.maximum(got[:, 512:640] - d2 * inv, 0.0)
                push = depth * inv * (40.0 + (dz * rz + dx * rx) * inv)
                out.append(acc[2 * j] + jnp.sum((push * rz).reshape(BLOCK // 8, 8, 128), axis=0))
                out.append(acc[2 * j + 1] + jnp.sum((push * rx).reshape(BLOCK // 8, 8, 128), axis=0))
            return tuple(out)

        acc = lax.fori_loop(0, jnp.maximum(blocks[0], blocks[1]), block, (zero8,) * 4)
        for j in range(2):
            for k in range(2):
                frc[pl.ds(pl.multiple_of(((k * 2 + j) * 16 + i) * 8, 8), 8), :] = acc[2 * j + k]
        return carry

    lax.fori_loop(0, 16, row_step, 0)
    return [sum(frc[pl.ds(k * 256 + r, 32, stride=8), :] for r in range(8)) for k in range(2)]


def first_kernel(ext, gv, rate, idx, frac, coef, pat, st2, dp, tot, dr2, inv_out,
                 meta, ints, qt, lst, rhs, frc, itp, sem):
    def weights(r, t4):
        index = idx[pl.ds(r, 1), :]
        row, column = index >> 4, index & 15
        share_z = frac[0, pl.ds(r, 1), :].astype(F32) / 1024.0
        share_x = frac[1, pl.ds(r, 1), :].astype(F32) / 1024.0
        c64 = iota((64, 128), 0) - t4 * 16
        wx = jnp.where(c64 == column, 1.0 - share_x, jnp.where(c64 == column + 1, share_x, 0.0))
        r16 = iota((16, 128), 0)
        wz = jnp.where(r16 == row, 1.0 - share_z, jnp.where(r16 == row + 1, share_z, 0.0))
        return wz, wx

    def sample(h, carry):
        field = gv[h][:, 0:64]
        for t in range(2):
            for j in range(2):
                wz, wx = weights(4 * h + 2 * t + j, t * 2 + j)
                along = jnp.dot(field, wx, precision=lax.Precision.HIGHEST, preferred_element_type=F32)
                for k in range(2):
                    itp[k, pl.ds(j * 16 + 2 * h + t, 1), :] = jnp.sum(
                        wz * along[k * 16:(k + 1) * 16], axis=0, keepdims=True)
        return carry

    lax.fori_loop(0, 8, sample, 0)
    force = contact_forces(ext, pat, meta, ints, qt, lst, rhs, frc, sem)
    step = 0.2 / rate[0:1, :]
    drag = by_column(coef)
    radius = ext[4 * 128:4 * 128 + 32, :]
    alive = jnp.where(radius > 0.0, 1.0, 0.0)
    inverse = jnp.where(radius > 0.0, 0.36 / (radius * radius), 0.0)
    inv_out[...] = inverse
    means = []
    moved = jnp.zeros((32, 128), F32)
    for k in range(2):
        place = ext[k * 128:k * 128 + 32, :]
        speed = ext[(2 + k) * 128:(2 + k) * 128 + 32, :]
        drag1 = drag * (itp[k] - speed)
        speed2 = speed + step * (inverse * (force[k] + drag1) - (alive if k == 0 else 0.0))
        st2[k] = place + step * speed2
        moved = jnp.maximum(moved, alive * jnp.abs(step * speed2))
        st2[2 + k] = speed2
        drag2 = drag * (itp[k] - speed2)
        dr2[k] = drag2
        mean = 0.5 * (alive * drag1 + alive * drag2)
        itp[k] = mean
        means.append(jnp.sum(jnp.sum(mean, axis=1, keepdims=True), axis=0, keepdims=True))
    st2[4] = radius
    st2[5] = ext[5 * 128:5 * 128 + 32, :]
    far = jnp.max(moved, axis=1, keepdims=True)
    far = jnp.where(far < 100.0, far, 100.0) * 4096.0 + 1.0
    st2[6] = jnp.where(iota((32, 128), 1) == 20, far, ext[6 * 128:6 * 128 + 32, :])
    st2[7] = jnp.zeros((32, 128), F32)
    tot[...] = jnp.where(iota((8, 128), 0) == 0, means[0], means[1])

    def spread(h, carry):
        total = jnp.zeros((32, 64), F32)
        for t in range(2):
            for j in range(2):
                wz, wx = weights(4 * h + 2 * t + j, t * 2 + j)
                m0 = itp[0, pl.ds(j * 16 + 2 * h + t, 1), :]
                m1 = itp[1, pl.ds(j * 16 + 2 * h + t, 1), :]
                lhs = jnp.concatenate([wz * m0, wz * m1], axis=0)
                total = total + lax.dot_general(lhs, wx, (((1,), (1,)), ((), ())),
                                                precision=lax.Precision.HIGHEST, preferred_element_type=F32)
        dp[h, :, 0:64] = total
        dp[h, :, 64:128] = jnp.zeros((32, 64), F32)
        return carry

    lax.fori_loop(0, 8, spread, 0)


def gas_step_update(gas, visc, gr, gc, dv, tot, rate, out):
    gas_step = 0.4 / rate[0:1, 0:1]
    lane = iota((32, 256), 1)
    row = iota((32, 256), 0)
    lane16 = iota((16, 128), 1) >> 5
    for k in range(2):
        u = gas[k]
        upper = jnp.where(row == 31, gr[1, k, 0:1, :], pltpu.roll(u, 31, 0))
        lower = jnp.where(row == 0, gr[0, k, 7:8, :], pltpu.roll(u, 1, 0))
        right = jnp.where(lane == 255, gc[1, k, :, 0:1], pltpu.roll(u, 255, 1))
        left = jnp.where(lane == 0, gc[0, k, :, 127:128], pltpu.roll(u, 1, 1))
        laplace = upper + lower + right + left - 4.0 * u
        advect = gas[0] * (upper - lower) * 0.5 + gas[1] * (right - left) * 0.5
        quads = []
        for t in range(2):
            halves = []
            for b in range(2):
                whole = None
                for q in range(4):
                    piece = dv[4 * b + q, k * 16:(k + 1) * 16, :]
                    shift = (q * 32 - t * 32) % 128
                    piece = pltpu.roll(piece, shift, 1) if shift else piece
                    whole = piece if whole is None else jnp.where(lane16 == q, piece, whole)
                halves.append(whole)
            quads.append(jnp.concatenate(halves, axis=1))
        deposit = jnp.concatenate(quads, axis=0)
        source = tot[k:k + 1, 0:1] / 2097152.0 - deposit
        out[k] = u + gas_step * (visc[...] * laplace - advect + source)


def second_kernel(ext, dv, tot, rate, dr2, inverse, gas, visc, gr, gc, pat, part, out,
                  meta, ints, qt, lst, rhs, frc, sem):
    force = contact_forces(ext, pat, meta, ints, qt, lst, rhs, frc, sem)
    step = 0.2 / rate[0:1, :]
    radius = ext[4 * 128:4 * 128 + 32, :]
    alive = jnp.where(radius > 0.0, 1.0, 0.0)
    for k in range(2):
        place = ext[k * 128:k * 128 + 32, :]
        speed = ext[(2 + k) * 128:(2 + k) * 128 + 32, :]
        speed2 = speed + step * (inverse[...] * (force[k] + dr2[k]) - (alive if k == 0 else 0.0))
        place2 = (place + step * speed2) * 0.0625
        for j in range(2):
            part[k, pl.ds(j, 16, stride=2), :] = place2[j * 16:(j + 1) * 16]
            part[2 + k, pl.ds(j, 16, stride=2), :] = speed2[j * 16:(j + 1) * 16]
    gas_step_update(gas, visc, gr, gc, dv, tot, rate, out)


CONTACT_SCRATCH = [
    pltpu.SMEM((128, 128), jnp.int32),
    pltpu.VMEM((128, 128), jnp.int32),
    pltpu.VMEM((128 * STRIDE, 128), F32),
    pltpu.VMEM((2, 1408, 128), F32),
    pltpu.VMEM((2, 64, 640), BF16),
    pltpu.VMEM((512, 128), F32),
]


def general(gas, visc, pos, vel, rad, coef, counts_t, pattern_t, idx, frac):

    def shapes(*dims):
        return [jax.ShapeDtypeStruct(d, F32) for d in dims]

    st, gp, mx = pl.pallas_call(
        prep_kernel,
        out_shape=shapes((8, 32, 128), (8, 32, 128), (8, 128)),
        in_specs=[VMEM_SPEC] * 5 + [SMEM_SPEC],
        out_specs=[VMEM_SPEC] * 3,
        name="prepare",
    )(gas, visc, pos, vel, rad, counts_t)
    ext, gv, rate, gr, gc = exchange(True, st, gp, mx, gas)
    st2, dp, tot, dr2, inverse = pl.pallas_call(
        first_kernel,
        out_shape=shapes((8, 32, 128), (8, 32, 128), (8, 128), (2, 32, 128), (32, 128)),
        in_specs=[VMEM_SPEC] * 6 + [SMEM_SPEC],
        out_specs=[VMEM_SPEC] * 5,
        scratch_shapes=CONTACT_SCRATCH + [pltpu.VMEM((2, 32, 128), F32), pltpu.SemaphoreType.DMA],
        name="first_substep",
    )(ext.reshape(1024, 128), gv, rate, idx, frac, coef, pattern_t)
    ext2, dv, total = exchange(False, st2, dp, tot)
    part, out = pl.pallas_call(
        second_kernel,
        out_shape=shapes((4, 32, 128), (2, 32, 256)),
        in_specs=[VMEM_SPEC] * 10 + [SMEM_SPEC],
        out_specs=[VMEM_SPEC] * 2,
        scratch_shapes=CONTACT_SCRATCH + [pltpu.SemaphoreType.DMA],
        name="second_substep",
    )(ext2.reshape(1024, 128), dv, total, rate, dr2, inverse, gas, visc, gr, gc, pattern_t)
    return part, out


EDGE_BASE, CORNER_BASE, WINDOW_ROWS = 48, 192, 256
CORNER = 16
WINDOWS = ((-1, 0), (1, 0), (0, -1), (0, 1), (-1, -1), (-1, 1), (1, -1), (1, 1))
NEAR = ((1.82, 0.0), (2.25, 0.43))
EDGE = 40
EARLY = 8


def fused_kernel(*refs):
    inputs, (part, out, flag, pat_copy, counts_copy), refs = refs[:10], refs[10:15], refs[15:]
    gas, visc, pos, vel, rad, coef, idx, frac, pat, counts = refs[:10]
    (in_sem, ext, ext2, gp, gv, dp, dv, gr, gc, mb, mv, sb, sv, rk, qs, qw, rhs, frc, itp, wts, wx, wz,
     hs, hr, ps, pr, rs, rr, es, er) = refs[10:]
    loads = [pltpu.make_async_copy(a, b, in_sem.at[n]) for n, (a, b) in enumerate(zip(inputs, refs[:10]))]
    for c in loads:
        c.start()
    ax, al, g = lax.axis_index("across"), lax.axis_index("along"), lax.axis_index("gas")

    def around(value, size):
        return value - jnp.where(value >= size, size, 0)

    up, down = around(al + 1, N_ALONG), around(al + N_ALONG - 1, N_ALONG)
    first_g, last_g = g == 0, g == N_GAS - 1
    has_left = jnp.logical_or(ax > 0, g > 0)
    has_right = jnp.logical_or(ax < N_ACROSS - 1, g < N_GAS - 1)
    left = (jnp.maximum(ax - jnp.where(first_g, 1, 0), 0), jnp.where(first_g, N_GAS - 1, g - 1))
    right = (jnp.minimum(ax + jnp.where(last_g, 1, 0), N_ACROSS - 1), jnp.where(last_g, 0, g + 1))

    def device(a=ax, l=al, y=g):
        return {"across": a, "along": l, "gas": y}

    def col(side, along):
        return device(a=side[0], l=along, y=side[1])

    def peer_id(axis, index):
        return device(**{{"across": "a", "along": "l", "gas": "y"}[axis]: index})

    after = device(l=jnp.where(last_g, up, al), y=jnp.where(last_g, 0, g + 1))
    before = device(l=jnp.where(first_g, down, al), y=jnp.where(first_g, N_GAS - 1, g - 1))

    barrier = pltpu.get_barrier_semaphore()

    def greet(target):
        pl.semaphore_signal(barrier, inc=1, device_id=target, device_id_type=MESH_ID)

    for k in range(1, N_ALONG):
        greet(device(l=around(al + k, N_ALONG)))
    for k in range(1, N_ACROSS):
        greet(device(a=around(ax + k, N_ACROSS)))
    for k in range(1, N_GAS):
        greet(device(y=around(g + k, N_GAS)))
    greet(after)
    greet(before)
    expect = N_ACROSS + N_GAS + N_ALONG - 3 + 2

    @pl.when(has_left)
    def _():
        for along in (down, al, up):
            greet(col(left, along))

    @pl.when(has_right)
    def _():
        for along in (down, al, up):
            greet(col(right, along))

    for c in loads:
        c.wait()
    rate = jnp.abs(gas[0]) + jnp.abs(gas[1]) + 4.0 * visc[...]
    top = jnp.max(jnp.max(rate, axis=1, keepdims=True), axis=0, keepdims=True)
    mv[0] = jnp.broadcast_to(top, (8, 128))
    lane = iota((16, 128), 1)
    for d in range(N_GAS):
        blk = slice((d // 4) * 128, (d // 4) * 128 + 128)
        off = (d % 4) * 32
        for k in range(2):
            low = gas[k, 0:16, blk]
            high = gas[k, 16:32, blk]
            low = pltpu.roll(low, (128 - off) % 128, 1) if off else low
            shift = (160 - off) % 128
            high = pltpu.roll(high, shift, 1) if shift else high
            piece = jnp.where(lane < 32, low, high)
            gp[d, k * 16:(k + 1) * 16, :] = jnp.where(lane < 64, piece, pltpu.roll(piece, 64, 1))
    row32 = iota((32, 128), 0)
    cnt = jnp.zeros((32, 128), jnp.int32)
    for j in range(2):
        for i in range(16):
            cnt = jnp.where(row32 == j * 16 + i, counts[j, i], cnt)
    ext[0, 0:32, :], ext[1, 0:32, :] = by_column(pos, 0) * 16.0, by_column(pos, 1) * 16.0
    ext[2, 0:32, :], ext[3, 0:32, :] = by_column(vel, 0), by_column(vel, 1)
    ext[4, 0:32, :] = jnp.where(iota((32, 128), 1) < cnt, by_column(rad), DEAD)

    def dots(e, low, high):
        e[5, low:high, :] = e[0, low:high, :] * e[2, low:high, :] + e[1, low:high, :] * e[3, low:high, :]

    dots(ext, 0, 32)
    for e in (ext, ext2):
        @pl.when(jnp.logical_not(has_left))
        def _():
            e[:, 32:48, :] = jnp.zeros((8, 16, 128), F32)
            e[:, 64:72, :] = jnp.zeros((8, 8, 128), F32)
            e[:, 96:104, :] = jnp.zeros((8, 8, 128), F32)

        @pl.when(jnp.logical_not(has_right))
        def _():
            e[:, 48:64, :] = jnp.zeros((8, 16, 128), F32)
            e[:, 88:96, :] = jnp.zeros((8, 8, 128), F32)
            e[:, 120:128, :] = jnp.zeros((8, 8, 128), F32)

    @pl.when(ax == 0)
    def _():
        gc[0] = jnp.zeros((2, 32, 128), F32)

    @pl.when(ax == N_ACROSS - 1)
    def _():
        gc[1] = jnp.zeros((2, 32, 128), F32)

    sides = jnp.where(has_left, 3, 0) + jnp.where(has_right, 3, 0)
    pl.semaphore_wait(barrier, expect + sides)

    def remote(src, dst, send, recv, target):
        return pltpu.make_async_remote_copy(
            src_ref=src, dst_ref=dst, send_sem=send, recv_sem=recv,
            device_id=target, device_id_type=MESH_ID,
        )

    axes = (("across", ax, N_ACROSS), ("gas", g, N_GAS), ("along", al, N_ALONG))

    def reduce_start(which, phase):
        slots, value = ((mb, mv), (sb, sv))[which]
        axis, me, size = axes[phase]
        out = [remote(value.at[phase], slots.at[phase, me], rs.at[which, phase, k], rr.at[which, phase, k],
                      peer_id(axis, around(me + k, size))) for k in range(1, size)]
        for c in out:
            c.start()
        slots[phase, me] = value[phase]
        return out

    def reduce_end(which, phase, copies):
        slots, value = ((mb, mv), (sb, sv))[which]
        size = axes[phase][2]
        for c in copies:
            c.wait_recv()
        total = slots[phase, 0]
        for k in range(1, size):
            total = total + slots[phase, k] if which else jnp.maximum(total, slots[phase, k])
        value[phase + 1] = total
        for c in copies:
            c.wait_send()

    def halo_start(which):
        e, attrs = ((ext, 5), (ext2, 5))[which]

        def halo(c, src_row, size, dst_row, target):
            return remote(e.at[pl.ds(0, attrs), pl.ds(src_row, size)],
                          e.at[pl.ds(0, attrs), pl.ds(dst_row, size)], hs.at[which, c], hr.at[which, c], target)

        lefts = [halo(0, 0, 16, 48, col(left, al)),
                 halo(1, 8, 8, 64 + 24, col(left, up)),
                 halo(2, 0, 8, 96 + 24, col(left, down))]
        rights = [halo(3, 16, 16, 32, col(right, al)),
                  halo(4, 24, 8, 64, col(right, up)),
                  halo(5, 16, 8, 96, col(right, down))]
        rows = [halo(6, 8, 8, 64 + 8, device(l=up)),
                halo(7, 24, 8, 64 + 16, device(l=up)),
                halo(8, 0, 8, 96 + 8, device(l=down)),
                halo(9, 16, 8, 96 + 16, device(l=down))]

        @pl.when(has_left)
        def _():
            for c in lefts:
                c.start()

        @pl.when(has_right)
        def _():
            for c in rights:
                c.start()

        for c in rows:
            c.start()
        return lefts, rights, rows

    def halo_end(copies):
        lefts, rights, rows = copies
        for c in rows:
            c.wait()

        @pl.when(has_left)
        def _():
            for c in lefts:
                c.wait_send()
            for c in rights:
                c.wait_recv()

        @pl.when(has_right)
        def _():
            for c in rights:
                c.wait_send()
            for c in lefts:
                c.wait_recv()

    def pieces_start(which):
        src, dst = ((gp, gv), (dp, dv))[which]
        out = []
        for k in range(1, N_GAS):
            peer = around(g + k, N_GAS)
            c = remote(src.at[peer], dst.at[g], ps.at[which, k], pr.at[which, k], device(y=peer))
            c.start()
            out.append(c)
        dst[g] = src[g]
        return out

    phase = reduce_start(0, 0)
    halos = halo_start(0)
    pieces = pieces_start(0)
    edges = [remote(gas.at[:, pl.ds(24, 8)], gr.at[0], es.at[0], er.at[0], after),
             remote(gas.at[:, pl.ds(0, 8)], gr.at[1], es.at[1], er.at[1], before)]
    for c in edges:
        c.start()
    to_right = remote(gas.at[:, :, pl.ds(128, 128)], gc.at[0], es.at[2], er.at[2],
                      device(a=jnp.minimum(ax + 1, N_ACROSS - 1)))
    to_left = remote(gas.at[:, :, pl.ds(0, 128)], gc.at[1], es.at[3], er.at[3],
                     device(a=jnp.maximum(ax - 1, 0)))

    @pl.when(ax < N_ACROSS - 1)
    def _():
        to_right.start()

    @pl.when(ax > 0)
    def _():
        to_left.start()

    lists = [pltpu.make_async_copy(pat, pat_copy, in_sem.at[10]), pltpu.make_async_copy(counts, counts_copy, in_sem.at[11])]
    for c in lists:
        c.start()

    slot_row = iota((48, 128), 0)
    slots = (jnp.where(slot_row < EDGE, slot_row, -5).astype(F32),
             jnp.where(slot_row < 32, slot_row, jnp.where(slot_row < 40, -5, slot_row - 8)).astype(F32))
    attr_row = iota((8, 128), 0)
    zero8 = jnp.zeros((8, 128), F32)
    one_tail = jnp.concatenate([zero8, jnp.ones((24, 128), F32)], axis=0)
    flat = (ext.reshape(1024, 128), ext2.reshape(1024, 128))
    eye = jnp.where(iota((128, 128), 0) == iota((128, 128), 1), 1.0, 0.0).astype(BF16)
    before_slot = jnp.where(iota((128, 128), 0) < iota((128, 128), 1), 1.0, 0.0).astype(BF16)

    def rank(which, low, high, windows=range(8)):
        e = (ext, ext2)[which]
        reach, _ = NEAR[which]
        z, x, live = e[0, low:high, :], e[1, low:high, :], e[4, low:high, :] > 0.0

        def flags(cond):
            return jnp.where(cond & live, 1.0, 0.0)

        lz, hz, lx, hx = flags(z < reach), flags(z > 16.0 - reach), flags(x < reach), flags(x > 16.0 - reach)
        member = [hz, lz, hx, lx, hz * hx, hz * lx, lz * hx, lz * lx]
        size = high - low
        places = jnp.dot(jnp.concatenate([member[w] for w in windows], axis=0).astype(BF16), before_slot,
                         preferred_element_type=F32)
        lost = jnp.zeros((size, 128), F32)
        for order, w in enumerate(windows):
            place = places[order * size:(order + 1) * size]
            rk[w, low:high, :] = jnp.where(member[w] > 0.0, place, -1.0)
            lost = lost + jnp.where(place >= (EDGE if w < 4 else CORNER), member[w], 0.0)
        return lost

    def parts(which, row):
        block = flat[which][pl.ds(row, 8, stride=128), :]
        return split3(jnp.where(attr_row < 6, block, 0.0))

    def stacked(hi, mid, lo, own=False):
        shifted = jnp.where(attr_row < 2, pltpu.roll(hi, 6, 0), jnp.where(attr_row < 4, mid, 0.0))
        return jnp.concatenate([hi, mid, lo, hi, mid, zero8 if own else shifted, one_tail], axis=0)

    def partner(v):
        return jnp.where(attr_row < 2, pltpu.roll(v, 6, 0), jnp.where(attr_row < 4, pltpu.roll(v, 2, 0), 0.0))

    def window_rows(which, row, rows, windows):
        sizes = [48 if w < 4 else CORNER for w in windows]
        place = jnp.concatenate(
            [(slots[w & 1 if w < 4 else 0][0:n] == rk[w, pl.ds(row, 1), :]).astype(F32) for w, n in zip(windows, sizes)], axis=0)
        turned = lax.dot_general(place.astype(BF16), rows, (((1,), (1,)), ((), ())), preferred_element_type=F32)
        turned = turned.astype(BF16)
        at = 0
        for w, n in zip(windows, sizes):
            start = row * WINDOW_ROWS + (w * EDGE_BASE if w < 4 else CORNER_BASE + (w - 4) * CORNER)
            if not isinstance(row, int):
                start = pl.multiple_of(start, 16)
            qw[pl.ds(start, n), 0:80] = turned[at:at + n]
            at += n

    def own_tiles(which):
        def some(step, carry):
            for u in range(8):
                row = step * 8 + u
                hi, mid, lo = parts(which, row)
                turned = stacked(hi, mid, lo, True).T
                rows = stacked(hi, mid, lo).astype(BF16)
                qs[pl.ds(pl.multiple_of(row * 128, 128), 128), 0:80] = turned.astype(BF16)
                window_rows(which, row, rows, range(8))
                with_hi, with_mid = 2.0 * partner(hi), 2.0 * partner(mid)
                own = jnp.where(attr_row == 5, -2.0, with_hi)
                marked = 16.0 * jnp.where(attr_row < 2, with_hi, jnp.where(attr_row < 4, pltpu.roll(with_mid, 2, 0), 0.0))
                columns = []
                for a, scale in ((0, 1.0), (1, 1.0), (5, -2.0), (4, 1.0)):
                    ends = [jnp.where(attr_row == a, v * scale, 0.0) for v in (hi, mid, lo)]
                    if a == 5:
                        start = [own, own, jnp.where(attr_row == 5, -2.0, 0.0), with_mid, with_mid,
                                 jnp.where(attr_row < 4, -32.0, 0.0), marked]
                    else:
                        one = jnp.where(attr_row == a, 1.0 if a == 4 else -1.0, 0.0)
                        start = [one, one, one, zero8, zero8, zero8,
                                 jnp.where(attr_row == a, DEAD if a == 4 else -16.0, 0.0)]
                    columns.append(jnp.concatenate(start + ends, axis=0))
                rhs[row] = jnp.concatenate(columns, axis=1).astype(BF16)
            return carry
        lax.fori_loop(0, 4, some, 0)

    def halo_tile(which, row, windows):
        hi, mid, lo = parts(which, row)
        window_rows(which, row, stacked(hi, mid, lo).astype(BF16), windows)

    def halo_tiles(which, beside=None):
        dots((ext, ext2)[which], 32, 128)
        rank(which, 32, 48, (2, 4, 6))
        rank(which, 48, 64, (3, 5, 7))
        rank(which, 64, 96, (0, 4, 5))
        rank(which, 96, 128, (1, 6, 7))

        def some(step, carry):
            if beside is not None:
                beside(step)
            for u in range(4):
                halo_tile(which, 32 + step * 4 + u, (2, 4, 6))
                halo_tile(which, 48 + step * 4 + u, (3, 5, 7))
            return carry
        lax.fori_loop(0, 4, some, 0)
        for c in range(4):
            halo_tile(which, 64 + 8 * c + 7, (0, 4, 5))
            halo_tile(which, 96 + 8 * c, (1, 6, 7))

    lane16 = iota((16, 128), 1)
    half = iota((16, 128), 0) < 8

    lost = rank(0, 0, 32)
    own_tiles(0)

    unlisted = jnp.where(lane16 == 52, 1.0, 0.0)

    def by_offset(low, di, dj, rest):
        lane = lane16 - low
        inside = (lane >= 0) & (lane < 4)
        return jnp.where(inside, jnp.where((lane & 1) == 0, float(di), float(dj)), rest)

    def contact_rows(first, last, own_part=True, border_part=True):

        def step(four, carry):
            for u, j in ((0, 0), (0, 1), (1, 0), (1, 1), (2, 0), (2, 1), (3, 0), (3, 1)):
                i = four * 4 + u
                t = j * 16 + i
                right = rhs[t]

                def mark_of(n):
                    di, dj = OFFSETS[n]
                    base = by_offset(48, di, dj, 0.0)
                    return base + unlisted * (1 - pat[n, j, i]).astype(F32)

                def times(di, dj):
                    return by_offset(40, di, dj, 1.0).astype(BF16)

                def border(w):
                    di, dj = WINDOWS[w]
                    row = ext_row(i + di, j + dj)
                    n = 48 if w < 4 else CORNER
                    start = row * WINDOW_ROWS + (w * EDGE_BASE if w < 4 else CORNER_BASE + (w - 4) * CORNER)
                    block, factor = qw[pl.ds(pl.multiple_of(start, 16), n), :], times(di, dj)
                    return [block[c:c + 16] * factor for c in range(0, n, 16)], mark_of(3 * (di + 1) + dj + 1)

                def edges_of(w):
                    (one, mark1), (two, mark2) = border(w), border(w + 1)
                    both = one[2] + two[2] + jnp.where(half, mark1, mark2).astype(BF16)
                    mark1, mark2 = mark1.astype(BF16), mark2.astype(BF16)
                    return [one[0] + mark1, one[1] + mark1, two[0] + mark2, two[1] + mark2, both]

                def corner(w):
                    (block,), here = border(w)
                    return block + here.astype(BF16)

                groups = []
                if own_part:
                    own = qs[pl.ds(pl.multiple_of(t * 128, 128), 128), :]
                    here = mark_of(4).astype(BF16)
                    groups += [own[c:c + 16] + here for c in range(0, 128, 16)]
                if border_part:
                    groups += edges_of(0) + edges_of(2) + [corner(w) for w in range(4, 8)]
                got = jnp.dot(jnp.concatenate(groups, axis=0)[:, 0:80], right, preferred_element_type=F32)
                rz, rx = got[:, 0:128], got[:, 128:256]
                inv = lax.rsqrt(rz * rz + rx * rx + 0.0001)
                push = jnp.maximum(got[:, 384:512] * inv - 1.0, 0.0) * (40.0 + got[:, 256:384] * inv)
                count = got.shape[0] // 8
                fz = jnp.sum((push * rz).reshape(count, 8, 128), axis=0)
                fx = jnp.sum((push * rx).reshape(count, 8, 128), axis=0)
                at_z, at_x = pl.ds(pl.multiple_of(t * 8, 8), 8), pl.ds(pl.multiple_of(t * 8 + 256, 8), 8)
                if not own_part:
                    fz, fx = fz + frc[at_z, :], fx + frc[at_x, :]
                frc[at_z, :], frc[at_x, :] = fz, fx
            return carry
        lax.fori_loop(first // 4, last // 4, step, 0)

    def forces():
        return [sum(frc[pl.ds(k * 256 + r, 32, stride=8), :] for r in range(8)) for k in range(2)]

    phase_end = reduce_end
    index = idx[...]
    share_z = frac[0].astype(F32) / 1024.0
    share_x = frac[1].astype(F32) / 1024.0
    wts[0] = (index >> 4).astype(F32)
    wts[1] = (index & 15).astype(F32)
    wts[2], wts[3] = 1.0 - share_z, share_z
    for n, share in ((4, 1.0 - share_x), (6, share_x)):
        high = share.astype(BF16).astype(F32)
        wts[n], wts[n + 1] = high, share - high
    c64 = iota((64, 128), 0).astype(F32)
    r16 = iota((16, 128), 0).astype(F32)

    def weigh(r, t4, t):
        def get(n):
            return wts[n, pl.ds(r, 1), :]
        column, row = get(1) + (16.0 * t4), get(0)
        here, there = c64 == column, c64 == column + 1.0
        wx[t, 0:64, :] = jnp.where(here, get(4), jnp.where(there, get(6), 0.0)).astype(BF16)
        wx[t, 64:128, :] = jnp.where(here, get(5), jnp.where(there, get(7), 0.0)).astype(BF16)
        wz[t] = jnp.where(r16 == row, get(2), jnp.where(r16 == row + 1.0, get(3), 0.0))

    def some_weights(h, carry):
        for t in range(2):
            for j in range(2):
                weigh(4 * h + 2 * t + j, t * 2 + j, 4 * h + 2 * t + j)
        return carry

    lax.fori_loop(0, 8, some_weights, 0)
    contact_rows(0, EARLY, True, False)

    for c in pieces:
        c.wait()
    lane32 = iota((32, 128), 1)

    def sample(h):
        field = gv[h]
        high = field.astype(BF16).astype(F32)
        both = jnp.where(lane32 < 64, high, field - high).astype(BF16)
        for t in range(2):
            for j in range(2):
                r = 4 * h + 2 * t + j
                whi, wlo = wx[r, 0:64, :], wx[r, 64:128, :]
                right = jnp.concatenate([jnp.concatenate([whi, whi], axis=0),
                                         jnp.concatenate([wlo, wlo], axis=0)], axis=1)
                got = jnp.dot(both, right, preferred_element_type=F32)
                got = got[:, 0:128] + got[:, 128:256]
                for k in range(2):
                    itp[k, pl.ds(j * 16 + 2 * h + t, 1), :] = jnp.sum(
                        wz[r] * got[k * 16:(k + 1) * 16], axis=0, keepdims=True)

    def two_samples(step):
        sample(2 * step)
        sample(2 * step + 1)

    phase_end(0, 0, phase)
    phase = reduce_start(0, 1)
    halo_end(halos)
    halo_tiles(0, two_samples)

    contact_rows(0, EARLY, False, True)
    phase_end(0, 1, phase)
    phase = reduce_start(0, 2)
    contact_rows(EARLY, 16)
    phase_end(0, 2, phase)
    step = 0.2 / mv[3][0:1, :]
    drag = by_column(coef)
    radius = ext[4, 0:32, :]
    alive = jnp.where(radius > 0.0, 1.0, 0.0)
    inverse = jnp.where(radius > 0.0, 0.36 / (radius * radius), 0.0)
    force = forces()
    drags = []
    slack = NEAR[1][1]
    for k in range(2):
        speed = ext[2 + k, 0:32, :]
        drag1 = drag * (itp[k] - speed)
        speed2 = speed + step * (inverse * (force[k] + drag1) - (alive if k == 0 else 0.0))
        place2 = ext[k, 0:32, :] + step * speed2
        ext2[k, 0:32, :] = place2
        inside = (place2 >= -slack) & (place2 <= 16.0 + slack)
        lost = lost + jnp.where(inside, 0.0, alive)
        ext2[2 + k, 0:32, :] = speed2
        drag2 = drag * (itp[k] - speed2)
        drags.append((drag1, drag2))
    ext2[4, 0:32, :] = radius
    dots(ext2, 0, 32)
    halos = halo_start(1)
    bad = lost + rank(1, 0, 32)
    sums = []
    for k in range(2):
        drag1, drag2 = drags[k]
        mean = 0.5 * (alive * drag1 + alive * drag2)
        itp[k] = mean
        itp[2 + k] = drag2
        sums.append(jnp.sum(jnp.sum(mean, axis=1, keepdims=True), axis=0, keepdims=True))
    bad = jnp.sum(jnp.sum(bad, axis=1, keepdims=True), axis=0, keepdims=True)
    sv[0] = jnp.where(attr_row == 0, sums[0], jnp.where(attr_row == 1, sums[1], bad))
    phase = reduce_start(1, 0)

    def spread(h):
        total = jnp.zeros((64, 128), F32)
        for t in range(2):
            for j in range(2):
                r = 4 * h + 2 * t + j
                m0 = itp[0, pl.ds(j * 16 + 2 * h + t, 1), :]
                m1 = itp[1, pl.ds(j * 16 + 2 * h + t, 1), :]
                lhs = jnp.concatenate([wz[r] * m0, wz[r] * m1], axis=0)
                high = lhs.astype(BF16)
                low = (lhs - high.astype(F32)).astype(BF16)
                total = total + lax.dot_general(
                    jnp.concatenate([high, low], axis=0), wx[r],
                    (((1,), (1,)), ((), ())), preferred_element_type=F32)
        total = total[0:32] + total[32:64]
        dp[h] = total + pltpu.roll(total, 64, 1)

    lax.fori_loop(0, 8, lambda h, carry: (spread(h), carry)[1], 0)
    pieces = pieces_start(1)
    own_tiles(1)
    phase_end(1, 0, phase)
    phase = reduce_start(1, 1)
    halo_end(halos)
    halo_tiles(1)

    contact_rows(0, 4)
    phase_end(1, 1, phase)
    phase = reduce_start(1, 2)
    contact_rows(4, 16)
    force = forces()
    for k in range(2):
        speed = ext2[2 + k, 0:32, :]
        speed2 = speed + step * (inverse * (force[k] + itp[2 + k]) - (alive if k == 0 else 0.0))
        place2 = (ext2[k, 0:32, :] + step * speed2) * 0.0625
        for j in range(2):
            part[k, pl.ds(j, 16, stride=2), :] = place2[j * 16:(j + 1) * 16]
            part[2 + k, pl.ds(j, 16, stride=2), :] = speed2[j * 16:(j + 1) * 16]
    for c in edges + lists:
        c.wait()

    @pl.when(ax < N_ACROSS - 1)
    def _():
        to_right.wait_send()
        to_left.wait_recv()

    @pl.when(ax > 0)
    def _():
        to_left.wait_send()
        to_right.wait_recv()

    for c in pieces:
        c.wait()
    phase_end(1, 2, phase)
    flag[...] = sv[3][2:3, 0:1]
    gas_step_update(gas, visc, gr, gc, dv, sv.at[3], mv.at[3], out)


def fused(gas, visc, pos, vel, rad, coef, counts_t, pattern_t, idx, frac):
    dma = pltpu.SemaphoreType.DMA
    return pl.pallas_call(
        fused_kernel,
        out_shape=[jax.ShapeDtypeStruct((4, 32, 128), F32), jax.ShapeDtypeStruct((2, 32, 256), F32),
                   jax.ShapeDtypeStruct((1, 1), F32), jax.ShapeDtypeStruct((9, 2, 16), jnp.int32),
                   jax.ShapeDtypeStruct((2, 16), jnp.int32)],
        in_specs=[pl.BlockSpec(memory_space=pltpu.HBM)] * 10,
        out_specs=[VMEM_SPEC] * 3 + [pl.BlockSpec(memory_space=pltpu.HBM)] * 2,
        scratch_shapes=[
            pltpu.VMEM((2, 32, 256), F32), pltpu.VMEM((32, 256), F32),
            pltpu.VMEM((2, 32, 128), F32), pltpu.VMEM((2, 32, 128), F32), pltpu.VMEM((32, 128), F32),
            pltpu.VMEM((32, 128), F32), pltpu.VMEM((32, 128), jnp.int32), pltpu.VMEM((2, 32, 128), jnp.int32),
            pltpu.SMEM((9, 2, 16), jnp.int32), pltpu.SMEM((2, 16), jnp.int32), dma((12,)),
            pltpu.VMEM((8, 128, 128), F32), pltpu.VMEM((8, 128, 128), F32),
            pltpu.VMEM((8, 32, 128), F32), pltpu.VMEM((8, 32, 128), F32),
            pltpu.VMEM((8, 32, 128), F32), pltpu.VMEM((8, 32, 128), F32),
            pltpu.VMEM((2, 2, 8, 256), F32), pltpu.VMEM((2, 2, 32, 128), F32),
            pltpu.VMEM((3, 8, 8, 128), F32), pltpu.VMEM((4, 8, 128), F32),
            pltpu.VMEM((3, 8, 8, 128), F32), pltpu.VMEM((4, 8, 128), F32),
            pltpu.VMEM((8, 128, 128), F32), pltpu.VMEM((32 * 128, 128), BF16),
            pltpu.VMEM((128 * WINDOW_ROWS, 128), BF16), pltpu.VMEM((32, 80, 512), BF16),
            pltpu.VMEM((512, 128), F32), pltpu.VMEM((4, 32, 128), F32), pltpu.VMEM((8, 32, 128), F32),
            pltpu.VMEM((32, 128, 128), BF16), pltpu.VMEM((32, 16, 128), F32),
            dma((2, 10)), dma((2, 10)), dma((2, 8)), dma((2, 8)), dma((2, 3, 8)), dma((2, 3, 8)),
            dma((4,)), dma((4,)),
        ],
        compiler_params=pltpu.CompilerParams(collective_id=2, has_side_effects=True),
        name="interval",
    )(gas, visc, pos, vel, rad, coef, idx, frac, pattern_t, counts_t)


def body(gas, visc, pos, vel, rad, coef, counts, pattern, idx, frac):
    pos, vel, frac = (x.reshape(2, 32, 128) for x in (pos, vel, frac))
    rad, coef, idx = (x.reshape(32, 128) for x in (rad, coef, idx))
    args = (gas, visc, pos, vel, rad, coef, counts.T, pattern.transpose(2, 1, 0), idx, frac)
    part, out, flag, pattern_t, counts_t = fused(*args)
    args = args[:6] + (counts_t, pattern_t) + args[8:]
    part, out = lax.cond(flag[0, 0] > 0.0, lambda p, o: tuple(general(*args)), lambda p, o: (p, o), part, out)
    return part.reshape(4, 16, 2, 128), out


def solution(mesh):
    return jax.shard_map(
        body,
        mesh=mesh,
        in_specs=(
            P(None, ALONG_GAS, "across"),
            P(ALONG_GAS, "across"),
            P(None, "along", ACROSS_GAS, None),
            P(None, "along", ACROSS_GAS, None),
            P("along", ACROSS_GAS, None),
            P("along", ACROSS_GAS, None),
            P("along", ACROSS_GAS),
            P("along", ACROSS_GAS, None),
            P("along", ACROSS_GAS, None),
            P(None, "along", ACROSS_GAS, None),
        ),
        out_specs=(P(None, "along", ACROSS_GAS, None), P(None, ALONG_GAS, "across")),
        check_vma=False,
    )
```

```python
import functools

import jax
import jax.numpy as jnp
from jax import lax
from jax.experimental import pallas as pl
from jax.experimental.pallas import tpu as pltpu
from jax.sharding import PartitionSpec as P

ALONG_GAS = ("along", "gas")
ACROSS_GAS = ("across", "gas")
MESH_ID = pl.DeviceIdType.MESH
OFFSETS = [(-1, -1), (-1, 0), (-1, 1), (0, -1), (0, 0), (0, 1), (1, -1), (1, 0), (1, 1)]
DEAD = -16384.0
F32 = jnp.float32
BF16 = jnp.bfloat16
STRIDE = 136
BLOCK, BLOCK_BITS = 64, 6
EMPTY = 1344
REACH = 2.4
MOVE_LIMIT = int((REACH - 1.9) * 4096)
VMEM_SPEC = pl.BlockSpec(memory_space=pltpu.VMEM)
SMEM_SPEC = pl.BlockSpec(memory_space=pltpu.SMEM)
N_ACROSS, N_ALONG, N_GAS = 4, 8, 8


def iota(shape, dim):
    return lax.broadcasted_iota(jnp.int32, shape, dim)


def ext_row(ii, jj):
    base = {-1: 32, 0: 0, 1: 16, 2: 48}[jj]
    return jnp.where(ii < 0, 64 + 8 * (jj + 1) + 7, jnp.where(ii > 15, 96 + 8 * (jj + 1), base + ii))


def by_column(ref, *lead):
    return jnp.concatenate([ref[(*lead, pl.ds(0, 16, stride=2), slice(None))],
                            ref[(*lead, pl.ds(1, 16, stride=2), slice(None))]], axis=0)


def prepare_state(st, pos, vel, rad, counts):
    row32 = iota((32, 128), 0)
    slot = iota((32, 128), 1)
    cnt = jnp.zeros((32, 128), jnp.int32)
    for j in range(2):
        for i in range(16):
            cnt = jnp.where(row32 == j * 16 + i, counts[j, i], cnt)
    alive = slot < cnt
    z, x = by_column(pos, 0) * 16.0, by_column(pos, 1) * 16.0
    st[0, 0:32, :], st[1, 0:32, :] = z, x
    st[2, 0:32, :], st[3, 0:32, :] = by_column(vel, 0), by_column(vel, 1)
    st[4, 0:32, :] = jnp.where(alive, by_column(rad), DEAD)
    low_x, high_x = x < REACH, x > 16.0 - REACH

    def three(low, mid, high):
        return jnp.where(low_x, low, jnp.where(high_x, high, mid))

    kind = jnp.where(z < REACH, three(0, 1, 2), jnp.where(z > 16.0 - REACH, three(6, 5, 4), three(7, 8, 3)))
    kind = jnp.where(alive, kind, 9)
    member = jnp.concatenate([jnp.where(kind == c, 1.0, 0.0) for c in range(9)], axis=0).astype(BF16)
    before = jnp.where((iota((128, 256), 0) < iota((128, 256), 1)) | (iota((128, 256), 1) >= 128), 1.0, 0.0)
    ranks = jnp.dot(member, before.astype(BF16), preferred_element_type=F32)
    rank = jnp.full((32, 128), -1.0, F32)
    start = [jnp.zeros((32, 128), F32)]
    for c in range(9):
        here = ranks[c * 32:(c + 1) * 32]
        rank = jnp.where(kind == c, start[c] + here[:, 0:128], rank)
        start.append(start[c] + here[:, 128:256])
    st[5, 0:32, :] = rank
    start = [v.astype(jnp.int32) for v in start]
    wrap = ((start[1] + 7) & -8) > start[6]
    zero = jnp.zeros((32, 128), jnp.int32)
    windows = [(start[4], start[5]), (start[4], start[7]), (start[6], start[7]), (start[2], start[5]),
               (zero, start[9]), (jnp.where(wrap, 0, start[6]), start[8]), (start[2], start[3]),
               (zero, start[3]), (zero, start[1]), (zero, jnp.where(wrap, 0, start[1]))]
    table = zero
    for w, (low, high) in enumerate(windows):
        table = jnp.where(slot == 2 * w, low, jnp.where(slot == 2 * w + 1, (high - low + 7) & -8, table))
    st[6, 0:32, :] = table.astype(F32)


def prep_kernel(gas, visc, pos, vel, rad, counts, st, gp, mx):
    rate = jnp.abs(gas[0]) + jnp.abs(gas[1]) + 4.0 * visc[...]
    top = jnp.max(jnp.max(rate, axis=1, keepdims=True), axis=0, keepdims=True)
    mx[...] = jnp.broadcast_to(top, (8, 128))
    lane = iota((16, 128), 1)
    for g in range(N_GAS):
        blk = slice((g // 4) * 128, (g // 4) * 128 + 128)
        off = (g % 4) * 32
        for k in range(2):
            low = gas[k, 0:16, blk]
            high = gas[k, 16:32, blk]
            low = pltpu.roll(low, (128 - off) % 128, 1) if off else low
            shift = (160 - off) % 128
            high = pltpu.roll(high, shift, 1) if shift else high
            piece = jnp.where(lane < 32, low, jnp.where(lane < 64, high, 0.0))
            gp[g, k * 16:(k + 1) * 16, :] = piece
    prepare_state(st, pos, vel, rad, counts)
    st[7] = jnp.zeros((32, 128), F32)


def comm_kernel(first, *refs):
    if first:
        (st, pc, mx, gas, ext, pv, red, gr, gc, mb, m1, m2,
         own_sem, hs, hr, ps, pr, rs, rr, es, er) = refs
    else:
        (st, pc, mx, ext, pv, red, mb, m1, m2,
         own_sem, hs, hr, ps, pr, rs, rr) = refs
    ax, al, g = lax.axis_index("across"), lax.axis_index("along"), lax.axis_index("gas")
    up, down = lax.rem(al + 1, N_ALONG), lax.rem(al + N_ALONG - 1, N_ALONG)
    lin = ax * N_GAS + g
    has_left, has_right = lin > 0, lin < N_ACROSS * N_GAS - 1
    left = jnp.maximum(lin - 1, 0)
    right = jnp.minimum(lin + 1, N_ACROSS * N_GAS - 1)

    def col(index, along):
        return {"across": lax.div(index, N_GAS), "along": along, "gas": lax.rem(index, N_GAS)}

    slab = al * N_GAS + g
    slabs = N_ALONG * N_GAS
    after, before = lax.rem(slab + 1, slabs), lax.rem(slab + slabs - 1, slabs)

    def slab_id(index):
        return {"across": ax, "along": lax.div(index, N_GAS), "gas": lax.rem(index, N_GAS)}

    barrier = pltpu.get_barrier_semaphore()

    def greet(device):
        pl.semaphore_signal(barrier, inc=1, device_id=device, device_id_type=MESH_ID)

    for k in range(1, N_ACROSS):
        greet({"across": lax.rem(ax + k, N_ACROSS)})
    for k in range(1, N_GAS):
        greet({"gas": lax.rem(g + k, N_GAS)})
    for k in range(1, N_ALONG):
        greet({"along": lax.rem(al + k, N_ALONG)})
    expect = N_ACROSS + N_GAS + N_ALONG - 3
    if first:
        greet(slab_id(after))
        greet(slab_id(before))
        expect += 2

    @pl.when(has_left)
    def _():
        for along in (down, al, up):
            greet(col(left, along))

    @pl.when(has_right)
    def _():
        for along in (down, al, up):
            greet(col(right, along))

    own = pltpu.make_async_copy(st, ext.at[:, pl.ds(0, 32)], own_sem.at[0])
    own.start()
    own_piece = pltpu.make_async_copy(pc.at[g], pv.at[g], own_sem.at[1])
    own_piece.start()

    @pl.when(jnp.logical_not(has_left))
    def _():
        ext[:, 32:48, :] = jnp.zeros((8, 16, 128), F32)
        ext[:, 64:72, :] = jnp.zeros((8, 8, 128), F32)
        ext[:, 96:104, :] = jnp.zeros((8, 8, 128), F32)

    @pl.when(jnp.logical_not(has_right))
    def _():
        ext[:, 48:64, :] = jnp.zeros((8, 16, 128), F32)
        ext[:, 88:96, :] = jnp.zeros((8, 8, 128), F32)
        ext[:, 120:128, :] = jnp.zeros((8, 8, 128), F32)

    if first:
        @pl.when(ax == 0)
        def _():
            gc[0] = jnp.zeros((2, 32, 128), F32)

        @pl.when(ax == N_ACROSS - 1)
        def _():
            gc[1] = jnp.zeros((2, 32, 128), F32)

    sides = jnp.where(has_left, 3, 0) + jnp.where(has_right, 3, 0)
    pl.semaphore_wait(barrier, expect + sides)

    def remote(src, dst, send, recv, device):
        return pltpu.make_async_remote_copy(
            src_ref=src, dst_ref=dst, send_sem=send, recv_sem=recv,
            device_id=device, device_id_type=MESH_ID,
        )

    def reduce_sends(phase, src, axis, me, size):
        out = []
        for k in range(1, size):
            out.append(remote(src, mb.at[phase, me], rs.at[phase, k], rr.at[phase, k],
                              {axis: lax.rem(me + k, size)}))
        for c in out:
            c.start()
        return out

    phase0 = reduce_sends(0, mx, "across", ax, N_ACROSS)

    def halo(c, src_rows, size, dst_row, device):
        return remote(st.at[pl.ds(0, 7), pl.ds(src_rows, size)],
                      ext.at[pl.ds(0, 7), pl.ds(dst_row, size)], hs.at[c], hr.at[c], device)

    lefts = [halo(0, 0, 16, 48, col(left, al)),
             halo(1, 8, 8, 64 + 24, col(left, up)),
             halo(2, 0, 8, 96 + 24, col(left, down))]
    rights = [halo(3, 16, 16, 32, col(right, al)),
              halo(4, 24, 8, 64, col(right, up)),
              halo(5, 16, 8, 96, col(right, down))]
    rows = [halo(6, 8, 8, 64 + 8, {"along": up}),
            halo(7, 24, 8, 64 + 16, {"along": up}),
            halo(8, 0, 8, 96 + 8, {"along": down}),
            halo(9, 16, 8, 96 + 16, {"along": down})]

    @pl.when(has_left)
    def _():
        for c in lefts:
            c.start()

    @pl.when(has_right)
    def _():
        for c in rights:
            c.start()

    for c in rows:
        c.start()
    pieces = []
    for k in range(1, N_GAS):
        peer = lax.rem(g + k, N_GAS)
        c = remote(pc.at[peer], pv.at[g], ps.at[k], pr.at[k], {"gas": peer})
        c.start()
        pieces.append(c)
    if first:
        edges = [remote(gas.at[:, pl.ds(24, 8)], gr.at[0], es.at[0], er.at[0], slab_id(after)),
                 remote(gas.at[:, pl.ds(0, 8)], gr.at[1], es.at[1], er.at[1], slab_id(before))]
        for c in edges:
            c.start()
        to_right = remote(gas.at[:, :, pl.ds(128, 128)], gc.at[0], es.at[2], er.at[2],
                          {"across": jnp.minimum(ax + 1, N_ACROSS - 1)})
        to_left = remote(gas.at[:, :, pl.ds(0, 128)], gc.at[1], es.at[3], er.at[3],
                         {"across": jnp.maximum(ax - 1, 0)})

        @pl.when(ax < N_ACROSS - 1)
        def _():
            to_right.start()

        @pl.when(ax > 0)
        def _():
            to_left.start()

    def combine(phase, mine, me, size, copies):
        for c in copies:
            c.wait_recv()
        mb[phase, me] = mine
        total = mb[phase, 0]
        for k in range(1, size):
            total = jnp.maximum(total, mb[phase, k]) if first else total + mb[phase, k]
        return total

    m1[...] = combine(0, mx[...], ax, N_ACROSS, phase0)
    phase1 = reduce_sends(1, m1, "gas", g, N_GAS)
    m2[...] = combine(1, m1[...], g, N_GAS, phase1)
    phase2 = reduce_sends(2, m2, "along", al, N_ALONG)
    red[...] = combine(2, m2[...], al, N_ALONG, phase2)

    own.wait()
    own_piece.wait()
    for c in phase0 + phase1 + phase2:
        c.wait_send()
    for c in rows + pieces:
        c.wait()

    @pl.when(has_left)
    def _():
        for c in lefts:
            c.wait_send()
        for c in rights:
            c.wait_recv()

    @pl.when(has_right)
    def _():
        for c in rights:
            c.wait_send()
        for c in lefts:
            c.wait_recv()

    if first:
        for c in edges:
            c.wait()

        @pl.when(ax < N_ACROSS - 1)
        def _():
            to_right.wait_send()
            to_left.wait_recv()

        @pl.when(ax > 0)
        def _():
            to_left.wait_send()
            to_right.wait_recv()


def exchange(first, st, pc, mx, gas=None):
    out_shape = [jax.ShapeDtypeStruct((8, 128, 128), F32),
                 jax.ShapeDtypeStruct((8, 32, 128), F32),
                 jax.ShapeDtypeStruct((8, 128), F32)]
    scratch = [pltpu.VMEM((3, 8, 8, 128), F32), pltpu.VMEM((8, 128), F32), pltpu.VMEM((8, 128), F32),
               pltpu.SemaphoreType.DMA((2,)),
               pltpu.SemaphoreType.DMA((10,)), pltpu.SemaphoreType.DMA((10,)),
               pltpu.SemaphoreType.DMA((8,)), pltpu.SemaphoreType.DMA((8,)),
               pltpu.SemaphoreType.DMA((3, 8)), pltpu.SemaphoreType.DMA((3, 8))]
    args = [st, pc, mx]
    if first:
        args.append(gas)
        out_shape += [jax.ShapeDtypeStruct((2, 2, 8, 256), F32), jax.ShapeDtypeStruct((2, 2, 32, 128), F32)]
        scratch += [pltpu.SemaphoreType.DMA((4,)), pltpu.SemaphoreType.DMA((4,))]
    return pl.pallas_call(
        functools.partial(comm_kernel, first),
        out_shape=out_shape,
        in_specs=[VMEM_SPEC] * len(args),
        out_specs=[VMEM_SPEC] * len(out_shape),
        scratch_shapes=scratch,
        compiler_params=pltpu.CompilerParams(collective_id=0 if first else 1, has_side_effects=True),
        name="exchange_first" if first else "exchange_second",
    )(*args)


def split3(x):
    hi = x.astype(BF16).astype(F32)
    rest = x - hi
    mid = rest.astype(BF16).astype(F32)
    return hi, mid, rest - mid


def contact_forces(ext, pat, meta, ints, qt, lst, rhs, frc, sem):
    ints[...] = ext[6 * 128:7 * 128, :].astype(jnp.int32)
    to_smem = pltpu.make_async_copy(ints, meta, sem)
    to_smem.start()
    slot = iota((128, 128), 0).astype(F32)
    attr_row = iota((8, 128), 0)
    zero8 = jnp.zeros((8, 128), F32)
    tail = jnp.concatenate([zero8, jnp.ones((24, 128), F32), zero8], axis=0)

    def parts(row):
        block = ext[pl.ds(row, 8, stride=128), :]
        return split3(jnp.where(attr_row < 5, block, 0.0))

    def transposed(row):
        hi, mid, lo = parts(row)
        rows = jnp.concatenate([hi, mid, lo, tail], axis=0).astype(BF16)
        place = (slot == ext[pl.ds(row + 5 * 128, 1), :]).astype(F32).astype(BF16)
        turned = lax.dot_general(place, rows, (((1,), (1,)), ((), ())), preferred_element_type=F32)
        start = row * STRIDE if isinstance(row, int) else pl.multiple_of(row * STRIDE, 8)
        qt[pl.ds(start, 128), 0:64] = turned
        start = start + 128 if isinstance(row, int) else pl.multiple_of(start + 128, 8)
        qt[pl.ds(start, 8), :] = zero8

    def some(step, carry):
        for u in range(4):
            transposed(step * 4 + u)
        return carry

    lax.fori_loop(0, 16, some, 0)
    for c in range(4):
        transposed(64 + 8 * c + 7)
        transposed(96 + 8 * c)

    block_of = iota((32, 640), 1) >> 7
    row_of = iota((32, 640), 0)
    attr_of = row_of & 7
    own_scale = jnp.where(block_of < 2, -1.0, jnp.where(block_of < 4, 2.0, 1.0))
    const = jnp.where((attr_of == block_of) & (row_of < 24), own_scale, 0.0)
    const = jnp.where((row_of == 24) & (block_of == 0) | (row_of == 25) & (block_of == 1), -16.0, const)
    for u in range(2):
        rhs[u, 0:32, :] = const.astype(BF16)
        lst[u, EMPTY:EMPTY + BLOCK, :] = jnp.zeros((BLOCK, 128), F32)
    to_smem.wait()
    lane = iota((8, 128), 1)

    def row_step(i, carry):
        blocks = []
        for j in range(2):
            work = lst.at[j]
            mine = j * 16 + i
            hi, mid, lo = parts(mine)
            columns = []
            for a in range(5):
                keep = attr_row == a
                scale = 1.0 if a in (0, 1, 4) else -2.0
                columns.append(jnp.concatenate(
                    [jnp.where(keep, hi * scale, 0.0), jnp.where(keep, mid * scale, 0.0),
                     jnp.where(keep, lo * scale, 0.0), zero8], axis=0))
            rhs[j, 32:64, :] = jnp.concatenate(columns, axis=1).astype(BF16)
            moved = meta[mine, 20]
            off = i * 0
            over = i * 0
            windows = []
            for w in (4, 0, 1, 2, 3, 5, 6, 7, 8, 9):
                di, dj = OFFSETS[5 if w == 9 else w]
                row = ext_row(i + di, j + dj)
                first, size = meta[row, 2 * w], meta[row, 2 * w + 1]
                if w != 4:
                    near = moved + meta[row, 20] <= MOVE_LIMIT
                    first = jnp.where(near, first, 0)
                    size = jnp.where(near, size, 0 if w == 9 else meta[row, 9])
                size = size * pat[5 if w == 9 else w, j, i]
                mark = jnp.where(lane == 24, float(di), jnp.where(lane == 25, float(dj), 0.0))
                start = row * STRIDE + first
                chunks = 16 if w == 4 else 4 if w in (1, 3, 5, 7) else 1
                for c in range(chunks):
                    work[pl.ds(pl.multiple_of(off + c * 8, 8), 8), :] = qt[pl.ds(start + c * 8, 8), :] + mark
                windows.append((start, size, mark))
                off = off + size
                over = jnp.maximum(over, size - chunks * 8)

            @pl.when(over > 0)
            def _():
                to = i * 0
                for start, size, mark in windows:
                    def copy(c, carry, start=start, mark=mark, to=to):
                        work[pl.ds(pl.multiple_of(to + c * 8, 8), 8), :] = qt[pl.ds(start + c * 8, 8), :] + mark
                        return carry
                    lax.fori_loop(0, size >> 3, copy, 0)
                    to = to + size

            for c in range(BLOCK // 8):
                work[pl.ds(pl.multiple_of(off + c * 8, 8), 8), :] = zero8
            blocks.append((off + BLOCK - 1) >> BLOCK_BITS)
        right = [rhs[0], rhs[1]]

        def block(b, acc):
            out = []
            for j in range(2):
                at = jnp.where(b < blocks[j], b * BLOCK, EMPTY)
                q = lst[j, pl.ds(pl.multiple_of(at, 8), BLOCK), 0:64].astype(BF16)
                got = jnp.dot(q, right[j], preferred_element_type=F32)
                rz, rx = got[:, 0:128], got[:, 128:256]
                dz, dx = got[:, 256:384], got[:, 384:512]
                d2 = rz * rz + rx * rx + 0.0001
                inv = lax.rsqrt(d2)
                depth = jnp.maximum(got[:, 512:640] - d2 * inv, 0.0)
                push = depth * inv * (40.0 + (dz * rz + dx * rx) * inv)
                out.append(acc[2 * j] + jnp.sum((push * rz).reshape(BLOCK // 8, 8, 128), axis=0))
                out.append(acc[2 * j + 1] + jnp.sum((push * rx).reshape(BLOCK // 8, 8, 128), axis=0))
            return tuple(out)

        acc = lax.fori_loop(0, jnp.maximum(blocks[0], blocks[1]), block, (zero8,) * 4)
        for j in range(2):
            for k in range(2):
                frc[pl.ds(pl.multiple_of(((k * 2 + j) * 16 + i) * 8, 8), 8), :] = acc[2 * j + k]
        return carry

    lax.fori_loop(0, 16, row_step, 0)
    return [sum(frc[pl.ds(k * 256 + r, 32, stride=8), :] for r in range(8)) for k in range(2)]


def first_kernel(ext, gv, rate, idx, frac, coef, pat, st2, dp, tot, dr2, inv_out,
                 meta, ints, qt, lst, rhs, frc, itp, sem):
    def weights(r, t4):
        index = idx[pl.ds(r, 1), :]
        row, column = index >> 4, index & 15
        share_z = frac[0, pl.ds(r, 1), :].astype(F32) / 1024.0
        share_x = frac[1, pl.ds(r, 1), :].astype(F32) / 1024.0
        c64 = iota((64, 128), 0) - t4 * 16
        wx = jnp.where(c64 == column, 1.0 - share_x, jnp.where(c64 == column + 1, share_x, 0.0))
        r16 = iota((16, 128), 0)
        wz = jnp.where(r16 == row, 1.0 - share_z, jnp.where(r16 == row + 1, share_z, 0.0))
        return wz, wx

    def sample(h, carry):
        field = gv[h][:, 0:64]
        for t in range(2):
            for j in range(2):
                wz, wx = weights(4 * h + 2 * t + j, t * 2 + j)
                along = jnp.dot(field, wx, precision=lax.Precision.HIGHEST, preferred_element_type=F32)
                for k in range(2):
                    itp[k, pl.ds(j * 16 + 2 * h + t, 1), :] = jnp.sum(
                        wz * along[k * 16:(k + 1) * 16], axis=0, keepdims=True)
        return carry

    lax.fori_loop(0, 8, sample, 0)
    force = contact_forces(ext, pat, meta, ints, qt, lst, rhs, frc, sem)
    step = 0.2 / rate[0:1, :]
    drag = by_column(coef)
    radius = ext[4 * 128:4 * 128 + 32, :]
    alive = jnp.where(radius > 0.0, 1.0, 0.0)
    inverse = jnp.where(radius > 0.0, 0.36 / (radius * radius), 0.0)
    inv_out[...] = inverse
    means = []
    moved = jnp.zeros((32, 128), F32)
    for k in range(2):
        place = ext[k * 128:k * 128 + 32, :]
        speed = ext[(2 + k) * 128:(2 + k) * 128 + 32, :]
        drag1 = drag * (itp[k] - speed)
        speed2 = speed + step * (inverse * (force[k] + drag1) - (alive if k == 0 else 0.0))
        st2[k] = place + step * speed2
        moved = jnp.maximum(moved, alive * jnp.abs(step * speed2))
        st2[2 + k] = speed2
        drag2 = drag * (itp[k] - speed2)
        dr2[k] = drag2
        mean = 0.5 * (alive * drag1 + alive * drag2)
        itp[k] = mean
        means.append(jnp.sum(jnp.sum(mean, axis=1, keepdims=True), axis=0, keepdims=True))
    st2[4] = radius
    st2[5] = ext[5 * 128:5 * 128 + 32, :]
    far = jnp.max(moved, axis=1, keepdims=True)
    far = jnp.where(far < 100.0, far, 100.0) * 4096.0 + 1.0
    st2[6] = jnp.where(iota((32, 128), 1) == 20, far, ext[6 * 128:6 * 128 + 32, :])
    st2[7] = jnp.zeros((32, 128), F32)
    tot[...] = jnp.where(iota((8, 128), 0) == 0, means[0], means[1])

    def spread(h, carry):
        total = jnp.zeros((32, 64), F32)
        for t in range(2):
            for j in range(2):
                wz, wx = weights(4 * h + 2 * t + j, t * 2 + j)
                m0 = itp[0, pl.ds(j * 16 + 2 * h + t, 1), :]
                m1 = itp[1, pl.ds(j * 16 + 2 * h + t, 1), :]
                lhs = jnp.concatenate([wz * m0, wz * m1], axis=0)
                total = total + lax.dot_general(lhs, wx, (((1,), (1,)), ((), ())),
                                                precision=lax.Precision.HIGHEST, preferred_element_type=F32)
        dp[h, :, 0:64] = total
        dp[h, :, 64:128] = jnp.zeros((32, 64), F32)
        return carry

    lax.fori_loop(0, 8, spread, 0)


def gas_step_update(gas, visc, gr, gc, dv, tot, rate, out):
    gas_step = 0.4 / rate[0:1, 0:1]
    lane = iota((32, 256), 1)
    row = iota((32, 256), 0)
    lane16 = iota((16, 128), 1) >> 5
    for k in range(2):
        u = gas[k]
        upper = jnp.where(row == 31, gr[1, k, 0:1, :], pltpu.roll(u, 31, 0))
        lower = jnp.where(row == 0, gr[0, k, 7:8, :], pltpu.roll(u, 1, 0))
        right = jnp.where(lane == 255, gc[1, k, :, 0:1], pltpu.roll(u, 255, 1))
        left = jnp.where(lane == 0, gc[0, k, :, 127:128], pltpu.roll(u, 1, 1))
        laplace = upper + lower + right + left - 4.0 * u
        advect = gas[0] * (upper - lower) * 0.5 + gas[1] * (right - left) * 0.5
        quads = []
        for t in range(2):
            halves = []
            for b in range(2):
                whole = None
                for q in range(4):
                    piece = dv[4 * b + q, k * 16:(k + 1) * 16, :]
                    shift = (q * 32 - t * 32) % 128
                    piece = pltpu.roll(piece, shift, 1) if shift else piece
                    whole = piece if whole is None else jnp.where(lane16 == q, piece, whole)
                halves.append(whole)
            quads.append(jnp.concatenate(halves, axis=1))
        deposit = jnp.concatenate(quads, axis=0)
        source = tot[k:k + 1, 0:1] / 2097152.0 - deposit
        out[k] = u + gas_step * (visc[...] * laplace - advect + source)


def second_kernel(ext, dv, tot, rate, dr2, inverse, gas, visc, gr, gc, pat, part, out,
                  meta, ints, qt, lst, rhs, frc, sem):
    force = contact_forces(ext, pat, meta, ints, qt, lst, rhs, frc, sem)
    step = 0.2 / rate[0:1, :]
    radius = ext[4 * 128:4 * 128 + 32, :]
    alive = jnp.where(radius > 0.0, 1.0, 0.0)
    for k in range(2):
        place = ext[k * 128:k * 128 + 32, :]
        speed = ext[(2 + k) * 128:(2 + k) * 128 + 32, :]
        speed2 = speed + step * (inverse[...] * (force[k] + dr2[k]) - (alive if k == 0 else 0.0))
        place2 = (place + step * speed2) * 0.0625
        for j in range(2):
            part[k, pl.ds(j, 16, stride=2), :] = place2[j * 16:(j + 1) * 16]
            part[2 + k, pl.ds(j, 16, stride=2), :] = speed2[j * 16:(j + 1) * 16]
    gas_step_update(gas, visc, gr, gc, dv, tot, rate, out)


CONTACT_SCRATCH = [
    pltpu.SMEM((128, 128), jnp.int32),
    pltpu.VMEM((128, 128), jnp.int32),
    pltpu.VMEM((128 * STRIDE, 128), F32),
    pltpu.VMEM((2, 1408, 128), F32),
    pltpu.VMEM((2, 64, 640), BF16),
    pltpu.VMEM((512, 128), F32),
]


def general(gas, visc, pos, vel, rad, coef, counts_t, pattern_t, idx, frac):

    def shapes(*dims):
        return [jax.ShapeDtypeStruct(d, F32) for d in dims]

    st, gp, mx = pl.pallas_call(
        prep_kernel,
        out_shape=shapes((8, 32, 128), (8, 32, 128), (8, 128)),
        in_specs=[VMEM_SPEC] * 5 + [SMEM_SPEC],
        out_specs=[VMEM_SPEC] * 3,
        name="prepare",
    )(gas, visc, pos, vel, rad, counts_t)
    ext, gv, rate, gr, gc = exchange(True, st, gp, mx, gas)
    st2, dp, tot, dr2, inverse = pl.pallas_call(
        first_kernel,
        out_shape=shapes((8, 32, 128), (8, 32, 128), (8, 128), (2, 32, 128), (32, 128)),
        in_specs=[VMEM_SPEC] * 6 + [SMEM_SPEC],
        out_specs=[VMEM_SPEC] * 5,
        scratch_shapes=CONTACT_SCRATCH + [pltpu.VMEM((2, 32, 128), F32), pltpu.SemaphoreType.DMA],
        name="first_substep",
    )(ext.reshape(1024, 128), gv, rate, idx, frac, coef, pattern_t)
    ext2, dv, total = exchange(False, st2, dp, tot)
    part, out = pl.pallas_call(
        second_kernel,
        out_shape=shapes((4, 32, 128), (2, 32, 256)),
        in_specs=[VMEM_SPEC] * 10 + [SMEM_SPEC],
        out_specs=[VMEM_SPEC] * 2,
        scratch_shapes=CONTACT_SCRATCH + [pltpu.SemaphoreType.DMA],
        name="second_substep",
    )(ext2.reshape(1024, 128), dv, total, rate, dr2, inverse, gas, visc, gr, gc, pattern_t)
    return part, out


EDGE_BASE, CORNER_BASE, WINDOW_ROWS = 48, 192, 256
CORNER = 16
WINDOWS = ((-1, 0), (1, 0), (0, -1), (0, 1), (-1, -1), (-1, 1), (1, -1), (1, 1))
NEAR = ((1.82, 0.0), (2.25, 0.43))
EDGE = 40
EARLY = 8


def fused_kernel(*refs):
    inputs, (part, out, flag, pat_copy, counts_copy), refs = refs[:10], refs[10:15], refs[15:]
    gas, visc, pos, vel, rad, coef, idx, frac, pat, counts = refs[:10]
    (in_sem, ext, ext2, gp, gv, dp, dv, gr, gc, mb, mv, sb, sv, rk, qs, qw, rhs, frc, itp, wts, wx, wz,
     hs, hr, ps, pr, rs, rr, es, er) = refs[10:]
    loads = [pltpu.make_async_copy(a, b, in_sem.at[n]) for n, (a, b) in enumerate(zip(inputs, refs[:10]))]
    for c in loads:
        c.start()
    ax, al, g = lax.axis_index("across"), lax.axis_index("along"), lax.axis_index("gas")

    def around(value, size):
        return value - jnp.where(value >= size, size, 0)

    up, down = around(al + 1, N_ALONG), around(al + N_ALONG - 1, N_ALONG)
    first_g, last_g = g == 0, g == N_GAS - 1
    has_left = jnp.logical_or(ax > 0, g > 0)
    has_right = jnp.logical_or(ax < N_ACROSS - 1, g < N_GAS - 1)
    left = (jnp.maximum(ax - jnp.where(first_g, 1, 0), 0), jnp.where(first_g, N_GAS - 1, g - 1))
    right = (jnp.minimum(ax + jnp.where(last_g, 1, 0), N_ACROSS - 1), jnp.where(last_g, 0, g + 1))

    def device(a=ax, l=al, y=g):
        return {"across": a, "along": l, "gas": y}

    def col(side, along):
        return device(a=side[0], l=along, y=side[1])

    def peer_id(axis, index):
        return device(**{{"across": "a", "along": "l", "gas": "y"}[axis]: index})

    after = device(l=jnp.where(last_g, up, al), y=jnp.where(last_g, 0, g + 1))
    before = device(l=jnp.where(first_g, down, al), y=jnp.where(first_g, N_GAS - 1, g - 1))

    barrier = pltpu.get_barrier_semaphore()

    def greet(target):
        pl.semaphore_signal(barrier, inc=1, device_id=target, device_id_type=MESH_ID)

    for k in range(1, N_ALONG):
        greet(device(l=around(al + k, N_ALONG)))
    for k in range(1, N_ACROSS):
        greet(device(a=around(ax + k, N_ACROSS)))
    for k in range(1, N_GAS):
        greet(device(y=around(g + k, N_GAS)))
    greet(after)
    greet(before)
    expect = N_ACROSS + N_GAS + N_ALONG - 3 + 2

    @pl.when(has_left)
    def _():
        for along in (down, al, up):
            greet(col(left, along))

    @pl.when(has_right)
    def _():
        for along in (down, al, up):
            greet(col(right, along))

    for c in loads:
        c.wait()
    rate = jnp.abs(gas[0]) + jnp.abs(gas[1]) + 4.0 * visc[...]
    top = jnp.max(jnp.max(rate, axis=1, keepdims=True), axis=0, keepdims=True)
    mv[0] = jnp.broadcast_to(top, (8, 128))
    lane = iota((16, 128), 1)
    for d in range(N_GAS):
        blk = slice((d // 4) * 128, (d // 4) * 128 + 128)
        off = (d % 4) * 32
        for k in range(2):
            low = gas[k, 0:16, blk]
            high = gas[k, 16:32, blk]
            low = pltpu.roll(low, (128 - off) % 128, 1) if off else low
            shift = (160 - off) % 128
            high = pltpu.roll(high, shift, 1) if shift else high
            piece = jnp.where(lane < 32, low, high)
            gp[d, k * 16:(k + 1) * 16, :] = jnp.where(lane < 64, piece, pltpu.roll(piece, 64, 1))
    row32 = iota((32, 128), 0)
    cnt = jnp.zeros((32, 128), jnp.int32)
    for j in range(2):
        for i in range(16):
            cnt = jnp.where(row32 == j * 16 + i, counts[j, i], cnt)
    ext[0, 0:32, :], ext[1, 0:32, :] = by_column(pos, 0) * 16.0, by_column(pos, 1) * 16.0
    ext[2, 0:32, :], ext[3, 0:32, :] = by_column(vel, 0), by_column(vel, 1)
    ext[4, 0:32, :] = jnp.where(iota((32, 128), 1) < cnt, by_column(rad), DEAD)

    def dots(e, low, high):
        e[5, low:high, :] = e[0, low:high, :] * e[2, low:high, :] + e[1, low:high, :] * e[3, low:high, :]

    dots(ext, 0, 32)
    for e in (ext, ext2):
        @pl.when(jnp.logical_not(has_left))
        def _():
            e[:, 32:48, :] = jnp.zeros((8, 16, 128), F32)
            e[:, 64:72, :] = jnp.zeros((8, 8, 128), F32)
            e[:, 96:104, :] = jnp.zeros((8, 8, 128), F32)

        @pl.when(jnp.logical_not(has_right))
        def _():
            e[:, 48:64, :] = jnp.zeros((8, 16, 128), F32)
            e[:, 88:96, :] = jnp.zeros((8, 8, 128), F32)
            e[:, 120:128, :] = jnp.zeros((8, 8, 128), F32)

    @pl.when(ax == 0)
    def _():
        gc[0] = jnp.zeros((2, 32, 128), F32)

    @pl.when(ax == N_ACROSS - 1)
    def _():
        gc[1] = jnp.zeros((2, 32, 128), F32)

    sides = jnp.where(has_left, 3, 0) + jnp.where(has_right, 3, 0)
    pl.semaphore_wait(barrier, expect + sides)

    def remote(src, dst, send, recv, target):
        return pltpu.make_async_remote_copy(
            src_ref=src, dst_ref=dst, send_sem=send, recv_sem=recv,
            device_id=target, device_id_type=MESH_ID,
        )

    axes = (("across", ax, N_ACROSS), ("gas", g, N_GAS), ("along", al, N_ALONG))

    def reduce_copies(which, phase):
        slots, value = ((mb, mv), (sb, sv))[which]
        axis, me, size = axes[phase]
        return [remote(value.at[phase], slots.at[phase, me], rs.at[which, phase, k], rr.at[which, phase, k],
                       peer_id(axis, around(me + k, size))) for k in range(1, size)]

    def reduce_go(which, phase, copies):
        slots, value = ((mb, mv), (sb, sv))[which]
        for c in copies:
            c.start()
        slots[phase, axes[phase][1]] = value[phase]

    def reduce_start(which, phase):
        out = reduce_copies(which, phase)
        reduce_go(which, phase, out)
        return out

    def reduce_end(which, phase, copies):
        slots, value = ((mb, mv), (sb, sv))[which]
        size = axes[phase][2]
        for c in copies:
            c.wait_recv()
        total = slots[phase, 0]
        for k in range(1, size):
            total = total + slots[phase, k] if which else jnp.maximum(total, slots[phase, k])
        value[phase + 1] = total
        for c in copies:
            c.wait_send()

    def halo_start(which):
        e, attrs = ((ext, 5), (ext2, 5))[which]

        def halo(c, src_row, size, dst_row, target):
            return remote(e.at[pl.ds(0, attrs), pl.ds(src_row, size)],
                          e.at[pl.ds(0, attrs), pl.ds(dst_row, size)], hs.at[which, c], hr.at[which, c], target)

        lefts = [halo(0, 0, 16, 48, col(left, al)),
                 halo(1, 8, 8, 64 + 24, col(left, up)),
                 halo(2, 0, 8, 96 + 24, col(left, down))]
        rights = [halo(3, 16, 16, 32, col(right, al)),
                  halo(4, 24, 8, 64, col(right, up)),
                  halo(5, 16, 8, 96, col(right, down))]
        rows = [halo(6, 8, 8, 64 + 8, device(l=up)),
                halo(7, 24, 8, 64 + 16, device(l=up)),
                halo(8, 0, 8, 96 + 8, device(l=down)),
                halo(9, 16, 8, 96 + 16, device(l=down))]

        @pl.when(has_left)
        def _():
            for c in lefts:
                c.start()

        @pl.when(has_right)
        def _():
            for c in rights:
                c.start()

        for c in rows:
            c.start()
        return lefts, rights, rows

    def halo_end(copies):
        lefts, rights, rows = copies
        for c in rows:
            c.wait()

        @pl.when(has_left)
        def _():
            for c in lefts:
                c.wait_send()
            for c in rights:
                c.wait_recv()

        @pl.when(has_right)
        def _():
            for c in rights:
                c.wait_send()
            for c in lefts:
                c.wait_recv()

    def pieces_start(which):
        src, dst = ((gp, gv), (dp, dv))[which]
        out = []
        for k in range(1, N_GAS):
            peer = around(g + k, N_GAS)
            c = remote(src.at[peer], dst.at[g], ps.at[which, k], pr.at[which, k], device(y=peer))
            c.start()
            out.append(c)
        dst[g] = src[g]
        return out

    phase = reduce_start(0, 0)
    halos = halo_start(0)
    pieces = pieces_start(0)
    edges = [remote(gas.at[:, pl.ds(24, 8)], gr.at[0], es.at[0], er.at[0], after),
             remote(gas.at[:, pl.ds(0, 8)], gr.at[1], es.at[1], er.at[1], before)]
    for c in edges:
        c.start()
    to_right = remote(gas.at[:, :, pl.ds(128, 128)], gc.at[0], es.at[2], er.at[2],
                      device(a=jnp.minimum(ax + 1, N_ACROSS - 1)))
    to_left = remote(gas.at[:, :, pl.ds(0, 128)], gc.at[1], es.at[3], er.at[3],
                     device(a=jnp.maximum(ax - 1, 0)))

    @pl.when(ax < N_ACROSS - 1)
    def _():
        to_right.start()

    @pl.when(ax > 0)
    def _():
        to_left.start()

    lists = [pltpu.make_async_copy(pat, pat_copy, in_sem.at[10]), pltpu.make_async_copy(counts, counts_copy, in_sem.at[11])]
    for c in lists:
        c.start()

    slot_row = iota((48, 128), 0)
    slots = (jnp.where(slot_row < EDGE, slot_row, -5).astype(F32),
             jnp.where(slot_row < 32, slot_row, jnp.where(slot_row < 40, -5, slot_row - 8)).astype(F32))
    attr_row = iota((8, 128), 0)
    zero8 = jnp.zeros((8, 128), F32)
    one_tail = jnp.concatenate([zero8, jnp.ones((24, 128), F32)], axis=0)
    flat = (ext.reshape(1024, 128), ext2.reshape(1024, 128))
    eye = jnp.where(iota((128, 128), 0) == iota((128, 128), 1), 1.0, 0.0).astype(BF16)
    before_slot = jnp.where(iota((128, 128), 0) < iota((128, 128), 1), 1.0, 0.0).astype(BF16)

    def rank(which, low, high, windows=range(8)):
        e = (ext, ext2)[which]
        reach, _ = NEAR[which]
        z, x, live = e[0, low:high, :], e[1, low:high, :], e[4, low:high, :] > 0.0

        def flags(cond):
            return jnp.where(cond & live, 1.0, 0.0)

        lz, hz, lx, hx = flags(z < reach), flags(z > 16.0 - reach), flags(x < reach), flags(x > 16.0 - reach)
        member = [hz, lz, hx, lx, hz * hx, hz * lx, lz * hx, lz * lx]
        size = high - low
        places = jnp.dot(jnp.concatenate([member[w] for w in windows], axis=0).astype(BF16), before_slot,
                         preferred_element_type=F32)
        lost = jnp.zeros((size, 128), F32)
        for order, w in enumerate(windows):
            place = places[order * size:(order + 1) * size]
            rk[w, low:high, :] = jnp.where(member[w] > 0.0, place, -1.0)
            lost = lost + jnp.where(place >= (EDGE if w < 4 else CORNER), member[w], 0.0)
        return lost

    def parts(which, row):
        block = flat[which][pl.ds(row, 8, stride=128), :]
        return split3(jnp.where(attr_row < 6, block, 0.0))

    def stacked(hi, mid, lo, own=False):
        shifted = jnp.where(attr_row < 2, pltpu.roll(hi, 6, 0), jnp.where(attr_row < 4, mid, 0.0))
        return jnp.concatenate([hi, mid, lo, hi, mid, zero8 if own else shifted, one_tail], axis=0)

    def partner(v):
        return jnp.where(attr_row < 2, pltpu.roll(v, 6, 0), jnp.where(attr_row < 4, pltpu.roll(v, 2, 0), 0.0))

    def window_rows(which, row, rows, windows):
        sizes = [48 if w < 4 else CORNER for w in windows]
        place = jnp.concatenate(
            [(slots[w & 1 if w < 4 else 0][0:n] == rk[w, pl.ds(row, 1), :]).astype(F32) for w, n in zip(windows, sizes)], axis=0)
        turned = lax.dot_general(place.astype(BF16), rows, (((1,), (1,)), ((), ())), preferred_element_type=F32)
        turned = turned.astype(BF16)
        at = 0
        for w, n in zip(windows, sizes):
            start = row * WINDOW_ROWS + (w * EDGE_BASE if w < 4 else CORNER_BASE + (w - 4) * CORNER)
            if not isinstance(row, int):
                start = pl.multiple_of(start, 16)
            qw[pl.ds(start, n), 0:80] = turned[at:at + n]
            at += n

    def own_tiles(which):
        def some(step, carry):
            for u in range(8):
                row = step * 8 + u
                hi, mid, lo = parts(which, row)
                turned = stacked(hi, mid, lo, True).T
                rows = stacked(hi, mid, lo).astype(BF16)
                qs[pl.ds(pl.multiple_of(row * 128, 128), 128), 0:80] = turned.astype(BF16)
                window_rows(which, row, rows, range(8))
                with_hi, with_mid = 2.0 * partner(hi), 2.0 * partner(mid)
                own = jnp.where(attr_row == 5, -2.0, with_hi)
                marked = 16.0 * jnp.where(attr_row < 2, with_hi, jnp.where(attr_row < 4, pltpu.roll(with_mid, 2, 0), 0.0))
                columns = []
                for a, scale in ((0, 1.0), (1, 1.0), (5, -2.0), (4, 1.0)):
                    ends = [jnp.where(attr_row == a, v * scale, 0.0) for v in (hi, mid, lo)]
                    if a == 5:
                        start = [own, own, jnp.where(attr_row == 5, -2.0, 0.0), with_mid, with_mid,
                                 jnp.where(attr_row < 4, -32.0, 0.0), marked]
                    else:
                        one = jnp.where(attr_row == a, 1.0 if a == 4 else -1.0, 0.0)
                        start = [one, one, one, zero8, zero8, zero8,
                                 jnp.where(attr_row == a, DEAD if a == 4 else -16.0, 0.0)]
                    columns.append(jnp.concatenate(start + ends, axis=0))
                rhs[row] = jnp.concatenate(columns, axis=1).astype(BF16)
            return carry
        lax.fori_loop(0, 4, some, 0)

    def halo_tile(which, row, windows):
        hi, mid, lo = parts(which, row)
        window_rows(which, row, stacked(hi, mid, lo).astype(BF16), windows)

    def halo_tiles(which, beside=None):
        dots((ext, ext2)[which], 32, 128)
        rank(which, 32, 48, (2, 4, 6))
        rank(which, 48, 64, (3, 5, 7))
        rank(which, 64, 96, (0, 4, 5))
        rank(which, 96, 128, (1, 6, 7))

        def some(step, carry):
            if beside is not None:
                beside(step)
            for u in range(4):
                halo_tile(which, 32 + step * 4 + u, (2, 4, 6))
                halo_tile(which, 48 + step * 4 + u, (3, 5, 7))
            return carry
        lax.fori_loop(0, 4, some, 0)
        for c in range(4):
            halo_tile(which, 64 + 8 * c + 7, (0, 4, 5))
            halo_tile(which, 96 + 8 * c, (1, 6, 7))

    lane16 = iota((16, 128), 1)
    half = iota((16, 128), 0) < 8

    lost = rank(0, 0, 32)
    own_tiles(0)

    unlisted = jnp.where(lane16 == 52, 1.0, 0.0)

    def by_offset(low, di, dj, rest):
        lane = lane16 - low
        inside = (lane >= 0) & (lane < 4)
        return jnp.where(inside, jnp.where((lane & 1) == 0, float(di), float(dj)), rest)

    def contact_rows(first, last, own_part=True, border_part=True, ahead=None):

        def step(four, carry):
            if ahead is not None:
                pl.when(four == 1)(ahead)
            for u, j in ((0, 0), (0, 1), (1, 0), (1, 1), (2, 0), (2, 1), (3, 0), (3, 1)):
                i = four * 4 + u
                t = j * 16 + i
                right = rhs[t]

                def mark_of(n):
                    di, dj = OFFSETS[n]
                    base = by_offset(48, di, dj, 0.0)
                    return base + unlisted * (1 - pat[n, j, i]).astype(F32)

                def times(di, dj):
                    return by_offset(40, di, dj, 1.0).astype(BF16)

                def border(w):
                    di, dj = WINDOWS[w]
                    row = ext_row(i + di, j + dj)
                    n = 48 if w < 4 else CORNER
                    start = row * WINDOW_ROWS + (w * EDGE_BASE if w < 4 else CORNER_BASE + (w - 4) * CORNER)
                    block, factor = qw[pl.ds(pl.multiple_of(start, 16), n), :], times(di, dj)
                    return [block[c:c + 16] * factor for c in range(0, n, 16)], mark_of(3 * (di + 1) + dj + 1)

                def edges_of(w):
                    (one, mark1), (two, mark2) = border(w), border(w + 1)
                    both = one[2] + two[2] + jnp.where(half, mark1, mark2).astype(BF16)
                    mark1, mark2 = mark1.astype(BF16), mark2.astype(BF16)
                    return [one[0] + mark1, one[1] + mark1, two[0] + mark2, two[1] + mark2, both]

                def corner(w):
                    (block,), here = border(w)
                    return block + here.astype(BF16)

                groups = []
                if own_part:
                    own = qs[pl.ds(pl.multiple_of(t * 128, 128), 128), :]
                    here = mark_of(4).astype(BF16)
                    groups += [own[c:c + 16] + here for c in range(0, 128, 16)]
                if border_part:
                    groups += edges_of(0) + edges_of(2) + [corner(w) for w in range(4, 8)]
                got = jnp.dot(jnp.concatenate(groups, axis=0)[:, 0:80], right, preferred_element_type=F32)
                rz, rx = got[:, 0:128], got[:, 128:256]
                inv = lax.rsqrt(rz * rz + rx * rx + 0.0001)
                push = jnp.maximum(got[:, 384:512] * inv - 1.0, 0.0) * (40.0 + got[:, 256:384] * inv)
                count = got.shape[0] // 8
                fz = jnp.sum((push * rz).reshape(count, 8, 128), axis=0)
                fx = jnp.sum((push * rx).reshape(count, 8, 128), axis=0)
                at_z, at_x = pl.ds(pl.multiple_of(t * 8, 8), 8), pl.ds(pl.multiple_of(t * 8 + 256, 8), 8)
                if not own_part:
                    fz, fx = fz + frc[at_z, :], fx + frc[at_x, :]
                frc[at_z, :], frc[at_x, :] = fz, fx
            return carry
        lax.fori_loop(first // 4, last // 4, step, 0)

    def forces():
        return [sum(frc[pl.ds(k * 256 + r, 32, stride=8), :] for r in range(8)) for k in range(2)]

    phase_end = reduce_end
    index = idx[...]
    share_z = frac[0].astype(F32) / 1024.0
    share_x = frac[1].astype(F32) / 1024.0
    wts[0] = (index >> 4).astype(F32)
    wts[1] = (index & 15).astype(F32)
    wts[2], wts[3] = 1.0 - share_z, share_z
    for n, share in ((4, 1.0 - share_x), (6, share_x)):
        high = share.astype(BF16).astype(F32)
        wts[n], wts[n + 1] = high, share - high
    c64 = iota((64, 128), 0).astype(F32)
    r16 = iota((16, 128), 0).astype(F32)

    def weigh(r, t4, t):
        def get(n):
            return wts[n, pl.ds(r, 1), :]
        column, row = get(1) + (16.0 * t4), get(0)
        here, there = c64 == column, c64 == column + 1.0
        wx[t, 0:64, :] = jnp.where(here, get(4), jnp.where(there, get(6), 0.0)).astype(BF16)
        wx[t, 64:128, :] = jnp.where(here, get(5), jnp.where(there, get(7), 0.0)).astype(BF16)
        wz[t] = jnp.where(r16 == row, get(2), jnp.where(r16 == row + 1.0, get(3), 0.0))

    def some_weights(h, carry):
        for t in range(2):
            for j in range(2):
                weigh(4 * h + 2 * t + j, t * 2 + j, 4 * h + 2 * t + j)
        return carry

    lax.fori_loop(0, 8, some_weights, 0)
    contact_rows(0, EARLY, True, False)

    for c in pieces:
        c.wait()
    lane32 = iota((32, 128), 1)

    def sample(h):
        field = gv[h]
        high = field.astype(BF16).astype(F32)
        both = jnp.where(lane32 < 64, high, field - high).astype(BF16)
        for t in range(2):
            for j in range(2):
                r = 4 * h + 2 * t + j
                whi, wlo = wx[r, 0:64, :], wx[r, 64:128, :]
                right = jnp.concatenate([jnp.concatenate([whi, whi], axis=0),
                                         jnp.concatenate([wlo, wlo], axis=0)], axis=1)
                got = jnp.dot(both, right, preferred_element_type=F32)
                got = got[:, 0:128] + got[:, 128:256]
                for k in range(2):
                    itp[k, pl.ds(j * 16 + 2 * h + t, 1), :] = jnp.sum(
                        wz[r] * got[k * 16:(k + 1) * 16], axis=0, keepdims=True)

    def two_samples(step):
        sample(2 * step)
        sample(2 * step + 1)

    phase_end(0, 0, phase)
    max_phase = reduce_start(0, 1)
    halo_end(halos)
    halo_tiles(0, two_samples)

    last_phase = reduce_copies(0, 2)

    def pass_maximum():
        phase_end(0, 1, max_phase)
        reduce_go(0, 2, last_phase)

    contact_rows(0, EARLY, False, True, pass_maximum)
    contact_rows(EARLY, 16)
    phase_end(0, 2, last_phase)
    step = 0.2 / mv[3][0:1, :]
    drag = by_column(coef)
    radius = ext[4, 0:32, :]
    alive = jnp.where(radius > 0.0, 1.0, 0.0)
    inverse = jnp.where(radius > 0.0, 0.36 / (radius * radius), 0.0)
    force = forces()
    drags = []
    slack = NEAR[1][1]
    for k in range(2):
        speed = ext[2 + k, 0:32, :]
        drag1 = drag * (itp[k] - speed)
        speed2 = speed + step * (inverse * (force[k] + drag1) - (alive if k == 0 else 0.0))
        place2 = ext[k, 0:32, :] + step * speed2
        ext2[k, 0:32, :] = place2
        inside = (place2 >= -slack) & (place2 <= 16.0 + slack)
        lost = lost + jnp.where(inside, 0.0, alive)
        ext2[2 + k, 0:32, :] = speed2
        drag2 = drag * (itp[k] - speed2)
        drags.append((drag1, drag2))
    ext2[4, 0:32, :] = radius
    dots(ext2, 0, 32)
    halos = halo_start(1)
    bad = lost + rank(1, 0, 32)
    sums = []
    for k in range(2):
        drag1, drag2 = drags[k]
        mean = 0.5 * (alive * drag1 + alive * drag2)
        itp[k] = mean
        itp[2 + k] = drag2
        sums.append(jnp.sum(jnp.sum(mean, axis=1, keepdims=True), axis=0, keepdims=True))
    bad = jnp.sum(jnp.sum(bad, axis=1, keepdims=True), axis=0, keepdims=True)
    sv[0] = jnp.where(attr_row == 0, sums[0], jnp.where(attr_row == 1, sums[1], bad))
    phase = reduce_start(1, 0)

    def spread(h):
        total = jnp.zeros((64, 128), F32)
        for t in range(2):
            for j in range(2):
                r = 4 * h + 2 * t + j
                m0 = itp[0, pl.ds(j * 16 + 2 * h + t, 1), :]
                m1 = itp[1, pl.ds(j * 16 + 2 * h + t, 1), :]
                lhs = jnp.concatenate([wz[r] * m0, wz[r] * m1], axis=0)
                high = lhs.astype(BF16)
                low = (lhs - high.astype(F32)).astype(BF16)
                total = total + lax.dot_general(
                    jnp.concatenate([high, low], axis=0), wx[r],
                    (((1,), (1,)), ((), ())), preferred_element_type=F32)
        total = total[0:32] + total[32:64]
        dp[h] = total + pltpu.roll(total, 64, 1)

    lax.fori_loop(0, 8, lambda h, carry: (spread(h), carry)[1], 0)
    pieces = pieces_start(1)
    own_tiles(1)
    phase_end(1, 0, phase)
    sum_phase = reduce_start(1, 1)
    halo_end(halos)
    halo_tiles(1)

    last_sum = reduce_copies(1, 2)

    def pass_sum():
        phase_end(1, 1, sum_phase)
        reduce_go(1, 2, last_sum)

    contact_rows(0, 16, ahead=pass_sum)
    force = forces()
    step = 0.2 / mv[3][0:1, :]
    radius = ext2[4, 0:32, :]
    alive = jnp.where(radius > 0.0, 1.0, 0.0)
    inverse = jnp.where(radius > 0.0, 0.36 / (radius * radius), 0.0)
    for k in range(2):
        speed = ext2[2 + k, 0:32, :]
        speed2 = speed + step * (inverse * (force[k] + itp[2 + k]) - (alive if k == 0 else 0.0))
        place2 = (ext2[k, 0:32, :] + step * speed2) * 0.0625
        for j in range(2):
            part[k, pl.ds(j, 16, stride=2), :] = place2[j * 16:(j + 1) * 16]
            part[2 + k, pl.ds(j, 16, stride=2), :] = speed2[j * 16:(j + 1) * 16]
    for c in edges + lists:
        c.wait()

    @pl.when(ax < N_ACROSS - 1)
    def _():
        to_right.wait_send()
        to_left.wait_recv()

    @pl.when(ax > 0)
    def _():
        to_left.wait_send()
        to_right.wait_recv()

    for c in pieces:
        c.wait()
    phase_end(1, 2, last_sum)
    flag[...] = sv[3][2:3, 0:1]
    gas_step_update(gas, visc, gr, gc, dv, sv.at[3], mv.at[3], out)


def fused(gas, visc, pos, vel, rad, coef, counts_t, pattern_t, idx, frac):
    dma = pltpu.SemaphoreType.DMA
    return pl.pallas_call(
        fused_kernel,
        out_shape=[jax.ShapeDtypeStruct((4, 32, 128), F32), jax.ShapeDtypeStruct((2, 32, 256), F32),
                   jax.ShapeDtypeStruct((1, 1), F32), jax.ShapeDtypeStruct((9, 2, 16), jnp.int32),
                   jax.ShapeDtypeStruct((2, 16), jnp.int32)],
        in_specs=[pl.BlockSpec(memory_space=pltpu.HBM)] * 10,
        out_specs=[VMEM_SPEC] * 3 + [pl.BlockSpec(memory_space=pltpu.HBM)] * 2,
        scratch_shapes=[
            pltpu.VMEM((2, 32, 256), F32), pltpu.VMEM((32, 256), F32),
            pltpu.VMEM((2, 32, 128), F32), pltpu.VMEM((2, 32, 128), F32), pltpu.VMEM((32, 128), F32),
            pltpu.VMEM((32, 128), F32), pltpu.VMEM((32, 128), jnp.int32), pltpu.VMEM((2, 32, 128), jnp.int32),
            pltpu.SMEM((9, 2, 16), jnp.int32), pltpu.SMEM((2, 16), jnp.int32), dma((12,)),
            pltpu.VMEM((8, 128, 128), F32), pltpu.VMEM((8, 128, 128), F32),
            pltpu.VMEM((8, 32, 128), F32), pltpu.VMEM((8, 32, 128), F32),
            pltpu.VMEM((8, 32, 128), F32), pltpu.VMEM((8, 32, 128), F32),
            pltpu.VMEM((2, 2, 8, 256), F32), pltpu.VMEM((2, 2, 32, 128), F32),
            pltpu.VMEM((3, 8, 8, 128), F32), pltpu.VMEM((4, 8, 128), F32),
            pltpu.VMEM((3, 8, 8, 128), F32), pltpu.VMEM((4, 8, 128), F32),
            pltpu.VMEM((8, 128, 128), F32), pltpu.VMEM((32 * 128, 128), BF16),
            pltpu.VMEM((128 * WINDOW_ROWS, 128), BF16), pltpu.VMEM((32, 80, 512), BF16),
            pltpu.VMEM((512, 128), F32), pltpu.VMEM((4, 32, 128), F32), pltpu.VMEM((8, 32, 128), F32),
            pltpu.VMEM((32, 128, 128), BF16), pltpu.VMEM((32, 16, 128), F32),
            dma((2, 10)), dma((2, 10)), dma((2, 8)), dma((2, 8)), dma((2, 3, 8)), dma((2, 3, 8)),
            dma((4,)), dma((4,)),
        ],
        compiler_params=pltpu.CompilerParams(collective_id=2, has_side_effects=True),
        name="interval",
    )(gas, visc, pos, vel, rad, coef, idx, frac, pattern_t, counts_t)


def body(gas, visc, pos, vel, rad, coef, counts, pattern, idx, frac):
    pos, vel, frac = (x.reshape(2, 32, 128) for x in (pos, vel, frac))
    rad, coef, idx = (x.reshape(32, 128) for x in (rad, coef, idx))
    args = (gas, visc, pos, vel, rad, coef, counts.T, pattern.transpose(2, 1, 0), idx, frac)
    part, out, flag, pattern_t, counts_t = fused(*args)
    args = args[:6] + (counts_t, pattern_t) + args[8:]
    part, out = lax.cond(flag[0, 0] > 0.0, lambda p, o: tuple(general(*args)), lambda p, o: (p, o), part, out)
    return part.reshape(4, 16, 2, 128), out


def solution(mesh):
    return jax.shard_map(
        body,
        mesh=mesh,
        in_specs=(
            P(None, ALONG_GAS, "across"),
            P(ALONG_GAS, "across"),
            P(None, "along", ACROSS_GAS, None),
            P(None, "along", ACROSS_GAS, None),
            P("along", ACROSS_GAS, None),
            P("along", ACROSS_GAS, None),
            P("along", ACROSS_GAS),
            P("along", ACROSS_GAS, None),
            P("along", ACROSS_GAS, None),
            P(None, "along", ACROSS_GAS, None),
        ),
        out_specs=(P(None, "along", ACROSS_GAS, None), P(None, ALONG_GAS, "across")),
        check_vma=False,
    )
```

```python
import functools

import jax
import jax.numpy as jnp
from jax import lax
from jax.experimental import pallas as pl
from jax.experimental.pallas import tpu as pltpu
from jax.sharding import PartitionSpec as P

ALONG_GAS = ("along", "gas")
ACROSS_GAS = ("across", "gas")
MESH_ID = pl.DeviceIdType.MESH
OFFSETS = [(-1, -1), (-1, 0), (-1, 1), (0, -1), (0, 0), (0, 1), (1, -1), (1, 0), (1, 1)]
DEAD = -16384.0
F32 = jnp.float32
BF16 = jnp.bfloat16
STRIDE = 136
BLOCK, BLOCK_BITS = 64, 6
EMPTY = 1344
REACH = 2.4
MOVE_LIMIT = int((REACH - 1.9) * 4096)
VMEM_SPEC = pl.BlockSpec(memory_space=pltpu.VMEM)
SMEM_SPEC = pl.BlockSpec(memory_space=pltpu.SMEM)
N_ACROSS, N_ALONG, N_GAS = 4, 8, 8


def iota(shape, dim):
    return lax.broadcasted_iota(jnp.int32, shape, dim)


def ext_row(ii, jj):
    base = {-1: 32, 0: 0, 1: 16, 2: 48}[jj]
    return jnp.where(ii < 0, 64 + 8 * (jj + 1) + 7, jnp.where(ii > 15, 96 + 8 * (jj + 1), base + ii))


def by_column(ref, *lead):
    return jnp.concatenate([ref[(*lead, pl.ds(0, 16, stride=2), slice(None))],
                            ref[(*lead, pl.ds(1, 16, stride=2), slice(None))]], axis=0)


def prepare_state(st, pos, vel, rad, counts):
    row32 = iota((32, 128), 0)
    slot = iota((32, 128), 1)
    cnt = jnp.zeros((32, 128), jnp.int32)
    for j in range(2):
        for i in range(16):
            cnt = jnp.where(row32 == j * 16 + i, counts[j, i], cnt)
    alive = slot < cnt
    z, x = by_column(pos, 0) * 16.0, by_column(pos, 1) * 16.0
    st[0, 0:32, :], st[1, 0:32, :] = z, x
    st[2, 0:32, :], st[3, 0:32, :] = by_column(vel, 0), by_column(vel, 1)
    st[4, 0:32, :] = jnp.where(alive, by_column(rad), DEAD)
    low_x, high_x = x < REACH, x > 16.0 - REACH

    def three(low, mid, high):
        return jnp.where(low_x, low, jnp.where(high_x, high, mid))

    kind = jnp.where(z < REACH, three(0, 1, 2), jnp.where(z > 16.0 - REACH, three(6, 5, 4), three(7, 8, 3)))
    kind = jnp.where(alive, kind, 9)
    member = jnp.concatenate([jnp.where(kind == c, 1.0, 0.0) for c in range(9)], axis=0).astype(BF16)
    before = jnp.where((iota((128, 256), 0) < iota((128, 256), 1)) | (iota((128, 256), 1) >= 128), 1.0, 0.0)
    ranks = jnp.dot(member, before.astype(BF16), preferred_element_type=F32)
    rank = jnp.full((32, 128), -1.0, F32)
    start = [jnp.zeros((32, 128), F32)]
    for c in range(9):
        here = ranks[c * 32:(c + 1) * 32]
        rank = jnp.where(kind == c, start[c] + here[:, 0:128], rank)
        start.append(start[c] + here[:, 128:256])
    st[5, 0:32, :] = rank
    start = [v.astype(jnp.int32) for v in start]
    wrap = ((start[1] + 7) & -8) > start[6]
    zero = jnp.zeros((32, 128), jnp.int32)
    windows = [(start[4], start[5]), (start[4], start[7]), (start[6], start[7]), (start[2], start[5]),
               (zero, start[9]), (jnp.where(wrap, 0, start[6]), start[8]), (start[2], start[3]),
               (zero, start[3]), (zero, start[1]), (zero, jnp.where(wrap, 0, start[1]))]
    table = zero
    for w, (low, high) in enumerate(windows):
        table = jnp.where(slot == 2 * w, low, jnp.where(slot == 2 * w + 1, (high - low + 7) & -8, table))
    st[6, 0:32, :] = table.astype(F32)


def prep_kernel(gas, visc, pos, vel, rad, counts, st, gp, mx):
    rate = jnp.abs(gas[0]) + jnp.abs(gas[1]) + 4.0 * visc[...]
    top = jnp.max(jnp.max(rate, axis=1, keepdims=True), axis=0, keepdims=True)
    mx[...] = jnp.broadcast_to(top, (8, 128))
    lane = iota((16, 128), 1)
    for g in range(N_GAS):
        blk = slice((g // 4) * 128, (g // 4) * 128 + 128)
        off = (g % 4) * 32
        for k in range(2):
            low = gas[k, 0:16, blk]
            high = gas[k, 16:32, blk]
            low = pltpu.roll(low, (128 - off) % 128, 1) if off else low
            shift = (160 - off) % 128
            high = pltpu.roll(high, shift, 1) if shift else high
            piece = jnp.where(lane < 32, low, jnp.where(lane < 64, high, 0.0))
            gp[g, k * 16:(k + 1) * 16, :] = piece
    prepare_state(st, pos, vel, rad, counts)
    st[7] = jnp.zeros((32, 128), F32)


def comm_kernel(first, *refs):
    if first:
        (st, pc, mx, gas, ext, pv, red, gr, gc, mb, m1, m2,
         own_sem, hs, hr, ps, pr, rs, rr, es, er) = refs
    else:
        (st, pc, mx, ext, pv, red, mb, m1, m2,
         own_sem, hs, hr, ps, pr, rs, rr) = refs
    ax, al, g = lax.axis_index("across"), lax.axis_index("along"), lax.axis_index("gas")
    up, down = lax.rem(al + 1, N_ALONG), lax.rem(al + N_ALONG - 1, N_ALONG)
    lin = ax * N_GAS + g
    has_left, has_right = lin > 0, lin < N_ACROSS * N_GAS - 1
    left = jnp.maximum(lin - 1, 0)
    right = jnp.minimum(lin + 1, N_ACROSS * N_GAS - 1)

    def col(index, along):
        return {"across": lax.div(index, N_GAS), "along": along, "gas": lax.rem(index, N_GAS)}

    slab = al * N_GAS + g
    slabs = N_ALONG * N_GAS
    after, before = lax.rem(slab + 1, slabs), lax.rem(slab + slabs - 1, slabs)

    def slab_id(index):
        return {"across": ax, "along": lax.div(index, N_GAS), "gas": lax.rem(index, N_GAS)}

    barrier = pltpu.get_barrier_semaphore()

    def greet(device):
        pl.semaphore_signal(barrier, inc=1, device_id=device, device_id_type=MESH_ID)

    for k in range(1, N_ACROSS):
        greet({"across": lax.rem(ax + k, N_ACROSS)})
    for k in range(1, N_GAS):
        greet({"gas": lax.rem(g + k, N_GAS)})
    for k in range(1, N_ALONG):
        greet({"along": lax.rem(al + k, N_ALONG)})
    expect = N_ACROSS + N_GAS + N_ALONG - 3
    if first:
        greet(slab_id(after))
        greet(slab_id(before))
        expect += 2

    @pl.when(has_left)
    def _():
        for along in (down, al, up):
            greet(col(left, along))

    @pl.when(has_right)
    def _():
        for along in (down, al, up):
            greet(col(right, along))

    own = pltpu.make_async_copy(st, ext.at[:, pl.ds(0, 32)], own_sem.at[0])
    own.start()
    own_piece = pltpu.make_async_copy(pc.at[g], pv.at[g], own_sem.at[1])
    own_piece.start()

    @pl.when(jnp.logical_not(has_left))
    def _():
        ext[:, 32:48, :] = jnp.zeros((8, 16, 128), F32)
        ext[:, 64:72, :] = jnp.zeros((8, 8, 128), F32)
        ext[:, 96:104, :] = jnp.zeros((8, 8, 128), F32)

    @pl.when(jnp.logical_not(has_right))
    def _():
        ext[:, 48:64, :] = jnp.zeros((8, 16, 128), F32)
        ext[:, 88:96, :] = jnp.zeros((8, 8, 128), F32)
        ext[:, 120:128, :] = jnp.zeros((8, 8, 128), F32)

    if first:
        @pl.when(ax == 0)
        def _():
            gc[0] = jnp.zeros((2, 32, 128), F32)

        @pl.when(ax == N_ACROSS - 1)
        def _():
            gc[1] = jnp.zeros((2, 32, 128), F32)

    sides = jnp.where(has_left, 3, 0) + jnp.where(has_right, 3, 0)
    pl.semaphore_wait(barrier, expect + sides)

    def remote(src, dst, send, recv, device):
        return pltpu.make_async_remote_copy(
            src_ref=src, dst_ref=dst, send_sem=send, recv_sem=recv,
            device_id=device, device_id_type=MESH_ID,
        )

    def reduce_sends(phase, src, axis, me, size):
        out = []
        for k in range(1, size):
            out.append(remote(src, mb.at[phase, me], rs.at[phase, k], rr.at[phase, k],
                              {axis: lax.rem(me + k, size)}))
        for c in out:
            c.start()
        return out

    phase0 = reduce_sends(0, mx, "across", ax, N_ACROSS)

    def halo(c, src_rows, size, dst_row, device):
        return remote(st.at[pl.ds(0, 7), pl.ds(src_rows, size)],
                      ext.at[pl.ds(0, 7), pl.ds(dst_row, size)], hs.at[c], hr.at[c], device)

    lefts = [halo(0, 0, 16, 48, col(left, al)),
             halo(1, 8, 8, 64 + 24, col(left, up)),
             halo(2, 0, 8, 96 + 24, col(left, down))]
    rights = [halo(3, 16, 16, 32, col(right, al)),
              halo(4, 24, 8, 64, col(right, up)),
              halo(5, 16, 8, 96, col(right, down))]
    rows = [halo(6, 8, 8, 64 + 8, {"along": up}),
            halo(7, 24, 8, 64 + 16, {"along": up}),
            halo(8, 0, 8, 96 + 8, {"along": down}),
            halo(9, 16, 8, 96 + 16, {"along": down})]

    @pl.when(has_left)
    def _():
        for c in lefts:
            c.start()

    @pl.when(has_right)
    def _():
        for c in rights:
            c.start()

    for c in rows:
        c.start()
    pieces = []
    for k in range(1, N_GAS):
        peer = lax.rem(g + k, N_GAS)
        c = remote(pc.at[peer], pv.at[g], ps.at[k], pr.at[k], {"gas": peer})
        c.start()
        pieces.append(c)
    if first:
        edges = [remote(gas.at[:, pl.ds(24, 8)], gr.at[0], es.at[0], er.at[0], slab_id(after)),
                 remote(gas.at[:, pl.ds(0, 8)], gr.at[1], es.at[1], er.at[1], slab_id(before))]
        for c in edges:
            c.start()
        to_right = remote(gas.at[:, :, pl.ds(128, 128)], gc.at[0], es.at[2], er.at[2],
                          {"across": jnp.minimum(ax + 1, N_ACROSS - 1)})
        to_left = remote(gas.at[:, :, pl.ds(0, 128)], gc.at[1], es.at[3], er.at[3],
                         {"across": jnp.maximum(ax - 1, 0)})

        @pl.when(ax < N_ACROSS - 1)
        def _():
            to_right.start()

        @pl.when(ax > 0)
        def _():
            to_left.start()

    def combine(phase, mine, me, size, copies):
        for c in copies:
            c.wait_recv()
        mb[phase, me] = mine
        total = mb[phase, 0]
        for k in range(1, size):
            total = jnp.maximum(total, mb[phase, k]) if first else total + mb[phase, k]
        return total

    m1[...] = combine(0, mx[...], ax, N_ACROSS, phase0)
    phase1 = reduce_sends(1, m1, "gas", g, N_GAS)
    m2[...] = combine(1, m1[...], g, N_GAS, phase1)
    phase2 = reduce_sends(2, m2, "along", al, N_ALONG)
    red[...] = combine(2, m2[...], al, N_ALONG, phase2)

    own.wait()
    own_piece.wait()
    for c in phase0 + phase1 + phase2:
        c.wait_send()
    for c in rows + pieces:
        c.wait()

    @pl.when(has_left)
    def _():
        for c in lefts:
            c.wait_send()
        for c in rights:
            c.wait_recv()

    @pl.when(has_right)
    def _():
        for c in rights:
            c.wait_send()
        for c in lefts:
            c.wait_recv()

    if first:
        for c in edges:
            c.wait()

        @pl.when(ax < N_ACROSS - 1)
        def _():
            to_right.wait_send()
            to_left.wait_recv()

        @pl.when(ax > 0)
        def _():
            to_left.wait_send()
            to_right.wait_recv()


def exchange(first, st, pc, mx, gas=None):
    out_shape = [jax.ShapeDtypeStruct((8, 128, 128), F32),
                 jax.ShapeDtypeStruct((8, 32, 128), F32),
                 jax.ShapeDtypeStruct((8, 128), F32)]
    scratch = [pltpu.VMEM((3, 8, 8, 128), F32), pltpu.VMEM((8, 128), F32), pltpu.VMEM((8, 128), F32),
               pltpu.SemaphoreType.DMA((2,)),
               pltpu.SemaphoreType.DMA((10,)), pltpu.SemaphoreType.DMA((10,)),
               pltpu.SemaphoreType.DMA((8,)), pltpu.SemaphoreType.DMA((8,)),
               pltpu.SemaphoreType.DMA((3, 8)), pltpu.SemaphoreType.DMA((3, 8))]
    args = [st, pc, mx]
    if first:
        args.append(gas)
        out_shape += [jax.ShapeDtypeStruct((2, 2, 8, 256), F32), jax.ShapeDtypeStruct((2, 2, 32, 128), F32)]
        scratch += [pltpu.SemaphoreType.DMA((4,)), pltpu.SemaphoreType.DMA((4,))]
    return pl.pallas_call(
        functools.partial(comm_kernel, first),
        out_shape=out_shape,
        in_specs=[VMEM_SPEC] * len(args),
        out_specs=[VMEM_SPEC] * len(out_shape),
        scratch_shapes=scratch,
        compiler_params=pltpu.CompilerParams(collective_id=0 if first else 1, has_side_effects=True),
        name="exchange_first" if first else "exchange_second",
    )(*args)


def split3(x):
    hi = x.astype(BF16).astype(F32)
    rest = x - hi
    mid = rest.astype(BF16).astype(F32)
    return hi, mid, rest - mid


def contact_forces(ext, pat, meta, ints, qt, lst, rhs, frc, sem):
    ints[...] = ext[6 * 128:7 * 128, :].astype(jnp.int32)
    to_smem = pltpu.make_async_copy(ints, meta, sem)
    to_smem.start()
    slot = iota((128, 128), 0).astype(F32)
    attr_row = iota((8, 128), 0)
    zero8 = jnp.zeros((8, 128), F32)
    tail = jnp.concatenate([zero8, jnp.ones((24, 128), F32), zero8], axis=0)

    def parts(row):
        block = ext[pl.ds(row, 8, stride=128), :]
        return split3(jnp.where(attr_row < 5, block, 0.0))

    def transposed(row):
        hi, mid, lo = parts(row)
        rows = jnp.concatenate([hi, mid, lo, tail], axis=0).astype(BF16)
        place = (slot == ext[pl.ds(row + 5 * 128, 1), :]).astype(F32).astype(BF16)
        turned = lax.dot_general(place, rows, (((1,), (1,)), ((), ())), preferred_element_type=F32)
        start = row * STRIDE if isinstance(row, int) else pl.multiple_of(row * STRIDE, 8)
        qt[pl.ds(start, 128), 0:64] = turned
        start = start + 128 if isinstance(row, int) else pl.multiple_of(start + 128, 8)
        qt[pl.ds(start, 8), :] = zero8

    def some(step, carry):
        for u in range(4):
            transposed(step * 4 + u)
        return carry

    lax.fori_loop(0, 16, some, 0)
    for c in range(4):
        transposed(64 + 8 * c + 7)
        transposed(96 + 8 * c)

    block_of = iota((32, 640), 1) >> 7
    row_of = iota((32, 640), 0)
    attr_of = row_of & 7
    own_scale = jnp.where(block_of < 2, -1.0, jnp.where(block_of < 4, 2.0, 1.0))
    const = jnp.where((attr_of == block_of) & (row_of < 24), own_scale, 0.0)
    const = jnp.where((row_of == 24) & (block_of == 0) | (row_of == 25) & (block_of == 1), -16.0, const)
    for u in range(2):
        rhs[u, 0:32, :] = const.astype(BF16)
        lst[u, EMPTY:EMPTY + BLOCK, :] = jnp.zeros((BLOCK, 128), F32)
    to_smem.wait()
    lane = iota((8, 128), 1)

    def row_step(i, carry):
        blocks = []
        for j in range(2):
            work = lst.at[j]
            mine = j * 16 + i
            hi, mid, lo = parts(mine)
            columns = []
            for a in range(5):
                keep = attr_row == a
                scale = 1.0 if a in (0, 1, 4) else -2.0
                columns.append(jnp.concatenate(
                    [jnp.where(keep, hi * scale, 0.0), jnp.where(keep, mid * scale, 0.0),
                     jnp.where(keep, lo * scale, 0.0), zero8], axis=0))
            rhs[j, 32:64, :] = jnp.concatenate(columns, axis=1).astype(BF16)
            moved = meta[mine, 20]
            off = i * 0
            over = i * 0
            windows = []
            for w in (4, 0, 1, 2, 3, 5, 6, 7, 8, 9):
                di, dj = OFFSETS[5 if w == 9 else w]
                row = ext_row(i + di, j + dj)
                first, size = meta[row, 2 * w], meta[row, 2 * w + 1]
                if w != 4:
                    near = moved + meta[row, 20] <= MOVE_LIMIT
                    first = jnp.where(near, first, 0)
                    size = jnp.where(near, size, 0 if w == 9 else meta[row, 9])
                size = size * pat[5 if w == 9 else w, j, i]
                mark = jnp.where(lane == 24, float(di), jnp.where(lane == 25, float(dj), 0.0))
                start = row * STRIDE + first
                chunks = 16 if w == 4 else 4 if w in (1, 3, 5, 7) else 1
                for c in range(chunks):
                    work[pl.ds(pl.multiple_of(off + c * 8, 8), 8), :] = qt[pl.ds(start + c * 8, 8), :] + mark
                windows.append((start, size, mark))
                off = off + size
                over = jnp.maximum(over, size - chunks * 8)

            @pl.when(over > 0)
            def _():
                to = i * 0
                for start, size, mark in windows:
                    def copy(c, carry, start=start, mark=mark, to=to):
                        work[pl.ds(pl.multiple_of(to + c * 8, 8), 8), :] = qt[pl.ds(start + c * 8, 8), :] + mark
                        return carry
                    lax.fori_loop(0, size >> 3, copy, 0)
                    to = to + size

            for c in range(BLOCK // 8):
                work[pl.ds(pl.multiple_of(off + c * 8, 8), 8), :] = zero8
            blocks.append((off + BLOCK - 1) >> BLOCK_BITS)
        right = [rhs[0], rhs[1]]

        def block(b, acc):
            out = []
            for j in range(2):
                at = jnp.where(b < blocks[j], b * BLOCK, EMPTY)
                q = lst[j, pl.ds(pl.multiple_of(at, 8), BLOCK), 0:64].astype(BF16)
                got = jnp.dot(q, right[j], preferred_element_type=F32)
                rz, rx = got[:, 0:128], got[:, 128:256]
                dz, dx = got[:, 256:384], got[:, 384:512]
                d2 = rz * rz + rx * rx + 0.0001
                inv = lax.rsqrt(d2)
                depth = jnp.maximum(got[:, 512:640] - d2 * inv, 0.0)
                push = depth * inv * (40.0 + (dz * rz + dx * rx) * inv)
                out.append(acc[2 * j] + jnp.sum((push * rz).reshape(BLOCK // 8, 8, 128), axis=0))
                out.append(acc[2 * j + 1] + jnp.sum((push * rx).reshape(BLOCK // 8, 8, 128), axis=0))
            return tuple(out)

        acc = lax.fori_loop(0, jnp.maximum(blocks[0], blocks[1]), block, (zero8,) * 4)
        for j in range(2):
            for k in range(2):
                frc[pl.ds(pl.multiple_of(((k * 2 + j) * 16 + i) * 8, 8), 8), :] = acc[2 * j + k]
        return carry

    lax.fori_loop(0, 16, row_step, 0)
    return [sum(frc[pl.ds(k * 256 + r, 32, stride=8), :] for r in range(8)) for k in range(2)]


def first_kernel(ext, gv, rate, idx, frac, coef, pat, st2, dp, tot, dr2, inv_out,
                 meta, ints, qt, lst, rhs, frc, itp, sem):
    def weights(r, t4):
        index = idx[pl.ds(r, 1), :]
        row, column = index >> 4, index & 15
        share_z = frac[0, pl.ds(r, 1), :].astype(F32) / 1024.0
        share_x = frac[1, pl.ds(r, 1), :].astype(F32) / 1024.0
        c64 = iota((64, 128), 0) - t4 * 16
        wx = jnp.where(c64 == column, 1.0 - share_x, jnp.where(c64 == column + 1, share_x, 0.0))
        r16 = iota((16, 128), 0)
        wz = jnp.where(r16 == row, 1.0 - share_z, jnp.where(r16 == row + 1, share_z, 0.0))
        return wz, wx

    def sample(h, carry):
        field = gv[h][:, 0:64]
        for t in range(2):
            for j in range(2):
                wz, wx = weights(4 * h + 2 * t + j, t * 2 + j)
                along = jnp.dot(field, wx, precision=lax.Precision.HIGHEST, preferred_element_type=F32)
                for k in range(2):
                    itp[k, pl.ds(j * 16 + 2 * h + t, 1), :] = jnp.sum(
                        wz * along[k * 16:(k + 1) * 16], axis=0, keepdims=True)
        return carry

    lax.fori_loop(0, 8, sample, 0)
    force = contact_forces(ext, pat, meta, ints, qt, lst, rhs, frc, sem)
    step = 0.2 / rate[0:1, :]
    drag = by_column(coef)
    radius = ext[4 * 128:4 * 128 + 32, :]
    alive = jnp.where(radius > 0.0, 1.0, 0.0)
    inverse = jnp.where(radius > 0.0, 0.36 / (radius * radius), 0.0)
    inv_out[...] = inverse
    means = []
    moved = jnp.zeros((32, 128), F32)
    for k in range(2):
        place = ext[k * 128:k * 128 + 32, :]
        speed = ext[(2 + k) * 128:(2 + k) * 128 + 32, :]
        drag1 = drag * (itp[k] - speed)
        speed2 = speed + step * (inverse * (force[k] + drag1) - (alive if k == 0 else 0.0))
        st2[k] = place + step * speed2
        moved = jnp.maximum(moved, alive * jnp.abs(step * speed2))
        st2[2 + k] = speed2
        drag2 = drag * (itp[k] - speed2)
        dr2[k] = drag2
        mean = 0.5 * (alive * drag1 + alive * drag2)
        itp[k] = mean
        means.append(jnp.sum(jnp.sum(mean, axis=1, keepdims=True), axis=0, keepdims=True))
    st2[4] = radius
    st2[5] = ext[5 * 128:5 * 128 + 32, :]
    far = jnp.max(moved, axis=1, keepdims=True)
    far = jnp.where(far < 100.0, far, 100.0) * 4096.0 + 1.0
    st2[6] = jnp.where(iota((32, 128), 1) == 20, far, ext[6 * 128:6 * 128 + 32, :])
    st2[7] = jnp.zeros((32, 128), F32)
    tot[...] = jnp.where(iota((8, 128), 0) == 0, means[0], means[1])

    def spread(h, carry):
        total = jnp.zeros((32, 64), F32)
        for t in range(2):
            for j in range(2):
                wz, wx = weights(4 * h + 2 * t + j, t * 2 + j)
                m0 = itp[0, pl.ds(j * 16 + 2 * h + t, 1), :]
                m1 = itp[1, pl.ds(j * 16 + 2 * h + t, 1), :]
                lhs = jnp.concatenate([wz * m0, wz * m1], axis=0)
                total = total + lax.dot_general(lhs, wx, (((1,), (1,)), ((), ())),
                                                precision=lax.Precision.HIGHEST, preferred_element_type=F32)
        dp[h, :, 0:64] = total
        dp[h, :, 64:128] = jnp.zeros((32, 64), F32)
        return carry

    lax.fori_loop(0, 8, spread, 0)


def gas_step_update(gas, visc, gr, gc, dv, tot, rate, out):
    gas_step = 0.4 / rate[0:1, 0:1]
    lane = iota((32, 256), 1)
    row = iota((32, 256), 0)
    lane16 = iota((16, 128), 1) >> 5
    for k in range(2):
        u = gas[k]
        upper = jnp.where(row == 31, gr[1, k, 0:1, :], pltpu.roll(u, 31, 0))
        lower = jnp.where(row == 0, gr[0, k, 7:8, :], pltpu.roll(u, 1, 0))
        right = jnp.where(lane == 255, gc[1, k, :, 0:1], pltpu.roll(u, 255, 1))
        left = jnp.where(lane == 0, gc[0, k, :, 127:128], pltpu.roll(u, 1, 1))
        laplace = upper + lower + right + left - 4.0 * u
        advect = gas[0] * (upper - lower) * 0.5 + gas[1] * (right - left) * 0.5
        quads = []
        for t in range(2):
            halves = []
            for b in range(2):
                whole = None
                for q in range(4):
                    piece = dv[4 * b + q, k * 16:(k + 1) * 16, :]
                    shift = (q * 32 - t * 32) % 128
                    piece = pltpu.roll(piece, shift, 1) if shift else piece
                    whole = piece if whole is None else jnp.where(lane16 == q, piece, whole)
                halves.append(whole)
            quads.append(jnp.concatenate(halves, axis=1))
        deposit = jnp.concatenate(quads, axis=0)
        source = tot[k:k + 1, 0:1] / 2097152.0 - deposit
        out[k] = u + gas_step * (visc[...] * laplace - advect + source)


def second_kernel(ext, dv, tot, rate, dr2, inverse, gas, visc, gr, gc, pat, part, out,
                  meta, ints, qt, lst, rhs, frc, sem):
    force = contact_forces(ext, pat, meta, ints, qt, lst, rhs, frc, sem)
    step = 0.2 / rate[0:1, :]
    radius = ext[4 * 128:4 * 128 + 32, :]
    alive = jnp.where(radius > 0.0, 1.0, 0.0)
    for k in range(2):
        place = ext[k * 128:k * 128 + 32, :]
        speed = ext[(2 + k) * 128:(2 + k) * 128 + 32, :]
        speed2 = speed + step * (inverse[...] * (force[k] + dr2[k]) - (alive if k == 0 else 0.0))
        place2 = (place + step * speed2) * 0.0625
        for j in range(2):
            part[k, pl.ds(j, 16, stride=2), :] = place2[j * 16:(j + 1) * 16]
            part[2 + k, pl.ds(j, 16, stride=2), :] = speed2[j * 16:(j + 1) * 16]
    gas_step_update(gas, visc, gr, gc, dv, tot, rate, out)


CONTACT_SCRATCH = [
    pltpu.SMEM((128, 128), jnp.int32),
    pltpu.VMEM((128, 128), jnp.int32),
    pltpu.VMEM((128 * STRIDE, 128), F32),
    pltpu.VMEM((2, 1408, 128), F32),
    pltpu.VMEM((2, 64, 640), BF16),
    pltpu.VMEM((512, 128), F32),
]


def general(gas, visc, pos, vel, rad, coef, counts_t, pattern_t, idx, frac):

    def shapes(*dims):
        return [jax.ShapeDtypeStruct(d, F32) for d in dims]

    st, gp, mx = pl.pallas_call(
        prep_kernel,
        out_shape=shapes((8, 32, 128), (8, 32, 128), (8, 128)),
        in_specs=[VMEM_SPEC] * 5 + [SMEM_SPEC],
        out_specs=[VMEM_SPEC] * 3,
        name="prepare",
    )(gas, visc, pos, vel, rad, counts_t)
    ext, gv, rate, gr, gc = exchange(True, st, gp, mx, gas)
    st2, dp, tot, dr2, inverse = pl.pallas_call(
        first_kernel,
        out_shape=shapes((8, 32, 128), (8, 32, 128), (8, 128), (2, 32, 128), (32, 128)),
        in_specs=[VMEM_SPEC] * 6 + [SMEM_SPEC],
        out_specs=[VMEM_SPEC] * 5,
        scratch_shapes=CONTACT_SCRATCH + [pltpu.VMEM((2, 32, 128), F32), pltpu.SemaphoreType.DMA],
        name="first_substep",
    )(ext.reshape(1024, 128), gv, rate, idx, frac, coef, pattern_t)
    ext2, dv, total = exchange(False, st2, dp, tot)
    part, out = pl.pallas_call(
        second_kernel,
        out_shape=shapes((4, 32, 128), (2, 32, 256)),
        in_specs=[VMEM_SPEC] * 10 + [SMEM_SPEC],
        out_specs=[VMEM_SPEC] * 2,
        scratch_shapes=CONTACT_SCRATCH + [pltpu.SemaphoreType.DMA],
        name="second_substep",
    )(ext2.reshape(1024, 128), dv, total, rate, dr2, inverse, gas, visc, gr, gc, pattern_t)
    return part, out


EDGE_BASE, CORNER_BASE, WINDOW_ROWS = 48, 192, 256
CORNER = 16
WINDOWS = ((-1, 0), (1, 0), (0, -1), (0, 1), (-1, -1), (-1, 1), (1, -1), (1, 1))
NEAR = ((1.82, 0.0), (2.25, 0.43))
EDGE = 40
EARLY = 8


def fused_kernel(*refs):
    inputs, (part, out, flag, pat_copy, counts_copy), refs = refs[:10], refs[10:15], refs[15:]
    gas, visc, pos, vel, rad, coef, idx, frac, pat, counts = refs[:10]
    (in_sem, ext, ext2, gp, gv, dp, dv, gr, gc, mb, mv, sb, sv, rk, qs, qw, rhs, frc, itp, wts, wx, wz,
     hs, hr, ps, pr, rs, rr, es, er) = refs[10:]
    loads = [pltpu.make_async_copy(a, b, in_sem.at[n]) for n, (a, b) in enumerate(zip(inputs, refs[:10]))]
    for c in loads:
        c.start()
    ax, al, g = lax.axis_index("across"), lax.axis_index("along"), lax.axis_index("gas")

    def around(value, size):
        return value - jnp.where(value >= size, size, 0)

    up, down = around(al + 1, N_ALONG), around(al + N_ALONG - 1, N_ALONG)
    first_g, last_g = g == 0, g == N_GAS - 1
    has_left = jnp.logical_or(ax > 0, g > 0)
    has_right = jnp.logical_or(ax < N_ACROSS - 1, g < N_GAS - 1)
    left = (jnp.maximum(ax - jnp.where(first_g, 1, 0), 0), jnp.where(first_g, N_GAS - 1, g - 1))
    right = (jnp.minimum(ax + jnp.where(last_g, 1, 0), N_ACROSS - 1), jnp.where(last_g, 0, g + 1))

    def device(a=ax, l=al, y=g):
        return {"across": a, "along": l, "gas": y}

    def col(side, along):
        return device(a=side[0], l=along, y=side[1])

    def peer_id(axis, index):
        return device(**{{"across": "a", "along": "l", "gas": "y"}[axis]: index})

    after = device(l=jnp.where(last_g, up, al), y=jnp.where(last_g, 0, g + 1))
    before = device(l=jnp.where(first_g, down, al), y=jnp.where(first_g, N_GAS - 1, g - 1))

    barrier = pltpu.get_barrier_semaphore()

    def greet(target):
        pl.semaphore_signal(barrier, inc=1, device_id=target, device_id_type=MESH_ID)

    for k in range(1, N_ALONG):
        greet(device(l=around(al + k, N_ALONG)))
    columns_x = [around(ax + k, N_ACROSS) for k in range(N_ACROSS)]
    columns_g = [around(g + k, N_GAS) for k in range(N_GAS)]
    plane = [device(a=columns_x[k // N_GAS], y=columns_g[k % N_GAS]) for k in range(N_ACROSS * N_GAS)]
    for target in plane[1:]:
        greet(target)
    greet(after)
    greet(before)
    expect = N_ACROSS * N_GAS + N_ALONG - 2 + 2

    @pl.when(has_left)
    def _():
        for along in (down, al, up):
            greet(col(left, along))

    @pl.when(has_right)
    def _():
        for along in (down, al, up):
            greet(col(right, along))

    for c in loads:
        c.wait()
    rate = jnp.abs(gas[0]) + jnp.abs(gas[1]) + 4.0 * visc[...]
    top = jnp.max(jnp.max(rate, axis=1, keepdims=True), axis=0, keepdims=True)
    mv[0] = jnp.broadcast_to(top, (8, 128))
    lane = iota((16, 128), 1)
    for d in range(N_GAS):
        blk = slice((d // 4) * 128, (d // 4) * 128 + 128)
        off = (d % 4) * 32
        for k in range(2):
            low = gas[k, 0:16, blk]
            high = gas[k, 16:32, blk]
            low = pltpu.roll(low, (128 - off) % 128, 1) if off else low
            shift = (160 - off) % 128
            high = pltpu.roll(high, shift, 1) if shift else high
            piece = jnp.where(lane < 32, low, high)
            gp[d, k * 16:(k + 1) * 16, :] = jnp.where(lane < 64, piece, pltpu.roll(piece, 64, 1))
    row32 = iota((32, 128), 0)
    cnt = jnp.zeros((32, 128), jnp.int32)
    for j in range(2):
        for i in range(16):
            cnt = jnp.where(row32 == j * 16 + i, counts[j, i], cnt)
    ext[0, 0:32, :], ext[1, 0:32, :] = by_column(pos, 0) * 16.0, by_column(pos, 1) * 16.0
    ext[2, 0:32, :], ext[3, 0:32, :] = by_column(vel, 0), by_column(vel, 1)
    ext[4, 0:32, :] = jnp.where(iota((32, 128), 1) < cnt, by_column(rad), DEAD)

    def dots(e, low, high):
        e[5, low:high, :] = e[0, low:high, :] * e[2, low:high, :] + e[1, low:high, :] * e[3, low:high, :]

    dots(ext, 0, 32)
    for e in (ext, ext2):
        @pl.when(jnp.logical_not(has_left))
        def _():
            e[:, 32:48, :] = jnp.zeros((8, 16, 128), F32)
            e[:, 64:72, :] = jnp.zeros((8, 8, 128), F32)
            e[:, 96:104, :] = jnp.zeros((8, 8, 128), F32)

        @pl.when(jnp.logical_not(has_right))
        def _():
            e[:, 48:64, :] = jnp.zeros((8, 16, 128), F32)
            e[:, 88:96, :] = jnp.zeros((8, 8, 128), F32)
            e[:, 120:128, :] = jnp.zeros((8, 8, 128), F32)

    @pl.when(ax == 0)
    def _():
        gc[0] = jnp.zeros((2, 32, 128), F32)

    @pl.when(ax == N_ACROSS - 1)
    def _():
        gc[1] = jnp.zeros((2, 32, 128), F32)

    sides = jnp.where(has_left, 3, 0) + jnp.where(has_right, 3, 0)
    pl.semaphore_wait(barrier, expect + sides)

    def remote(src, dst, send, recv, target):
        return pltpu.make_async_remote_copy(
            src_ref=src, dst_ref=dst, send_sem=send, recv_sem=recv,
            device_id=target, device_id_type=MESH_ID,
        )

    line = [device(l=around(al + k, N_ALONG)) for k in range(N_ALONG)]
    groups_of = ((plane, ax * N_GAS + g), (line, al))

    def reduce_copies(which, phase):
        slots, value = ((mb, mv), (sb, sv))[which]
        peers, me = groups_of[phase]
        return [remote(value.at[phase], slots.at[phase, me], rs.at[which, phase, k], rr.at[which, phase, k], peers[k])
                for k in range(1, len(peers))]

    def reduce_go(which, phase, copies):
        slots, value = ((mb, mv), (sb, sv))[which]
        for c in copies:
            c.start()
        slots[phase, groups_of[phase][1]] = value[phase]

    def reduce_start(which, phase):
        out = reduce_copies(which, phase)
        reduce_go(which, phase, out)
        return out

    def reduce_end(which, phase, copies):
        slots, value = ((mb, mv), (sb, sv))[which]
        size = len(groups_of[phase][0])
        for c in copies:
            c.wait_recv()
        total = slots[phase, 0]
        for k in range(1, size):
            total = total + slots[phase, k] if which else jnp.maximum(total, slots[phase, k])
        value[phase + 1] = total
        for c in copies:
            c.wait_send()

    def halo_start(which):
        e, attrs = ((ext, 5), (ext2, 5))[which]

        def halo(c, src_row, size, dst_row, target):
            return remote(e.at[pl.ds(0, attrs), pl.ds(src_row, size)],
                          e.at[pl.ds(0, attrs), pl.ds(dst_row, size)], hs.at[which, c], hr.at[which, c], target)

        lefts = [halo(0, 0, 16, 48, col(left, al)),
                 halo(1, 8, 8, 64 + 24, col(left, up)),
                 halo(2, 0, 8, 96 + 24, col(left, down))]
        rights = [halo(3, 16, 16, 32, col(right, al)),
                  halo(4, 24, 8, 64, col(right, up)),
                  halo(5, 16, 8, 96, col(right, down))]
        rows = [halo(6, 8, 8, 64 + 8, device(l=up)),
                halo(7, 24, 8, 64 + 16, device(l=up)),
                halo(8, 0, 8, 96 + 8, device(l=down)),
                halo(9, 16, 8, 96 + 16, device(l=down))]

        @pl.when(has_left)
        def _():
            for c in lefts:
                c.start()

        @pl.when(has_right)
        def _():
            for c in rights:
                c.start()

        for c in rows:
            c.start()
        return lefts, rights, rows

    def halo_end(copies):
        lefts, rights, rows = copies
        for c in rows:
            c.wait()

        @pl.when(has_left)
        def _():
            for c in lefts:
                c.wait_send()
            for c in rights:
                c.wait_recv()

        @pl.when(has_right)
        def _():
            for c in rights:
                c.wait_send()
            for c in lefts:
                c.wait_recv()

    def pieces_start(which):
        src, dst = ((gp, gv), (dp, dv))[which]
        out = []
        for k in range(1, N_GAS):
            peer = around(g + k, N_GAS)
            c = remote(src.at[peer], dst.at[g], ps.at[which, k], pr.at[which, k], device(y=peer))
            c.start()
            out.append(c)
        dst[g] = src[g]
        return out

    phase = reduce_start(0, 0)
    halos = halo_start(0)
    pieces = pieces_start(0)
    edges = [remote(gas.at[:, pl.ds(24, 8)], gr.at[0], es.at[0], er.at[0], after),
             remote(gas.at[:, pl.ds(0, 8)], gr.at[1], es.at[1], er.at[1], before)]
    for c in edges:
        c.start()
    to_right = remote(gas.at[:, :, pl.ds(128, 128)], gc.at[0], es.at[2], er.at[2],
                      device(a=jnp.minimum(ax + 1, N_ACROSS - 1)))
    to_left = remote(gas.at[:, :, pl.ds(0, 128)], gc.at[1], es.at[3], er.at[3],
                     device(a=jnp.maximum(ax - 1, 0)))

    @pl.when(ax < N_ACROSS - 1)
    def _():
        to_right.start()

    @pl.when(ax > 0)
    def _():
        to_left.start()

    lists = [pltpu.make_async_copy(pat, pat_copy, in_sem.at[10]), pltpu.make_async_copy(counts, counts_copy, in_sem.at[11])]
    for c in lists:
        c.start()

    slot_row = iota((48, 128), 0)
    slots = (jnp.where(slot_row < EDGE, slot_row, -5).astype(F32),
             jnp.where(slot_row < 32, slot_row, jnp.where(slot_row < 40, -5, slot_row - 8)).astype(F32))
    attr_row = iota((8, 128), 0)
    zero8 = jnp.zeros((8, 128), F32)
    one_tail = jnp.concatenate([zero8, jnp.ones((24, 128), F32)], axis=0)
    flat = (ext.reshape(1024, 128), ext2.reshape(1024, 128))
    eye = jnp.where(iota((128, 128), 0) == iota((128, 128), 1), 1.0, 0.0).astype(BF16)
    before_slot = jnp.where(iota((128, 128), 0) < iota((128, 128), 1), 1.0, 0.0).astype(BF16)

    def rank(which, low, high, windows=range(8)):
        e = (ext, ext2)[which]
        reach, _ = NEAR[which]
        z, x, live = e[0, low:high, :], e[1, low:high, :], e[4, low:high, :] > 0.0

        def flags(cond):
            return jnp.where(cond & live, 1.0, 0.0)

        lz, hz, lx, hx = flags(z < reach), flags(z > 16.0 - reach), flags(x < reach), flags(x > 16.0 - reach)
        member = [hz, lz, hx, lx, hz * hx, hz * lx, lz * hx, lz * lx]
        size = high - low
        places = jnp.dot(jnp.concatenate([member[w] for w in windows], axis=0).astype(BF16), before_slot,
                         preferred_element_type=F32)
        lost = jnp.zeros((size, 128), F32)
        for order, w in enumerate(windows):
            place = places[order * size:(order + 1) * size]
            rk[w, low:high, :] = jnp.where(member[w] > 0.0, place, -1.0)
            lost = lost + jnp.where(place >= (EDGE if w < 4 else CORNER), member[w], 0.0)
        return lost

    def parts(which, row):
        block = flat[which][pl.ds(row, 8, stride=128), :]
        return split3(jnp.where(attr_row < 6, block, 0.0))

    def stacked(hi, mid, lo, own=False):
        shifted = jnp.where(attr_row < 2, pltpu.roll(hi, 6, 0), jnp.where(attr_row < 4, mid, 0.0))
        return jnp.concatenate([hi, mid, lo, hi, mid, zero8 if own else shifted, one_tail], axis=0)

    def partner(v):
        return jnp.where(attr_row < 2, pltpu.roll(v, 6, 0), jnp.where(attr_row < 4, pltpu.roll(v, 2, 0), 0.0))

    def window_rows(which, row, rows, windows):
        sizes = [48 if w < 4 else CORNER for w in windows]
        place = jnp.concatenate(
            [(slots[w & 1 if w < 4 else 0][0:n] == rk[w, pl.ds(row, 1), :]).astype(F32) for w, n in zip(windows, sizes)], axis=0)
        turned = lax.dot_general(place.astype(BF16), rows, (((1,), (1,)), ((), ())), preferred_element_type=F32)
        turned = turned.astype(BF16)
        at = 0
        for w, n in zip(windows, sizes):
            start = row * WINDOW_ROWS + (w * EDGE_BASE if w < 4 else CORNER_BASE + (w - 4) * CORNER)
            if not isinstance(row, int):
                start = pl.multiple_of(start, 16)
            qw[pl.ds(start, n), 0:80] = turned[at:at + n]
            at += n

    def own_tiles(which):
        def some(step, carry):
            for u in range(8):
                row = step * 8 + u
                hi, mid, lo = parts(which, row)
                turned = stacked(hi, mid, lo, True).T
                rows = stacked(hi, mid, lo).astype(BF16)
                qs[pl.ds(pl.multiple_of(row * 128, 128), 128), 0:80] = turned.astype(BF16)
                window_rows(which, row, rows, range(8))
                with_hi, with_mid = 2.0 * partner(hi), 2.0 * partner(mid)
                own = jnp.where(attr_row == 5, -2.0, with_hi)
                marked = 16.0 * jnp.where(attr_row < 2, with_hi, jnp.where(attr_row < 4, pltpu.roll(with_mid, 2, 0), 0.0))
                columns = []
                for a, scale in ((0, 1.0), (1, 1.0), (5, -2.0), (4, 1.0)):
                    ends = [jnp.where(attr_row == a, v * scale, 0.0) for v in (hi, mid, lo)]
                    if a == 5:
                        start = [own, own, jnp.where(attr_row == 5, -2.0, 0.0), with_mid, with_mid,
                                 jnp.where(attr_row < 4, -32.0, 0.0), marked]
                    else:
                        one = jnp.where(attr_row == a, 1.0 if a == 4 else -1.0, 0.0)
                        start = [one, one, one, zero8, zero8, zero8,
                                 jnp.where(attr_row == a, DEAD if a == 4 else -16.0, 0.0)]
                    columns.append(jnp.concatenate(start + ends, axis=0))
                rhs[row] = jnp.concatenate(columns, axis=1).astype(BF16)
            return carry
        lax.fori_loop(0, 4, some, 0)

    def halo_tile(which, row, windows):
        hi, mid, lo = parts(which, row)
        window_rows(which, row, stacked(hi, mid, lo).astype(BF16), windows)

    def halo_tiles(which, beside=None):
        dots((ext, ext2)[which], 32, 128)
        rank(which, 32, 48, (2, 4, 6))
        rank(which, 48, 64, (3, 5, 7))
        rank(which, 64, 96, (0, 4, 5))
        rank(which, 96, 128, (1, 6, 7))

        def some(step, carry):
            if beside is not None:
                beside(step)
            for u in range(4):
                halo_tile(which, 32 + step * 4 + u, (2, 4, 6))
                halo_tile(which, 48 + step * 4 + u, (3, 5, 7))
            return carry
        lax.fori_loop(0, 4, some, 0)
        for c in range(4):
            halo_tile(which, 64 + 8 * c + 7, (0, 4, 5))
            halo_tile(which, 96 + 8 * c, (1, 6, 7))

    lane16 = iota((16, 128), 1)
    half = iota((16, 128), 0) < 8

    lost = rank(0, 0, 32)
    own_tiles(0)

    unlisted = jnp.where(lane16 == 52, 1.0, 0.0)

    def by_offset(low, di, dj, rest):
        lane = lane16 - low
        inside = (lane >= 0) & (lane < 4)
        return jnp.where(inside, jnp.where((lane & 1) == 0, float(di), float(dj)), rest)

    def contact_rows(first, last, own_part=True, border_part=True, ahead=None):

        def step(four, carry):
            if ahead is not None:
                pl.when(four == 1)(ahead)
            for u, j in ((0, 0), (0, 1), (1, 0), (1, 1), (2, 0), (2, 1), (3, 0), (3, 1)):
                i = four * 4 + u
                t = j * 16 + i
                right = rhs[t]

                def mark_of(n):
                    di, dj = OFFSETS[n]
                    base = by_offset(48, di, dj, 0.0)
                    return base + unlisted * (1 - pat[n, j, i]).astype(F32)

                def times(di, dj):
                    return by_offset(40, di, dj, 1.0).astype(BF16)

                def border(w):
                    di, dj = WINDOWS[w]
                    row = ext_row(i + di, j + dj)
                    n = 48 if w < 4 else CORNER
                    start = row * WINDOW_ROWS + (w * EDGE_BASE if w < 4 else CORNER_BASE + (w - 4) * CORNER)
                    block, factor = qw[pl.ds(pl.multiple_of(start, 16), n), :], times(di, dj)
                    return [block[c:c + 16] * factor for c in range(0, n, 16)], mark_of(3 * (di + 1) + dj + 1)

                def edges_of(w):
                    (one, mark1), (two, mark2) = border(w), border(w + 1)
                    both = one[2] + two[2] + jnp.where(half, mark1, mark2).astype(BF16)
                    mark1, mark2 = mark1.astype(BF16), mark2.astype(BF16)
                    return [one[0] + mark1, one[1] + mark1, two[0] + mark2, two[1] + mark2, both]

                def corner(w):
                    (block,), here = border(w)
                    return block + here.astype(BF16)

                groups = []
                if own_part:
                    own = qs[pl.ds(pl.multiple_of(t * 128, 128), 128), :]
                    here = mark_of(4).astype(BF16)
                    groups += [own[c:c + 16] + here for c in range(0, 128, 16)]
                if border_part:
                    groups += edges_of(0) + edges_of(2) + [corner(w) for w in range(4, 8)]
                got = jnp.dot(jnp.concatenate(groups, axis=0)[:, 0:80], right, preferred_element_type=F32)
                rz, rx = got[:, 0:128], got[:, 128:256]
                inv = lax.rsqrt(rz * rz + rx * rx + 0.0001)
                push = jnp.maximum(got[:, 384:512] * inv - 1.0, 0.0) * (40.0 + got[:, 256:384] * inv)
                count = got.shape[0] // 8
                fz = jnp.sum((push * rz).reshape(count, 8, 128), axis=0)
                fx = jnp.sum((push * rx).reshape(count, 8, 128), axis=0)
                at_z, at_x = pl.ds(pl.multiple_of(t * 8, 8), 8), pl.ds(pl.multiple_of(t * 8 + 256, 8), 8)
                if not own_part:
                    fz, fx = fz + frc[at_z, :], fx + frc[at_x, :]
                frc[at_z, :], frc[at_x, :] = fz, fx
            return carry
        lax.fori_loop(first // 4, last // 4, step, 0)

    def forces():
        return [sum(frc[pl.ds(k * 256 + r, 32, stride=8), :] for r in range(8)) for k in range(2)]

    phase_end = reduce_end
    index = idx[...]
    share_z = frac[0].astype(F32) / 1024.0
    share_x = frac[1].astype(F32) / 1024.0
    wts[0] = (index >> 4).astype(F32)
    wts[1] = (index & 15).astype(F32)
    wts[2], wts[3] = 1.0 - share_z, share_z
    for n, share in ((4, 1.0 - share_x), (6, share_x)):
        high = share.astype(BF16).astype(F32)
        wts[n], wts[n + 1] = high, share - high
    c64 = iota((64, 128), 0).astype(F32)
    r16 = iota((16, 128), 0).astype(F32)

    def weigh(r, t4, t):
        def get(n):
            return wts[n, pl.ds(r, 1), :]
        column, row = get(1) + (16.0 * t4), get(0)
        here, there = c64 == column, c64 == column + 1.0
        wx[t, 0:64, :] = jnp.where(here, get(4), jnp.where(there, get(6), 0.0)).astype(BF16)
        wx[t, 64:128, :] = jnp.where(here, get(5), jnp.where(there, get(7), 0.0)).astype(BF16)
        wz[t] = jnp.where(r16 == row, get(2), jnp.where(r16 == row + 1.0, get(3), 0.0))

    def some_weights(h, carry):
        for t in range(2):
            for j in range(2):
                weigh(4 * h + 2 * t + j, t * 2 + j, 4 * h + 2 * t + j)
        return carry

    lax.fori_loop(0, 8, some_weights, 0)
    contact_rows(0, EARLY, True, False)

    for c in pieces:
        c.wait()
    lane32 = iota((32, 128), 1)

    def sample(h):
        field = gv[h]
        high = field.astype(BF16).astype(F32)
        both = jnp.where(lane32 < 64, high, field - high).astype(BF16)
        for t in range(2):
            for j in range(2):
                r = 4 * h + 2 * t + j
                whi, wlo = wx[r, 0:64, :], wx[r, 64:128, :]
                right = jnp.concatenate([jnp.concatenate([whi, whi], axis=0),
                                         jnp.concatenate([wlo, wlo], axis=0)], axis=1)
                got = jnp.dot(both, right, preferred_element_type=F32)
                got = got[:, 0:128] + got[:, 128:256]
                for k in range(2):
                    itp[k, pl.ds(j * 16 + 2 * h + t, 1), :] = jnp.sum(
                        wz[r] * got[k * 16:(k + 1) * 16], axis=0, keepdims=True)

    def two_samples(step):
        sample(2 * step)
        sample(2 * step + 1)

    halo_end(halos)
    halo_tiles(0, two_samples)

    last_phase = reduce_copies(0, 1)

    def pass_maximum():
        phase_end(0, 0, phase)
        reduce_go(0, 1, last_phase)

    contact_rows(0, EARLY, False, True, pass_maximum)
    contact_rows(EARLY, 16)
    phase_end(0, 1, last_phase)
    step = 0.2 / mv[2][0:1, :]
    drag = by_column(coef)
    radius = ext[4, 0:32, :]
    alive = jnp.where(radius > 0.0, 1.0, 0.0)
    inverse = jnp.where(radius > 0.0, 0.36 / (radius * radius), 0.0)
    force = forces()
    drags = []
    slack = NEAR[1][1]
    for k in range(2):
        speed = ext[2 + k, 0:32, :]
        drag1 = drag * (itp[k] - speed)
        speed2 = speed + step * (inverse * (force[k] + drag1) - (alive if k == 0 else 0.0))
        place2 = ext[k, 0:32, :] + step * speed2
        ext2[k, 0:32, :] = place2
        inside = (place2 >= -slack) & (place2 <= 16.0 + slack)
        lost = lost + jnp.where(inside, 0.0, alive)
        ext2[2 + k, 0:32, :] = speed2
        drag2 = drag * (itp[k] - speed2)
        drags.append((drag1, drag2))
    ext2[4, 0:32, :] = radius
    dots(ext2, 0, 32)
    halos = halo_start(1)
    bad = lost + rank(1, 0, 32)
    sums = []
    for k in range(2):
        drag1, drag2 = drags[k]
        mean = 0.5 * (alive * drag1 + alive * drag2)
        itp[k] = mean
        itp[2 + k] = drag2
        sums.append(jnp.sum(jnp.sum(mean, axis=1, keepdims=True), axis=0, keepdims=True))
    bad = jnp.sum(jnp.sum(bad, axis=1, keepdims=True), axis=0, keepdims=True)
    sv[0] = jnp.where(attr_row == 0, sums[0], jnp.where(attr_row == 1, sums[1], bad))
    sum_phase = reduce_start(1, 0)

    def spread(h):
        total = jnp.zeros((64, 128), F32)
        for t in range(2):
            for j in range(2):
                r = 4 * h + 2 * t + j
                m0 = itp[0, pl.ds(j * 16 + 2 * h + t, 1), :]
                m1 = itp[1, pl.ds(j * 16 + 2 * h + t, 1), :]
                lhs = jnp.concatenate([wz[r] * m0, wz[r] * m1], axis=0)
                high = lhs.astype(BF16)
                low = (lhs - high.astype(F32)).astype(BF16)
                total = total + lax.dot_general(
                    jnp.concatenate([high, low], axis=0), wx[r],
                    (((1,), (1,)), ((), ())), preferred_element_type=F32)
        total = total[0:32] + total[32:64]
        dp[h] = total + pltpu.roll(total, 64, 1)

    lax.fori_loop(0, 8, lambda h, carry: (spread(h), carry)[1], 0)
    pieces = pieces_start(1)
    own_tiles(1)
    halo_end(halos)
    halo_tiles(1)

    phase_end(1, 0, sum_phase)
    last_sum = reduce_start(1, 1)
    contact_rows(0, 16)
    force = forces()
    step = 0.2 / mv[2][0:1, :]
    radius = ext2[4, 0:32, :]
    alive = jnp.where(radius > 0.0, 1.0, 0.0)
    inverse = jnp.where(radius > 0.0, 0.36 / (radius * radius), 0.0)
    for k in range(2):
        speed = ext2[2 + k, 0:32, :]
        speed2 = speed + step * (inverse * (force[k] + itp[2 + k]) - (alive if k == 0 else 0.0))
        place2 = (ext2[k, 0:32, :] + step * speed2) * 0.0625
        for j in range(2):
            part[k, pl.ds(j, 16, stride=2), :] = place2[j * 16:(j + 1) * 16]
            part[2 + k, pl.ds(j, 16, stride=2), :] = speed2[j * 16:(j + 1) * 16]
    for c in edges + lists:
        c.wait()

    @pl.when(ax < N_ACROSS - 1)
    def _():
        to_right.wait_send()
        to_left.wait_recv()

    @pl.when(ax > 0)
    def _():
        to_left.wait_send()
        to_right.wait_recv()

    for c in pieces:
        c.wait()
    phase_end(1, 1, last_sum)
    flag[...] = sv[2][2:3, 0:1]
    gas_step_update(gas, visc, gr, gc, dv, sv.at[2], mv.at[2], out)


def fused(gas, visc, pos, vel, rad, coef, counts_t, pattern_t, idx, frac):
    dma = pltpu.SemaphoreType.DMA
    return pl.pallas_call(
        fused_kernel,
        out_shape=[jax.ShapeDtypeStruct((4, 32, 128), F32), jax.ShapeDtypeStruct((2, 32, 256), F32),
                   jax.ShapeDtypeStruct((1, 1), F32), jax.ShapeDtypeStruct((9, 2, 16), jnp.int32),
                   jax.ShapeDtypeStruct((2, 16), jnp.int32)],
        in_specs=[pl.BlockSpec(memory_space=pltpu.HBM)] * 10,
        out_specs=[VMEM_SPEC] * 3 + [pl.BlockSpec(memory_space=pltpu.HBM)] * 2,
        scratch_shapes=[
            pltpu.VMEM((2, 32, 256), F32), pltpu.VMEM((32, 256), F32),
            pltpu.VMEM((2, 32, 128), F32), pltpu.VMEM((2, 32, 128), F32), pltpu.VMEM((32, 128), F32),
            pltpu.VMEM((32, 128), F32), pltpu.VMEM((32, 128), jnp.int32), pltpu.VMEM((2, 32, 128), jnp.int32),
            pltpu.SMEM((9, 2, 16), jnp.int32), pltpu.SMEM((2, 16), jnp.int32), dma((12,)),
            pltpu.VMEM((8, 128, 128), F32), pltpu.VMEM((8, 128, 128), F32),
            pltpu.VMEM((8, 32, 128), F32), pltpu.VMEM((8, 32, 128), F32),
            pltpu.VMEM((8, 32, 128), F32), pltpu.VMEM((8, 32, 128), F32),
            pltpu.VMEM((2, 2, 8, 256), F32), pltpu.VMEM((2, 2, 32, 128), F32),
            pltpu.VMEM((2, 32, 8, 128), F32), pltpu.VMEM((3, 8, 128), F32),
            pltpu.VMEM((2, 32, 8, 128), F32), pltpu.VMEM((3, 8, 128), F32),
            pltpu.VMEM((8, 128, 128), F32), pltpu.VMEM((32 * 128, 128), BF16),
            pltpu.VMEM((128 * WINDOW_ROWS, 128), BF16), pltpu.VMEM((32, 80, 512), BF16),
            pltpu.VMEM((512, 128), F32), pltpu.VMEM((4, 32, 128), F32), pltpu.VMEM((8, 32, 128), F32),
            pltpu.VMEM((32, 128, 128), BF16), pltpu.VMEM((32, 16, 128), F32),
            dma((2, 10)), dma((2, 10)), dma((2, 8)), dma((2, 8)), dma((2, 2, 32)), dma((2, 2, 32)),
            dma((4,)), dma((4,)),
        ],
        compiler_params=pltpu.CompilerParams(collective_id=2, has_side_effects=True),
        name="interval",
    )(gas, visc, pos, vel, rad, coef, idx, frac, pattern_t, counts_t)


def body(gas, visc, pos, vel, rad, coef, counts, pattern, idx, frac):
    pos, vel, frac = (x.reshape(2, 32, 128) for x in (pos, vel, frac))
    rad, coef, idx = (x.reshape(32, 128) for x in (rad, coef, idx))
    args = (gas, visc, pos, vel, rad, coef, counts.T, pattern.transpose(2, 1, 0), idx, frac)
    part, out, flag, pattern_t, counts_t = fused(*args)
    args = args[:6] + (counts_t, pattern_t) + args[8:]
    part, out = lax.cond(flag[0, 0] > 0.0, lambda p, o: tuple(general(*args)), lambda p, o: (p, o), part, out)
    return part.reshape(4, 16, 2, 128), out


def solution(mesh):
    return jax.shard_map(
        body,
        mesh=mesh,
        in_specs=(
            P(None, ALONG_GAS, "across"),
            P(ALONG_GAS, "across"),
            P(None, "along", ACROSS_GAS, None),
            P(None, "along", ACROSS_GAS, None),
            P("along", ACROSS_GAS, None),
            P("along", ACROSS_GAS, None),
            P("along", ACROSS_GAS),
            P("along", ACROSS_GAS, None),
            P("along", ACROSS_GAS, None),
            P(None, "along", ACROSS_GAS, None),
        ),
        out_specs=(P(None, "along", ACROSS_GAS, None), P(None, ALONG_GAS, "across")),
        check_vma=False,
    )
```

```python
import functools

import jax
import jax.numpy as jnp
from jax import lax
from jax.experimental import pallas as pl
from jax.experimental.pallas import tpu as pltpu
from jax.sharding import PartitionSpec as P

ALONG_GAS = ("along", "gas")
ACROSS_GAS = ("across", "gas")
MESH_ID = pl.DeviceIdType.MESH
OFFSETS = [(-1, -1), (-1, 0), (-1, 1), (0, -1), (0, 0), (0, 1), (1, -1), (1, 0), (1, 1)]
DEAD = -16384.0
F32 = jnp.float32
BF16 = jnp.bfloat16
STRIDE = 136
BLOCK, BLOCK_BITS = 64, 6
EMPTY = 1344
REACH = 2.4
MOVE_LIMIT = int((REACH - 1.9) * 4096)
VMEM_SPEC = pl.BlockSpec(memory_space=pltpu.VMEM)
SMEM_SPEC = pl.BlockSpec(memory_space=pltpu.SMEM)
N_ACROSS, N_ALONG, N_GAS = 4, 8, 8


def iota(shape, dim):
    return lax.broadcasted_iota(jnp.int32, shape, dim)


def ext_row(ii, jj):
    base = {-1: 32, 0: 0, 1: 16, 2: 48}[jj]
    return jnp.where(ii < 0, 64 + 8 * (jj + 1) + 7, jnp.where(ii > 15, 96 + 8 * (jj + 1), base + ii))


def by_column(ref, *lead):
    return jnp.concatenate([ref[(*lead, pl.ds(0, 16, stride=2), slice(None))],
                            ref[(*lead, pl.ds(1, 16, stride=2), slice(None))]], axis=0)


def prepare_state(st, pos, vel, rad, counts):
    row32 = iota((32, 128), 0)
    slot = iota((32, 128), 1)
    cnt = jnp.zeros((32, 128), jnp.int32)
    for j in range(2):
        for i in range(16):
            cnt = jnp.where(row32 == j * 16 + i, counts[j, i], cnt)
    alive = slot < cnt
    z, x = by_column(pos, 0) * 16.0, by_column(pos, 1) * 16.0
    st[0, 0:32, :], st[1, 0:32, :] = z, x
    st[2, 0:32, :], st[3, 0:32, :] = by_column(vel, 0), by_column(vel, 1)
    st[4, 0:32, :] = jnp.where(alive, by_column(rad), DEAD)
    low_x, high_x = x < REACH, x > 16.0 - REACH

    def three(low, mid, high):
        return jnp.where(low_x, low, jnp.where(high_x, high, mid))

    kind = jnp.where(z < REACH, three(0, 1, 2), jnp.where(z > 16.0 - REACH, three(6, 5, 4), three(7, 8, 3)))
    kind = jnp.where(alive, kind, 9)
    member = jnp.concatenate([jnp.where(kind == c, 1.0, 0.0) for c in range(9)], axis=0).astype(BF16)
    before = jnp.where((iota((128, 256), 0) < iota((128, 256), 1)) | (iota((128, 256), 1) >= 128), 1.0, 0.0)
    ranks = jnp.dot(member, before.astype(BF16), preferred_element_type=F32)
    rank = jnp.full((32, 128), -1.0, F32)
    start = [jnp.zeros((32, 128), F32)]
    for c in range(9):
        here = ranks[c * 32:(c + 1) * 32]
        rank = jnp.where(kind == c, start[c] + here[:, 0:128], rank)
        start.append(start[c] + here[:, 128:256])
    st[5, 0:32, :] = rank
    start = [v.astype(jnp.int32) for v in start]
    wrap = ((start[1] + 7) & -8) > start[6]
    zero = jnp.zeros((32, 128), jnp.int32)
    windows = [(start[4], start[5]), (start[4], start[7]), (start[6], start[7]), (start[2], start[5]),
               (zero, start[9]), (jnp.where(wrap, 0, start[6]), start[8]), (start[2], start[3]),
               (zero, start[3]), (zero, start[1]), (zero, jnp.where(wrap, 0, start[1]))]
    table = zero
    for w, (low, high) in enumerate(windows):
        table = jnp.where(slot == 2 * w, low, jnp.where(slot == 2 * w + 1, (high - low + 7) & -8, table))
    st[6, 0:32, :] = table.astype(F32)


def prep_kernel(gas, visc, pos, vel, rad, counts, st, gp, mx):
    rate = jnp.abs(gas[0]) + jnp.abs(gas[1]) + 4.0 * visc[...]
    top = jnp.max(jnp.max(rate, axis=1, keepdims=True), axis=0, keepdims=True)
    mx[...] = jnp.broadcast_to(top, (8, 128))
    lane = iota((16, 128), 1)
    for g in range(N_GAS):
        blk = slice((g // 4) * 128, (g // 4) * 128 + 128)
        off = (g % 4) * 32
        for k in range(2):
            low = gas[k, 0:16, blk]
            high = gas[k, 16:32, blk]
            low = pltpu.roll(low, (128 - off) % 128, 1) if off else low
            shift = (160 - off) % 128
            high = pltpu.roll(high, shift, 1) if shift else high
            piece = jnp.where(lane < 32, low, jnp.where(lane < 64, high, 0.0))
            gp[g, k * 16:(k + 1) * 16, :] = piece
    prepare_state(st, pos, vel, rad, counts)
    st[7] = jnp.zeros((32, 128), F32)


def comm_kernel(first, *refs):
    if first:
        (st, pc, mx, gas, ext, pv, red, gr, gc, mb, m1, m2,
         own_sem, hs, hr, ps, pr, rs, rr, es, er) = refs
    else:
        (st, pc, mx, ext, pv, red, mb, m1, m2,
         own_sem, hs, hr, ps, pr, rs, rr) = refs
    ax, al, g = lax.axis_index("across"), lax.axis_index("along"), lax.axis_index("gas")
    up, down = lax.rem(al + 1, N_ALONG), lax.rem(al + N_ALONG - 1, N_ALONG)
    lin = ax * N_GAS + g
    has_left, has_right = lin > 0, lin < N_ACROSS * N_GAS - 1
    left = jnp.maximum(lin - 1, 0)
    right = jnp.minimum(lin + 1, N_ACROSS * N_GAS - 1)

    def col(index, along):
        return {"across": lax.div(index, N_GAS), "along": along, "gas": lax.rem(index, N_GAS)}

    slab = al * N_GAS + g
    slabs = N_ALONG * N_GAS
    after, before = lax.rem(slab + 1, slabs), lax.rem(slab + slabs - 1, slabs)

    def slab_id(index):
        return {"across": ax, "along": lax.div(index, N_GAS), "gas": lax.rem(index, N_GAS)}

    barrier = pltpu.get_barrier_semaphore()

    def greet(device):
        pl.semaphore_signal(barrier, inc=1, device_id=device, device_id_type=MESH_ID)

    for k in range(1, N_ACROSS):
        greet({"across": lax.rem(ax + k, N_ACROSS)})
    for k in range(1, N_GAS):
        greet({"gas": lax.rem(g + k, N_GAS)})
    for k in range(1, N_ALONG):
        greet({"along": lax.rem(al + k, N_ALONG)})
    expect = N_ACROSS + N_GAS + N_ALONG - 3
    if first:
        greet(slab_id(after))
        greet(slab_id(before))
        expect += 2

    @pl.when(has_left)
    def _():
        for along in (down, al, up):
            greet(col(left, along))

    @pl.when(has_right)
    def _():
        for along in (down, al, up):
            greet(col(right, along))

    own = pltpu.make_async_copy(st, ext.at[:, pl.ds(0, 32)], own_sem.at[0])
    own.start()
    own_piece = pltpu.make_async_copy(pc.at[g], pv.at[g], own_sem.at[1])
    own_piece.start()

    @pl.when(jnp.logical_not(has_left))
    def _():
        ext[:, 32:48, :] = jnp.zeros((8, 16, 128), F32)
        ext[:, 64:72, :] = jnp.zeros((8, 8, 128), F32)
        ext[:, 96:104, :] = jnp.zeros((8, 8, 128), F32)

    @pl.when(jnp.logical_not(has_right))
    def _():
        ext[:, 48:64, :] = jnp.zeros((8, 16, 128), F32)
        ext[:, 88:96, :] = jnp.zeros((8, 8, 128), F32)
        ext[:, 120:128, :] = jnp.zeros((8, 8, 128), F32)

    if first:
        @pl.when(ax == 0)
        def _():
            gc[0] = jnp.zeros((2, 32, 128), F32)

        @pl.when(ax == N_ACROSS - 1)
        def _():
            gc[1] = jnp.zeros((2, 32, 128), F32)

    sides = jnp.where(has_left, 3, 0) + jnp.where(has_right, 3, 0)
    pl.semaphore_wait(barrier, expect + sides)

    def remote(src, dst, send, recv, device):
        return pltpu.make_async_remote_copy(
            src_ref=src, dst_ref=dst, send_sem=send, recv_sem=recv,
            device_id=device, device_id_type=MESH_ID,
        )

    def reduce_sends(phase, src, axis, me, size):
        out = []
        for k in range(1, size):
            out.append(remote(src, mb.at[phase, me], rs.at[phase, k], rr.at[phase, k],
                              {axis: lax.rem(me + k, size)}))
        for c in out:
            c.start()
        return out

    phase0 = reduce_sends(0, mx, "across", ax, N_ACROSS)

    def halo(c, src_rows, size, dst_row, device):
        return remote(st.at[pl.ds(0, 7), pl.ds(src_rows, size)],
                      ext.at[pl.ds(0, 7), pl.ds(dst_row, size)], hs.at[c], hr.at[c], device)

    lefts = [halo(0, 0, 16, 48, col(left, al)),
             halo(1, 8, 8, 64 + 24, col(left, up)),
             halo(2, 0, 8, 96 + 24, col(left, down))]
    rights = [halo(3, 16, 16, 32, col(right, al)),
              halo(4, 24, 8, 64, col(right, up)),
              halo(5, 16, 8, 96, col(right, down))]
    rows = [halo(6, 8, 8, 64 + 8, {"along": up}),
            halo(7, 24, 8, 64 + 16, {"along": up}),
            halo(8, 0, 8, 96 + 8, {"along": down}),
            halo(9, 16, 8, 96 + 16, {"along": down})]

    @pl.when(has_left)
    def _():
        for c in lefts:
            c.start()

    @pl.when(has_right)
    def _():
        for c in rights:
            c.start()

    for c in rows:
        c.start()
    pieces = []
    for k in range(1, N_GAS):
        peer = lax.rem(g + k, N_GAS)
        c = remote(pc.at[peer], pv.at[g], ps.at[k], pr.at[k], {"gas": peer})
        c.start()
        pieces.append(c)
    if first:
        edges = [remote(gas.at[:, pl.ds(24, 8)], gr.at[0], es.at[0], er.at[0], slab_id(after)),
                 remote(gas.at[:, pl.ds(0, 8)], gr.at[1], es.at[1], er.at[1], slab_id(before))]
        for c in edges:
            c.start()
        to_right = remote(gas.at[:, :, pl.ds(128, 128)], gc.at[0], es.at[2], er.at[2],
                          {"across": jnp.minimum(ax + 1, N_ACROSS - 1)})
        to_left = remote(gas.at[:, :, pl.ds(0, 128)], gc.at[1], es.at[3], er.at[3],
                         {"across": jnp.maximum(ax - 1, 0)})

        @pl.when(ax < N_ACROSS - 1)
        def _():
            to_right.start()

        @pl.when(ax > 0)
        def _():
            to_left.start()

    def combine(phase, mine, me, size, copies):
        for c in copies:
            c.wait_recv()
        mb[phase, me] = mine
        total = mb[phase, 0]
        for k in range(1, size):
            total = jnp.maximum(total, mb[phase, k]) if first else total + mb[phase, k]
        return total

    m1[...] = combine(0, mx[...], ax, N_ACROSS, phase0)
    phase1 = reduce_sends(1, m1, "gas", g, N_GAS)
    m2[...] = combine(1, m1[...], g, N_GAS, phase1)
    phase2 = reduce_sends(2, m2, "along", al, N_ALONG)
    red[...] = combine(2, m2[...], al, N_ALONG, phase2)

    own.wait()
    own_piece.wait()
    for c in phase0 + phase1 + phase2:
        c.wait_send()
    for c in rows + pieces:
        c.wait()

    @pl.when(has_left)
    def _():
        for c in lefts:
            c.wait_send()
        for c in rights:
            c.wait_recv()

    @pl.when(has_right)
    def _():
        for c in rights:
            c.wait_send()
        for c in lefts:
            c.wait_recv()

    if first:
        for c in edges:
            c.wait()

        @pl.when(ax < N_ACROSS - 1)
        def _():
            to_right.wait_send()
            to_left.wait_recv()

        @pl.when(ax > 0)
        def _():
            to_left.wait_send()
            to_right.wait_recv()


def exchange(first, st, pc, mx, gas=None):
    out_shape = [jax.ShapeDtypeStruct((8, 128, 128), F32),
                 jax.ShapeDtypeStruct((8, 32, 128), F32),
                 jax.ShapeDtypeStruct((8, 128), F32)]
    scratch = [pltpu.VMEM((3, 8, 8, 128), F32), pltpu.VMEM((8, 128), F32), pltpu.VMEM((8, 128), F32),
               pltpu.SemaphoreType.DMA((2,)),
               pltpu.SemaphoreType.DMA((10,)), pltpu.SemaphoreType.DMA((10,)),
               pltpu.SemaphoreType.DMA((8,)), pltpu.SemaphoreType.DMA((8,)),
               pltpu.SemaphoreType.DMA((3, 8)), pltpu.SemaphoreType.DMA((3, 8))]
    args = [st, pc, mx]
    if first:
        args.append(gas)
        out_shape += [jax.ShapeDtypeStruct((2, 2, 8, 256), F32), jax.ShapeDtypeStruct((2, 2, 32, 128), F32)]
        scratch += [pltpu.SemaphoreType.DMA((4,)), pltpu.SemaphoreType.DMA((4,))]
    return pl.pallas_call(
        functools.partial(comm_kernel, first),
        out_shape=out_shape,
        in_specs=[VMEM_SPEC] * len(args),
        out_specs=[VMEM_SPEC] * len(out_shape),
        scratch_shapes=scratch,
        compiler_params=pltpu.CompilerParams(collective_id=0 if first else 1, has_side_effects=True),
        name="exchange_first" if first else "exchange_second",
    )(*args)


def split3(x):
    hi = x.astype(BF16).astype(F32)
    rest = x - hi
    mid = rest.astype(BF16).astype(F32)
    return hi, mid, rest - mid


def contact_forces(ext, pat, meta, ints, qt, lst, rhs, frc, sem):
    ints[...] = ext[6 * 128:7 * 128, :].astype(jnp.int32)
    to_smem = pltpu.make_async_copy(ints, meta, sem)
    to_smem.start()
    slot = iota((128, 128), 0).astype(F32)
    attr_row = iota((8, 128), 0)
    zero8 = jnp.zeros((8, 128), F32)
    tail = jnp.concatenate([zero8, jnp.ones((24, 128), F32), zero8], axis=0)

    def parts(row):
        block = ext[pl.ds(row, 8, stride=128), :]
        return split3(jnp.where(attr_row < 5, block, 0.0))

    def transposed(row):
        hi, mid, lo = parts(row)
        rows = jnp.concatenate([hi, mid, lo, tail], axis=0).astype(BF16)
        place = (slot == ext[pl.ds(row + 5 * 128, 1), :]).astype(F32).astype(BF16)
        turned = lax.dot_general(place, rows, (((1,), (1,)), ((), ())), preferred_element_type=F32)
        start = row * STRIDE if isinstance(row, int) else pl.multiple_of(row * STRIDE, 8)
        qt[pl.ds(start, 128), 0:64] = turned
        start = start + 128 if isinstance(row, int) else pl.multiple_of(start + 128, 8)
        qt[pl.ds(start, 8), :] = zero8

    def some(step, carry):
        for u in range(4):
            transposed(step * 4 + u)
        return carry

    lax.fori_loop(0, 16, some, 0)
    for c in range(4):
        transposed(64 + 8 * c + 7)
        transposed(96 + 8 * c)

    block_of = iota((32, 640), 1) >> 7
    row_of = iota((32, 640), 0)
    attr_of = row_of & 7
    own_scale = jnp.where(block_of < 2, -1.0, jnp.where(block_of < 4, 2.0, 1.0))
    const = jnp.where((attr_of == block_of) & (row_of < 24), own_scale, 0.0)
    const = jnp.where((row_of == 24) & (block_of == 0) | (row_of == 25) & (block_of == 1), -16.0, const)
    for u in range(2):
        rhs[u, 0:32, :] = const.astype(BF16)
        lst[u, EMPTY:EMPTY + BLOCK, :] = jnp.zeros((BLOCK, 128), F32)
    to_smem.wait()
    lane = iota((8, 128), 1)

    def row_step(i, carry):
        blocks = []
        for j in range(2):
            work = lst.at[j]
            mine = j * 16 + i
            hi, mid, lo = parts(mine)
            columns = []
            for a in range(5):
                keep = attr_row == a
                scale = 1.0 if a in (0, 1, 4) else -2.0
                columns.append(jnp.concatenate(
                    [jnp.where(keep, hi * scale, 0.0), jnp.where(keep, mid * scale, 0.0),
                     jnp.where(keep, lo * scale, 0.0), zero8], axis=0))
            rhs[j, 32:64, :] = jnp.concatenate(columns, axis=1).astype(BF16)
            moved = meta[mine, 20]
            off = i * 0
            over = i * 0
            windows = []
            for w in (4, 0, 1, 2, 3, 5, 6, 7, 8, 9):
                di, dj = OFFSETS[5 if w == 9 else w]
                row = ext_row(i + di, j + dj)
                first, size = meta[row, 2 * w], meta[row, 2 * w + 1]
                if w != 4:
                    near = moved + meta[row, 20] <= MOVE_LIMIT
                    first = jnp.where(near, first, 0)
                    size = jnp.where(near, size, 0 if w == 9 else meta[row, 9])
                size = size * pat[5 if w == 9 else w, j, i]
                mark = jnp.where(lane == 24, float(di), jnp.where(lane == 25, float(dj), 0.0))
                start = row * STRIDE + first
                chunks = 16 if w == 4 else 4 if w in (1, 3, 5, 7) else 1
                for c in range(chunks):
                    work[pl.ds(pl.multiple_of(off + c * 8, 8), 8), :] = qt[pl.ds(start + c * 8, 8), :] + mark
                windows.append((start, size, mark))
                off = off + size
                over = jnp.maximum(over, size - chunks * 8)

            @pl.when(over > 0)
            def _():
                to = i * 0
                for start, size, mark in windows:
                    def copy(c, carry, start=start, mark=mark, to=to):
                        work[pl.ds(pl.multiple_of(to + c * 8, 8), 8), :] = qt[pl.ds(start + c * 8, 8), :] + mark
                        return carry
                    lax.fori_loop(0, size >> 3, copy, 0)
                    to = to + size

            for c in range(BLOCK // 8):
                work[pl.ds(pl.multiple_of(off + c * 8, 8), 8), :] = zero8
            blocks.append((off + BLOCK - 1) >> BLOCK_BITS)
        right = [rhs[0], rhs[1]]

        def block(b, acc):
            out = []
            for j in range(2):
                at = jnp.where(b < blocks[j], b * BLOCK, EMPTY)
                q = lst[j, pl.ds(pl.multiple_of(at, 8), BLOCK), 0:64].astype(BF16)
                got = jnp.dot(q, right[j], preferred_element_type=F32)
                rz, rx = got[:, 0:128], got[:, 128:256]
                dz, dx = got[:, 256:384], got[:, 384:512]
                d2 = rz * rz + rx * rx + 0.0001
                inv = lax.rsqrt(d2)
                depth = jnp.maximum(got[:, 512:640] - d2 * inv, 0.0)
                push = depth * inv * (40.0 + (dz * rz + dx * rx) * inv)
                out.append(acc[2 * j] + jnp.sum((push * rz).reshape(BLOCK // 8, 8, 128), axis=0))
                out.append(acc[2 * j + 1] + jnp.sum((push * rx).reshape(BLOCK // 8, 8, 128), axis=0))
            return tuple(out)

        acc = lax.fori_loop(0, jnp.maximum(blocks[0], blocks[1]), block, (zero8,) * 4)
        for j in range(2):
            for k in range(2):
                frc[pl.ds(pl.multiple_of(((k * 2 + j) * 16 + i) * 8, 8), 8), :] = acc[2 * j + k]
        return carry

    lax.fori_loop(0, 16, row_step, 0)
    return [sum(frc[pl.ds(k * 256 + r, 32, stride=8), :] for r in range(8)) for k in range(2)]


def first_kernel(ext, gv, rate, idx, frac, coef, pat, st2, dp, tot, dr2, inv_out,
                 meta, ints, qt, lst, rhs, frc, itp, sem):
    def weights(r, t4):
        index = idx[pl.ds(r, 1), :]
        row, column = index >> 4, index & 15
        share_z = frac[0, pl.ds(r, 1), :].astype(F32) / 1024.0
        share_x = frac[1, pl.ds(r, 1), :].astype(F32) / 1024.0
        c64 = iota((64, 128), 0) - t4 * 16
        wx = jnp.where(c64 == column, 1.0 - share_x, jnp.where(c64 == column + 1, share_x, 0.0))
        r16 = iota((16, 128), 0)
        wz = jnp.where(r16 == row, 1.0 - share_z, jnp.where(r16 == row + 1, share_z, 0.0))
        return wz, wx

    def sample(h, carry):
        field = gv[h][:, 0:64]
        for t in range(2):
            for j in range(2):
                wz, wx = weights(4 * h + 2 * t + j, t * 2 + j)
                along = jnp.dot(field, wx, precision=lax.Precision.HIGHEST, preferred_element_type=F32)
                for k in range(2):
                    itp[k, pl.ds(j * 16 + 2 * h + t, 1), :] = jnp.sum(
                        wz * along[k * 16:(k + 1) * 16], axis=0, keepdims=True)
        return carry

    lax.fori_loop(0, 8, sample, 0)
    force = contact_forces(ext, pat, meta, ints, qt, lst, rhs, frc, sem)
    step = 0.2 / rate[0:1, :]
    drag = by_column(coef)
    radius = ext[4 * 128:4 * 128 + 32, :]
    alive = jnp.where(radius > 0.0, 1.0, 0.0)
    inverse = jnp.where(radius > 0.0, 0.36 / (radius * radius), 0.0)
    inv_out[...] = inverse
    means = []
    moved = jnp.zeros((32, 128), F32)
    for k in range(2):
        place = ext[k * 128:k * 128 + 32, :]
        speed = ext[(2 + k) * 128:(2 + k) * 128 + 32, :]
        drag1 = drag * (itp[k] - speed)
        speed2 = speed + step * (inverse * (force[k] + drag1) - (alive if k == 0 else 0.0))
        st2[k] = place + step * speed2
        moved = jnp.maximum(moved, alive * jnp.abs(step * speed2))
        st2[2 + k] = speed2
        drag2 = drag * (itp[k] - speed2)
        dr2[k] = drag2
        mean = 0.5 * (alive * drag1 + alive * drag2)
        itp[k] = mean
        means.append(jnp.sum(jnp.sum(mean, axis=1, keepdims=True), axis=0, keepdims=True))
    st2[4] = radius
    st2[5] = ext[5 * 128:5 * 128 + 32, :]
    far = jnp.max(moved, axis=1, keepdims=True)
    far = jnp.where(far < 100.0, far, 100.0) * 4096.0 + 1.0
    st2[6] = jnp.where(iota((32, 128), 1) == 20, far, ext[6 * 128:6 * 128 + 32, :])
    st2[7] = jnp.zeros((32, 128), F32)
    tot[...] = jnp.where(iota((8, 128), 0) == 0, means[0], means[1])

    def spread(h, carry):
        total = jnp.zeros((32, 64), F32)
        for t in range(2):
            for j in range(2):
                wz, wx = weights(4 * h + 2 * t + j, t * 2 + j)
                m0 = itp[0, pl.ds(j * 16 + 2 * h + t, 1), :]
                m1 = itp[1, pl.ds(j * 16 + 2 * h + t, 1), :]
                lhs = jnp.concatenate([wz * m0, wz * m1], axis=0)
                total = total + lax.dot_general(lhs, wx, (((1,), (1,)), ((), ())),
                                                precision=lax.Precision.HIGHEST, preferred_element_type=F32)
        dp[h, :, 0:64] = total
        dp[h, :, 64:128] = jnp.zeros((32, 64), F32)
        return carry

    lax.fori_loop(0, 8, spread, 0)


def gas_step_update(gas, visc, gr, gc, dv, tot, rate, out):
    gas_step = 0.4 / rate[0:1, 0:1]
    lane = iota((32, 256), 1)
    row = iota((32, 256), 0)
    lane16 = iota((16, 128), 1) >> 5
    for k in range(2):
        u = gas[k]
        upper = jnp.where(row == 31, gr[1, k, 0:1, :], pltpu.roll(u, 31, 0))
        lower = jnp.where(row == 0, gr[0, k, 7:8, :], pltpu.roll(u, 1, 0))
        right = jnp.where(lane == 255, gc[1, k, :, 0:1], pltpu.roll(u, 255, 1))
        left = jnp.where(lane == 0, gc[0, k, :, 127:128], pltpu.roll(u, 1, 1))
        laplace = upper + lower + right + left - 4.0 * u
        advect = gas[0] * (upper - lower) * 0.5 + gas[1] * (right - left) * 0.5
        quads = []
        for t in range(2):
            halves = []
            for b in range(2):
                whole = None
                for q in range(4):
                    piece = dv[4 * b + q, k * 16:(k + 1) * 16, :]
                    shift = (q * 32 - t * 32) % 128
                    piece = pltpu.roll(piece, shift, 1) if shift else piece
                    whole = piece if whole is None else jnp.where(lane16 == q, piece, whole)
                halves.append(whole)
            quads.append(jnp.concatenate(halves, axis=1))
        deposit = jnp.concatenate(quads, axis=0)
        source = tot[k:k + 1, 0:1] / 2097152.0 - deposit
        out[k] = u + gas_step * (visc[...] * laplace - advect + source)


def second_kernel(ext, dv, tot, rate, dr2, inverse, gas, visc, gr, gc, pat, part, out,
                  meta, ints, qt, lst, rhs, frc, sem):
    force = contact_forces(ext, pat, meta, ints, qt, lst, rhs, frc, sem)
    step = 0.2 / rate[0:1, :]
    radius = ext[4 * 128:4 * 128 + 32, :]
    alive = jnp.where(radius > 0.0, 1.0, 0.0)
    for k in range(2):
        place = ext[k * 128:k * 128 + 32, :]
        speed = ext[(2 + k) * 128:(2 + k) * 128 + 32, :]
        speed2 = speed + step * (inverse[...] * (force[k] + dr2[k]) - (alive if k == 0 else 0.0))
        place2 = (place + step * speed2) * 0.0625
        for j in range(2):
            part[k, pl.ds(j, 16, stride=2), :] = place2[j * 16:(j + 1) * 16]
            part[2 + k, pl.ds(j, 16, stride=2), :] = speed2[j * 16:(j + 1) * 16]
    gas_step_update(gas, visc, gr, gc, dv, tot, rate, out)


CONTACT_SCRATCH = [
    pltpu.SMEM((128, 128), jnp.int32),
    pltpu.VMEM((128, 128), jnp.int32),
    pltpu.VMEM((128 * STRIDE, 128), F32),
    pltpu.VMEM((2, 1408, 128), F32),
    pltpu.VMEM((2, 64, 640), BF16),
    pltpu.VMEM((512, 128), F32),
]


def general(gas, visc, pos, vel, rad, coef, counts_t, pattern_t, idx, frac):

    def shapes(*dims):
        return [jax.ShapeDtypeStruct(d, F32) for d in dims]

    st, gp, mx = pl.pallas_call(
        prep_kernel,
        out_shape=shapes((8, 32, 128), (8, 32, 128), (8, 128)),
        in_specs=[VMEM_SPEC] * 5 + [SMEM_SPEC],
        out_specs=[VMEM_SPEC] * 3,
        name="prepare",
    )(gas, visc, pos, vel, rad, counts_t)
    ext, gv, rate, gr, gc = exchange(True, st, gp, mx, gas)
    st2, dp, tot, dr2, inverse = pl.pallas_call(
        first_kernel,
        out_shape=shapes((8, 32, 128), (8, 32, 128), (8, 128), (2, 32, 128), (32, 128)),
        in_specs=[VMEM_SPEC] * 6 + [SMEM_SPEC],
        out_specs=[VMEM_SPEC] * 5,
        scratch_shapes=CONTACT_SCRATCH + [pltpu.VMEM((2, 32, 128), F32), pltpu.SemaphoreType.DMA],
        name="first_substep",
    )(ext.reshape(1024, 128), gv, rate, idx, frac, coef, pattern_t)
    ext2, dv, total = exchange(False, st2, dp, tot)
    part, out = pl.pallas_call(
        second_kernel,
        out_shape=shapes((4, 32, 128), (2, 32, 256)),
        in_specs=[VMEM_SPEC] * 10 + [SMEM_SPEC],
        out_specs=[VMEM_SPEC] * 2,
        scratch_shapes=CONTACT_SCRATCH + [pltpu.SemaphoreType.DMA],
        name="second_substep",
    )(ext2.reshape(1024, 128), dv, total, rate, dr2, inverse, gas, visc, gr, gc, pattern_t)
    return part, out


EDGE_BASE, CORNER_BASE, WINDOW_ROWS = 48, 192, 256
CORNER = 16
WINDOWS = ((-1, 0), (1, 0), (0, -1), (0, 1), (-1, -1), (-1, 1), (1, -1), (1, 1))
NEAR = ((1.82, 0.0), (2.25, 0.43))
EDGE = 40
EARLY = 8


def fused_kernel(*refs):
    inputs, (part, out, flag, pat_copy, counts_copy), refs = refs[:10], refs[10:15], refs[15:]
    gas, visc, pos, vel, rad, coef, idx, frac, pat, counts = refs[:10]
    (in_sem, ext, ext2, gp, gv, dp, dv, gr, gc, mb, mv, sb, sv, rk, qs, qw, rhs, frc, itp, wts, wx, wz,
     hs, hr, ps, pr, rs, rr, es, er) = refs[10:]
    loads = [pltpu.make_async_copy(a, b, in_sem.at[n]) for n, (a, b) in enumerate(zip(inputs, refs[:10]))]
    for c in loads:
        c.start()
    ax, al, g = lax.axis_index("across"), lax.axis_index("along"), lax.axis_index("gas")

    def around(value, size):
        return value - jnp.where(value >= size, size, 0)

    up, down = around(al + 1, N_ALONG), around(al + N_ALONG - 1, N_ALONG)
    first_g, last_g = g == 0, g == N_GAS - 1
    has_left = jnp.logical_or(ax > 0, g > 0)
    has_right = jnp.logical_or(ax < N_ACROSS - 1, g < N_GAS - 1)
    left = (jnp.maximum(ax - jnp.where(first_g, 1, 0), 0), jnp.where(first_g, N_GAS - 1, g - 1))
    right = (jnp.minimum(ax + jnp.where(last_g, 1, 0), N_ACROSS - 1), jnp.where(last_g, 0, g + 1))

    def device(a=ax, l=al, y=g):
        return {"across": a, "along": l, "gas": y}

    def col(side, along):
        return device(a=side[0], l=along, y=side[1])

    def peer_id(axis, index):
        return device(**{{"across": "a", "along": "l", "gas": "y"}[axis]: index})

    after = device(l=jnp.where(last_g, up, al), y=jnp.where(last_g, 0, g + 1))
    before = device(l=jnp.where(first_g, down, al), y=jnp.where(first_g, N_GAS - 1, g - 1))

    barrier = pltpu.get_barrier_semaphore()

    def greet(target):
        pl.semaphore_signal(barrier, inc=1, device_id=target, device_id_type=MESH_ID)

    for k in range(1, N_ALONG):
        greet(device(l=around(al + k, N_ALONG)))
    for k in range(1, N_ACROSS):
        greet(device(a=around(ax + k, N_ACROSS)))
    for k in range(1, N_GAS):
        greet(device(y=around(g + k, N_GAS)))
    greet(after)
    greet(before)
    expect = N_ACROSS + N_GAS + N_ALONG - 3 + 2

    @pl.when(has_left)
    def _():
        for along in (down, al, up):
            greet(col(left, along))

    @pl.when(has_right)
    def _():
        for along in (down, al, up):
            greet(col(right, along))

    for c in loads:
        c.wait()
    rate = jnp.abs(gas[0]) + jnp.abs(gas[1]) + 4.0 * visc[...]
    top = jnp.max(jnp.max(rate, axis=1, keepdims=True), axis=0, keepdims=True)
    mv[0] = jnp.broadcast_to(top, (8, 128))
    lane = iota((16, 128), 1)
    for d in range(N_GAS):
        blk = slice((d // 4) * 128, (d // 4) * 128 + 128)
        off = (d % 4) * 32
        for k in range(2):
            low = gas[k, 0:16, blk]
            high = gas[k, 16:32, blk]
            low = pltpu.roll(low, (128 - off) % 128, 1) if off else low
            shift = (160 - off) % 128
            high = pltpu.roll(high, shift, 1) if shift else high
            piece = jnp.where(lane < 32, low, high)
            gp[d, k * 16:(k + 1) * 16, :] = jnp.where(lane < 64, piece, pltpu.roll(piece, 64, 1))
    row32 = iota((32, 128), 0)
    cnt = jnp.zeros((32, 128), jnp.int32)
    for j in range(2):
        for i in range(16):
            cnt = jnp.where(row32 == j * 16 + i, counts[j, i], cnt)
    ext[0, 0:32, :], ext[1, 0:32, :] = by_column(pos, 0) * 16.0, by_column(pos, 1) * 16.0
    ext[2, 0:32, :], ext[3, 0:32, :] = by_column(vel, 0), by_column(vel, 1)
    ext[4, 0:32, :] = jnp.where(iota((32, 128), 1) < cnt, by_column(rad), DEAD)

    def dots(e, low, high):
        e[5, low:high, :] = e[0, low:high, :] * e[2, low:high, :] + e[1, low:high, :] * e[3, low:high, :]

    dots(ext, 0, 32)
    for e in (ext, ext2):
        @pl.when(jnp.logical_not(has_left))
        def _():
            e[:, 32:48, :] = jnp.zeros((8, 16, 128), F32)
            e[:, 64:72, :] = jnp.zeros((8, 8, 128), F32)
            e[:, 96:104, :] = jnp.zeros((8, 8, 128), F32)

        @pl.when(jnp.logical_not(has_right))
        def _():
            e[:, 48:64, :] = jnp.zeros((8, 16, 128), F32)
            e[:, 88:96, :] = jnp.zeros((8, 8, 128), F32)
            e[:, 120:128, :] = jnp.zeros((8, 8, 128), F32)

    @pl.when(ax == 0)
    def _():
        gc[0] = jnp.zeros((2, 32, 128), F32)

    @pl.when(ax == N_ACROSS - 1)
    def _():
        gc[1] = jnp.zeros((2, 32, 128), F32)

    sides = jnp.where(has_left, 3, 0) + jnp.where(has_right, 3, 0)
    pl.semaphore_wait(barrier, expect + sides)

    def remote(src, dst, send, recv, target):
        return pltpu.make_async_remote_copy(
            src_ref=src, dst_ref=dst, send_sem=send, recv_sem=recv,
            device_id=target, device_id_type=MESH_ID,
        )

    axes = (("across", ax, N_ACROSS), ("gas", g, N_GAS), ("along", al, N_ALONG))

    def reduce_copies(which, phase):
        slots, value = ((mb, mv), (sb, sv))[which]
        axis, me, size = axes[phase]
        return [remote(value.at[phase], slots.at[phase, me], rs.at[which, phase, k], rr.at[which, phase, k],
                       peer_id(axis, around(me + k, size))) for k in range(1, size)]

    def reduce_go(which, phase, copies):
        slots, value = ((mb, mv), (sb, sv))[which]
        for c in copies:
            c.start()
        slots[phase, axes[phase][1]] = value[phase]

    def reduce_start(which, phase):
        out = reduce_copies(which, phase)
        reduce_go(which, phase, out)
        return out

    def reduce_end(which, phase, copies):
        slots, value = ((mb, mv), (sb, sv))[which]
        size = axes[phase][2]
        for c in copies:
            c.wait_recv()
        total = slots[phase, 0]
        for k in range(1, size):
            total = total + slots[phase, k] if which else jnp.maximum(total, slots[phase, k])
        value[phase + 1] = total
        for c in copies:
            c.wait_send()

    def halo_start(which):
        e, attrs = ((ext, 5), (ext2, 5))[which]

        def halo(c, src_row, size, dst_row, target):
            return remote(e.at[pl.ds(0, attrs), pl.ds(src_row, size)],
                          e.at[pl.ds(0, attrs), pl.ds(dst_row, size)], hs.at[which, c], hr.at[which, c], target)

        lefts = [halo(0, 0, 16, 48, col(left, al)),
                 halo(1, 8, 8, 64 + 24, col(left, up)),
                 halo(2, 0, 8, 96 + 24, col(left, down))]
        rights = [halo(3, 16, 16, 32, col(right, al)),
                  halo(4, 24, 8, 64, col(right, up)),
                  halo(5, 16, 8, 96, col(right, down))]
        rows = [halo(6, 8, 8, 64 + 8, device(l=up)),
                halo(7, 24, 8, 64 + 16, device(l=up)),
                halo(8, 0, 8, 96 + 8, device(l=down)),
                halo(9, 16, 8, 96 + 16, device(l=down))]

        @pl.when(has_left)
        def _():
            for c in lefts:
                c.start()

        @pl.when(has_right)
        def _():
            for c in rights:
                c.start()

        for c in rows:
            c.start()
        return lefts, rights, rows

    def halo_end(copies):
        lefts, rights, rows = copies
        for c in rows:
            c.wait()

        @pl.when(has_left)
        def _():
            for c in lefts:
                c.wait_send()
            for c in rights:
                c.wait_recv()

        @pl.when(has_right)
        def _():
            for c in rights:
                c.wait_send()
            for c in lefts:
                c.wait_recv()

    def pieces_start(which):
        src, dst = ((gp, gv), (dp, dv))[which]
        out = []
        for k in range(1, N_GAS):
            peer = around(g + k, N_GAS)
            c = remote(src.at[peer], dst.at[g], ps.at[which, k], pr.at[which, k], device(y=peer))
            c.start()
            out.append(c)
        dst[g] = src[g]
        return out

    phase = reduce_start(0, 0)
    halos = halo_start(0)
    pieces = pieces_start(0)
    edges = [remote(gas.at[:, pl.ds(24, 8)], gr.at[0], es.at[0], er.at[0], after),
             remote(gas.at[:, pl.ds(0, 8)], gr.at[1], es.at[1], er.at[1], before)]
    for c in edges:
        c.start()
    to_right = remote(gas.at[:, :, pl.ds(128, 128)], gc.at[0], es.at[2], er.at[2],
                      device(a=jnp.minimum(ax + 1, N_ACROSS - 1)))
    to_left = remote(gas.at[:, :, pl.ds(0, 128)], gc.at[1], es.at[3], er.at[3],
                     device(a=jnp.maximum(ax - 1, 0)))

    @pl.when(ax < N_ACROSS - 1)
    def _():
        to_right.start()

    @pl.when(ax > 0)
    def _():
        to_left.start()

    lists = [pltpu.make_async_copy(pat, pat_copy, in_sem.at[10]), pltpu.make_async_copy(counts, counts_copy, in_sem.at[11])]
    for c in lists:
        c.start()

    slot_row = iota((48, 128), 0)
    slots = (jnp.where(slot_row < EDGE, slot_row, -5).astype(F32),
             jnp.where(slot_row < 32, slot_row, jnp.where(slot_row < 40, -5, slot_row - 8)).astype(F32))
    attr_row = iota((8, 128), 0)
    zero8 = jnp.zeros((8, 128), F32)
    one_tail = jnp.concatenate([zero8, jnp.ones((24, 128), F32)], axis=0)
    flat = (ext.reshape(1024, 128), ext2.reshape(1024, 128))
    eye = jnp.where(iota((128, 128), 0) == iota((128, 128), 1), 1.0, 0.0).astype(BF16)
    before_slot = jnp.where(iota((128, 128), 0) < iota((128, 128), 1), 1.0, 0.0).astype(BF16)

    def rank(which, low, high, windows=range(8)):
        e = (ext, ext2)[which]
        reach, _ = NEAR[which]
        z, x, live = e[0, low:high, :], e[1, low:high, :], e[4, low:high, :] > 0.0

        def flags(cond):
            return jnp.where(cond & live, 1.0, 0.0)

        lz, hz, lx, hx = flags(z < reach), flags(z > 16.0 - reach), flags(x < reach), flags(x > 16.0 - reach)
        member = [hz, lz, hx, lx, hz * hx, hz * lx, lz * hx, lz * lx]
        size = high - low
        places = jnp.dot(jnp.concatenate([member[w] for w in windows], axis=0).astype(BF16), before_slot,
                         preferred_element_type=F32)
        lost = jnp.zeros((size, 128), F32)
        for order, w in enumerate(windows):
            place = places[order * size:(order + 1) * size]
            rk[w, low:high, :] = jnp.where(member[w] > 0.0, place, -1.0)
            lost = lost + jnp.where(place >= (EDGE if w < 4 else CORNER), member[w], 0.0)
        return lost

    def parts(which, row):
        block = flat[which][pl.ds(row, 8, stride=128), :]
        return split3(jnp.where(attr_row < 6, block, 0.0))

    def stacked(hi, mid, lo, own=False):
        shifted = jnp.where(attr_row < 2, pltpu.roll(hi, 6, 0), jnp.where(attr_row < 4, mid, 0.0))
        return jnp.concatenate([hi, mid, lo, hi, mid, zero8 if own else shifted, one_tail], axis=0)

    def partner(v):
        return jnp.where(attr_row < 2, pltpu.roll(v, 6, 0), jnp.where(attr_row < 4, pltpu.roll(v, 2, 0), 0.0))

    def window_rows(which, row, rows, windows):
        sizes = [48 if w < 4 else CORNER for w in windows]
        place = jnp.concatenate(
            [(slots[w & 1 if w < 4 else 0][0:n] == rk[w, pl.ds(row, 1), :]).astype(F32) for w, n in zip(windows, sizes)], axis=0)
        turned = lax.dot_general(place.astype(BF16), rows, (((1,), (1,)), ((), ())), preferred_element_type=F32)
        turned = turned.astype(BF16)
        at = 0
        for w, n in zip(windows, sizes):
            start = row * WINDOW_ROWS + (w * EDGE_BASE if w < 4 else CORNER_BASE + (w - 4) * CORNER)
            if not isinstance(row, int):
                start = pl.multiple_of(start, 16)
            qw[pl.ds(start, n), 0:80] = turned[at:at + n]
            at += n

    def own_tiles(which):
        def some(step, carry):
            for u in range(8):
                row = step * 8 + u
                hi, mid, lo = parts(which, row)
                turned = stacked(hi, mid, lo, True).T
                rows = stacked(hi, mid, lo).astype(BF16)
                qs[pl.ds(pl.multiple_of(row * 128, 128), 128), 0:80] = turned.astype(BF16)
                window_rows(which, row, rows, range(8))
                with_hi, with_mid = 2.0 * partner(hi), 2.0 * partner(mid)
                own = jnp.where(attr_row == 5, -2.0, with_hi)
                marked = 16.0 * jnp.where(attr_row < 2, with_hi, jnp.where(attr_row < 4, pltpu.roll(with_mid, 2, 0), 0.0))
                columns = []
                for a, scale in ((0, 1.0), (1, 1.0), (5, -2.0), (4, 1.0)):
                    ends = [jnp.where(attr_row == a, v * scale, 0.0) for v in (hi, mid, lo)]
                    if a == 5:
                        start = [own, own, jnp.where(attr_row == 5, -2.0, 0.0), with_mid, with_mid,
                                 jnp.where(attr_row < 4, -32.0, 0.0), marked]
                    else:
                        one = jnp.where(attr_row == a, 1.0 if a == 4 else -1.0, 0.0)
                        start = [one, one, one, zero8, zero8, zero8,
                                 jnp.where(attr_row == a, DEAD if a == 4 else -16.0, 0.0)]
                    columns.append(jnp.concatenate(start + ends, axis=0))
                rhs[row] = jnp.concatenate(columns, axis=1).astype(BF16)
            return carry
        lax.fori_loop(0, 4, some, 0)

    def halo_tile(which, row, windows):
        hi, mid, lo = parts(which, row)
        window_rows(which, row, stacked(hi, mid, lo).astype(BF16), windows)

    def halo_tiles(which, beside=None):
        dots((ext, ext2)[which], 32, 128)
        rank(which, 32, 48, (2, 4, 6))
        rank(which, 48, 64, (3, 5, 7))
        rank(which, 64, 96, (0, 4, 5))
        rank(which, 96, 128, (1, 6, 7))

        def some(step, carry):
            if beside is not None:
                beside(step)
            for u in range(4):
                halo_tile(which, 32 + step * 4 + u, (2, 4, 6))
                halo_tile(which, 48 + step * 4 + u, (3, 5, 7))
            return carry
        lax.fori_loop(0, 4, some, 0)
        for c in range(4):
            halo_tile(which, 64 + 8 * c + 7, (0, 4, 5))
            halo_tile(which, 96 + 8 * c, (1, 6, 7))

    lane16 = iota((16, 128), 1)
    half = iota((16, 128), 0) < 8

    lost = rank(0, 0, 32)
    own_tiles(0)

    unlisted = jnp.where(lane16 == 52, 1.0, 0.0)

    def by_offset(low, di, dj, rest):
        lane = lane16 - low
        inside = (lane >= 0) & (lane < 4)
        return jnp.where(inside, jnp.where((lane & 1) == 0, float(di), float(dj)), rest)

    def contact_rows(first, last, own_part=True, border_part=True, ahead=None):

        def step(four, carry):
            if ahead is not None:
                pl.when(four == 1)(ahead)
            for u, j in ((0, 0), (0, 1), (1, 0), (1, 1), (2, 0), (2, 1), (3, 0), (3, 1)):
                i = four * 4 + u
                t = j * 16 + i
                right = rhs[t]

                def mark_of(n):
                    di, dj = OFFSETS[n]
                    base = by_offset(48, di, dj, 0.0)
                    return base + unlisted * (1 - pat[n, j, i]).astype(F32)

                def times(di, dj):
                    return by_offset(40, di, dj, 1.0).astype(BF16)

                def border(w):
                    di, dj = WINDOWS[w]
                    row = ext_row(i + di, j + dj)
                    n = 48 if w < 4 else CORNER
                    start = row * WINDOW_ROWS + (w * EDGE_BASE if w < 4 else CORNER_BASE + (w - 4) * CORNER)
                    block, factor = qw[pl.ds(pl.multiple_of(start, 16), n), :], times(di, dj)
                    return [block[c:c + 16] * factor for c in range(0, n, 16)], mark_of(3 * (di + 1) + dj + 1)

                def edges_of(w):
                    (one, mark1), (two, mark2) = border(w), border(w + 1)
                    both = one[2] + two[2] + jnp.where(half, mark1, mark2).astype(BF16)
                    mark1, mark2 = mark1.astype(BF16), mark2.astype(BF16)
                    return [one[0] + mark1, one[1] + mark1, two[0] + mark2, two[1] + mark2, both]

                def corner(w):
                    (block,), here = border(w)
                    return block + here.astype(BF16)

                groups = []
                if own_part:
                    own = qs[pl.ds(pl.multiple_of(t * 128, 128), 128), :]
                    here = mark_of(4).astype(BF16)
                    groups += [own[c:c + 16] + here for c in range(0, 128, 16)]
                if border_part:
                    groups += edges_of(0) + edges_of(2) + [corner(w) for w in range(4, 8)]
                got = jnp.dot(jnp.concatenate(groups, axis=0)[:, 0:80], right, preferred_element_type=F32)
                rz, rx = got[:, 0:128], got[:, 128:256]
                inv = lax.rsqrt(rz * rz + rx * rx + 0.0001)
                push = jnp.maximum(got[:, 384:512] * inv - 1.0, 0.0) * (40.0 + got[:, 256:384] * inv)
                count = got.shape[0] // 8
                fz = jnp.sum((push * rz).reshape(count, 8, 128), axis=0)
                fx = jnp.sum((push * rx).reshape(count, 8, 128), axis=0)
                at_z, at_x = pl.ds(pl.multiple_of(t * 8, 8), 8), pl.ds(pl.multiple_of(t * 8 + 256, 8), 8)
                if not own_part:
                    fz, fx = fz + frc[at_z, :], fx + frc[at_x, :]
                frc[at_z, :], frc[at_x, :] = fz, fx
            return carry
        lax.fori_loop(first // 4, last // 4, step, 0)

    def forces():
        return [sum(frc[pl.ds(k * 256 + r, 32, stride=8), :] for r in range(8)) for k in range(2)]

    phase_end = reduce_end
    index = idx[...]
    share_z = frac[0].astype(F32) / 1024.0
    share_x = frac[1].astype(F32) / 1024.0
    wts[0] = (index >> 4).astype(F32)
    wts[1] = (index & 15).astype(F32)
    wts[2], wts[3] = 1.0 - share_z, share_z
    for n, share in ((4, 1.0 - share_x), (6, share_x)):
        high = share.astype(BF16).astype(F32)
        wts[n], wts[n + 1] = high, share - high
    c64 = iota((64, 128), 0).astype(F32)
    r16 = iota((16, 128), 0).astype(F32)

    def weigh(r, t4, t):
        def get(n):
            return wts[n, pl.ds(r, 1), :]
        column, row = get(1) + (16.0 * t4), get(0)
        here, there = c64 == column, c64 == column + 1.0
        wx[t, 0:64, :] = jnp.where(here, get(4), jnp.where(there, get(6), 0.0)).astype(BF16)
        wx[t, 64:128, :] = jnp.where(here, get(5), jnp.where(there, get(7), 0.0)).astype(BF16)
        wz[t] = jnp.where(r16 == row, get(2), jnp.where(r16 == row + 1.0, get(3), 0.0))

    def some_weights(h, carry):
        for t in range(2):
            for j in range(2):
                weigh(4 * h + 2 * t + j, t * 2 + j, 4 * h + 2 * t + j)
        return carry

    lax.fori_loop(0, 8, some_weights, 0)
    contact_rows(0, EARLY, True, False)

    for c in pieces:
        c.wait()
    lane32 = iota((32, 128), 1)

    def sample(h):
        field = gv[h]
        high = field.astype(BF16).astype(F32)
        both = jnp.where(lane32 < 64, high, field - high).astype(BF16)
        for t in range(2):
            for j in range(2):
                r = 4 * h + 2 * t + j
                whi, wlo = wx[r, 0:64, :], wx[r, 64:128, :]
                right = jnp.concatenate([jnp.concatenate([whi, whi], axis=0),
                                         jnp.concatenate([wlo, wlo], axis=0)], axis=1)
                got = jnp.dot(both, right, preferred_element_type=F32)
                got = got[:, 0:128] + got[:, 128:256]
                for k in range(2):
                    itp[k, pl.ds(j * 16 + 2 * h + t, 1), :] = jnp.sum(
                        wz[r] * got[k * 16:(k + 1) * 16], axis=0, keepdims=True)

    def two_samples(step):
        sample(2 * step)
        sample(2 * step + 1)

    phase_end(0, 0, phase)
    max_phase = reduce_start(0, 1)
    halo_end(halos)
    halo_tiles(0, two_samples)

    last_phase = reduce_copies(0, 2)

    def pass_maximum():
        phase_end(0, 1, max_phase)
        reduce_go(0, 2, last_phase)

    contact_rows(0, EARLY, False, True, pass_maximum)
    contact_rows(EARLY, 16)
    drag = by_column(coef)
    radius = ext[4, 0:32, :]
    alive = jnp.where(radius > 0.0, 1.0, 0.0)
    inverse = jnp.where(radius > 0.0, 0.36 / (radius * radius), 0.0)
    force = forces()
    reach, slack = NEAR[1]
    longest = 0.2 / mv[0][0:1, :]
    bad, drags, pushes, borders, sums = lost, [], [], [], []
    for k in range(2):
        place, speed = ext[k, 0:32, :], ext[2 + k, 0:32, :]
        drag1 = drag * (itp[k] - speed)
        push = inverse * (force[k] + drag1) - (alive if k == 0 else 0.0)
        once, twice = longest * speed, longest * longest * push
        high = place + jnp.maximum(once, 0.0) + jnp.maximum(twice, 0.0)
        low = place + jnp.minimum(once, 0.0) + jnp.minimum(twice, 0.0)
        bad = bad + jnp.where((low >= -slack) & (high <= 16.0 + slack), 0.0, alive)
        borders.append((jnp.where(low < reach + 0.001, alive, 0.0), jnp.where(high > 15.999 - reach, alive, 0.0)))
        drags.append(drag1)
        pushes.append(push)
        sums += [alive * drag1, 0.5 * alive * drag * push]
    (lz, hz), (lx, hx) = borders
    for member, room in ((lz, EDGE), (hz, EDGE), (lx, EDGE), (hx, EDGE),
                         (lz * lx, CORNER), (lz * hx, CORNER), (hz * lx, CORNER), (hz * hx, CORNER)):
        bad = bad + jnp.where(jnp.sum(member, axis=1, keepdims=True) > room, 1.0, 0.0)
    message = zero8
    for row, v in ((0, sums[0]), (1, sums[2]), (2, bad), (3, sums[1]), (4, sums[3])):
        message = jnp.where(attr_row == row,
                            jnp.sum(jnp.sum(v, axis=1, keepdims=True), axis=0, keepdims=True), message)
    sv[0] = message
    phase = reduce_start(1, 0)
    phase_end(0, 2, last_phase)
    step = 0.2 / mv[3][0:1, :]
    for k in range(2):
        speed2 = ext[2 + k, 0:32, :] + step * pushes[k]
        ext2[k, 0:32, :] = ext[k, 0:32, :] + step * speed2
        ext2[2 + k, 0:32, :] = speed2
        drag2 = drag * (itp[k] - speed2)
        itp[k] = 0.5 * (alive * drags[k] + alive * drag2)
        itp[2 + k] = drag2
    ext2[4, 0:32, :] = radius
    dots(ext2, 0, 32)
    halos = halo_start(1)
    rank(1, 0, 32)

    def spread(h):
        total = jnp.zeros((64, 128), F32)
        for t in range(2):
            for j in range(2):
                r = 4 * h + 2 * t + j
                m0 = itp[0, pl.ds(j * 16 + 2 * h + t, 1), :]
                m1 = itp[1, pl.ds(j * 16 + 2 * h + t, 1), :]
                lhs = jnp.concatenate([wz[r] * m0, wz[r] * m1], axis=0)
                high = lhs.astype(BF16)
                low = (lhs - high.astype(F32)).astype(BF16)
                total = total + lax.dot_general(
                    jnp.concatenate([high, low], axis=0), wx[r],
                    (((1,), (1,)), ((), ())), preferred_element_type=F32)
        total = total[0:32] + total[32:64]
        dp[h] = total + pltpu.roll(total, 64, 1)

    lax.fori_loop(0, 8, lambda h, carry: (spread(h), carry)[1], 0)
    pieces = pieces_start(1)
    phase_end(1, 0, phase)
    sum_phase = reduce_start(1, 1)
    own_tiles(1)
    phase_end(1, 1, sum_phase)
    last_sum = reduce_start(1, 2)
    halo_end(halos)
    halo_tiles(1)

    contact_rows(0, 16)
    force = forces()
    step = 0.2 / mv[3][0:1, :]
    radius = ext2[4, 0:32, :]
    alive = jnp.where(radius > 0.0, 1.0, 0.0)
    inverse = jnp.where(radius > 0.0, 0.36 / (radius * radius), 0.0)
    for k in range(2):
        speed = ext2[2 + k, 0:32, :]
        speed2 = speed + step * (inverse * (force[k] + itp[2 + k]) - (alive if k == 0 else 0.0))
        place2 = (ext2[k, 0:32, :] + step * speed2) * 0.0625
        for j in range(2):
            part[k, pl.ds(j, 16, stride=2), :] = place2[j * 16:(j + 1) * 16]
            part[2 + k, pl.ds(j, 16, stride=2), :] = speed2[j * 16:(j + 1) * 16]
    for c in edges + lists:
        c.wait()

    @pl.when(ax < N_ACROSS - 1)
    def _():
        to_right.wait_send()
        to_left.wait_recv()

    @pl.when(ax > 0)
    def _():
        to_left.wait_send()
        to_right.wait_recv()

    for c in pieces:
        c.wait()
    phase_end(1, 2, last_sum)
    total = sv[3]
    flag[...] = total[2:3, 0:1]
    sv[3] = jnp.where(attr_row == 0, total[0:1] - step * total[3:4], total[1:2] - step * total[4:5])
    gas_step_update(gas, visc, gr, gc, dv, sv.at[3], mv.at[3], out)


def fused(gas, visc, pos, vel, rad, coef, counts_t, pattern_t, idx, frac):
    dma = pltpu.SemaphoreType.DMA
    return pl.pallas_call(
        fused_kernel,
        out_shape=[jax.ShapeDtypeStruct((4, 32, 128), F32), jax.ShapeDtypeStruct((2, 32, 256), F32),
                   jax.ShapeDtypeStruct((1, 1), F32), jax.ShapeDtypeStruct((9, 2, 16), jnp.int32),
                   jax.ShapeDtypeStruct((2, 16), jnp.int32)],
        in_specs=[pl.BlockSpec(memory_space=pltpu.HBM)] * 10,
        out_specs=[VMEM_SPEC] * 3 + [pl.BlockSpec(memory_space=pltpu.HBM)] * 2,
        scratch_shapes=[
            pltpu.VMEM((2, 32, 256), F32), pltpu.VMEM((32, 256), F32),
            pltpu.VMEM((2, 32, 128), F32), pltpu.VMEM((2, 32, 128), F32), pltpu.VMEM((32, 128), F32),
            pltpu.VMEM((32, 128), F32), pltpu.VMEM((32, 128), jnp.int32), pltpu.VMEM((2, 32, 128), jnp.int32),
            pltpu.SMEM((9, 2, 16), jnp.int32), pltpu.SMEM((2, 16), jnp.int32), dma((12,)),
            pltpu.VMEM((8, 128, 128), F32), pltpu.VMEM((8, 128, 128), F32),
            pltpu.VMEM((8, 32, 128), F32), pltpu.VMEM((8, 32, 128), F32),
            pltpu.VMEM((8, 32, 128), F32), pltpu.VMEM((8, 32, 128), F32),
            pltpu.VMEM((2, 2, 8, 256), F32), pltpu.VMEM((2, 2, 32, 128), F32),
            pltpu.VMEM((3, 8, 8, 128), F32), pltpu.VMEM((4, 8, 128), F32),
            pltpu.VMEM((3, 8, 8, 128), F32), pltpu.VMEM((4, 8, 128), F32),
            pltpu.VMEM((8, 128, 128), F32), pltpu.VMEM((32 * 128, 128), BF16),
            pltpu.VMEM((128 * WINDOW_ROWS, 128), BF16), pltpu.VMEM((32, 80, 512), BF16),
            pltpu.VMEM((512, 128), F32), pltpu.VMEM((4, 32, 128), F32), pltpu.VMEM((8, 32, 128), F32),
            pltpu.VMEM((32, 128, 128), BF16), pltpu.VMEM((32, 16, 128), F32),
            dma((2, 10)), dma((2, 10)), dma((2, 8)), dma((2, 8)), dma((2, 3, 8)), dma((2, 3, 8)),
            dma((4,)), dma((4,)),
        ],
        compiler_params=pltpu.CompilerParams(collective_id=2, has_side_effects=True),
        name="interval",
    )(gas, visc, pos, vel, rad, coef, idx, frac, pattern_t, counts_t)


def body(gas, visc, pos, vel, rad, coef, counts, pattern, idx, frac):
    pos, vel, frac = (x.reshape(2, 32, 128) for x in (pos, vel, frac))
    rad, coef, idx = (x.reshape(32, 128) for x in (rad, coef, idx))
    args = (gas, visc, pos, vel, rad, coef, counts.T, pattern.transpose(2, 1, 0), idx, frac)
    part, out, flag, pattern_t, counts_t = fused(*args)
    args = args[:6] + (counts_t, pattern_t) + args[8:]
    part, out = lax.cond(flag[0, 0] > 0.0, lambda p, o: tuple(general(*args)), lambda p, o: (p, o), part, out)
    return part.reshape(4, 16, 2, 128), out


def solution(mesh):
    return jax.shard_map(
        body,
        mesh=mesh,
        in_specs=(
            P(None, ALONG_GAS, "across"),
            P(ALONG_GAS, "across"),
            P(None, "along", ACROSS_GAS, None),
            P(None, "along", ACROSS_GAS, None),
            P("along", ACROSS_GAS, None),
            P("along", ACROSS_GAS, None),
            P("along", ACROSS_GAS),
            P("along", ACROSS_GAS, None),
            P("along", ACROSS_GAS, None),
            P(None, "along", ACROSS_GAS, None),
        ),
        out_specs=(P(None, "along", ACROSS_GAS, None), P(None, ALONG_GAS, "across")),
        check_vma=False,
    )
```

```python
import functools

import jax
import jax.numpy as jnp
from jax import lax
from jax.experimental import pallas as pl
from jax.experimental.pallas import tpu as pltpu
from jax.sharding import PartitionSpec as P

ALONG_GAS = ("along", "gas")
ACROSS_GAS = ("across", "gas")
MESH_ID = pl.DeviceIdType.MESH
OFFSETS = [(-1, -1), (-1, 0), (-1, 1), (0, -1), (0, 0), (0, 1), (1, -1), (1, 0), (1, 1)]
DEAD = -16384.0
F32 = jnp.float32
BF16 = jnp.bfloat16
STRIDE = 136
BLOCK, BLOCK_BITS = 64, 6
EMPTY = 1344
REACH = 2.4
MOVE_LIMIT = int((REACH - 1.9) * 4096)
VMEM_SPEC = pl.BlockSpec(memory_space=pltpu.VMEM)
SMEM_SPEC = pl.BlockSpec(memory_space=pltpu.SMEM)
N_ACROSS, N_ALONG, N_GAS = 4, 8, 8


def iota(shape, dim):
    return lax.broadcasted_iota(jnp.int32, shape, dim)


def ext_row(ii, jj):
    base = {-1: 32, 0: 0, 1: 16, 2: 48}[jj]
    return jnp.where(ii < 0, 64 + 8 * (jj + 1) + 7, jnp.where(ii > 15, 96 + 8 * (jj + 1), base + ii))


def by_column(ref, *lead):
    return jnp.concatenate([ref[(*lead, pl.ds(0, 16, stride=2), slice(None))],
                            ref[(*lead, pl.ds(1, 16, stride=2), slice(None))]], axis=0)


def prepare_state(st, pos, vel, rad, counts):
    row32 = iota((32, 128), 0)
    slot = iota((32, 128), 1)
    cnt = jnp.zeros((32, 128), jnp.int32)
    for j in range(2):
        for i in range(16):
            cnt = jnp.where(row32 == j * 16 + i, counts[j, i], cnt)
    alive = slot < cnt
    z, x = by_column(pos, 0) * 16.0, by_column(pos, 1) * 16.0
    st[0, 0:32, :], st[1, 0:32, :] = z, x
    st[2, 0:32, :], st[3, 0:32, :] = by_column(vel, 0), by_column(vel, 1)
    st[4, 0:32, :] = jnp.where(alive, by_column(rad), DEAD)
    low_x, high_x = x < REACH, x > 16.0 - REACH

    def three(low, mid, high):
        return jnp.where(low_x, low, jnp.where(high_x, high, mid))

    kind = jnp.where(z < REACH, three(0, 1, 2), jnp.where(z > 16.0 - REACH, three(6, 5, 4), three(7, 8, 3)))
    kind = jnp.where(alive, kind, 9)
    member = jnp.concatenate([jnp.where(kind == c, 1.0, 0.0) for c in range(9)], axis=0).astype(BF16)
    before = jnp.where((iota((128, 256), 0) < iota((128, 256), 1)) | (iota((128, 256), 1) >= 128), 1.0, 0.0)
    ranks = jnp.dot(member, before.astype(BF16), preferred_element_type=F32)
    rank = jnp.full((32, 128), -1.0, F32)
    start = [jnp.zeros((32, 128), F32)]
    for c in range(9):
        here = ranks[c * 32:(c + 1) * 32]
        rank = jnp.where(kind == c, start[c] + here[:, 0:128], rank)
        start.append(start[c] + here[:, 128:256])
    st[5, 0:32, :] = rank
    start = [v.astype(jnp.int32) for v in start]
    wrap = ((start[1] + 7) & -8) > start[6]
    zero = jnp.zeros((32, 128), jnp.int32)
    windows = [(start[4], start[5]), (start[4], start[7]), (start[6], start[7]), (start[2], start[5]),
               (zero, start[9]), (jnp.where(wrap, 0, start[6]), start[8]), (start[2], start[3]),
               (zero, start[3]), (zero, start[1]), (zero, jnp.where(wrap, 0, start[1]))]
    table = zero
    for w, (low, high) in enumerate(windows):
        table = jnp.where(slot == 2 * w, low, jnp.where(slot == 2 * w + 1, (high - low + 7) & -8, table))
    st[6, 0:32, :] = table.astype(F32)


def prep_kernel(gas, visc, pos, vel, rad, counts, st, gp, mx):
    rate = jnp.abs(gas[0]) + jnp.abs(gas[1]) + 4.0 * visc[...]
    top = jnp.max(jnp.max(rate, axis=1, keepdims=True), axis=0, keepdims=True)
    mx[...] = jnp.broadcast_to(top, (8, 128))
    lane = iota((16, 128), 1)
    for g in range(N_GAS):
        blk = slice((g // 4) * 128, (g // 4) * 128 + 128)
        off = (g % 4) * 32
        for k in range(2):
            low = gas[k, 0:16, blk]
            high = gas[k, 16:32, blk]
            low = pltpu.roll(low, (128 - off) % 128, 1) if off else low
            shift = (160 - off) % 128
            high = pltpu.roll(high, shift, 1) if shift else high
            piece = jnp.where(lane < 32, low, jnp.where(lane < 64, high, 0.0))
            gp[g, k * 16:(k + 1) * 16, :] = piece
    prepare_state(st, pos, vel, rad, counts)
    st[7] = jnp.zeros((32, 128), F32)


def comm_kernel(first, *refs):
    if first:
        (st, pc, mx, gas, ext, pv, red, gr, gc, mb, m1, m2,
         own_sem, hs, hr, ps, pr, rs, rr, es, er) = refs
    else:
        (st, pc, mx, ext, pv, red, mb, m1, m2,
         own_sem, hs, hr, ps, pr, rs, rr) = refs
    ax, al, g = lax.axis_index("across"), lax.axis_index("along"), lax.axis_index("gas")
    up, down = lax.rem(al + 1, N_ALONG), lax.rem(al + N_ALONG - 1, N_ALONG)
    lin = ax * N_GAS + g
    has_left, has_right = lin > 0, lin < N_ACROSS * N_GAS - 1
    left = jnp.maximum(lin - 1, 0)
    right = jnp.minimum(lin + 1, N_ACROSS * N_GAS - 1)

    def col(index, along):
        return {"across": lax.div(index, N_GAS), "along": along, "gas": lax.rem(index, N_GAS)}

    slab = al * N_GAS + g
    slabs = N_ALONG * N_GAS
    after, before = lax.rem(slab + 1, slabs), lax.rem(slab + slabs - 1, slabs)

    def slab_id(index):
        return {"across": ax, "along": lax.div(index, N_GAS), "gas": lax.rem(index, N_GAS)}

    barrier = pltpu.get_barrier_semaphore()

    def greet(device):
        pl.semaphore_signal(barrier, inc=1, device_id=device, device_id_type=MESH_ID)

    for k in range(1, N_ACROSS):
        greet({"across": lax.rem(ax + k, N_ACROSS)})
    for k in range(1, N_GAS):
        greet({"gas": lax.rem(g + k, N_GAS)})
    for k in range(1, N_ALONG):
        greet({"along": lax.rem(al + k, N_ALONG)})
    expect = N_ACROSS + N_GAS + N_ALONG - 3
    if first:
        greet(slab_id(after))
        greet(slab_id(before))
        expect += 2

    @pl.when(has_left)
    def _():
        for along in (down, al, up):
            greet(col(left, along))

    @pl.when(has_right)
    def _():
        for along in (down, al, up):
            greet(col(right, along))

    own = pltpu.make_async_copy(st, ext.at[:, pl.ds(0, 32)], own_sem.at[0])
    own.start()
    own_piece = pltpu.make_async_copy(pc.at[g], pv.at[g], own_sem.at[1])
    own_piece.start()

    @pl.when(jnp.logical_not(has_left))
    def _():
        ext[:, 32:48, :] = jnp.zeros((8, 16, 128), F32)
        ext[:, 64:72, :] = jnp.zeros((8, 8, 128), F32)
        ext[:, 96:104, :] = jnp.zeros((8, 8, 128), F32)

    @pl.when(jnp.logical_not(has_right))
    def _():
        ext[:, 48:64, :] = jnp.zeros((8, 16, 128), F32)
        ext[:, 88:96, :] = jnp.zeros((8, 8, 128), F32)
        ext[:, 120:128, :] = jnp.zeros((8, 8, 128), F32)

    if first:
        @pl.when(ax == 0)
        def _():
            gc[0] = jnp.zeros((2, 32, 128), F32)

        @pl.when(ax == N_ACROSS - 1)
        def _():
            gc[1] = jnp.zeros((2, 32, 128), F32)

    sides = jnp.where(has_left, 3, 0) + jnp.where(has_right, 3, 0)
    pl.semaphore_wait(barrier, expect + sides)

    def remote(src, dst, send, recv, device):
        return pltpu.make_async_remote_copy(
            src_ref=src, dst_ref=dst, send_sem=send, recv_sem=recv,
            device_id=device, device_id_type=MESH_ID,
        )

    def reduce_sends(phase, src, axis, me, size):
        out = []
        for k in range(1, size):
            out.append(remote(src, mb.at[phase, me], rs.at[phase, k], rr.at[phase, k],
                              {axis: lax.rem(me + k, size)}))
        for c in out:
            c.start()
        return out

    phase0 = reduce_sends(0, mx, "across", ax, N_ACROSS)

    def halo(c, src_rows, size, dst_row, device):
        return remote(st.at[pl.ds(0, 7), pl.ds(src_rows, size)],
                      ext.at[pl.ds(0, 7), pl.ds(dst_row, size)], hs.at[c], hr.at[c], device)

    lefts = [halo(0, 0, 16, 48, col(left, al)),
             halo(1, 8, 8, 64 + 24, col(left, up)),
             halo(2, 0, 8, 96 + 24, col(left, down))]
    rights = [halo(3, 16, 16, 32, col(right, al)),
              halo(4, 24, 8, 64, col(right, up)),
              halo(5, 16, 8, 96, col(right, down))]
    rows = [halo(6, 8, 8, 64 + 8, {"along": up}),
            halo(7, 24, 8, 64 + 16, {"along": up}),
            halo(8, 0, 8, 96 + 8, {"along": down}),
            halo(9, 16, 8, 96 + 16, {"along": down})]

    @pl.when(has_left)
    def _():
        for c in lefts:
            c.start()

    @pl.when(has_right)
    def _():
        for c in rights:
            c.start()

    for c in rows:
        c.start()
    pieces = []
    for k in range(1, N_GAS):
        peer = lax.rem(g + k, N_GAS)
        c = remote(pc.at[peer], pv.at[g], ps.at[k], pr.at[k], {"gas": peer})
        c.start()
        pieces.append(c)
    if first:
        edges = [remote(gas.at[:, pl.ds(24, 8)], gr.at[0], es.at[0], er.at[0], slab_id(after)),
                 remote(gas.at[:, pl.ds(0, 8)], gr.at[1], es.at[1], er.at[1], slab_id(before))]
        for c in edges:
            c.start()
        to_right = remote(gas.at[:, :, pl.ds(128, 128)], gc.at[0], es.at[2], er.at[2],
                          {"across": jnp.minimum(ax + 1, N_ACROSS - 1)})
        to_left = remote(gas.at[:, :, pl.ds(0, 128)], gc.at[1], es.at[3], er.at[3],
                         {"across": jnp.maximum(ax - 1, 0)})

        @pl.when(ax < N_ACROSS - 1)
        def _():
            to_right.start()

        @pl.when(ax > 0)
        def _():
            to_left.start()

    def combine(phase, mine, me, size, copies):
        for c in copies:
            c.wait_recv()
        mb[phase, me] = mine
        total = mb[phase, 0]
        for k in range(1, size):
            total = jnp.maximum(total, mb[phase, k]) if first else total + mb[phase, k]
        return total

    m1[...] = combine(0, mx[...], ax, N_ACROSS, phase0)
    phase1 = reduce_sends(1, m1, "gas", g, N_GAS)
    m2[...] = combine(1, m1[...], g, N_GAS, phase1)
    phase2 = reduce_sends(2, m2, "along", al, N_ALONG)
    red[...] = combine(2, m2[...], al, N_ALONG, phase2)

    own.wait()
    own_piece.wait()
    for c in phase0 + phase1 + phase2:
        c.wait_send()
    for c in rows + pieces:
        c.wait()

    @pl.when(has_left)
    def _():
        for c in lefts:
            c.wait_send()
        for c in rights:
            c.wait_recv()

    @pl.when(has_right)
    def _():
        for c in rights:
            c.wait_send()
        for c in lefts:
            c.wait_recv()

    if first:
        for c in edges:
            c.wait()

        @pl.when(ax < N_ACROSS - 1)
        def _():
            to_right.wait_send()
            to_left.wait_recv()

        @pl.when(ax > 0)
        def _():
            to_left.wait_send()
            to_right.wait_recv()


def exchange(first, st, pc, mx, gas=None):
    out_shape = [jax.ShapeDtypeStruct((8, 128, 128), F32),
                 jax.ShapeDtypeStruct((8, 32, 128), F32),
                 jax.ShapeDtypeStruct((8, 128), F32)]
    scratch = [pltpu.VMEM((3, 8, 8, 128), F32), pltpu.VMEM((8, 128), F32), pltpu.VMEM((8, 128), F32),
               pltpu.SemaphoreType.DMA((2,)),
               pltpu.SemaphoreType.DMA((10,)), pltpu.SemaphoreType.DMA((10,)),
               pltpu.SemaphoreType.DMA((8,)), pltpu.SemaphoreType.DMA((8,)),
               pltpu.SemaphoreType.DMA((3, 8)), pltpu.SemaphoreType.DMA((3, 8))]
    args = [st, pc, mx]
    if first:
        args.append(gas)
        out_shape += [jax.ShapeDtypeStruct((2, 2, 8, 256), F32), jax.ShapeDtypeStruct((2, 2, 32, 128), F32)]
        scratch += [pltpu.SemaphoreType.DMA((4,)), pltpu.SemaphoreType.DMA((4,))]
    return pl.pallas_call(
        functools.partial(comm_kernel, first),
        out_shape=out_shape,
        in_specs=[VMEM_SPEC] * len(args),
        out_specs=[VMEM_SPEC] * len(out_shape),
        scratch_shapes=scratch,
        compiler_params=pltpu.CompilerParams(collective_id=0 if first else 1, has_side_effects=True),
        name="exchange_first" if first else "exchange_second",
    )(*args)


def split3(x):
    hi = x.astype(BF16).astype(F32)
    rest = x - hi
    mid = rest.astype(BF16).astype(F32)
    return hi, mid, rest - mid


def contact_forces(ext, pat, meta, ints, qt, lst, rhs, frc, sem):
    ints[...] = ext[6 * 128:7 * 128, :].astype(jnp.int32)
    to_smem = pltpu.make_async_copy(ints, meta, sem)
    to_smem.start()
    slot = iota((128, 128), 0).astype(F32)
    attr_row = iota((8, 128), 0)
    zero8 = jnp.zeros((8, 128), F32)
    tail = jnp.concatenate([zero8, jnp.ones((24, 128), F32), zero8], axis=0)

    def parts(row):
        block = ext[pl.ds(row, 8, stride=128), :]
        return split3(jnp.where(attr_row < 5, block, 0.0))

    def transposed(row):
        hi, mid, lo = parts(row)
        rows = jnp.concatenate([hi, mid, lo, tail], axis=0).astype(BF16)
        place = (slot == ext[pl.ds(row + 5 * 128, 1), :]).astype(F32).astype(BF16)
        turned = lax.dot_general(place, rows, (((1,), (1,)), ((), ())), preferred_element_type=F32)
        start = row * STRIDE if isinstance(row, int) else pl.multiple_of(row * STRIDE, 8)
        qt[pl.ds(start, 128), 0:64] = turned
        start = start + 128 if isinstance(row, int) else pl.multiple_of(start + 128, 8)
        qt[pl.ds(start, 8), :] = zero8

    def some(step, carry):
        for u in range(4):
            transposed(step * 4 + u)
        return carry

    lax.fori_loop(0, 16, some, 0)
    for c in range(4):
        transposed(64 + 8 * c + 7)
        transposed(96 + 8 * c)

    block_of = iota((32, 640), 1) >> 7
    row_of = iota((32, 640), 0)
    attr_of = row_of & 7
    own_scale = jnp.where(block_of < 2, -1.0, jnp.where(block_of < 4, 2.0, 1.0))
    const = jnp.where((attr_of == block_of) & (row_of < 24), own_scale, 0.0)
    const = jnp.where((row_of == 24) & (block_of == 0) | (row_of == 25) & (block_of == 1), -16.0, const)
    for u in range(2):
        rhs[u, 0:32, :] = const.astype(BF16)
        lst[u, EMPTY:EMPTY + BLOCK, :] = jnp.zeros((BLOCK, 128), F32)
    to_smem.wait()
    lane = iota((8, 128), 1)

    def row_step(i, carry):
        blocks = []
        for j in range(2):
            work = lst.at[j]
            mine = j * 16 + i
            hi, mid, lo = parts(mine)
            columns = []
            for a in range(5):
                keep = attr_row == a
                scale = 1.0 if a in (0, 1, 4) else -2.0
                columns.append(jnp.concatenate(
                    [jnp.where(keep, hi * scale, 0.0), jnp.where(keep, mid * scale, 0.0),
                     jnp.where(keep, lo * scale, 0.0), zero8], axis=0))
            rhs[j, 32:64, :] = jnp.concatenate(columns, axis=1).astype(BF16)
            moved = meta[mine, 20]
            off = i * 0
            over = i * 0
            windows = []
            for w in (4, 0, 1, 2, 3, 5, 6, 7, 8, 9):
                di, dj = OFFSETS[5 if w == 9 else w]
                row = ext_row(i + di, j + dj)
                first, size = meta[row, 2 * w], meta[row, 2 * w + 1]
                if w != 4:
                    near = moved + meta[row, 20] <= MOVE_LIMIT
                    first = jnp.where(near, first, 0)
                    size = jnp.where(near, size, 0 if w == 9 else meta[row, 9])
                size = size * pat[5 if w == 9 else w, j, i]
                mark = jnp.where(lane == 24, float(di), jnp.where(lane == 25, float(dj), 0.0))
                start = row * STRIDE + first
                chunks = 16 if w == 4 else 4 if w in (1, 3, 5, 7) else 1
                for c in range(chunks):
                    work[pl.ds(pl.multiple_of(off + c * 8, 8), 8), :] = qt[pl.ds(start + c * 8, 8), :] + mark
                windows.append((start, size, mark))
                off = off + size
                over = jnp.maximum(over, size - chunks * 8)

            @pl.when(over > 0)
            def _():
                to = i * 0
                for start, size, mark in windows:
                    def copy(c, carry, start=start, mark=mark, to=to):
                        work[pl.ds(pl.multiple_of(to + c * 8, 8), 8), :] = qt[pl.ds(start + c * 8, 8), :] + mark
                        return carry
                    lax.fori_loop(0, size >> 3, copy, 0)
                    to = to + size

            for c in range(BLOCK // 8):
                work[pl.ds(pl.multiple_of(off + c * 8, 8), 8), :] = zero8
            blocks.append((off + BLOCK - 1) >> BLOCK_BITS)
        right = [rhs[0], rhs[1]]

        def block(b, acc):
            out = []
            for j in range(2):
                at = jnp.where(b < blocks[j], b * BLOCK, EMPTY)
                q = lst[j, pl.ds(pl.multiple_of(at, 8), BLOCK), 0:64].astype(BF16)
                got = jnp.dot(q, right[j], preferred_element_type=F32)
                rz, rx = got[:, 0:128], got[:, 128:256]
                dz, dx = got[:, 256:384], got[:, 384:512]
                d2 = rz * rz + rx * rx + 0.0001
                inv = lax.rsqrt(d2)
                depth = jnp.maximum(got[:, 512:640] - d2 * inv, 0.0)
                push = depth * inv * (40.0 + (dz * rz + dx * rx) * inv)
                out.append(acc[2 * j] + jnp.sum((push * rz).reshape(BLOCK // 8, 8, 128), axis=0))
                out.append(acc[2 * j + 1] + jnp.sum((push * rx).reshape(BLOCK // 8, 8, 128), axis=0))
            return tuple(out)

        acc = lax.fori_loop(0, jnp.maximum(blocks[0], blocks[1]), block, (zero8,) * 4)
        for j in range(2):
            for k in range(2):
                frc[pl.ds(pl.multiple_of(((k * 2 + j) * 16 + i) * 8, 8), 8), :] = acc[2 * j + k]
        return carry

    lax.fori_loop(0, 16, row_step, 0)
    return [sum(frc[pl.ds(k * 256 + r, 32, stride=8), :] for r in range(8)) for k in range(2)]


def first_kernel(ext, gv, rate, idx, frac, coef, pat, st2, dp, tot, dr2, inv_out,
                 meta, ints, qt, lst, rhs, frc, itp, sem):
    def weights(r, t4):
        index = idx[pl.ds(r, 1), :]
        row, column = index >> 4, index & 15
        share_z = frac[0, pl.ds(r, 1), :].astype(F32) / 1024.0
        share_x = frac[1, pl.ds(r, 1), :].astype(F32) / 1024.0
        c64 = iota((64, 128), 0) - t4 * 16
        wx = jnp.where(c64 == column, 1.0 - share_x, jnp.where(c64 == column + 1, share_x, 0.0))
        r16 = iota((16, 128), 0)
        wz = jnp.where(r16 == row, 1.0 - share_z, jnp.where(r16 == row + 1, share_z, 0.0))
        return wz, wx

    def sample(h, carry):
        field = gv[h][:, 0:64]
        for t in range(2):
            for j in range(2):
                wz, wx = weights(4 * h + 2 * t + j, t * 2 + j)
                along = jnp.dot(field, wx, precision=lax.Precision.HIGHEST, preferred_element_type=F32)
                for k in range(2):
                    itp[k, pl.ds(j * 16 + 2 * h + t, 1), :] = jnp.sum(
                        wz * along[k * 16:(k + 1) * 16], axis=0, keepdims=True)
        return carry

    lax.fori_loop(0, 8, sample, 0)
    force = contact_forces(ext, pat, meta, ints, qt, lst, rhs, frc, sem)
    step = 0.2 / rate[0:1, :]
    drag = by_column(coef)
    radius = ext[4 * 128:4 * 128 + 32, :]
    alive = jnp.where(radius > 0.0, 1.0, 0.0)
    inverse = jnp.where(radius > 0.0, 0.36 / (radius * radius), 0.0)
    inv_out[...] = inverse
    means = []
    moved = jnp.zeros((32, 128), F32)
    for k in range(2):
        place = ext[k * 128:k * 128 + 32, :]
        speed = ext[(2 + k) * 128:(2 + k) * 128 + 32, :]
        drag1 = drag * (itp[k] - speed)
        speed2 = speed + step * (inverse * (force[k] + drag1) - (alive if k == 0 else 0.0))
        st2[k] = place + step * speed2
        moved = jnp.maximum(moved, alive * jnp.abs(step * speed2))
        st2[2 + k] = speed2
        drag2 = drag * (itp[k] - speed2)
        dr2[k] = drag2
        mean = 0.5 * (alive * drag1 + alive * drag2)
        itp[k] = mean
        means.append(jnp.sum(jnp.sum(mean, axis=1, keepdims=True), axis=0, keepdims=True))
    st2[4] = radius
    st2[5] = ext[5 * 128:5 * 128 + 32, :]
    far = jnp.max(moved, axis=1, keepdims=True)
    far = jnp.where(far < 100.0, far, 100.0) * 4096.0 + 1.0
    st2[6] = jnp.where(iota((32, 128), 1) == 20, far, ext[6 * 128:6 * 128 + 32, :])
    st2[7] = jnp.zeros((32, 128), F32)
    tot[...] = jnp.where(iota((8, 128), 0) == 0, means[0], means[1])

    def spread(h, carry):
        total = jnp.zeros((32, 64), F32)
        for t in range(2):
            for j in range(2):
                wz, wx = weights(4 * h + 2 * t + j, t * 2 + j)
                m0 = itp[0, pl.ds(j * 16 + 2 * h + t, 1), :]
                m1 = itp[1, pl.ds(j * 16 + 2 * h + t, 1), :]
                lhs = jnp.concatenate([wz * m0, wz * m1], axis=0)
                total = total + lax.dot_general(lhs, wx, (((1,), (1,)), ((), ())),
                                                precision=lax.Precision.HIGHEST, preferred_element_type=F32)
        dp[h, :, 0:64] = total
        dp[h, :, 64:128] = jnp.zeros((32, 64), F32)
        return carry

    lax.fori_loop(0, 8, spread, 0)


def gas_step_update(gas, visc, gr, gc, dv, tot, rate, out):
    gas_step = 0.4 / rate[0:1, 0:1]
    lane = iota((32, 256), 1)
    row = iota((32, 256), 0)
    lane16 = iota((16, 128), 1) >> 5
    for k in range(2):
        u = gas[k]
        upper = jnp.where(row == 31, gr[1, k, 0:1, :], pltpu.roll(u, 31, 0))
        lower = jnp.where(row == 0, gr[0, k, 7:8, :], pltpu.roll(u, 1, 0))
        right = jnp.where(lane == 255, gc[1, k, :, 0:1], pltpu.roll(u, 255, 1))
        left = jnp.where(lane == 0, gc[0, k, :, 127:128], pltpu.roll(u, 1, 1))
        laplace = upper + lower + right + left - 4.0 * u
        advect = gas[0] * (upper - lower) * 0.5 + gas[1] * (right - left) * 0.5
        quads = []
        for t in range(2):
            halves = []
            for b in range(2):
                whole = None
                for q in range(4):
                    piece = dv[4 * b + q, k * 16:(k + 1) * 16, :]
                    shift = (q * 32 - t * 32) % 128
                    piece = pltpu.roll(piece, shift, 1) if shift else piece
                    whole = piece if whole is None else jnp.where(lane16 == q, piece, whole)
                halves.append(whole)
            quads.append(jnp.concatenate(halves, axis=1))
        deposit = jnp.concatenate(quads, axis=0)
        source = tot[k:k + 1, 0:1] / 2097152.0 - deposit
        out[k] = u + gas_step * (visc[...] * laplace - advect + source)


def second_kernel(ext, dv, tot, rate, dr2, inverse, gas, visc, gr, gc, pat, part, out,
                  meta, ints, qt, lst, rhs, frc, sem):
    force = contact_forces(ext, pat, meta, ints, qt, lst, rhs, frc, sem)
    step = 0.2 / rate[0:1, :]
    radius = ext[4 * 128:4 * 128 + 32, :]
    alive = jnp.where(radius > 0.0, 1.0, 0.0)
    for k in range(2):
        place = ext[k * 128:k * 128 + 32, :]
        speed = ext[(2 + k) * 128:(2 + k) * 128 + 32, :]
        speed2 = speed + step * (inverse[...] * (force[k] + dr2[k]) - (alive if k == 0 else 0.0))
        place2 = (place + step * speed2) * 0.0625
        for j in range(2):
            part[k, pl.ds(j, 16, stride=2), :] = place2[j * 16:(j + 1) * 16]
            part[2 + k, pl.ds(j, 16, stride=2), :] = speed2[j * 16:(j + 1) * 16]
    gas_step_update(gas, visc, gr, gc, dv, tot, rate, out)


CONTACT_SCRATCH = [
    pltpu.SMEM((128, 128), jnp.int32),
    pltpu.VMEM((128, 128), jnp.int32),
    pltpu.VMEM((128 * STRIDE, 128), F32),
    pltpu.VMEM((2, 1408, 128), F32),
    pltpu.VMEM((2, 64, 640), BF16),
    pltpu.VMEM((512, 128), F32),
]


def general(gas, visc, pos, vel, rad, coef, counts_t, pattern_t, idx, frac):

    def shapes(*dims):
        return [jax.ShapeDtypeStruct(d, F32) for d in dims]

    st, gp, mx = pl.pallas_call(
        prep_kernel,
        out_shape=shapes((8, 32, 128), (8, 32, 128), (8, 128)),
        in_specs=[VMEM_SPEC] * 5 + [SMEM_SPEC],
        out_specs=[VMEM_SPEC] * 3,
        name="prepare",
    )(gas, visc, pos, vel, rad, counts_t)
    ext, gv, rate, gr, gc = exchange(True, st, gp, mx, gas)
    st2, dp, tot, dr2, inverse = pl.pallas_call(
        first_kernel,
        out_shape=shapes((8, 32, 128), (8, 32, 128), (8, 128), (2, 32, 128), (32, 128)),
        in_specs=[VMEM_SPEC] * 6 + [SMEM_SPEC],
        out_specs=[VMEM_SPEC] * 5,
        scratch_shapes=CONTACT_SCRATCH + [pltpu.VMEM((2, 32, 128), F32), pltpu.SemaphoreType.DMA],
        name="first_substep",
    )(ext.reshape(1024, 128), gv, rate, idx, frac, coef, pattern_t)
    ext2, dv, total = exchange(False, st2, dp, tot)
    part, out = pl.pallas_call(
        second_kernel,
        out_shape=shapes((4, 32, 128), (2, 32, 256)),
        in_specs=[VMEM_SPEC] * 10 + [SMEM_SPEC],
        out_specs=[VMEM_SPEC] * 2,
        scratch_shapes=CONTACT_SCRATCH + [pltpu.SemaphoreType.DMA],
        name="second_substep",
    )(ext2.reshape(1024, 128), dv, total, rate, dr2, inverse, gas, visc, gr, gc, pattern_t)
    return part, out


EDGE_BASE, CORNER_BASE, WINDOW_ROWS = 48, 192, 256
CORNER = 16
WINDOWS = ((-1, 0), (1, 0), (0, -1), (0, 1), (-1, -1), (-1, 1), (1, -1), (1, 1))
NEAR = ((1.82, 0.0), (2.25, 0.43))
EDGE = 40
EARLY = 12


def fused_kernel(*refs):
    inputs, (part, out, flag, pat_copy, counts_copy), refs = refs[:10], refs[10:15], refs[15:]
    gas, visc, pos, vel, rad, coef, idx, frac, pat, counts = refs[:10]
    (in_sem, ext, ext2, gp, gv, dp, dv, gr, gc, mb, mv, sb, sv, rk, qs, qw, rhs, frc, itp, wts, wx, wz,
     hs, hr, ps, pr, rs, rr, es, er) = refs[10:]
    loads = [pltpu.make_async_copy(a, b, in_sem.at[n]) for n, (a, b) in enumerate(zip(inputs, refs[:10]))]
    for c in loads:
        c.start()
    ax, al, g = lax.axis_index("across"), lax.axis_index("along"), lax.axis_index("gas")

    def around(value, size):
        return value - jnp.where(value >= size, size, 0)

    up, down = around(al + 1, N_ALONG), around(al + N_ALONG - 1, N_ALONG)
    first_g, last_g = g == 0, g == N_GAS - 1
    has_left = jnp.logical_or(ax > 0, g > 0)
    has_right = jnp.logical_or(ax < N_ACROSS - 1, g < N_GAS - 1)
    left = (jnp.maximum(ax - jnp.where(first_g, 1, 0), 0), jnp.where(first_g, N_GAS - 1, g - 1))
    right = (jnp.minimum(ax + jnp.where(last_g, 1, 0), N_ACROSS - 1), jnp.where(last_g, 0, g + 1))

    def device(a=ax, l=al, y=g):
        return {"across": a, "along": l, "gas": y}

    def col(side, along):
        return device(a=side[0], l=along, y=side[1])

    def peer_id(axis, index):
        return device(**{{"across": "a", "along": "l", "gas": "y"}[axis]: index})

    after = device(l=jnp.where(last_g, up, al), y=jnp.where(last_g, 0, g + 1))
    before = device(l=jnp.where(first_g, down, al), y=jnp.where(first_g, N_GAS - 1, g - 1))

    barrier = pltpu.get_barrier_semaphore()

    def greet(target):
        pl.semaphore_signal(barrier, inc=1, device_id=target, device_id_type=MESH_ID)

    for k in range(1, N_ALONG):
        greet(device(l=around(al + k, N_ALONG)))
    for k in range(1, N_ACROSS):
        greet(device(a=around(ax + k, N_ACROSS)))
    for k in range(1, N_GAS):
        greet(device(y=around(g + k, N_GAS)))
    greet(after)
    greet(before)
    expect = N_ACROSS + N_GAS + N_ALONG - 3 + 2

    @pl.when(has_left)
    def _():
        for along in (down, al, up):
            greet(col(left, along))

    @pl.when(has_right)
    def _():
        for along in (down, al, up):
            greet(col(right, along))

    for c in loads:
        c.wait()
    rate = jnp.abs(gas[0]) + jnp.abs(gas[1]) + 4.0 * visc[...]
    top = jnp.max(jnp.max(rate, axis=1, keepdims=True), axis=0, keepdims=True)
    mv[0] = jnp.broadcast_to(top, (8, 128))
    lane = iota((16, 128), 1)
    for d in range(N_GAS):
        blk = slice((d // 4) * 128, (d // 4) * 128 + 128)
        off = (d % 4) * 32
        for k in range(2):
            low = gas[k, 0:16, blk]
            high = gas[k, 16:32, blk]
            low = pltpu.roll(low, (128 - off) % 128, 1) if off else low
            shift = (160 - off) % 128
            high = pltpu.roll(high, shift, 1) if shift else high
            piece = jnp.where(lane < 32, low, high)
            gp[d, k * 16:(k + 1) * 16, :] = jnp.where(lane < 64, piece, pltpu.roll(piece, 64, 1))
    row32 = iota((32, 128), 0)
    cnt = jnp.zeros((32, 128), jnp.int32)
    for j in range(2):
        for i in range(16):
            cnt = jnp.where(row32 == j * 16 + i, counts[j, i], cnt)
    ext[0, 0:32, :], ext[1, 0:32, :] = by_column(pos, 0) * 16.0, by_column(pos, 1) * 16.0
    ext[2, 0:32, :], ext[3, 0:32, :] = by_column(vel, 0), by_column(vel, 1)
    ext[4, 0:32, :] = jnp.where(iota((32, 128), 1) < cnt, by_column(rad), DEAD)

    def dots(e, low, high):
        e[5, low:high, :] = e[0, low:high, :] * e[2, low:high, :] + e[1, low:high, :] * e[3, low:high, :]

    dots(ext, 0, 32)
    for e in (ext, ext2):
        @pl.when(jnp.logical_not(has_left))
        def _():
            e[:, 32:48, :] = jnp.zeros((8, 16, 128), F32)
            e[:, 64:72, :] = jnp.zeros((8, 8, 128), F32)
            e[:, 96:104, :] = jnp.zeros((8, 8, 128), F32)

        @pl.when(jnp.logical_not(has_right))
        def _():
            e[:, 48:64, :] = jnp.zeros((8, 16, 128), F32)
            e[:, 88:96, :] = jnp.zeros((8, 8, 128), F32)
            e[:, 120:128, :] = jnp.zeros((8, 8, 128), F32)

    @pl.when(ax == 0)
    def _():
        gc[0] = jnp.zeros((2, 32, 128), F32)

    @pl.when(ax == N_ACROSS - 1)
    def _():
        gc[1] = jnp.zeros((2, 32, 128), F32)

    sides = jnp.where(has_left, 3, 0) + jnp.where(has_right, 3, 0)
    pl.semaphore_wait(barrier, expect + sides)

    def remote(src, dst, send, recv, target):
        return pltpu.make_async_remote_copy(
            src_ref=src, dst_ref=dst, send_sem=send, recv_sem=recv,
            device_id=target, device_id_type=MESH_ID,
        )

    axes = (("across", ax, N_ACROSS), ("gas", g, N_GAS), ("along", al, N_ALONG))

    def reduce_copies(which, phase):
        slots, value = ((mb, mv), (sb, sv))[which]
        axis, me, size = axes[phase]
        return [remote(value.at[phase], slots.at[phase, me], rs.at[which, phase, k], rr.at[which, phase, k],
                       peer_id(axis, around(me + k, size))) for k in range(1, size)]

    def reduce_go(which, phase, copies):
        slots, value = ((mb, mv), (sb, sv))[which]
        for c in copies:
            c.start()
        slots[phase, axes[phase][1]] = value[phase]

    def reduce_start(which, phase):
        out = reduce_copies(which, phase)
        reduce_go(which, phase, out)
        return out

    def reduce_end(which, phase, copies):
        slots, value = ((mb, mv), (sb, sv))[which]
        size = axes[phase][2]
        for c in copies:
            c.wait_recv()
        total = slots[phase, 0]
        for k in range(1, size):
            total = total + slots[phase, k] if which else jnp.maximum(total, slots[phase, k])
        value[phase + 1] = total
        for c in copies:
            c.wait_send()

    def halo_start(which):
        e, attrs = ((ext, 5), (ext2, 5))[which]

        def halo(c, src_row, size, dst_row, target):
            return remote(e.at[pl.ds(0, attrs), pl.ds(src_row, size)],
                          e.at[pl.ds(0, attrs), pl.ds(dst_row, size)], hs.at[which, c], hr.at[which, c], target)

        lefts = [halo(0, 0, 16, 48, col(left, al)),
                 halo(1, 8, 8, 64 + 24, col(left, up)),
                 halo(2, 0, 8, 96 + 24, col(left, down))]
        rights = [halo(3, 16, 16, 32, col(right, al)),
                  halo(4, 24, 8, 64, col(right, up)),
                  halo(5, 16, 8, 96, col(right, down))]
        rows = [halo(6, 8, 8, 64 + 8, device(l=up)),
                halo(7, 24, 8, 64 + 16, device(l=up)),
                halo(8, 0, 8, 96 + 8, device(l=down)),
                halo(9, 16, 8, 96 + 16, device(l=down))]

        @pl.when(has_left)
        def _():
            for c in lefts:
                c.start()

        @pl.when(has_right)
        def _():
            for c in rights:
                c.start()

        for c in rows:
            c.start()
        return lefts, rights, rows

    def halo_end(copies):
        lefts, rights, rows = copies
        for c in rows:
            c.wait()

        @pl.when(has_left)
        def _():
            for c in lefts:
                c.wait_send()
            for c in rights:
                c.wait_recv()

        @pl.when(has_right)
        def _():
            for c in rights:
                c.wait_send()
            for c in lefts:
                c.wait_recv()

    def pieces_start(which):
        src, dst = ((gp, gv), (dp, dv))[which]
        out = []
        for k in range(1, N_GAS):
            peer = around(g + k, N_GAS)
            c = remote(src.at[peer], dst.at[g], ps.at[which, k], pr.at[which, k], device(y=peer))
            c.start()
            out.append(c)
        dst[g] = src[g]
        return out

    phase = reduce_start(0, 0)
    halos = halo_start(0)
    pieces = pieces_start(0)
    edges = [remote(gas.at[:, pl.ds(24, 8)], gr.at[0], es.at[0], er.at[0], after),
             remote(gas.at[:, pl.ds(0, 8)], gr.at[1], es.at[1], er.at[1], before)]
    for c in edges:
        c.start()
    to_right = remote(gas.at[:, :, pl.ds(128, 128)], gc.at[0], es.at[2], er.at[2],
                      device(a=jnp.minimum(ax + 1, N_ACROSS - 1)))
    to_left = remote(gas.at[:, :, pl.ds(0, 128)], gc.at[1], es.at[3], er.at[3],
                     device(a=jnp.maximum(ax - 1, 0)))

    @pl.when(ax < N_ACROSS - 1)
    def _():
        to_right.start()

    @pl.when(ax > 0)
    def _():
        to_left.start()

    lists = [pltpu.make_async_copy(pat, pat_copy, in_sem.at[10]), pltpu.make_async_copy(counts, counts_copy, in_sem.at[11])]
    for c in lists:
        c.start()

    slot_row = iota((48, 128), 0)
    slots = (jnp.where(slot_row < EDGE, slot_row, -5).astype(F32),
             jnp.where(slot_row < 32, slot_row, jnp.where(slot_row < 40, -5, slot_row - 8)).astype(F32))
    attr_row = iota((8, 128), 0)
    zero8 = jnp.zeros((8, 128), F32)
    one_tail = jnp.concatenate([zero8, jnp.ones((24, 128), F32)], axis=0)
    flat = (ext.reshape(1024, 128), ext2.reshape(1024, 128))
    eye = jnp.where(iota((128, 128), 0) == iota((128, 128), 1), 1.0, 0.0).astype(BF16)
    before_slot = jnp.where(iota((128, 128), 0) < iota((128, 128), 1), 1.0, 0.0).astype(BF16)

    def rank(which, low, high, windows=range(8)):
        e = (ext, ext2)[which]
        reach, _ = NEAR[which]
        z, x, live = e[0, low:high, :], e[1, low:high, :], e[4, low:high, :] > 0.0

        def flags(cond):
            return jnp.where(cond & live, 1.0, 0.0)

        lz, hz, lx, hx = flags(z < reach), flags(z > 16.0 - reach), flags(x < reach), flags(x > 16.0 - reach)
        member = [hz, lz, hx, lx, hz * hx, hz * lx, lz * hx, lz * lx]
        size = high - low
        places = jnp.dot(jnp.concatenate([member[w] for w in windows], axis=0).astype(BF16), before_slot,
                         preferred_element_type=F32)
        lost = jnp.zeros((size, 128), F32)
        for order, w in enumerate(windows):
            place = places[order * size:(order + 1) * size]
            rk[w, low:high, :] = jnp.where(member[w] > 0.0, place, -1.0)
            lost = lost + jnp.where(place >= (EDGE if w < 4 else CORNER), member[w], 0.0)
        return lost

    def parts(which, row):
        block = flat[which][pl.ds(row, 8, stride=128), :]
        return split3(jnp.where(attr_row < 6, block, 0.0))

    def stacked(hi, mid, lo, own=False):
        shifted = jnp.where(attr_row < 2, pltpu.roll(hi, 6, 0), jnp.where(attr_row < 4, mid, 0.0))
        return jnp.concatenate([hi, mid, lo, hi, mid, zero8 if own else shifted, one_tail], axis=0)

    def partner(v):
        return jnp.where(attr_row < 2, pltpu.roll(v, 6, 0), jnp.where(attr_row < 4, pltpu.roll(v, 2, 0), 0.0))

    def window_rows(which, row, rows, windows):
        sizes = [48 if w < 4 else CORNER for w in windows]
        place = jnp.concatenate(
            [(slots[w & 1 if w < 4 else 0][0:n] == rk[w, pl.ds(row, 1), :]).astype(F32) for w, n in zip(windows, sizes)], axis=0)
        turned = lax.dot_general(place.astype(BF16), rows, (((1,), (1,)), ((), ())), preferred_element_type=F32)
        turned = turned.astype(BF16)
        at = 0
        for w, n in zip(windows, sizes):
            start = row * WINDOW_ROWS + (w * EDGE_BASE if w < 4 else CORNER_BASE + (w - 4) * CORNER)
            if not isinstance(row, int):
                start = pl.multiple_of(start, 16)
            qw[pl.ds(start, n), 0:80] = turned[at:at + n]
            at += n

    def own_tiles(which):
        def some(step, carry):
            for u in range(8):
                row = step * 8 + u
                hi, mid, lo = parts(which, row)
                turned = stacked(hi, mid, lo, True).T
                rows = stacked(hi, mid, lo).astype(BF16)
                qs[pl.ds(pl.multiple_of(row * 128, 128), 128), 0:80] = turned.astype(BF16)
                window_rows(which, row, rows, range(8))
                with_hi, with_mid = 2.0 * partner(hi), 2.0 * partner(mid)
                own = jnp.where(attr_row == 5, -2.0, with_hi)
                marked = 16.0 * jnp.where(attr_row < 2, with_hi, jnp.where(attr_row < 4, pltpu.roll(with_mid, 2, 0), 0.0))
                columns = []
                for a, scale in ((0, 1.0), (1, 1.0), (5, -2.0), (4, 1.0)):
                    ends = [jnp.where(attr_row == a, v * scale, 0.0) for v in (hi, mid, lo)]
                    if a == 5:
                        start = [own, own, jnp.where(attr_row == 5, -2.0, 0.0), with_mid, with_mid,
                                 jnp.where(attr_row < 4, -32.0, 0.0), marked]
                    else:
                        one = jnp.where(attr_row == a, 1.0 if a == 4 else -1.0, 0.0)
                        start = [one, one, one, zero8, zero8, zero8,
                                 jnp.where(attr_row == a, DEAD if a == 4 else -16.0, 0.0)]
                    columns.append(jnp.concatenate(start + ends, axis=0))
                rhs[row] = jnp.concatenate(columns, axis=1).astype(BF16)
            return carry
        lax.fori_loop(0, 4, some, 0)

    def halo_tile(which, row, windows):
        hi, mid, lo = parts(which, row)
        window_rows(which, row, stacked(hi, mid, lo).astype(BF16), windows)

    def halo_tiles(which, beside=None):
        dots((ext, ext2)[which], 32, 128)
        rank(which, 32, 48, (2, 4, 6))
        rank(which, 48, 64, (3, 5, 7))
        rank(which, 64, 96, (0, 4, 5))
        rank(which, 96, 128, (1, 6, 7))

        def some(step, carry):
            if beside is not None:
                beside(step)
            for u in range(4):
                halo_tile(which, 32 + step * 4 + u, (2, 4, 6))
                halo_tile(which, 48 + step * 4 + u, (3, 5, 7))
            return carry
        lax.fori_loop(0, 4, some, 0)
        for c in range(4):
            halo_tile(which, 64 + 8 * c + 7, (0, 4, 5))
            halo_tile(which, 96 + 8 * c, (1, 6, 7))

    lane16 = iota((16, 128), 1)
    half = iota((16, 128), 0) < 8

    lost = rank(0, 0, 32)
    own_tiles(0)

    unlisted = jnp.where(lane16 == 52, 1.0, 0.0)

    def by_offset(low, di, dj, rest):
        lane = lane16 - low
        inside = (lane >= 0) & (lane < 4)
        return jnp.where(inside, jnp.where((lane & 1) == 0, float(di), float(dj)), rest)

    def contact_rows(first, last, own_part=True, border_part=True, ahead=None):

        def step(four, carry):
            if ahead is not None:
                pl.when(four == 1)(ahead)
            for u, j in ((0, 0), (0, 1), (1, 0), (1, 1), (2, 0), (2, 1), (3, 0), (3, 1)):
                i = four * 4 + u
                t = j * 16 + i
                right = rhs[t]

                def mark_of(n):
                    di, dj = OFFSETS[n]
                    base = by_offset(48, di, dj, 0.0)
                    return base + unlisted * (1 - pat[n, j, i]).astype(F32)

                def times(di, dj):
                    return by_offset(40, di, dj, 1.0).astype(BF16)

                def border(w):
                    di, dj = WINDOWS[w]
                    row = ext_row(i + di, j + dj)
                    n = 48 if w < 4 else CORNER
                    start = row * WINDOW_ROWS + (w * EDGE_BASE if w < 4 else CORNER_BASE + (w - 4) * CORNER)
                    block, factor = qw[pl.ds(pl.multiple_of(start, 16), n), :], times(di, dj)
                    return [block[c:c + 16] * factor for c in range(0, n, 16)], mark_of(3 * (di + 1) + dj + 1)

                def edges_of(w):
                    (one, mark1), (two, mark2) = border(w), border(w + 1)
                    both = one[2] + two[2] + jnp.where(half, mark1, mark2).astype(BF16)
                    mark1, mark2 = mark1.astype(BF16), mark2.astype(BF16)
                    return [one[0] + mark1, one[1] + mark1, two[0] + mark2, two[1] + mark2, both]

                def corner(w):
                    (block,), here = border(w)
                    return block + here.astype(BF16)

                groups = []
                if own_part:
                    own = qs[pl.ds(pl.multiple_of(t * 128, 128), 128), :]
                    here = mark_of(4).astype(BF16)
                    groups += [own[c:c + 16] + here for c in range(0, 128, 16)]
                if border_part:
                    groups += edges_of(0) + edges_of(2) + [corner(w) for w in range(4, 8)]
                got = jnp.dot(jnp.concatenate(groups, axis=0)[:, 0:80], right, preferred_element_type=F32)
                rz, rx = got[:, 0:128], got[:, 128:256]
                inv = lax.rsqrt(rz * rz + rx * rx + 0.0001)
                push = jnp.maximum(got[:, 384:512] * inv - 1.0, 0.0) * (40.0 + got[:, 256:384] * inv)
                count = got.shape[0] // 8
                fz = jnp.sum((push * rz).reshape(count, 8, 128), axis=0)
                fx = jnp.sum((push * rx).reshape(count, 8, 128), axis=0)
                at_z, at_x = pl.ds(pl.multiple_of(t * 8, 8), 8), pl.ds(pl.multiple_of(t * 8 + 256, 8), 8)
                if not own_part:
                    fz, fx = fz + frc[at_z, :], fx + frc[at_x, :]
                frc[at_z, :], frc[at_x, :] = fz, fx
            return carry
        lax.fori_loop(first // 4, last // 4, step, 0)

    def forces():
        return [sum(frc[pl.ds(k * 256 + r, 32, stride=8), :] for r in range(8)) for k in range(2)]

    phase_end = reduce_end
    index = idx[...]
    share_z = frac[0].astype(F32) / 1024.0
    share_x = frac[1].astype(F32) / 1024.0
    wts[0] = (index >> 4).astype(F32)
    wts[1] = (index & 15).astype(F32)
    wts[2], wts[3] = 1.0 - share_z, share_z
    for n, share in ((4, 1.0 - share_x), (6, share_x)):
        high = share.astype(BF16).astype(F32)
        wts[n], wts[n + 1] = high, share - high
    c64 = iota((64, 128), 0).astype(F32)
    r16 = iota((16, 128), 0).astype(F32)

    def weigh(r, t4, t):
        def get(n):
            return wts[n, pl.ds(r, 1), :]
        column, row = get(1) + (16.0 * t4), get(0)
        here, there = c64 == column, c64 == column + 1.0
        wx[t, 0:64, :] = jnp.where(here, get(4), jnp.where(there, get(6), 0.0)).astype(BF16)
        wx[t, 64:128, :] = jnp.where(here, get(5), jnp.where(there, get(7), 0.0)).astype(BF16)
        wz[t] = jnp.where(r16 == row, get(2), jnp.where(r16 == row + 1.0, get(3), 0.0))

    def some_weights(h, carry):
        for t in range(2):
            for j in range(2):
                weigh(4 * h + 2 * t + j, t * 2 + j, 4 * h + 2 * t + j)
        return carry

    lax.fori_loop(0, 8, some_weights, 0)
    contact_rows(0, EARLY, True, False)

    for c in pieces:
        c.wait()
    lane32 = iota((32, 128), 1)

    def sample(h):
        field = gv[h]
        high = field.astype(BF16).astype(F32)
        both = jnp.where(lane32 < 64, high, field - high).astype(BF16)
        for t in range(2):
            for j in range(2):
                r = 4 * h + 2 * t + j
                whi, wlo = wx[r, 0:64, :], wx[r, 64:128, :]
                right = jnp.concatenate([jnp.concatenate([whi, whi], axis=0),
                                         jnp.concatenate([wlo, wlo], axis=0)], axis=1)
                got = jnp.dot(both, right, preferred_element_type=F32)
                got = got[:, 0:128] + got[:, 128:256]
                for k in range(2):
                    itp[k, pl.ds(j * 16 + 2 * h + t, 1), :] = jnp.sum(
                        wz[r] * got[k * 16:(k + 1) * 16], axis=0, keepdims=True)

    def two_samples(step):
        sample(2 * step)
        sample(2 * step + 1)

    phase_end(0, 0, phase)
    max_phase = reduce_start(0, 1)
    halo_end(halos)
    halo_tiles(0, two_samples)

    last_phase = reduce_copies(0, 2)

    def pass_maximum():
        phase_end(0, 1, max_phase)
        reduce_go(0, 2, last_phase)

    contact_rows(0, EARLY, False, True, pass_maximum)
    contact_rows(EARLY, 16)
    drag = by_column(coef)
    radius = ext[4, 0:32, :]
    alive = jnp.where(radius > 0.0, 1.0, 0.0)
    inverse = jnp.where(radius > 0.0, 0.36 / (radius * radius), 0.0)
    force = forces()
    reach, slack = NEAR[1]
    longest = 0.2 / mv[0][0:1, :]
    bad, drags, pushes, borders, sums = lost, [], [], [], []
    for k in range(2):
        place, speed = ext[k, 0:32, :], ext[2 + k, 0:32, :]
        drag1 = drag * (itp[k] - speed)
        push = inverse * (force[k] + drag1) - (alive if k == 0 else 0.0)
        once, twice = longest * speed, longest * longest * push
        high = place + jnp.maximum(once, 0.0) + jnp.maximum(twice, 0.0)
        low = place + jnp.minimum(once, 0.0) + jnp.minimum(twice, 0.0)
        bad = bad + jnp.where((low >= -slack) & (high <= 16.0 + slack), 0.0, alive)
        borders.append((jnp.where(low < reach + 0.001, alive, 0.0), jnp.where(high > 15.999 - reach, alive, 0.0)))
        drags.append(drag1)
        pushes.append(push)
        sums += [alive * drag1, 0.5 * alive * drag * push]
    (lz, hz), (lx, hx) = borders
    for member, room in ((lz, EDGE), (hz, EDGE), (lx, EDGE), (hx, EDGE),
                         (lz * lx, CORNER), (lz * hx, CORNER), (hz * lx, CORNER), (hz * hx, CORNER)):
        bad = bad + jnp.where(jnp.sum(member, axis=1, keepdims=True) > room, 1.0, 0.0)
    message = zero8
    for row, v in ((0, sums[0]), (1, sums[2]), (2, bad), (3, sums[1]), (4, sums[3])):
        message = jnp.where(attr_row == row,
                            jnp.sum(jnp.sum(v, axis=1, keepdims=True), axis=0, keepdims=True), message)
    sv[0] = message
    phase = reduce_start(1, 0)
    phase_end(0, 2, last_phase)
    step = 0.2 / mv[3][0:1, :]
    for k in range(2):
        speed2 = ext[2 + k, 0:32, :] + step * pushes[k]
        ext2[k, 0:32, :] = ext[k, 0:32, :] + step * speed2
        ext2[2 + k, 0:32, :] = speed2
        drag2 = drag * (itp[k] - speed2)
        itp[k] = 0.5 * (alive * drags[k] + alive * drag2)
        itp[2 + k] = drag2
    ext2[4, 0:32, :] = radius
    dots(ext2, 0, 32)
    halos = halo_start(1)
    rank(1, 0, 32)

    def spread(h):
        total = jnp.zeros((64, 128), F32)
        for t in range(2):
            for j in range(2):
                r = 4 * h + 2 * t + j
                m0 = itp[0, pl.ds(j * 16 + 2 * h + t, 1), :]
                m1 = itp[1, pl.ds(j * 16 + 2 * h + t, 1), :]
                lhs = jnp.concatenate([wz[r] * m0, wz[r] * m1], axis=0)
                high = lhs.astype(BF16)
                low = (lhs - high.astype(F32)).astype(BF16)
                total = total + lax.dot_general(
                    jnp.concatenate([high, low], axis=0), wx[r],
                    (((1,), (1,)), ((), ())), preferred_element_type=F32)
        total = total[0:32] + total[32:64]
        dp[h] = total + pltpu.roll(total, 64, 1)

    lax.fori_loop(0, 8, lambda h, carry: (spread(h), carry)[1], 0)
    pieces = pieces_start(1)
    phase_end(1, 0, phase)
    sum_phase = reduce_start(1, 1)
    own_tiles(1)
    phase_end(1, 1, sum_phase)
    last_sum = reduce_start(1, 2)
    halo_end(halos)
    halo_tiles(1)

    contact_rows(0, 16)
    force = forces()
    step = 0.2 / mv[3][0:1, :]
    radius = ext2[4, 0:32, :]
    alive = jnp.where(radius > 0.0, 1.0, 0.0)
    inverse = jnp.where(radius > 0.0, 0.36 / (radius * radius), 0.0)
    for k in range(2):
        speed = ext2[2 + k, 0:32, :]
        speed2 = speed + step * (inverse * (force[k] + itp[2 + k]) - (alive if k == 0 else 0.0))
        place2 = (ext2[k, 0:32, :] + step * speed2) * 0.0625
        for j in range(2):
            part[k, pl.ds(j, 16, stride=2), :] = place2[j * 16:(j + 1) * 16]
            part[2 + k, pl.ds(j, 16, stride=2), :] = speed2[j * 16:(j + 1) * 16]
    for c in edges + lists:
        c.wait()

    @pl.when(ax < N_ACROSS - 1)
    def _():
        to_right.wait_send()
        to_left.wait_recv()

    @pl.when(ax > 0)
    def _():
        to_left.wait_send()
        to_right.wait_recv()

    for c in pieces:
        c.wait()
    phase_end(1, 2, last_sum)
    total = sv[3]
    flag[...] = total[2:3, 0:1]
    sv[3] = jnp.where(attr_row == 0, total[0:1] - step * total[3:4], total[1:2] - step * total[4:5])
    gas_step_update(gas, visc, gr, gc, dv, sv.at[3], mv.at[3], out)


def fused(gas, visc, pos, vel, rad, coef, counts_t, pattern_t, idx, frac):
    dma = pltpu.SemaphoreType.DMA
    return pl.pallas_call(
        fused_kernel,
        out_shape=[jax.ShapeDtypeStruct((4, 32, 128), F32), jax.ShapeDtypeStruct((2, 32, 256), F32),
                   jax.ShapeDtypeStruct((1, 1), F32), jax.ShapeDtypeStruct((9, 2, 16), jnp.int32),
                   jax.ShapeDtypeStruct((2, 16), jnp.int32)],
        in_specs=[pl.BlockSpec(memory_space=pltpu.HBM)] * 10,
        out_specs=[VMEM_SPEC] * 3 + [pl.BlockSpec(memory_space=pltpu.HBM)] * 2,
        scratch_shapes=[
            pltpu.VMEM((2, 32, 256), F32), pltpu.VMEM((32, 256), F32),
            pltpu.VMEM((2, 32, 128), F32), pltpu.VMEM((2, 32, 128), F32), pltpu.VMEM((32, 128), F32),
            pltpu.VMEM((32, 128), F32), pltpu.VMEM((32, 128), jnp.int32), pltpu.VMEM((2, 32, 128), jnp.int32),
            pltpu.SMEM((9, 2, 16), jnp.int32), pltpu.SMEM((2, 16), jnp.int32), dma((12,)),
            pltpu.VMEM((8, 128, 128), F32), pltpu.VMEM((8, 128, 128), F32),
            pltpu.VMEM((8, 32, 128), F32), pltpu.VMEM((8, 32, 128), F32),
            pltpu.VMEM((8, 32, 128), F32), pltpu.VMEM((8, 32, 128), F32),
            pltpu.VMEM((2, 2, 8, 256), F32), pltpu.VMEM((2, 2, 32, 128), F32),
            pltpu.VMEM((3, 8, 8, 128), F32), pltpu.VMEM((4, 8, 128), F32),
            pltpu.VMEM((3, 8, 8, 128), F32), pltpu.VMEM((4, 8, 128), F32),
            pltpu.VMEM((8, 128, 128), F32), pltpu.VMEM((32 * 128, 128), BF16),
            pltpu.VMEM((128 * WINDOW_ROWS, 128), BF16), pltpu.VMEM((32, 80, 512), BF16),
            pltpu.VMEM((512, 128), F32), pltpu.VMEM((4, 32, 128), F32), pltpu.VMEM((8, 32, 128), F32),
            pltpu.VMEM((32, 128, 128), BF16), pltpu.VMEM((32, 16, 128), F32),
            dma((2, 10)), dma((2, 10)), dma((2, 8)), dma((2, 8)), dma((2, 3, 8)), dma((2, 3, 8)),
            dma((4,)), dma((4,)),
        ],
        compiler_params=pltpu.CompilerParams(collective_id=2, has_side_effects=True),
        name="interval",
    )(gas, visc, pos, vel, rad, coef, idx, frac, pattern_t, counts_t)


def body(gas, visc, pos, vel, rad, coef, counts, pattern, idx, frac):
    pos, vel, frac = (x.reshape(2, 32, 128) for x in (pos, vel, frac))
    rad, coef, idx = (x.reshape(32, 128) for x in (rad, coef, idx))
    args = (gas, visc, pos, vel, rad, coef, counts.T, pattern.transpose(2, 1, 0), idx, frac)
    part, out, flag, pattern_t, counts_t = fused(*args)
    args = args[:6] + (counts_t, pattern_t) + args[8:]
    part, out = lax.cond(flag[0, 0] > 0.0, lambda p, o: tuple(general(*args)), lambda p, o: (p, o), part, out)
    return part.reshape(4, 16, 2, 128), out


def solution(mesh):
    return jax.shard_map(
        body,
        mesh=mesh,
        in_specs=(
            P(None, ALONG_GAS, "across"),
            P(ALONG_GAS, "across"),
            P(None, "along", ACROSS_GAS, None),
            P(None, "along", ACROSS_GAS, None),
            P("along", ACROSS_GAS, None),
            P("along", ACROSS_GAS, None),
            P("along", ACROSS_GAS),
            P("along", ACROSS_GAS, None),
            P("along", ACROSS_GAS, None),
            P(None, "along", ACROSS_GAS, None),
        ),
        out_specs=(P(None, "along", ACROSS_GAS, None), P(None, ALONG_GAS, "across")),
        check_vma=False,
    )
```
